32 devices in a mesh: ctx: 8 (over z, x), wsh: 4 (over y, core).
Axes of the slice: x: 2, y: 2, z: 4, core: 2. Of those that a mesh axis runs over, the one named last changes fastest.
Arguments:
- tokens: bfloat16 [4, 1536, 768], P('wsh', 'ctx'), may hold values from -6 to 6
- doc_lengths: int32 [4, 4], P('wsh'), may hold values from 1 to 768, 1536 in all within a row
- out_grad: bfloat16 [4, 1536, 768], P('wsh', 'ctx'), may hold values from -6 to 6
- norm1_gain: bfloat16 [768], P('wsh'), may hold values from 0.25 to 1.75
- norm1_bias: bfloat16 [768], P('wsh'), may hold values from -1.75 to 1.75
- w_query: bfloat16 [768, 768], P('wsh'), may hold values from -0.21875 to 0.21875
- b_query: bfloat16 [768], P('wsh'), may hold values from -1.75 to 1.75
- w_key: bfloat16 [768, 768], P('wsh'), may hold values from -0.21875 to 0.21875
- w_value: bfloat16 [768, 768], P('wsh'), may hold values from -0.21875 to 0.21875
- b_value: bfloat16 [768], P('wsh'), may hold values from -1.75 to 1.75
- w_out: bfloat16 [768, 768], P('wsh'), may hold values from -1.75 to 1.75
- b_out: bfloat16 [768], P('wsh'), may hold values from -1.75 to 1.75
- norm2_gain: bfloat16 [768], P('wsh'), may hold values from 0.25 to 1.75
- norm2_bias: bfloat16 [768], P('wsh'), may hold values from -1.75 to 1.75
- w_up: bfloat16 [768, 3072], P('wsh'), may hold values from -0.21875 to 0.21875
- b_up: bfloat16 [3072], P('wsh'), may hold values from -1.75 to 1.75
- w_down: bfloat16 [3072, 768], P('wsh'), may hold values from -0.109375 to 0.109375
- b_down: bfloat16 [768], P('wsh'), may hold values from -1.75 to 1.75
Outputs:
- layer_out: bfloat16 [4, 1536, 768], P('wsh', 'ctx')
- input_grad: bfloat16 [4, 1536, 768], P('wsh', 'ctx')
- grad_norm1_gain: float32 [768], P('wsh')
- grad_norm1_bias: float32 [768], P('wsh')
- grad_w_query: float32 [768, 768], P('wsh')
- grad_b_query: float32 [768], P('wsh')
- grad_w_key: float32 [768, 768], P('wsh')
- grad_w_value: float32 [768, 768], P('wsh')
- grad_b_value: float32 [768], P('wsh')
- grad_w_out: float32 [768, 768], P('wsh')
- grad_b_out: float32 [768], P('wsh')
- grad_norm2_gain: float32 [768], P('wsh')
- grad_norm2_bias: float32 [768], P('wsh')
- grad_w_up: float32 [768, 3072], P('wsh')
- grad_b_up: float32 [3072], P('wsh')
- grad_w_down: float32 [3072, 768], P('wsh')
- grad_b_down: float32 [768], P('wsh')
The draws below stay inside these ranges and needn't reach their ends.
Inputs may be any that keep to these rules, and one draw needn't show every extreme that they name: `doc_lengths`: in each stream the lengths add up to 1536.
All inputs are finite; a program needn't handle non-finite values.
Results may differ from the reference program's by a relative error of at most 0.015.
Values may be sent and summed in bfloat16 or wider, within the bound.
A program may use at most 320 MiB of HBM per device.

```python
import math
import jax
import jax.numpy as jnp
import numpy as np
from jax import lax

D = 768
HEADS = 12
HEAD_DIM = 64
FF = 3072
SEQ = 1536
STREAMS = 4
DOC_MAX = 768
NDOC = 4


def block_levels(own_key, shape, pieces, smallest, top_value):
    factor_of, own = 1.0, jax.random.fold_in(own_key, 6)
    for axis_at, parts in pieces:
        heights = jnp.exp(jax.random.uniform(jax.random.fold_in(own, axis_at), (parts,), jnp.float32, smallest / len(pieces), top_value / len(pieces)))
        factor_of = factor_of * jnp.repeat(heights, shape[axis_at] // parts).reshape([-1 if axis == axis_at else 1 for axis in range(len(shape))])
    return factor_of


def length_profile(number_of, total, most, lean):
    weights = [(1 << 20) // math.isqrt(standing ** lean) + 1 for standing in range(2, number_of + 1)]
    rest, holding = total - most - (number_of - 1), [1] * (number_of - 1)
    while rest > 0:
        movable = [i for i in range(number_of - 1) if holding[i] < most]
        pool, left = sum([weights[i] for i in movable]), rest
        for i in movable:
            more = min(most - holding[i], max(1, left * weights[i] // pool), rest)
            holding[i] = holding[i] + more
            rest = rest - more
    return np.array([most] + holding)


def ragged_sizes(stream_key, count, total, most, slope):
    if count == 2:
        one = jax.random.randint(stream_key, (), max(1, total - most), min(most, total - 1) + 1)
        return jnp.stack([one, total - one])
    lengths = jnp.asarray(length_profile(count, total, most, slope), jnp.int32)
    pairs = (count - 1) // 2
    giver, receiver = lengths[1:1 + 2 * pairs:2], lengths[2:2 + 2 * pairs:2]
    margin = jnp.minimum(giver - 1, most - receiver)
    passed = jax.random.randint(jax.random.fold_in(stream_key, 1), (pairs,), 0, 1 << 20) % (margin + 1)
    lengths = lengths.at[1:1 + 2 * pairs:2].set(giver - passed).at[2:2 + 2 * pairs:2].set(receiver + passed)
    return lengths[jax.random.permutation(jax.random.fold_in(stream_key, 2), count)]


def gaussian(rng, extent, spread, limit, split=(), held_as=jnp.bfloat16):
    values = jax.random.normal(rng, extent, jnp.float32) * spread
    if len(split) > 0:
        values = block_levels(rng, extent, split, -0.22, 0.18) * values
    return jnp.clip(values, min=-limit, max=limit).astype(held_as)


def setup_inputs(seed: int = 0) -> dict:
    seeds = jax.random.split(jax.random.key(seed), 19)
    tokens = gaussian(seeds[0], (STREAMS, SEQ, D), 1.0, 6.0, ((0, 4), (1, 8)))
    doc_lengths = jax.vmap(lambda own: ragged_sizes(own, NDOC, SEQ, DOC_MAX, 2))(jax.random.split(seeds[1], STREAMS)).reshape((STREAMS, NDOC)).astype(jnp.int32)
    out_grad = gaussian(seeds[2], (STREAMS, SEQ, D), 1.0, 6.0, ((0, 4), (1, 8)))
    norm1_gain = jnp.clip(1.0 + 0.15 * jax.random.normal(seeds[3], (D,), jnp.float32), 0.25, 1.75).astype(jnp.bfloat16)
    norm1_bias = gaussian(seeds[4], (D,), 0.3, 1.75, ((0, 4),))
    w_query = gaussian(seeds[5], (D, D), D ** -0.5, 0.21875, ((0, 4),))
    b_query = gaussian(seeds[6], (D,), 0.3, 1.75, ((0, 4),))
    w_key = gaussian(seeds[7], (D, D), D ** -0.5, 0.21875, ((0, 4),))
    w_value = gaussian(seeds[8], (D, D), D ** -0.5, 0.21875, ((0, 4),))
    b_value = gaussian(seeds[9], (D,), 0.3, 1.75, ((0, 4),))
    w_out = gaussian(seeds[10], (D, D), (max(1, D // 64)) ** -0.5, 1.75, ((0, 4),))
    b_out = gaussian(seeds[11], (D,), 0.3, 1.75, ((0, 4),))
    norm2_gain = jnp.clip(1.0 + 0.15 * jax.random.normal(seeds[12], (D,), jnp.float32), 0.25, 1.75).astype(jnp.bfloat16)
    norm2_bias = gaussian(seeds[13], (D,), 0.3, 1.75, ((0, 4),))
    w_up = gaussian(seeds[14], (D, FF), D ** -0.5, 0.21875, ((0, 4),))
    b_up = gaussian(seeds[15], (FF,), 0.3, 1.75, ((0, 4),))
    w_down = gaussian(seeds[16], (FF, D), FF ** -0.5, 0.109375, ((0, 4),))
    b_down = gaussian(seeds[17], (D,), 0.3, 1.75, ((0, 4),))
    return {"tokens": tokens, "doc_lengths": doc_lengths, "out_grad": out_grad, "norm1_gain": norm1_gain, "norm1_bias": norm1_bias, "w_query": w_query, "b_query": b_query, "w_key": w_key, "w_value": w_value, "b_value": b_value, "w_out": w_out, "b_out": b_out, "norm2_gain": norm2_gain, "norm2_bias": norm2_bias, "w_up": w_up, "b_up": b_up, "w_down": w_down, "b_down": b_down}


@jax.custom_vjp
def low(v):
    return lax.optimization_barrier(v.astype(jnp.bfloat16)).astype(jnp.float32)

@jax.custom_vjp
def low_back(v):
    return v

def low_keep(v):
    return (low(v), None)

def low_pass(kept, grad):
    return (grad,)

def back_keep(v):
    return (v, None)

def back_low(kept, grad):
    return (low(grad),)
low.defvjp(low_keep, low_pass)
low_back.defvjp(back_keep, back_low)
EPS = 1e-06
HIGHEST = lax.Precision.HIGHEST

def both_ways(inputs):
    return low(low_back(inputs))

def norm_rows(inputs, norm_gain, norm_bias):
    row_mean = lax.optimization_barrier(jnp.mean(inputs, axis=-1, keepdims=True))
    centred = inputs - row_mean
    variance = lax.optimization_barrier(jnp.mean(centred * centred, axis=-1, keepdims=True))
    return centred * lax.rsqrt(variance + EPS) * norm_gain + norm_bias

def dot_plain(left, right):
    return jnp.dot(left, right, precision=HIGHEST, preferred_element_type=jnp.float32)

def attention(queries, key_rows, values, doc_ids):
    query_rows = math.gcd(SEQ, 512)
    score_scale = HEAD_DIM ** (-0.5)
    key_heads = key_rows.reshape(SEQ, HEADS, HEAD_DIM)
    value_heads = values.reshape(SEQ, HEADS, HEAD_DIM)

    def one_block(block_pair):
        query_block, id_block = block_pair
        query_heads = query_block.reshape(query_rows, HEADS, HEAD_DIM)
        raw_scores = jnp.einsum('qhd,khd->hqk', query_heads, key_heads, precision=HIGHEST) * score_scale
        scores = low_back(raw_scores)
        same_doc = (id_block[:, None] == doc_ids[None, :])[None]
        scores = jnp.where(same_doc, scores, -jnp.inf)
        attn_prob = jax.nn.softmax(scores, axis=-1)
        mixture = jnp.einsum('hqk,khd->qhd', low(attn_prob), value_heads, precision=HIGHEST)
        return mixture.reshape(query_rows, D)
    blocks = lax.map(jax.checkpoint(one_block), (queries.reshape(SEQ // query_rows, query_rows, D), doc_ids.reshape(SEQ // query_rows, query_rows)))
    return blocks.reshape(SEQ, D)

def stream_layer(stream_rows, doc_ids, params):
    gain_one, bias_one, query_w, query_b, key_w, value_w, value_b, out_w, out_b, gain_two, bias_two, up_w, up_b, down_w, down_b = params
    normed_one = low(norm_rows(stream_rows, gain_one, bias_one))
    queries = both_ways(dot_plain(normed_one, query_w) + query_b)
    key_rows = both_ways(dot_plain(normed_one, key_w))
    values = both_ways(dot_plain(normed_one, value_w) + value_b)
    attended = both_ways(attention(queries, key_rows, values, doc_ids))
    middle = stream_rows + low_back(dot_plain(attended, out_w) + out_b)
    normed_two = low(norm_rows(middle, gain_two, bias_two))
    hidden = low_back(dot_plain(normed_two, up_w) + up_b)
    active = low(jax.nn.gelu(hidden, approximate=True))
    return middle + low_back(dot_plain(active, down_w) + down_b)

def whole_layer(inputs, doc_ids, params):
    return lax.map(lambda stream_pair: stream_layer(stream_pair[0], stream_pair[1], params), (inputs, doc_ids))

def reference(tokens, doc_lengths, out_grad, norm1_gain, norm1_bias, w_query, b_query, w_key, w_value, b_value, w_out, b_out, norm2_gain, norm2_bias, w_up, b_up, w_down, b_down):
    doc_ends = jnp.cumsum(doc_lengths, axis=-1).astype(jnp.int32)
    positions = jnp.arange(SEQ, dtype=jnp.int32)
    doc_ids = lax.optimization_barrier(jnp.sum((positions[None, :, None] >= doc_ends[:, None, :]).astype(jnp.int32), axis=-1))
    params = (norm1_gain.astype(jnp.float32), norm1_bias.astype(jnp.float32), w_query.astype(jnp.float32), b_query.astype(jnp.float32), w_key.astype(jnp.float32), w_value.astype(jnp.float32), b_value.astype(jnp.float32), w_out.astype(jnp.float32), b_out.astype(jnp.float32), norm2_gain.astype(jnp.float32), norm2_bias.astype(jnp.float32), w_up.astype(jnp.float32), b_up.astype(jnp.float32), w_down.astype(jnp.float32), b_down.astype(jnp.float32))

    def forward(inputs, *weights):
        return whole_layer(inputs, doc_ids, weights)
    output, pullback = jax.vjp(forward, tokens.astype(jnp.float32), *params)
    gradients = pullback(out_grad.astype(jnp.float32))
    return (output.astype(jnp.bfloat16), gradients[0].astype(jnp.bfloat16), gradients[1], gradients[2], gradients[3], gradients[4], gradients[5], gradients[6], gradients[7], gradients[8], gradients[9], gradients[10], gradients[11], gradients[12], gradients[13], gradients[14], gradients[15])
```

```python
from functools import partial
import math

import jax
import jax.numpy as jnp
from jax import lax
from jax.experimental import pallas as pl
from jax.experimental.pallas import tpu as pltpu
from jax.sharding import PartitionSpec as P

HEADS = 12


EPS = 1e-06
NEG_START = -1e30


def norm_rows(inputs, norm_gain, norm_bias):
    row_mean = jnp.mean(inputs, axis=-1, keepdims=True)
    centred = inputs - row_mean
    variance = jnp.mean(centred * centred, axis=-1, keepdims=True)
    return centred * lax.rsqrt(variance + EPS) * norm_gain + norm_bias


def doc_of(positions, doc_ends):
    return jnp.sum((positions[:, None] >= doc_ends[None, :]).astype(jnp.int32), axis=1)


def dot_plain(left, right):
    return jnp.dot(left, right, preferred_element_type=jnp.float32)


def dot_left(left, right):
    return lax.dot_general(
        left, right, (((0,), (0,)), ((), ())), preferred_element_type=jnp.float32
    )


def dot_right(left, right):
    return lax.dot_general(
        left, right, (((1,), (1,)), ((), ())), preferred_element_type=jnp.float32
    )


def masked_scores(query_heads, key_heads, query_ids, key_ids, score_scale):
    raw_scores = (
        jnp.einsum("qhd,khd->hqk", query_heads, key_heads, preferred_element_type=jnp.float32)
        * score_scale
    )
    same_doc = (query_ids[:, None] == key_ids[None, :])[None]
    return jnp.where(same_doc, raw_scores, -jnp.inf)


def per_device(
    tokens,
    doc_lengths,
    out_grad,
    norm1_gain,
    norm1_bias,
    w_query,
    b_query,
    w_key,
    w_value,
    b_value,
    w_out,
    b_out,
    norm2_gain,
    norm2_bias,
    w_up,
    b_up,
    w_down,
    b_down,
):
    (
        gain_one,
        bias_one,
        query_w,
        query_b,
        key_w,
        value_w,
        value_b,
        out_w,
        out_b,
        gain_two,
        bias_two,
        up_w,
        up_b,
        down_w,
        down_b,
    ) = (
        lax.all_gather(norm1_gain, "wsh", axis=0, tiled=True),
        lax.all_gather(norm1_bias, "wsh", axis=0, tiled=True),
        lax.all_gather(w_query, "wsh", axis=0, tiled=True),
        lax.all_gather(b_query, "wsh", axis=0, tiled=True),
        lax.all_gather(w_key, "wsh", axis=0, tiled=True),
        lax.all_gather(w_value, "wsh", axis=0, tiled=True),
        lax.all_gather(b_value, "wsh", axis=0, tiled=True),
        lax.all_gather(w_out, "wsh", axis=0, tiled=True),
        lax.all_gather(b_out, "wsh", axis=0, tiled=True),
        lax.all_gather(norm2_gain, "wsh", axis=0, tiled=True),
        lax.all_gather(norm2_bias, "wsh", axis=0, tiled=True),
        lax.all_gather(w_up, "wsh", axis=0, tiled=True),
        lax.all_gather(b_up, "wsh", axis=0, tiled=True),
        lax.all_gather(w_down, "wsh", axis=0, tiled=True),
        lax.all_gather(b_down, "wsh", axis=0, tiled=True),
    )
    row_count = tokens.shape[1]
    model_width = tokens.shape[2]
    head_dim = model_width // HEADS
    score_scale = head_dim ** (-0.5)
    first_gain = gain_one.astype(jnp.float32)
    first_bias = bias_one.astype(jnp.float32)
    second_gain = gain_two.astype(jnp.float32)
    second_bias = bias_two.astype(jnp.float32)
    inputs = tokens[0].astype(jnp.float32)
    doc_ends = jnp.cumsum(doc_lengths[0])
    own_ids = doc_of(
        lax.axis_index("ctx") * row_count + jnp.arange(row_count, dtype=jnp.int32), doc_ends
    )
    normed_one = norm_rows(inputs, first_gain, first_bias).astype(jnp.bfloat16)
    queries = (dot_plain(normed_one, query_w) + query_b.astype(jnp.float32)).astype(jnp.bfloat16)
    key_rows = dot_plain(normed_one, key_w).astype(jnp.bfloat16)
    values = (dot_plain(normed_one, value_w) + value_b.astype(jnp.float32)).astype(jnp.bfloat16)
    key_all, value_all = (
        lax.all_gather(key_rows, "ctx", axis=0, tiled=True),
        lax.all_gather(values, "ctx", axis=0, tiled=True),
    )
    total_rows = key_all.shape[0]
    key_block = math.gcd(total_rows, 2048)
    block_count = total_rows // key_block
    key_stack = key_all.reshape(block_count, key_block, HEADS, head_dim)
    value_stack = value_all.reshape(block_count, key_block, HEADS, head_dim)
    id_stack = doc_of(jnp.arange(total_rows, dtype=jnp.int32), doc_ends).reshape(
        block_count, key_block
    )
    query_heads = queries.reshape(row_count, HEADS, head_dim)

    def lse_step(running, block_in):
        run_max, run_sum = running
        key_heads, key_ids = block_in
        scores = masked_scores(query_heads, key_heads, own_ids, key_ids, score_scale)
        new_max = jnp.maximum(run_max, jnp.max(scores, axis=-1))
        new_sum = run_sum * jnp.exp(run_max - new_max) + jnp.sum(
            jnp.exp(scores - new_max[:, :, None]), axis=-1
        )
        return ((new_max, new_sum), None)

    start_max = jnp.full((HEADS, row_count), NEG_START, jnp.float32)
    (final_max, final_sum), unused = lax.scan(
        lse_step, (start_max, jnp.zeros_like(start_max)), (key_stack, id_stack)
    )
    log_total = final_max + jnp.log(final_sum)

    def out_step(running, block_in):
        key_heads, value_heads, key_ids = block_in
        scores = masked_scores(query_heads, key_heads, own_ids, key_ids, score_scale)
        attn_prob = jnp.exp(scores - log_total[:, :, None]).astype(jnp.bfloat16)
        return (
            running
            + jnp.einsum(
                "hqk,khd->qhd", attn_prob, value_heads, preferred_element_type=jnp.float32
            ),
            None,
        )

    attn_sum, unused = lax.scan(
        out_step,
        jnp.zeros((row_count, HEADS, head_dim), jnp.float32),
        (key_stack, value_stack, id_stack),
    )
    attended = attn_sum.reshape(row_count, model_width).astype(jnp.bfloat16)
    middle = inputs + dot_plain(attended, out_w) + out_b.astype(jnp.float32)
    normed_two = norm_rows(middle, second_gain, second_bias).astype(jnp.bfloat16)
    hidden = dot_plain(normed_two, up_w) + up_b.astype(jnp.float32)
    active = jax.nn.gelu(hidden, approximate=True).astype(jnp.bfloat16)
    output = middle + dot_plain(active, down_w) + down_b.astype(jnp.float32)
    top_grad = out_grad[0]
    top_float = top_grad.astype(jnp.float32)
    grad_down_w = dot_left(active, top_grad)
    grad_down_b = jnp.sum(top_float, axis=0)
    grad_active = dot_right(top_grad, down_w)
    unused, gelu_pull = jax.vjp(partial(jax.nn.gelu, approximate=True), hidden)
    grad_hidden = gelu_pull(grad_active)[0].astype(jnp.bfloat16)
    grad_up_w = dot_left(normed_two, grad_hidden)
    grad_up_b = jnp.sum(grad_hidden.astype(jnp.float32), axis=0)
    grad_normed_two = dot_right(grad_hidden, up_w)
    unused, second_pull = jax.vjp(norm_rows, middle, second_gain, second_bias)
    grad_middle, grad_gain_two, grad_bias_two = second_pull(grad_normed_two)
    grad_middle = grad_middle + top_float
    grad_branch = grad_middle.astype(jnp.bfloat16)
    grad_out_w = dot_left(attended, grad_branch)
    grad_out_b = jnp.sum(grad_branch.astype(jnp.float32), axis=0)
    grad_attended = dot_right(grad_branch, out_w).astype(jnp.bfloat16)
    grad_heads = grad_attended.reshape(row_count, HEADS, head_dim)
    row_delta = jnp.sum(grad_heads.astype(jnp.float32) * attn_sum, axis=-1)
    head_delta = row_delta.T
    query_start = jnp.zeros((row_count, HEADS, head_dim), jnp.float32)

    def full_step(grad_query, block_in):
        key_heads, value_heads, key_ids = block_in
        scores = masked_scores(query_heads, key_heads, own_ids, key_ids, score_scale)
        attn_prob = jnp.exp(scores - log_total[:, :, None])
        grad_prob = jnp.einsum(
            "qhd,khd->hqk", grad_heads, value_heads, preferred_element_type=jnp.float32
        )
        grad_score = (attn_prob * (grad_prob - head_delta[:, :, None])).astype(jnp.bfloat16)
        grad_query = grad_query + jnp.einsum(
            "hqk,khd->qhd", grad_score, key_heads, preferred_element_type=jnp.float32
        )
        grad_key = (
            jnp.einsum("hqk,qhd->khd", grad_score, query_heads, preferred_element_type=jnp.float32)
            * score_scale
        )
        grad_value = jnp.einsum(
            "hqk,qhd->khd",
            attn_prob.astype(jnp.bfloat16),
            grad_heads,
            preferred_element_type=jnp.float32,
        )
        return (
            grad_query,
            (grad_key.reshape(key_block, model_width), grad_value.reshape(key_block, model_width)),
        )

    grad_query, key_terms = lax.scan(full_step, query_start, (key_stack, value_stack, id_stack))
    key_grad, value_grad = (
        lax.psum_scatter(
            key_terms[0].reshape(total_rows, model_width), "ctx", scatter_dimension=0, tiled=True
        ),
        lax.psum_scatter(
            key_terms[1].reshape(total_rows, model_width), "ctx", scatter_dimension=0, tiled=True
        ),
    )
    grad_query_rows = (
        (grad_query * score_scale).reshape(row_count, model_width).astype(jnp.bfloat16)
    )
    grad_key_rows = key_grad.astype(jnp.bfloat16)
    grad_value_rows = value_grad.astype(jnp.bfloat16)
    grad_query_w = dot_left(normed_one, grad_query_rows)
    grad_query_b = jnp.sum(grad_query_rows.astype(jnp.float32), axis=0)
    grad_key_w = dot_left(normed_one, grad_key_rows)
    grad_value_w = dot_left(normed_one, grad_value_rows)
    grad_value_b = jnp.sum(grad_value_rows.astype(jnp.float32), axis=0)
    grad_normed_one = (
        dot_right(grad_query_rows, query_w)
        + dot_right(grad_key_rows, key_w)
        + dot_right(grad_value_rows, value_w)
    )
    unused, first_pull = jax.vjp(norm_rows, inputs, first_gain, first_bias)
    grad_inputs, grad_gain_one, grad_bias_one = first_pull(grad_normed_one)
    grad_inputs = grad_inputs + grad_middle
    (
        share_gain_one,
        share_bias_one,
        share_query_w,
        share_query_b,
        share_key_w,
        share_value_w,
        share_value_b,
        share_out_w,
        share_out_b,
        share_gain_two,
        share_bias_two,
        share_up_w,
        share_up_b,
        share_down_w,
        share_down_b,
    ) = (
        lax.psum_scatter(
            grad_gain_one.astype(jnp.bfloat16), "wsh", scatter_dimension=0, tiled=True
        ).astype(jnp.float32),
        lax.psum_scatter(
            grad_bias_one.astype(jnp.bfloat16), "wsh", scatter_dimension=0, tiled=True
        ).astype(jnp.float32),
        lax.psum_scatter(
            grad_query_w.astype(jnp.bfloat16), "wsh", scatter_dimension=0, tiled=True
        ).astype(jnp.float32),
        lax.psum_scatter(
            grad_query_b.astype(jnp.bfloat16), "wsh", scatter_dimension=0, tiled=True
        ).astype(jnp.float32),
        lax.psum_scatter(
            grad_key_w.astype(jnp.bfloat16), "wsh", scatter_dimension=0, tiled=True
        ).astype(jnp.float32),
        lax.psum_scatter(
            grad_value_w.astype(jnp.bfloat16), "wsh", scatter_dimension=0, tiled=True
        ).astype(jnp.float32),
        lax.psum_scatter(
            grad_value_b.astype(jnp.bfloat16), "wsh", scatter_dimension=0, tiled=True
        ).astype(jnp.float32),
        lax.psum_scatter(
            grad_out_w.astype(jnp.bfloat16), "wsh", scatter_dimension=0, tiled=True
        ).astype(jnp.float32),
        lax.psum_scatter(
            grad_out_b.astype(jnp.bfloat16), "wsh", scatter_dimension=0, tiled=True
        ).astype(jnp.float32),
        lax.psum_scatter(
            grad_gain_two.astype(jnp.bfloat16), "wsh", scatter_dimension=0, tiled=True
        ).astype(jnp.float32),
        lax.psum_scatter(
            grad_bias_two.astype(jnp.bfloat16), "wsh", scatter_dimension=0, tiled=True
        ).astype(jnp.float32),
        lax.psum_scatter(
            grad_up_w.astype(jnp.bfloat16), "wsh", scatter_dimension=0, tiled=True
        ).astype(jnp.float32),
        lax.psum_scatter(
            grad_up_b.astype(jnp.bfloat16), "wsh", scatter_dimension=0, tiled=True
        ).astype(jnp.float32),
        lax.psum_scatter(
            grad_down_w.astype(jnp.bfloat16), "wsh", scatter_dimension=0, tiled=True
        ).astype(jnp.float32),
        lax.psum_scatter(
            grad_down_b.astype(jnp.bfloat16), "wsh", scatter_dimension=0, tiled=True
        ).astype(jnp.float32),
    )
    totals = lax.psum(
        (
            share_gain_one,
            share_bias_one,
            share_query_w,
            share_query_b,
            share_key_w,
            share_value_w,
            share_value_b,
            share_out_w,
            share_out_b,
            share_gain_two,
            share_bias_two,
            share_up_w,
            share_up_b,
            share_down_w,
            share_down_b,
        ),
        "ctx",
    )
    return (
        output.astype(jnp.bfloat16)[None],
        grad_inputs.astype(jnp.bfloat16)[None],
        totals[0],
        totals[1],
        totals[2],
        totals[3],
        totals[4],
        totals[5],
        totals[6],
        totals[7],
        totals[8],
        totals[9],
        totals[10],
        totals[11],
        totals[12],
        totals[13],
        totals[14],
    )


MESH = pl.DeviceIdType.MESH
F32 = jnp.float32
BF = jnp.bfloat16
GROUPS = 4
LANES = 128
SMALL_ROWS = 16
SMALL_WIDTH = 1024


def flip(value, mask):
    return ((value // 2 + mask // 2) % 2) * 2 + (value + mask) % 2


def dot_nn(left, right):
    return lax.dot_general(left, right, (((1,), (0,)), ((), ())), preferred_element_type=F32)


def dot_nt(left, right):
    return lax.dot_general(left, right, (((1,), (1,)), ((), ())), preferred_element_type=F32)


def dot_tn(left, right):
    return lax.dot_general(left, right, (((0,), (0,)), ((), ())), preferred_element_type=F32)


def unit_rows(inputs):
    row_mean = jnp.mean(inputs, axis=-1, keepdims=True)
    centred = inputs - row_mean
    variance = jnp.mean(centred * centred, axis=-1, keepdims=True)
    scale = lax.rsqrt(variance + EPS)
    return centred * scale, scale


def unit_rows_back(grad_normed, unit, scale, gain):
    grad_unit = grad_normed * gain
    return scale * (
        grad_unit
        - jnp.mean(grad_unit, axis=-1, keepdims=True)
        - unit * jnp.mean(grad_unit * unit, axis=-1, keepdims=True)
    )


def rows_sum(values):
    return jnp.sum(values, axis=0, keepdims=True)


class Wires:
    def __init__(self, send_sems, recv_sems):
        self.send_sems, self.recv_sems, self.used, self.started = send_sems, recv_sems, 0, []

    def take(self, count=1):
        first = self.used
        self.used += count
        return first

    def copy(self, index, source, target, device):
        return pltpu.make_async_remote_copy(
            src_ref=source,
            dst_ref=target,
            send_sem=self.send_sems.at[index],
            recv_sem=self.recv_sems.at[index],
            device_id=device,
            device_id_type=MESH,
        )

    def send(self, source, target, device):
        one = self.copy(self.take(), source, target, device)
        one.start()
        self.started.append(one)
        return one

    def later(self, one):
        self.started.append(one)

    def drain(self):
        for one in self.started:
            one.wait_send()


def layer_kernel(
    sizes,
    doc_ref,
    tok_ref,
    dy_ref,
    ws_ref,
    par_ref,
    bup_ref,
    wout_ref,
    wup_ref,
    wdown_ref,
    y_ref,
    dx_ref,
    gdown_ref,
    gup_ref,
    gout_ref,
    gqkv_ref,
    gsm_ref,
    x_s,
    h1_s,
    wq_s,
    par_s,
    q_s,
    kv_s,
    e_s,
    li_s,
    oa_s,
    os_s,
    or_s,
    wo_s,
    wu_s,
    dy_s,
    x1_s,
    h2_s,
    g_s,
    da_s,
    ph_s,
    hr_s,
    py_s,
    yr_s,
    dz_s,
    dos_s,
    dor_s,
    dkv_s,
    kvt_s,
    kvr_s,
    dq_s,
    dqkv_s,
    dp_s,
    dn_s,
    dt_s,
    df_s,
    gds_s,
    gdr_s,
    gus_s,
    gua_s,
    gur_s,
    gos_s,
    gor_s,
    goc_s,
    gqs_s,
    gqr_s,
    gqc_s,
    sm_s,
    smr_s,
    send_sems,
    recv_sems,
):
    n_ctx, n_doc, R, D, S, FS = sizes
    G = n_ctx // GROUPS
    half = GROUPS * R
    c = lax.axis_index("ctx")
    w = lax.axis_index("wsh")
    hg, px = c // G, c % G
    near_bit, far_bit = hg % 2, hg // 2

    def zdev(group):
        return {"ctx": group * G + px, "wsh": w}

    def wdev(index):
        return {"ctx": c, "wsh": index}

    xdev = {"ctx": hg * G + 1 - px, "wsh": w}
    near, far = zdev(flip(hg, 1)), zdev(flip(hg, 2))
    w1, w2, w3 = flip(w, 1), flip(w, 2), flip(w, 3)
    sib, across, diag = wdev(w1), wdev(w2), wdev(w3)
    wires = Wires(send_sems, recv_sems)
    lane = lax.broadcasted_iota(jnp.int32, (1, LANES), 1)
    low_half = lane < LANES // 2

    barrier = pltpu.get_barrier_semaphore()
    partners = [near, far, zdev(flip(hg, 3)), xdev, sib, across, diag]
    for partner in partners:
        pl.semaphore_signal(barrier, inc=1, device_id=partner, device_id_type=MESH)
    pl.semaphore_wait(barrier, len(partners))

    class Gather:
        def __init__(self, own, slot_of):
            self.slot = slot_of
            self.to_sib = wires.send(own, slot_of(w), sib)
            self.to_across = wires.send(own, slot_of(w), across)

        def relay(self):
            self.to_across.wait_recv()
            self.on = wires.send(self.slot(w2), self.slot(w2), sib)

        def finish(self):
            self.to_sib.wait_recv()
            self.on.wait_recv()

    class Reduce:
        def __init__(self, part, recv):
            self.part, self.recv = part, recv

        def send_sib(self):
            self.b = wires.send(self.part(w1), self.recv.at[1], sib)

        def send_diag(self):
            self.a = wires.send(self.part(w3), self.recv.at[0], sib)

        def combine(self):
            self.a.wait_recv()
            self.recv[3] = (
                self.part(w2)[...].astype(F32) + self.recv[0].astype(F32)
            ).astype(BF)
            self.c = wires.send(self.recv.at[3], self.recv.at[2], across)

        def finish(self):
            self.b.wait_recv()
            self.c.wait_recv()
            return (
                self.part(w)[...].astype(F32)
                + self.recv[1].astype(F32)
                + self.recv[2].astype(F32)
            )

    tok_far = wires.send(tok_ref, x_s.at[hg], far)
    tok_near = wires.send(tok_ref, x_s.at[hg], near)
    ws_all = Gather(ws_ref, lambda i: wq_s.at[pl.ds(pl.multiple_of(i * S, S), S)])
    par_all = Gather(par_ref, lambda i: par_s.at[i])
    x_s[hg] = tok_ref[...]
    wq_s[pl.ds(pl.multiple_of(w * S, S), S), :] = ws_ref[...]
    par_s[w] = par_ref[...]
    dy_s[w] = dy_ref[...]
    wo_s[:, LANES : LANES + S - LANES, :] = jnp.zeros((GROUPS, S - LANES, D), BF)
    ws_all.relay()
    par_all.relay()
    ws_all.finish()
    par_all.finish()

    pars = jnp.concatenate([par_s[i][:, :S] for i in range(GROUPS)], axis=1)
    gain_one, bias_one, out_b, gain_two, bias_two, down_b = [pars[i : i + 1] for i in (0, 1, 4, 5, 6, 7)]
    up_b = bup_ref[...].astype(F32)
    own_par = par_s[hg]
    v_tile, v_last = own_par[3:4, :LANES], own_par[3:4, LANES:]
    qkv_b = jnp.concatenate(
        [
            own_par[2:3, :],
            jnp.zeros((1, LANES), F32),
            pltpu.roll(v_last, LANES // 2, 1),
            v_tile,
        ],
        axis=1,
    )

    wo_top = Gather(
        wout_ref.at[pl.ds(0, LANES)], lambda i: wo_s.at[i, pl.ds(0, LANES)]
    )
    wo_low = Gather(
        wout_ref.at[pl.ds(LANES, S - LANES)], lambda i: wo_s.at[i, pl.ds(S, S - LANES)]
    )
    wo_s[w, 0:LANES, :] = wout_ref[0:LANES, :]
    wo_s[w, S : S + S - LANES, :] = wout_ref[LANES:S, :]
    up_sends = [
        wires.send(
            wup_ref.at[:, pl.ds(pl.multiple_of(flip(w, k) * FS, FS), FS)],
            wu_s.at[w],
            wdev(flip(w, k)),
        )
        for k in (1, 2, 3)
    ]
    wu_s[w] = wup_ref[:, pl.ds(pl.multiple_of(w * FS, FS), FS)]
    dy_all = Gather(dy_ref, lambda i: dy_s.at[i])

    kv_first = wires.take(GROUPS)

    def kv_copy(k, block):
        rows = pl.ds(pl.multiple_of(block * R, R), R)
        return wires.copy(kv_first + k, kv_s.at[0, rows], kv_s.at[1, rows], xdev)

    def project(k):
        block = flip(hg, k)
        unit, unused = unit_rows(x_s[block].astype(F32))
        normed = (unit * gain_one + bias_one).astype(BF)
        h1_s[block] = normed
        qkv = dot_nn(normed, wq_s[...]) + qkv_b
        queries = (qkv[:, : 2 * LANES].astype(BF).astype(F32) * 0.125)
        q_s[0, block] = jnp.where(low_half, queries[:, :LANES], 0.0).astype(BF)
        q_s[1, block] = jnp.where(low_half, 0.0, queries[:, :LANES]).astype(BF)
        q_s[2, block] = queries[:, LANES:].astype(BF)
        kv_s[0, pl.ds(pl.multiple_of(block * R, R), R), :] = qkv[:, 2 * LANES :].astype(BF)
        one = kv_copy(k, block)
        one.start()
        return one

    kv_sends = [project(0)]
    tok_near.wait_recv()
    kv_sends.append(project(1))
    tok_far.wait_recv()
    tok_on = wires.send(x_s.at[flip(hg, 2)], x_s.at[flip(hg, 2)], near)
    kv_sends.append(project(2))
    tok_on.wait_recv()
    kv_sends.append(project(3))
    wo_top.relay()
    wo_low.relay()
    dy_all.relay()
    for one in kv_sends:
        one.wait_recv()
        wires.later(one)

    doc_ends = []
    for i in range(n_doc):
        doc_ends.append(doc_ref[0, i] + (doc_ends[-1] if i else 0))

    def doc_ids(positions):
        return sum([(positions >= end).astype(jnp.int32) for end in doc_ends])

    key_at = lax.broadcasted_iota(jnp.int32, (1, half), 1)
    key_block = sum([(key_at >= i * R).astype(jnp.int32) for i in range(1, GROUPS)])
    key_base = key_at + key_block * (R * (G - 1))
    key_ids = [doc_ids(key_base + px * R), doc_ids(key_base + (1 - px) * R)]
    KT, VT = (0, 0, LANES), (2 * LANES, 2 * LANES, LANES)

    o_first = wires.take(GROUPS)

    def o_copy(k):
        block = flip(hg, k)
        return wires.copy(o_first + k, os_s.at[block], or_s.at[hg], zdev(block))

    def attend(step, carry):
        k = (step + 1) % GROUPS
        block = flip(hg, k)
        row_at = (block * G + px) * R + lax.broadcasted_iota(jnp.int32, (R, 1), 0)
        row_ids = doc_ids(row_at)
        outs = []
        for h in range(3):
            queries = q_s[h, block]
            scores = [
                jnp.where(
                    row_ids == key_ids[side],
                    dot_nt(queries, kv_s[side, :, KT[h] : KT[h] + LANES]),
                    NEG_START,
                )
                for side in (0, 1)
            ]
            top = jnp.maximum(
                jnp.max(scores[0], axis=-1, keepdims=True), jnp.max(scores[1], axis=-1, keepdims=True)
            )
            weights = [jnp.exp(one - top) for one in scores]
            total = jnp.sum(weights[0], axis=-1, keepdims=True) + jnp.sum(
                weights[1], axis=-1, keepdims=True
            )
            inverse = 1.0 / total
            mixed = jnp.zeros((R, LANES), F32)
            for side in (0, 1):
                rounded = weights[side].astype(BF)
                e_s[h, block, side] = rounded
                mixed += dot_nn(rounded, kv_s[side, :, VT[h] : VT[h] + LANES])
            li_s[h, block] = jnp.broadcast_to(inverse, (R, LANES))
            outs.append(mixed * inverse)
        first = jnp.where(low_half, outs[0], outs[1])
        last = jnp.where(low_half, 0.0, outs[2])
        oa_s[block, :, :LANES] = first
        oa_s[block, :, LANES:] = last
        os_s[block, :, :LANES] = first.astype(BF)
        os_s[block, :, LANES:] = last.astype(BF)

        @pl.when(k != 0)
        def _():
            o_copy(k).start()

        return carry

    lax.fori_loop(0, GROUPS, attend, 0)
    or_s[hg] = os_s[hg]
    wo_top.finish()
    wo_low.finish()
    for k in (1, 2, 3):
        o_copy(k).wait_recv()
        wires.later(o_copy(k))

    middle = tok_ref[...].astype(F32) + out_b
    for i in range(GROUPS):
        middle += dot_nn(or_s[i], wo_s[i])
    x1_s[...] = middle
    unit_two, scale_two = unit_rows(middle)
    h2_s[w] = (unit_two * gain_two + bias_two).astype(BF)
    h2_all = Gather(h2_s.at[w], lambda i: h2_s.at[i])
    dy_all.finish()
    for one in up_sends:
        one.wait_recv()

    ph = Reduce(lambda i: ph_s.at[i], hr_s)

    def up_and_back(j):
        slot = flip(w, j)
        hidden = dot_nn(h2_s[slot], wu_s[...].reshape(D, FS)) + up_b
        square = hidden * hidden
        inner = math.sqrt(2.0 / math.pi) * (hidden + 0.044715 * (square * hidden))
        bent = jnp.tanh(inner)
        g_s[slot] = (0.5 * hidden * (1.0 + bent)).astype(BF)
        slope = 0.5 * (1.0 + bent) + 0.5 * hidden * (1.0 - bent * bent) * (
            math.sqrt(2.0 / math.pi) * (1.0 + 3.0 * 0.044715 * square)
        )
        grad_active = dot_nt(dy_s[slot], wdown_ref[...])
        grad_hidden = (grad_active * slope).astype(BF)
        da_s[slot] = grad_hidden
        ph_s[slot] = dot_nt(grad_hidden, wu_s[...].reshape(D, FS)).astype(BF)

    sib_in, on_in = h2_all.to_sib, wires.take()
    on_copy = wires.copy(on_in, h2_s.at[w2], h2_s.at[w2], sib)
    b_at, a_at = wires.take(), wires.take()
    b_copy = wires.copy(b_at, ph_s.at[w1], hr_s.at[1], sib)
    a_copy = wires.copy(a_at, ph_s.at[w3], hr_s.at[0], sib)

    def mlp_step(j, carry):
        @pl.when(j == 1)
        def _():
            sib_in.wait_recv()

        @pl.when(j == 2)
        def _():
            h2_all.to_across.wait_recv()
            on_copy.start()

        @pl.when(j == 3)
        def _():
            on_copy.wait_recv()

        up_and_back(j)

        @pl.when(j == 1)
        def _():
            b_copy.start()

        @pl.when(j == 3)
        def _():
            a_copy.start()

        return carry

    lax.fori_loop(0, GROUPS, mlp_step, 0)
    for one in (on_copy, b_copy, a_copy):
        wires.later(one)
    ph.a, ph.b = a_copy, b_copy

    def up_grad(i, carry):
        at = pl.ds(pl.multiple_of(i * 256, 256), 256)
        gus_s[at, :] = dot_tn(
            h2_s[:, :, at].reshape(half, 256), da_s[...].reshape(half, FS)
        ).astype(BF)
        return carry

    def down_grad(i, carry):
        at = pl.ds(pl.multiple_of(i * 256, 256), 256)
        gds_s[at, :] = dot_tn(
            g_s[:, :, at].reshape(half, 256), dy_s[...].reshape(half, D)
        ).astype(BF)
        return carry

    def y_part(j, carry):
        py_s[j] = dot_nn(g_s[j], wdown_ref[...]).astype(BF)
        return carry

    lax.fori_loop(0, GROUPS, y_part, 0)
    ph.combine()
    py = Reduce(lambda i: py_s.at[i], yr_s)
    py.send_diag()
    py.send_sib()
    lax.fori_loop(0, D // 256, up_grad, 0)
    up_back = [
        wires.send(
            gus_s.at[pl.ds(pl.multiple_of(flip(w, k) * S, S), S)],
            gua_s.at[pl.ds(pl.multiple_of(w * S, S), S)],
            wdev(flip(w, k)),
        )
        for k in (1, 2, 3)
    ]
    py.combine()
    lax.fori_loop(0, FS // 256, down_grad, 0)

    class Spread:
        def __init__(self, part, recv, final, rows):
            self.part, self.recv, self.final, self.n = part, recv, final, rows
            self.at1 = px * (rows // 2)
            self.at2 = self.at1 + near_bit * (rows // 4)
            self.at3 = self.at2 + far_bit * (rows // 8)

        def rows(self, start, count):
            return pl.ds(pl.multiple_of(start, 8), count)

        def x_out(self):
            n = self.n // 2
            self.m1 = wires.send(
                self.part.at[self.rows((1 - px) * n, n)], self.recv.at[pl.ds(0, n)], xdev
            )

        def fold(self, start, count, at):
            here = self.rows(start, count)
            self.part[here, :] = (
                self.part[here, :].astype(F32) + self.recv[at : at + count, :].astype(F32)
            ).astype(BF)

        def near_out(self):
            n = self.n // 4
            self.m1.wait_recv()
            self.fold(self.at1, 2 * n, 0)
            self.m2 = wires.send(
                self.part.at[self.rows(self.at1 + (1 - near_bit) * n, n)],
                self.recv.at[pl.ds(2 * n, n)],
                near,
            )

        def far_out(self):
            n = self.n // 8
            self.m2.wait_recv()
            self.fold(self.at2, 2 * n, 4 * n)
            self.m3 = wires.send(
                self.part.at[self.rows(self.at2 + (1 - far_bit) * n, n)],
                self.recv.at[pl.ds(6 * n, n)],
                far,
            )

        def far_back(self):
            n = self.n // 8
            self.m3.wait_recv()
            here = self.rows(self.at3, n)
            self.final[here, :] = (
                self.part[here, :].astype(F32) + self.recv[6 * n : 7 * n, :].astype(F32)
            ).astype(BF)
            self.m4 = wires.send(self.final.at[here], self.final.at[here], far)

        def near_back(self):
            here = self.rows(self.at2, self.n // 4)
            self.m4.wait_recv()
            self.m5 = wires.send(self.final.at[here], self.final.at[here], near)

        def x_back(self):
            here = self.rows(self.at1, self.n // 2)
            self.m5.wait_recv()
            self.m6 = wires.send(self.final.at[here], self.final.at[here], xdev)

        def done(self):
            self.m6.wait_recv()

    down = Spread(gds_s, gdr_s, gdown_ref, FS)
    down.x_out()

    grad_two = ph.finish()
    middle = x1_s[...]
    unit_two, scale_two = unit_rows(middle)
    top = dy_ref[...].astype(F32)
    grad_middle = top + unit_rows_back(grad_two, unit_two, scale_two, gain_two)
    dz = grad_middle.astype(BF)
    dz_s[...] = grad_middle

    do_first = wires.take(GROUPS)

    def do_copy(k):
        block = flip(hg, k)
        return wires.copy(do_first + k, dos_s.at[block], dor_s.at[hg], zdev(block))

    def out_back(step, carry):
        k = (step + 1) % GROUPS
        block = flip(hg, k)
        dos_s[block] = dot_nt(dz, wo_s[block]).astype(BF)

        @pl.when(k != 0)
        def _():
            do_copy(k).start()

        return carry

    lax.fori_loop(0, GROUPS, out_back, 0)
    dor_s[hg] = dos_s[hg]
    sm_s[0] = jnp.zeros((SMALL_ROWS, SMALL_WIDTH), F32)
    sm_s[0, 2:3, :D] = rows_sum(dz.astype(F32))
    sm_s[0, 3:4, :D] = rows_sum(grad_two * unit_two)
    sm_s[0, 4:5, :D] = rows_sum(grad_two)
    sm_s[0, 5:6, :D] = rows_sum(top)
    up_sum = rows_sum(da_s[...].reshape(half, FS).astype(F32))
    for i in range(GROUPS):
        sm_s[0, 8 + i : 9 + i, :FS] = jnp.where(w == i, up_sum, 0.0)

    for i in range(GROUPS):
        piece = dot_tn(or_s[i], dz)
        gos_s[i, 0:LANES, :] = piece[0:LANES, :].astype(BF)
        gos_s[i, LANES:S, :] = piece[S:, :].astype(BF)
    go = Reduce(lambda i: gos_s.at[i], gor_s)
    go.send_diag()
    go.send_sib()

    for one in up_back:
        one.wait_recv()
    own_rows = pl.ds(pl.multiple_of(w * S, S), S)
    gua_s[own_rows, :] = gus_s[own_rows, :]
    up = Spread(gua_s, gur_s, gup_ref, D)
    up.x_out()
    go.combine()

    layer_out = x1_s[...] + py.finish() + down_b
    y_ref[...] = layer_out.astype(BF)

    dkv_s[...] = jnp.zeros(dkv_s.shape, F32)

    def back_block(k, side):
        block = flip(hg, k)
        outs = dor_s[block].astype(F32)
        kept = oa_s[block]
        grads_q = []
        for h in range(3):
            tile = 0 if h < 2 else LANES
            keep = low_half if h == 0 else jnp.logical_not(low_half)
            scaled = jnp.where(keep, outs[:, tile : tile + LANES], 0.0) * li_s[h, block]
            delta = jnp.sum(scaled * kept[:, tile : tile + LANES], axis=-1, keepdims=True)
            rounded = scaled.astype(BF)
            grad_prob = dot_nt(rounded, kv_s[side, :, VT[h] : VT[h] + LANES])
            weights = e_s[h, block, side]
            grad_score = (weights.astype(F32) * (grad_prob - delta)).astype(BF)
            grads_q.append(dot_nn(grad_score, kv_s[side, :, KT[h] : KT[h] + LANES]))
            dkv_s[side, :, KT[h] : KT[h] + LANES] += dot_tn(grad_score, q_s[h, block])
            dkv_s[side, :, VT[h] : VT[h] + LANES] += dot_tn(weights, rounded)
        first = jnp.where(low_half, grads_q[0], grads_q[1]) * 0.125
        last = jnp.where(low_half, grads_q[2], 0.0) * 0.125
        if side == 1:
            dq_s[block, :, :LANES] = first
            dq_s[block, :, LANES:] = last
        else:
            rows = pl.ds(pl.multiple_of(block * R, R), R)
            dqkv_s[rows, :LANES] = (dq_s[block, :, :LANES] + first).astype(BF)
            dqkv_s[rows, LANES : 2 * LANES] = (dq_s[block, :, LANES:] + last).astype(BF)

    def back_other(k, carry):
        @pl.when(k != 0)
        def _():
            do_copy(k).wait_recv()

        back_block(k, 1)
        return carry

    def back_own(k, carry):
        back_block(k, 0)
        return carry

    lax.fori_loop(0, GROUPS, back_other, 0)
    for k in (1, 2, 3):
        wires.later(do_copy(k))
    kvt_s[...] = dkv_s[1].astype(BF)
    kv_back = wires.send(kvt_s, kvr_s, xdev)
    down.near_out()
    lax.fori_loop(0, GROUPS, back_own, 0)
    down.far_out()
    up.near_out()

    go_sum = go.finish()
    goc_s[...] = go_sum.astype(BF)
    kv_back.wait_recv()
    dqkv_s[:, 2 * LANES :] = (dkv_s[0] + kvr_s[...].astype(F32)).astype(BF)

    def h1_part(k):
        block = flip(hg, k)
        rows = pl.ds(pl.multiple_of(block * R, R), R)
        return dot_nt(dqkv_s[rows, :], wq_s[...])

    dp_s[0] = h1_part(3).astype(BF)
    part_a = wires.send(dp_s.at[0], dn_s.at[0], near)
    dp_s[1] = h1_part(1).astype(BF)
    part_b = wires.send(dp_s.at[1], dn_s.at[1], near)
    far_sum = h1_part(2)
    df_s[...] = h1_part(0)
    part_a.wait_recv()
    dt_s[0] = (far_sum + dn_s[0].astype(F32)).astype(BF)
    part_c = wires.send(dt_s.at[0], dt_s.at[1], far)

    down.far_back()
    up.far_out()

    def qkv_grad(i, carry):
        at = pl.ds(pl.multiple_of(i * 256, 256), 256)
        gqs_s[at, :] = dot_tn(h1_s[:, :, at].reshape(half, 256), dqkv_s[...]).astype(BF)
        return carry

    lax.fori_loop(0, D // 256, qkv_grad, 0)
    gq = Reduce(lambda i: gqs_s.at[pl.ds(pl.multiple_of(i * S, S), S)], gqr_s)
    gq.send_diag()
    gq.send_sib()
    q_sum = rows_sum(dqkv_s[:, : 2 * LANES].astype(F32))
    v_sum = rows_sum(dqkv_s[:, 3 * LANES :].astype(F32))
    group_at = pl.ds(pl.multiple_of(hg * 2 * LANES, LANES), 2 * LANES)
    sm_s[0, 6:7, group_at] = q_sum
    sm_s[0, 7:8, group_at] = v_sum
    gq.combine()

    part_b.wait_recv()
    part_c.wait_recv()
    grad_one = df_s[...] + dn_s[1].astype(F32) + dt_s[1].astype(F32)
    unit_one, scale_one = unit_rows(tok_ref[...].astype(F32))
    grad_in = dz_s[...] + unit_rows_back(grad_one, unit_one, scale_one, gain_one)
    dx_ref[...] = grad_in.astype(BF)
    sm_s[0, 0:1, :D] = rows_sum(grad_one * unit_one)
    sm_s[0, 1:2, :D] = rows_sum(grad_one)

    small_to = (sib, across, xdev, near, far)
    small = wires.send(sm_s.at[0], smr_s.at[0], small_to[0])

    gqc_s[...] = gq.finish().astype(BF)
    n = S // 2
    qx = wires.send(
        gqc_s.at[pl.ds(pl.multiple_of((1 - px) * n, 8), n)], gqr_s.at[4, pl.ds(0, n)], xdev
    )
    ox = wires.send(
        goc_s.at[pl.ds(pl.multiple_of((1 - px) * n, 8), n)], gor_s.at[4, pl.ds(0, n)], xdev
    )
    down.near_back()
    up.far_back()

    def small_step(i):
        nonlocal small
        small.wait_recv()
        sm_s[i + 1] = sm_s[i] + smr_s[i]
        if i < 4:
            small = wires.send(sm_s.at[i + 1], smr_s.at[i + 1], small_to[i + 1])

    small_step(0)
    mine = pl.ds(pl.multiple_of(px * n, 8), n)
    qx.wait_recv()
    gqkv_ref[hg, mine, :] = (
        gqc_s[mine, :].astype(F32) + gqr_s[4, 0:n, :].astype(F32)
    ).astype(BF)
    qb = wires.send(gqkv_ref.at[hg, mine], gqkv_ref.at[hg, mine], xdev)
    ox.wait_recv()
    goc_s[mine, :] = (goc_s[mine, :].astype(F32) + gor_s[4, 0:n, :].astype(F32)).astype(BF)
    m = n // 2
    near_there = pl.ds(pl.multiple_of(px * n + (1 - near_bit) * m, 8), m)
    near_here = pl.ds(pl.multiple_of(px * n + near_bit * m, 8), m)
    on = wires.send(goc_s.at[near_there], gor_s.at[4, pl.ds(n, m)], near)
    small_step(1)
    down.x_back()
    up.near_back()
    qb.wait_recv()
    q_far = wires.send(gqkv_ref.at[hg], gqkv_ref.at[hg], far)
    q_near = wires.send(gqkv_ref.at[hg], gqkv_ref.at[hg], near)
    on.wait_recv()
    gor_s[5, 0:m, :] = (
        goc_s[near_here, :].astype(F32) + gor_s[4, n : n + m, :].astype(F32)
    ).astype(BF)
    of = wires.send(gor_s.at[5, pl.ds(0, m)], gor_s.at[5, pl.ds(m, m)], far)
    small_step(2)
    up.x_back()
    of.wait_recv()
    gout_ref[near_here, :] = (
        gor_s[5, 0:m, :].astype(F32) + gor_s[5, m : 2 * m, :].astype(F32)
    ).astype(BF)
    ob = wires.send(gout_ref.at[near_here], gout_ref.at[near_here], near)
    small_step(3)
    q_far.wait_recv()
    q_on = wires.send(gqkv_ref.at[flip(hg, 2)], gqkv_ref.at[flip(hg, 2)], near)
    ob.wait_recv()
    oc = wires.send(gout_ref.at[mine], gout_ref.at[mine], xdev)
    small_step(4)
    gsm_ref[...] = sm_s[5]
    q_near.wait_recv()
    q_on.wait_recv()
    oc.wait_recv()
    down.done()
    up.done()
    wires.drain()


SEMS = 96


def fast_device(mesh_sizes, *arrays):
    (tokens, doc_lengths, out_grad, norm1_gain, norm1_bias, w_query, b_query, w_key, w_value,
     b_value, w_out, b_out, norm2_gain, norm2_bias, w_up, b_up, w_down, b_down) = arrays
    n_ctx, n_wsh = mesh_sizes
    R, D = tokens.shape[1], tokens.shape[2]
    S, FS, n_doc = D // GROUPS, w_down.shape[0], doc_lengths.shape[1]
    half = GROUPS * R
    group = lax.axis_index("ctx") // (n_ctx // GROUPS)

    def of_group(weight):
        return lax.dynamic_slice(weight, (0, group * S), (S, S))

    q_w, k_w, v_w = of_group(w_query), of_group(w_key), of_group(w_value)
    ws = jnp.concatenate(
        [q_w, jnp.zeros((S, 2 * LANES - S), BF), k_w, v_w[:, LANES:], v_w[:, :LANES]], axis=1
    )
    vectors = (norm1_gain, norm1_bias, b_query, b_value, b_out, norm2_gain, norm2_bias, b_down)
    par = jnp.pad(jnp.stack(vectors).astype(F32), ((0, 0), (0, 2 * LANES - S)))
    qkv_width = 5 * LANES
    v = pltpu.VMEM
    scratch = [
        v((GROUPS, R, D), BF),
        v((GROUPS, R, D), BF),
        v((D, qkv_width), BF),
        v((GROUPS, 8, 2 * LANES), F32),
        v((3, GROUPS, R, LANES), BF),
        v((2, half, 3 * LANES), BF),
        v((3, GROUPS, 2, R, half), BF),
        v((3, GROUPS, R, LANES), F32),
        v((GROUPS, R, 2 * LANES), F32),
        v((GROUPS, R, 2 * LANES), BF),
        v((GROUPS, R, 2 * LANES), BF),
        v((GROUPS, 2 * LANES, D), BF),
        v((GROUPS, S, FS), BF),
        v((GROUPS, R, D), BF),
        v((R, D), F32),
        v((GROUPS, R, D), BF),
        v((GROUPS, R, FS), BF),
        v((GROUPS, R, FS), BF),
        v((GROUPS, R, D), BF),
        v((4, R, D), BF),
        v((GROUPS, R, D), BF),
        v((4, R, D), BF),
        v((R, D), F32),
        v((GROUPS, R, 2 * LANES), BF),
        v((GROUPS, R, 2 * LANES), BF),
        v((2, half, 3 * LANES), F32),
        v((half, 3 * LANES), BF),
        v((half, 3 * LANES), BF),
        v((GROUPS, R, 2 * LANES), F32),
        v((half, qkv_width), BF),
        v((2, R, D), BF),
        v((2, R, D), BF),
        v((2, R, D), BF),
        v((R, D), F32),
        v((FS, D), BF),
        v((FS, D), BF),
        v((D, FS), BF),
        v((D, FS), BF),
        v((D, FS), BF),
        v((GROUPS, S, D), BF),
        v((6, S, D), BF),
        v((S, D), BF),
        v((D, qkv_width), BF),
        v((5, S, qkv_width), BF),
        v((S, qkv_width), BF),
        v((6, SMALL_ROWS, SMALL_WIDTH), F32),
        v((5, SMALL_ROWS, SMALL_WIDTH), F32),
        pltpu.SemaphoreType.DMA((SEMS,)),
        pltpu.SemaphoreType.DMA((SEMS,)),
    ]
    vmem = pl.BlockSpec(memory_space=pltpu.VMEM)
    out_shapes = [
        jax.ShapeDtypeStruct((R, D), BF),
        jax.ShapeDtypeStruct((R, D), BF),
        jax.ShapeDtypeStruct((FS, D), BF),
        jax.ShapeDtypeStruct((D, FS), BF),
        jax.ShapeDtypeStruct((S, D), BF),
        jax.ShapeDtypeStruct((GROUPS, S, qkv_width), BF),
        jax.ShapeDtypeStruct((SMALL_ROWS, SMALL_WIDTH), F32),
    ]
    outs = pl.pallas_call(
        partial(layer_kernel, (n_ctx, n_doc, R, D, S, FS)),
        out_shape=out_shapes,
        in_specs=[pl.BlockSpec(memory_space=pltpu.SMEM)] + [vmem] * 8,
        out_specs=[vmem] * len(out_shapes),
        scratch_shapes=scratch,
        compiler_params=pltpu.CompilerParams(
            collective_id=0, has_side_effects=True, vmem_limit_bytes=67043328
        ),
        name="layer",
    )(
        doc_lengths, tokens[0], out_grad[0], ws, par, b_up[None], w_out, w_up, w_down
    )
    layer_out, input_grad, g_down, g_up, g_out, g_qkv, small = outs
    column = lax.axis_index("wsh") * S

    def vector(row):
        return lax.dynamic_slice(small, (row, column), (1, S))[0]

    shard = lax.axis_index("wsh")
    q_row = lax.dynamic_slice(small, (6, shard * 2 * LANES), (1, S))[0]
    v_row = lax.dynamic_slice(small, (7, shard * 2 * LANES), (1, 2 * LANES))[0]
    v_row = jnp.concatenate([v_row[LANES:], v_row[LANES // 2 : LANES]])
    up_row = lax.dynamic_slice(small, (8 + shard, 0), (1, FS))[0]

    def heads(pieces):
        return jnp.concatenate(
            [g_qkv[i, :, a:b] for i in range(GROUPS) for a, b in pieces], axis=1
        ).astype(F32)

    return (
        layer_out[None],
        input_grad[None],
        vector(0),
        vector(1),
        heads([(0, S)]),
        q_row,
        heads([(256, 448)]),
        heads([(512, 640), (448, 512)]),
        v_row,
        g_out.astype(F32),
        vector(2),
        vector(3),
        vector(4),
        g_up.reshape(GROUPS, S, FS).transpose(1, 0, 2).reshape(S, GROUPS * FS).astype(F32),
        up_row,
        g_down.astype(F32),
        vector(5),
    )


def solution(mesh):
    in_specs = (
        P("wsh", "ctx", None),
        P("wsh", None),
        P("wsh", "ctx", None),
        P("wsh"),
        P("wsh"),
        P("wsh", None),
        P("wsh"),
        P("wsh", None),
        P("wsh", None),
        P("wsh"),
        P("wsh", None),
        P("wsh"),
        P("wsh"),
        P("wsh"),
        P("wsh", None),
        P("wsh"),
        P("wsh", None),
        P("wsh"),
    )
    out_specs = (
        P("wsh", "ctx", None),
        P("wsh", "ctx", None),
        P("wsh"),
        P("wsh"),
        P("wsh", None),
        P("wsh"),
        P("wsh", None),
        P("wsh", None),
        P("wsh"),
        P("wsh", None),
        P("wsh"),
        P("wsh"),
        P("wsh"),
        P("wsh", None),
        P("wsh"),
        P("wsh", None),
        P("wsh"),
    )
    sizes = (mesh.shape["ctx"], mesh.shape["wsh"])
    body = partial(fast_device, sizes) if sizes == (2 * GROUPS, GROUPS) else per_device
    return jax.shard_map(
        body, mesh=mesh, in_specs=in_specs, out_specs=out_specs, check_vma=False
    )
```

```python
from functools import partial
import math

import jax
import jax.numpy as jnp
from jax import lax
from jax.experimental import pallas as pl
from jax.experimental.pallas import tpu as pltpu
from jax.sharding import PartitionSpec as P

HEADS = 12


EPS = 1e-06
NEG_START = -1e30


def norm_rows(inputs, norm_gain, norm_bias):
    row_mean = jnp.mean(inputs, axis=-1, keepdims=True)
    centred = inputs - row_mean
    variance = jnp.mean(centred * centred, axis=-1, keepdims=True)
    return centred * lax.rsqrt(variance + EPS) * norm_gain + norm_bias


def doc_of(positions, doc_ends):
    return jnp.sum((positions[:, None] >= doc_ends[None, :]).astype(jnp.int32), axis=1)


def dot_plain(left, right):
    return jnp.dot(left, right, preferred_element_type=jnp.float32)


def dot_left(left, right):
    return lax.dot_general(
        left, right, (((0,), (0,)), ((), ())), preferred_element_type=jnp.float32
    )


def dot_right(left, right):
    return lax.dot_general(
        left, right, (((1,), (1,)), ((), ())), preferred_element_type=jnp.float32
    )


def masked_scores(query_heads, key_heads, query_ids, key_ids, score_scale):
    raw_scores = (
        jnp.einsum("qhd,khd->hqk", query_heads, key_heads, preferred_element_type=jnp.float32)
        * score_scale
    )
    same_doc = (query_ids[:, None] == key_ids[None, :])[None]
    return jnp.where(same_doc, raw_scores, -jnp.inf)


def per_device(
    tokens,
    doc_lengths,
    out_grad,
    norm1_gain,
    norm1_bias,
    w_query,
    b_query,
    w_key,
    w_value,
    b_value,
    w_out,
    b_out,
    norm2_gain,
    norm2_bias,
    w_up,
    b_up,
    w_down,
    b_down,
):
    (
        gain_one,
        bias_one,
        query_w,
        query_b,
        key_w,
        value_w,
        value_b,
        out_w,
        out_b,
        gain_two,
        bias_two,
        up_w,
        up_b,
        down_w,
        down_b,
    ) = (
        lax.all_gather(norm1_gain, "wsh", axis=0, tiled=True),
        lax.all_gather(norm1_bias, "wsh", axis=0, tiled=True),
        lax.all_gather(w_query, "wsh", axis=0, tiled=True),
        lax.all_gather(b_query, "wsh", axis=0, tiled=True),
        lax.all_gather(w_key, "wsh", axis=0, tiled=True),
        lax.all_gather(w_value, "wsh", axis=0, tiled=True),
        lax.all_gather(b_value, "wsh", axis=0, tiled=True),
        lax.all_gather(w_out, "wsh", axis=0, tiled=True),
        lax.all_gather(b_out, "wsh", axis=0, tiled=True),
        lax.all_gather(norm2_gain, "wsh", axis=0, tiled=True),
        lax.all_gather(norm2_bias, "wsh", axis=0, tiled=True),
        lax.all_gather(w_up, "wsh", axis=0, tiled=True),
        lax.all_gather(b_up, "wsh", axis=0, tiled=True),
        lax.all_gather(w_down, "wsh", axis=0, tiled=True),
        lax.all_gather(b_down, "wsh", axis=0, tiled=True),
    )
    row_count = tokens.shape[1]
    model_width = tokens.shape[2]
    head_dim = model_width // HEADS
    score_scale = head_dim ** (-0.5)
    first_gain = gain_one.astype(jnp.float32)
    first_bias = bias_one.astype(jnp.float32)
    second_gain = gain_two.astype(jnp.float32)
    second_bias = bias_two.astype(jnp.float32)
    inputs = tokens[0].astype(jnp.float32)
    doc_ends = jnp.cumsum(doc_lengths[0])
    own_ids = doc_of(
        lax.axis_index("ctx") * row_count + jnp.arange(row_count, dtype=jnp.int32), doc_ends
    )
    normed_one = norm_rows(inputs, first_gain, first_bias).astype(jnp.bfloat16)
    queries = (dot_plain(normed_one, query_w) + query_b.astype(jnp.float32)).astype(jnp.bfloat16)
    key_rows = dot_plain(normed_one, key_w).astype(jnp.bfloat16)
    values = (dot_plain(normed_one, value_w) + value_b.astype(jnp.float32)).astype(jnp.bfloat16)
    key_all, value_all = (
        lax.all_gather(key_rows, "ctx", axis=0, tiled=True),
        lax.all_gather(values, "ctx", axis=0, tiled=True),
    )
    total_rows = key_all.shape[0]
    key_block = math.gcd(total_rows, 2048)
    block_count = total_rows // key_block
    key_stack = key_all.reshape(block_count, key_block, HEADS, head_dim)
    value_stack = value_all.reshape(block_count, key_block, HEADS, head_dim)
    id_stack = doc_of(jnp.arange(total_rows, dtype=jnp.int32), doc_ends).reshape(
        block_count, key_block
    )
    query_heads = queries.reshape(row_count, HEADS, head_dim)

    def lse_step(running, block_in):
        run_max, run_sum = running
        key_heads, key_ids = block_in
        scores = masked_scores(query_heads, key_heads, own_ids, key_ids, score_scale)
        new_max = jnp.maximum(run_max, jnp.max(scores, axis=-1))
        new_sum = run_sum * jnp.exp(run_max - new_max) + jnp.sum(
            jnp.exp(scores - new_max[:, :, None]), axis=-1
        )
        return ((new_max, new_sum), None)

    start_max = jnp.full((HEADS, row_count), NEG_START, jnp.float32)
    (final_max, final_sum), unused = lax.scan(
        lse_step, (start_max, jnp.zeros_like(start_max)), (key_stack, id_stack)
    )
    log_total = final_max + jnp.log(final_sum)

    def out_step(running, block_in):
        key_heads, value_heads, key_ids = block_in
        scores = masked_scores(query_heads, key_heads, own_ids, key_ids, score_scale)
        attn_prob = jnp.exp(scores - log_total[:, :, None]).astype(jnp.bfloat16)
        return (
            running
            + jnp.einsum(
                "hqk,khd->qhd", attn_prob, value_heads, preferred_element_type=jnp.float32
            ),
            None,
        )

    attn_sum, unused = lax.scan(
        out_step,
        jnp.zeros((row_count, HEADS, head_dim), jnp.float32),
        (key_stack, value_stack, id_stack),
    )
    attended = attn_sum.reshape(row_count, model_width).astype(jnp.bfloat16)
    middle = inputs + dot_plain(attended, out_w) + out_b.astype(jnp.float32)
    normed_two = norm_rows(middle, second_gain, second_bias).astype(jnp.bfloat16)
    hidden = dot_plain(normed_two, up_w) + up_b.astype(jnp.float32)
    active = jax.nn.gelu(hidden, approximate=True).astype(jnp.bfloat16)
    output = middle + dot_plain(active, down_w) + down_b.astype(jnp.float32)
    top_grad = out_grad[0]
    top_float = top_grad.astype(jnp.float32)
    grad_down_w = dot_left(active, top_grad)
    grad_down_b = jnp.sum(top_float, axis=0)
    grad_active = dot_right(top_grad, down_w)
    unused, gelu_pull = jax.vjp(partial(jax.nn.gelu, approximate=True), hidden)
    grad_hidden = gelu_pull(grad_active)[0].astype(jnp.bfloat16)
    grad_up_w = dot_left(normed_two, grad_hidden)
    grad_up_b = jnp.sum(grad_hidden.astype(jnp.float32), axis=0)
    grad_normed_two = dot_right(grad_hidden, up_w)
    unused, second_pull = jax.vjp(norm_rows, middle, second_gain, second_bias)
    grad_middle, grad_gain_two, grad_bias_two = second_pull(grad_normed_two)
    grad_middle = grad_middle + top_float
    grad_branch = grad_middle.astype(jnp.bfloat16)
    grad_out_w = dot_left(attended, grad_branch)
    grad_out_b = jnp.sum(grad_branch.astype(jnp.float32), axis=0)
    grad_attended = dot_right(grad_branch, out_w).astype(jnp.bfloat16)
    grad_heads = grad_attended.reshape(row_count, HEADS, head_dim)
    row_delta = jnp.sum(grad_heads.astype(jnp.float32) * attn_sum, axis=-1)
    head_delta = row_delta.T
    query_start = jnp.zeros((row_count, HEADS, head_dim), jnp.float32)

    def full_step(grad_query, block_in):
        key_heads, value_heads, key_ids = block_in
        scores = masked_scores(query_heads, key_heads, own_ids, key_ids, score_scale)
        attn_prob = jnp.exp(scores - log_total[:, :, None])
        grad_prob = jnp.einsum(
            "qhd,khd->hqk", grad_heads, value_heads, preferred_element_type=jnp.float32
        )
        grad_score = (attn_prob * (grad_prob - head_delta[:, :, None])).astype(jnp.bfloat16)
        grad_query = grad_query + jnp.einsum(
            "hqk,khd->qhd", grad_score, key_heads, preferred_element_type=jnp.float32
        )
        grad_key = (
            jnp.einsum("hqk,qhd->khd", grad_score, query_heads, preferred_element_type=jnp.float32)
            * score_scale
        )
        grad_value = jnp.einsum(
            "hqk,qhd->khd",
            attn_prob.astype(jnp.bfloat16),
            grad_heads,
            preferred_element_type=jnp.float32,
        )
        return (
            grad_query,
            (grad_key.reshape(key_block, model_width), grad_value.reshape(key_block, model_width)),
        )

    grad_query, key_terms = lax.scan(full_step, query_start, (key_stack, value_stack, id_stack))
    key_grad, value_grad = (
        lax.psum_scatter(
            key_terms[0].reshape(total_rows, model_width), "ctx", scatter_dimension=0, tiled=True
        ),
        lax.psum_scatter(
            key_terms[1].reshape(total_rows, model_width), "ctx", scatter_dimension=0, tiled=True
        ),
    )
    grad_query_rows = (
        (grad_query * score_scale).reshape(row_count, model_width).astype(jnp.bfloat16)
    )
    grad_key_rows = key_grad.astype(jnp.bfloat16)
    grad_value_rows = value_grad.astype(jnp.bfloat16)
    grad_query_w = dot_left(normed_one, grad_query_rows)
    grad_query_b = jnp.sum(grad_query_rows.astype(jnp.float32), axis=0)
    grad_key_w = dot_left(normed_one, grad_key_rows)
    grad_value_w = dot_left(normed_one, grad_value_rows)
    grad_value_b = jnp.sum(grad_value_rows.astype(jnp.float32), axis=0)
    grad_normed_one = (
        dot_right(grad_query_rows, query_w)
        + dot_right(grad_key_rows, key_w)
        + dot_right(grad_value_rows, value_w)
    )
    unused, first_pull = jax.vjp(norm_rows, inputs, first_gain, first_bias)
    grad_inputs, grad_gain_one, grad_bias_one = first_pull(grad_normed_one)
    grad_inputs = grad_inputs + grad_middle
    (
        share_gain_one,
        share_bias_one,
        share_query_w,
        share_query_b,
        share_key_w,
        share_value_w,
        share_value_b,
        share_out_w,
        share_out_b,
        share_gain_two,
        share_bias_two,
        share_up_w,
        share_up_b,
        share_down_w,
        share_down_b,
    ) = (
        lax.psum_scatter(
            grad_gain_one.astype(jnp.bfloat16), "wsh", scatter_dimension=0, tiled=True
        ).astype(jnp.float32),
        lax.psum_scatter(
            grad_bias_one.astype(jnp.bfloat16), "wsh", scatter_dimension=0, tiled=True
        ).astype(jnp.float32),
        lax.psum_scatter(
            grad_query_w.astype(jnp.bfloat16), "wsh", scatter_dimension=0, tiled=True
        ).astype(jnp.float32),
        lax.psum_scatter(
            grad_query_b.astype(jnp.bfloat16), "wsh", scatter_dimension=0, tiled=True
        ).astype(jnp.float32),
        lax.psum_scatter(
            grad_key_w.astype(jnp.bfloat16), "wsh", scatter_dimension=0, tiled=True
        ).astype(jnp.float32),
        lax.psum_scatter(
            grad_value_w.astype(jnp.bfloat16), "wsh", scatter_dimension=0, tiled=True
        ).astype(jnp.float32),
        lax.psum_scatter(
            grad_value_b.astype(jnp.bfloat16), "wsh", scatter_dimension=0, tiled=True
        ).astype(jnp.float32),
        lax.psum_scatter(
            grad_out_w.astype(jnp.bfloat16), "wsh", scatter_dimension=0, tiled=True
        ).astype(jnp.float32),
        lax.psum_scatter(
            grad_out_b.astype(jnp.bfloat16), "wsh", scatter_dimension=0, tiled=True
        ).astype(jnp.float32),
        lax.psum_scatter(
            grad_gain_two.astype(jnp.bfloat16), "wsh", scatter_dimension=0, tiled=True
        ).astype(jnp.float32),
        lax.psum_scatter(
            grad_bias_two.astype(jnp.bfloat16), "wsh", scatter_dimension=0, tiled=True
        ).astype(jnp.float32),
        lax.psum_scatter(
            grad_up_w.astype(jnp.bfloat16), "wsh", scatter_dimension=0, tiled=True
        ).astype(jnp.float32),
        lax.psum_scatter(
            grad_up_b.astype(jnp.bfloat16), "wsh", scatter_dimension=0, tiled=True
        ).astype(jnp.float32),
        lax.psum_scatter(
            grad_down_w.astype(jnp.bfloat16), "wsh", scatter_dimension=0, tiled=True
        ).astype(jnp.float32),
        lax.psum_scatter(
            grad_down_b.astype(jnp.bfloat16), "wsh", scatter_dimension=0, tiled=True
        ).astype(jnp.float32),
    )
    totals = lax.psum(
        (
            share_gain_one,
            share_bias_one,
            share_query_w,
            share_query_b,
            share_key_w,
            share_value_w,
            share_value_b,
            share_out_w,
            share_out_b,
            share_gain_two,
            share_bias_two,
            share_up_w,
            share_up_b,
            share_down_w,
            share_down_b,
        ),
        "ctx",
    )
    return (
        output.astype(jnp.bfloat16)[None],
        grad_inputs.astype(jnp.bfloat16)[None],
        totals[0],
        totals[1],
        totals[2],
        totals[3],
        totals[4],
        totals[5],
        totals[6],
        totals[7],
        totals[8],
        totals[9],
        totals[10],
        totals[11],
        totals[12],
        totals[13],
        totals[14],
    )


MESH = pl.DeviceIdType.MESH
F32 = jnp.float32
BF = jnp.bfloat16
GROUPS = 4
LANES = 128


def flip(value, mask):
    return ((value // 2 + mask // 2) % 2) * 2 + (value + mask) % 2


def dot_nn(left, right):
    return lax.dot_general(left, right, (((1,), (0,)), ((), ())), preferred_element_type=F32)


def dot_nt(left, right):
    return lax.dot_general(left, right, (((1,), (1,)), ((), ())), preferred_element_type=F32)


def dot_tn(left, right):
    return lax.dot_general(left, right, (((0,), (0,)), ((), ())), preferred_element_type=F32)


def unit_rows(inputs):
    row_mean = jnp.mean(inputs, axis=-1, keepdims=True)
    centred = inputs - row_mean
    variance = jnp.mean(centred * centred, axis=-1, keepdims=True)
    scale = lax.rsqrt(variance + EPS)
    return centred * scale, scale


def unit_rows_back(grad_normed, unit, scale, gain):
    grad_unit = grad_normed * gain
    return scale * (
        grad_unit
        - jnp.mean(grad_unit, axis=-1, keepdims=True)
        - unit * jnp.mean(grad_unit * unit, axis=-1, keepdims=True)
    )


def rows_sum(values):
    return jnp.sum(values, axis=0, keepdims=True)


def sum_bf(*values):
    return sum([one.astype(F32) for one in values]).astype(BF)


class Wires:
    def __init__(self, send_sems, recv_sems):
        self.send_sems, self.recv_sems, self.used, self.started = send_sems, recv_sems, 0, []

    def take(self, count=1):
        first = self.used
        self.used += count
        return first

    def copy(self, index, source, target, device):
        return pltpu.make_async_remote_copy(
            src_ref=source,
            dst_ref=target,
            send_sem=self.send_sems.at[index],
            recv_sem=self.recv_sems.at[index],
            device_id=device,
            device_id_type=MESH,
        )

    def send(self, source, target, device):
        one = self.copy(self.take(), source, target, device)
        one.start()
        self.started.append((one, None))
        return one

    def later(self, one, when=None):
        self.started.append((one, when))

    def drain(self):
        for one, when in self.started:
            if when is None:
                one.wait_send()
            else:
                pl.when(when)(one.wait_send)


def layer_kernel(sizes, names, *refs):
    n_ctx, n_doc, R, D, S, FS = sizes
    r = dict(zip(names, refs, strict=True))
    G = n_ctx // GROUPS
    last = GROUPS - 1
    half = GROUPS * R
    c = lax.axis_index("ctx")
    w = lax.axis_index("wsh")
    hg, px = c // G, c % G

    def zdev(group):
        return {"ctx": group * G + px, "wsh": w}

    def wdev(index):
        return {"ctx": c, "wsh": index}

    xdev = {"ctx": hg * G + 1 - px, "wsh": w}
    left, right = zdev((hg + last) % GROUPS), zdev((hg + 1) % GROUPS)
    w1, w2, w3 = flip(w, 1), flip(w, 2), flip(w, 3)
    sib, across, diag = wdev(w1), wdev(w2), wdev(w3)
    wires = Wires(r["send_sems"], r["recv_sems"])
    lane = lax.broadcasted_iota(jnp.int32, (1, LANES), 1)
    low_half = lane < LANES // 2

    def pick(table):
        return sum([jnp.where(hg == i, one, 0) for i, one in enumerate(table)])

    def by_distance(step):
        return (
            jnp.where(step == 0, pick((3, 3, 0, 0)), 0)
            + jnp.where(step == 1, pick((2, 0, 3, 1)), 0)
            + jnp.where(step == 2, pick((1, 2, 1, 2)), 0)
            + jnp.where(step == 3, hg, 0)
        )

    local = r["local_sems"]

    def fetch(index, source, target):
        one = pltpu.make_async_copy(source, target, local.at[index])
        one.start()
        return one

    tok_in = fetch(0, r["tok"], r["x_s"].at[hg])
    qkv_in = [fetch(1 + i, r[name], r["win_s"].at[i]) for i, name in enumerate(("wq", "wk", "wv"))]
    dy_in = fetch(4, r["dy"], r["dy_s"].at[w])
    wo_in = [
        fetch(5, r["wout"].at[pl.ds(0, LANES)], r["wo_s"].at[w, pl.ds(0, LANES)]),
        fetch(6, r["wout"].at[pl.ds(LANES, S - LANES)], r["wo_s"].at[w, pl.ds(S, S - LANES)]),
    ]
    wu_in = fetch(7, r["wup"].at[:, pl.ds(pl.multiple_of(w * FS, FS), FS)], r["wu_s"].at[w])
    wd_in = fetch(8, r["wdown"], r["wd_s"])

    barrier = pltpu.get_barrier_semaphore()
    ctx_peers = [{"ctx": (c + i) % n_ctx, "wsh": w} for i in range(1, n_ctx)]
    partners = ctx_peers + [sib, across, diag]
    for partner in partners:
        pl.semaphore_signal(barrier, inc=1, device_id=partner, device_id_type=MESH)

    for one in qkv_in:
        one.wait()
    own_w = pl.ds(pl.multiple_of(w * S, S), S)
    win, wq_s = r["win_s"], r["wq_s"]
    for g in range(GROUPS):

        @pl.when(hg == g)
        def _():
            a = g * S
            wq_s[own_w, 0:S] = win[0, :, a : a + S]
            wq_s[own_w, S : 2 * LANES] = jnp.zeros((S, 2 * LANES - S), BF)
            wq_s[own_w, 2 * LANES : 2 * LANES + S] = win[1, :, a : a + S]
            wq_s[own_w, 2 * LANES + S : 4 * LANES] = win[2, :, a + LANES : a + S]
            wq_s[own_w, 4 * LANES : 5 * LANES] = win[2, :, a : a + LANES]

    par_s = r["par_s"]
    par_s[w] = jnp.zeros((8, 2 * LANES), F32)
    for i, name in enumerate(("n1g", "n1b", "bq", "bv", "bo", "n2g", "n2b", "bd")):
        par_s[w, i : i + 1, 0:S] = r[name][...].astype(F32)
    r["wo_s"][:, LANES:S, :] = jnp.zeros((GROUPS, S - LANES, D), BF)
    tok_in.wait()
    pl.semaphore_wait(barrier, len(partners))

    class Gather:
        def __init__(self, slot):
            self.slot = slot
            self.to_across = wires.send(slot(w), slot(w), across)
            self.to_sib = wires.send(slot(w), slot(w), sib)

        def relay(self):
            self.to_across.wait_recv()
            self.on = wires.send(self.slot(w2), self.slot(w2), sib)

        def finish(self):
            self.to_sib.wait_recv()
            self.on.wait_recv()

    class Reduce:
        def __init__(self, part, recv):
            self.part, self.recv = part, recv

        def send_sib(self):
            self.b = wires.send(self.part(w1), self.recv.at[1], sib)

        def send_diag(self):
            self.a = wires.send(self.part(w3), self.recv.at[0], sib)

        def combine(self):
            self.a.wait_recv()
            self.recv[3] = sum_bf(self.part(w2)[...], self.recv[0])
            self.c = wires.send(self.recv.at[3], self.recv.at[2], across)

        def finish(self):
            self.b.wait_recv()
            self.c.wait_recv()
            return (
                self.part(w)[...].astype(F32)
                + self.recv[1].astype(F32)
                + self.recv[2].astype(F32)
            )

    class LineSum:
        def __init__(self, part, recv):
            self.part, self.recv = part, recv
            self.first_at = wires.take(6)
            for i in range(3):
                wires.later(self.message(i, True), hg > i)
                wires.later(self.message(i, False), hg < last - i)

        def message(self, i, leftward):
            block, slot = (i, i) if leftward else (last - i, 3 + i)
            return wires.copy(
                self.first_at + slot, self.part(block), self.recv.at[slot], left if leftward else right
            )

        def ends_block(self, block):
            for i in range(3):

                @pl.when((hg == last) & (block == i))
                def _():
                    self.message(i, True).start()

                @pl.when((hg == 0) & (block == last - i))
                def _():
                    self.message(i, False).start()

        def ends(self):
            for i in range(3):

                @pl.when(hg == last)
                def _():
                    self.message(i, True).start()

                @pl.when(hg == 0)
                def _():
                    self.message(i, False).start()

        def pass_on(self, position, i, leftward):
            @pl.when(hg == position)
            def _():
                one = self.message(i, leftward)
                one.wait_recv()
                block, slot = (i, i) if leftward else (last - i, 3 + i)
                self.part(block)[...] = sum_bf(self.part(block)[...], self.recv[slot])
                one.start()

        def second(self):
            for i in range(2):
                self.pass_on(2, i, True)
                self.pass_on(1, i, False)

        def third(self):
            self.pass_on(1, 0, True)
            self.pass_on(2, 0, False)

        def final(self, put):
            for position in range(GROUPS):

                @pl.when(hg == position)
                def _():
                    total = self.part(position)[...].astype(F32)
                    if position < last:
                        self.message(position, True).wait_recv()
                        total = total + self.recv[position].astype(F32)
                    if position > 0:
                        self.message(last - position, False).wait_recv()
                        total = total + self.recv[3 + last - position].astype(F32)
                    put(total)

    class LineGather:
        def __init__(self, slot, to_x):
            self.slot, self.to_x = slot, to_x
            self.first_at = wires.take(6)
            self.x_at = wires.take(GROUPS) if to_x else None
            for d in (1, 2, 3):
                wires.later(self.message(d, 0), (hg >= d - 1) & (hg < last))
                wires.later(self.message(d, 1), (hg + d - 1 <= last) & (hg > 0))
            if to_x:
                for b in range(GROUPS):
                    wires.later(self.x_message(b))

        def message(self, d, side):
            block = (hg + GROUPS + (1 - d) * (1 - 2 * side)) % GROUPS
            device = zdev((hg + GROUPS + 1 - 2 * side) % GROUPS)
            return wires.copy(
                self.first_at + 3 * side + d - 1, self.slot(block), self.slot(block), device
            )

        def x_message(self, block):
            return wires.copy(self.x_at + block, self.slot(block), self.slot(block), xdev)

        def start(self):
            pl.when(hg < last)(self.message(1, 0).start)
            pl.when(hg > 0)(self.message(1, 1).start)
            if self.to_x:
                self.x_message(hg).start()

        def arrived(self, d, side, then=None):
            block = (hg + GROUPS - d * (1 - 2 * side)) % GROUPS
            here = jnp.where(side == 0, (hg >= d).astype(jnp.int32), (hg + d <= last).astype(jnp.int32))
            onward = here * jnp.where(side == 0, (hg < last).astype(jnp.int32), (hg > 0).astype(jnp.int32))

            @pl.when(here == 1)
            def _():
                wires.copy(
                    self.first_at + 3 * side + d - 1, self.slot(block), self.slot(block), left
                ).wait_recv()

            @pl.when(onward == 1)
            def _():
                self.message(d + 1, side).start()

            @pl.when(here == 1)
            def _():
                if self.to_x:
                    self.x_message(block).start()
                if then is not None:
                    then(block)

        def step(self, d):
            self.arrived(d, 0)
            self.arrived(d, 1)

        def done(self):
            for b in range(GROUPS):
                self.x_message(b).wait_recv()

    x_s, h1_s, q_s, kv_s = r["x_s"], r["h1_s"], r["q_s"], r["kv_s"]
    tokens = LineGather(lambda b: x_s.at[b], False)
    tokens.start()
    ws_all = Gather(lambda i: wq_s.at[pl.ds(pl.multiple_of(i * S, S), S)])
    par_all = Gather(lambda i: par_s.at[i])
    par_all.relay()
    ws_all.relay()
    par_all.finish()

    pars = jnp.concatenate([par_s[i][:, :S] for i in range(GROUPS)], axis=1)
    gain_one, bias_one, out_b, gain_two, bias_two, down_b = [
        pars[i : i + 1] for i in (0, 1, 4, 5, 6, 7)
    ]
    up_b = r["bup"][...].astype(F32)
    own_par = par_s[hg]
    v_tile, v_last = own_par[3:4, :LANES], own_par[3:4, LANES:]
    qkv_b = jnp.concatenate(
        [own_par[2:3, :], jnp.zeros((1, LANES), F32), pltpu.roll(v_last, LANES // 2, 1), v_tile],
        axis=1,
    )

    def norm_block(block):
        unit, unused = unit_rows(x_s[block].astype(F32))
        h1_s[block] = (unit * gain_one + bias_one).astype(BF)

    norm_block(hg)
    ws_all.finish()
    for one in wo_in:
        one.wait()
    dy_in.wait()
    wo_s, dy_s, wu_s = r["wo_s"], r["dy_s"], r["wu_s"]
    wo_top = Gather(lambda i: wo_s.at[i, pl.ds(0, LANES)])
    wo_low = Gather(lambda i: wo_s.at[i, pl.ds(S, S - LANES)])
    dy_all = Gather(lambda i: dy_s.at[i])

    kv_first = wires.take(GROUPS)

    def kv_copy(block):
        rows = pl.ds(pl.multiple_of(block * R, R), R)
        return wires.copy(kv_first + block, kv_s.at[0, rows], kv_s.at[1, rows], xdev)

    def project(block):
        qkv = dot_nn(h1_s[block], wq_s[...]) + qkv_b
        queries = qkv[:, : 2 * LANES].astype(BF).astype(F32) * 0.125
        q_s[0, block] = jnp.where(low_half, queries[:, :LANES], 0.0).astype(BF)
        q_s[1, block] = jnp.where(low_half, 0.0, queries[:, :LANES]).astype(BF)
        q_s[2, block] = queries[:, LANES:].astype(BF)
        kv_s[0, pl.ds(pl.multiple_of(block * R, R), R), :] = qkv[:, 2 * LANES :].astype(BF)
        kv_copy(block).start()

    def norm_project(block):
        norm_block(block)
        project(block)

    project(hg)

    def token_step(i, carry):
        tokens.arrived(i // 2 + 1, i % 2, norm_project)
        return carry

    lax.fori_loop(0, 6, token_step, 0)
    wo_top.relay()
    wo_low.relay()
    dy_all.relay()
    up_sends = [
        wires.send(
            r["wup"].at[:, pl.ds(pl.multiple_of(flip(w, k) * FS, FS), FS)],
            wu_s.at[w],
            wdev(flip(w, k)),
        )
        for k in (2, 3, 1)
    ]
    for b in range(GROUPS):
        kv_copy(b).wait_recv()
        wires.later(kv_copy(b))

    doc_ends = []
    for i in range(n_doc):
        doc_ends.append(r["doc"][0, i] + (doc_ends[-1] if i else 0))

    def doc_ids(positions):
        return sum([(positions >= end).astype(jnp.int32) for end in doc_ends])

    key_at = lax.broadcasted_iota(jnp.int32, (1, half), 1)
    key_block = sum([(key_at >= i * R).astype(jnp.int32) for i in range(1, GROUPS)])
    key_base = key_at + key_block * (R * (G - 1))
    key_ids = [doc_ids(key_base + px * R), doc_ids(key_base + (1 - px) * R)]
    KT, VT = (0, 0, LANES), (2 * LANES, 2 * LANES, LANES)
    e_s, li_s, oa_s, os_s, or_s = r["e_s"], r["li_s"], r["oa_s"], r["os_s"], r["or_s"]

    class Turn:
        def __init__(self, source, target):
            self.source, self.target = source, target
            self.first_at = wires.take(GROUPS)
            for i in (1, 2, 3):
                wires.later(self.message((hg + i) % GROUPS))

        def message(self, block):
            index = self.first_at + (block - hg + GROUPS) % GROUPS
            return wires.copy(index, self.source.at[block], self.target.at[hg], zdev(block))

        def arrived(self, block):
            index = self.first_at + (hg - block + GROUPS) % GROUPS
            wires.copy(index, self.target.at[block], self.target.at[block], left).wait_recv()

    o_turn = Turn(os_s, or_s)

    def attend(step, carry):
        block = by_distance(step)
        row_at = (block * G + px) * R + lax.broadcasted_iota(jnp.int32, (R, 1), 0)
        row_ids = doc_ids(row_at)
        outs = []
        for h in range(3):
            queries = q_s[h, block]
            scores = [
                jnp.where(
                    row_ids == key_ids[side],
                    dot_nt(queries, kv_s[side, :, KT[h] : KT[h] + LANES]),
                    NEG_START,
                )
                for side in (0, 1)
            ]
            top = jnp.maximum(
                jnp.max(scores[0], axis=-1, keepdims=True), jnp.max(scores[1], axis=-1, keepdims=True)
            )
            weights = [jnp.exp(one - top) for one in scores]
            total = jnp.sum(weights[0], axis=-1, keepdims=True) + jnp.sum(
                weights[1], axis=-1, keepdims=True
            )
            inverse = 1.0 / total
            mixed = jnp.zeros((R, LANES), F32)
            for side in (0, 1):
                rounded = weights[side].astype(BF)
                e_s[h, block, side] = rounded
                mixed += dot_nn(rounded, kv_s[side, :, VT[h] : VT[h] + LANES])
            li_s[h, block] = jnp.broadcast_to(inverse, (R, LANES))
            outs.append(mixed * inverse)
        first = jnp.where(low_half, outs[0], outs[1])
        final = jnp.where(low_half, 0.0, outs[2])
        oa_s[block, :, :LANES] = first
        oa_s[block, :, LANES:] = final
        os_s[block, :, :LANES] = first.astype(BF)
        os_s[block, :, LANES:] = final.astype(BF)

        @pl.when(step < last)
        def _():
            o_turn.message(block).start()

        return carry

    lax.fori_loop(0, GROUPS, attend, 0)
    or_s[hg] = os_s[hg]
    wo_top.finish()
    wo_low.finish()
    for i in (1, 2, 3):
        o_turn.arrived((hg + i) % GROUPS)

    middle = x_s[hg].astype(F32) + out_b
    for i in range(GROUPS):
        middle += dot_nn(or_s[i], wo_s[i])
    x1_s, h2_s, g_s, da_s = r["x1_s"], r["h2_s"], r["g_s"], r["da_s"]
    x1_s[...] = middle
    unit_two, scale_two = unit_rows(middle)
    h2_s[w] = (unit_two * gain_two + bias_two).astype(BF)
    h2_all = Gather(lambda i: h2_s.at[i])
    dy_all.finish()
    wu_in.wait()
    wd_in.wait()
    for one in up_sends:
        one.wait_recv()
    ph_s, hr_s, wd_s = r["ph_s"], r["hr_s"], r["wd_s"]
    ph = Reduce(lambda i: ph_s.at[i], hr_s)

    def up_and_back(slot):
        hidden = dot_nn(h2_s[slot], wu_s[...].reshape(D, FS)) + up_b
        square = hidden * hidden
        inner = math.sqrt(2.0 / math.pi) * (hidden + 0.044715 * (square * hidden))
        bent = jnp.tanh(inner)
        g_s[slot] = (0.5 * hidden * (1.0 + bent)).astype(BF)
        slope = 0.5 * (1.0 + bent) + 0.5 * hidden * (1.0 - bent * bent) * (
            math.sqrt(2.0 / math.pi) * (1.0 + 3.0 * 0.044715 * square)
        )
        grad_active = dot_nt(dy_s[slot], wd_s[...])
        grad_hidden = (grad_active * slope).astype(BF)
        da_s[slot] = grad_hidden
        ph_s[slot] = dot_nt(grad_hidden, wu_s[...].reshape(D, FS)).astype(BF)

    on_copy = wires.copy(wires.take(), h2_s.at[w2], h2_s.at[w2], sib)
    ph.b = wires.copy(wires.take(), ph_s.at[w1], hr_s.at[1], sib)
    ph.a = wires.copy(wires.take(), ph_s.at[w3], hr_s.at[0], sib)

    def mlp_step(j, carry):
        @pl.when(j == 1)
        def _():
            h2_all.to_sib.wait_recv()

        @pl.when(j == 2)
        def _():
            h2_all.to_across.wait_recv()
            on_copy.start()

        @pl.when(j == 3)
        def _():
            on_copy.wait_recv()

        up_and_back(flip(w, j))

        @pl.when(j == 1)
        def _():
            ph.b.start()

        @pl.when(j == 3)
        def _():
            ph.a.start()

        return carry

    lax.fori_loop(0, GROUPS, mlp_step, 0)
    for one in (on_copy, ph.b, ph.a):
        wires.later(one)

    gus_s, gds_s, py_s = r["gus_s"], r["gds_s"], r["py_s"]

    def up_grad(i, carry):
        at = pl.ds(pl.multiple_of(i * 256, 256), 256)
        gus_s[at, :] = dot_tn(
            h2_s[:, :, at].reshape(half, 256), da_s[...].reshape(half, FS)
        ).astype(BF)
        return carry

    def down_grad(i, carry):
        at = pl.ds(pl.multiple_of(i * 256, 256), 256)
        gds_s[at, :] = dot_tn(
            g_s[:, :, at].reshape(half, 256), dy_s[...].reshape(half, D)
        ).astype(BF)
        return carry

    def y_part(j, carry):
        py_s[j] = dot_nn(g_s[j], wd_s[...]).astype(BF)
        return carry

    lax.fori_loop(0, FS // 256, down_grad, 0)

    class Spread:
        def __init__(self, part, recv, final, rows):
            self.part, self.recv, self.n = part, recv, rows // 8
            n = self.n
            self.base = px * (4 * n)
            self.sum = LineSum(lambda b: part.at[self.rows(self.base + b * n, n)], recv)
            self.gather = LineGather(lambda b: final.at[self.rows(self.base + b * n, n)], True)

        def rows(self, start, count):
            return pl.ds(pl.multiple_of(start, 8), count)

        def x_out(self, recv_x):
            there = self.rows((1 - px) * 4 * self.n, 4 * self.n)
            self.recv_x = recv_x
            self.m1 = wires.send(self.part.at[there], recv_x, xdev)

        def x_in(self):
            self.m1.wait_recv()
            here = self.rows(self.base, 4 * self.n)
            self.part[here, :] = sum_bf(self.part[here, :], self.recv_x[...])
            self.sum.ends()

        def second(self):
            self.sum.second()

        def third(self):
            self.sum.third()

        def turn(self):
            def put(total):
                self.gather.slot(hg)[...] = total.astype(BF)

            self.sum.final(put)
            self.gather.start()

        def step(self, d):
            self.gather.step(d)

        def done(self):
            self.gather.done()

    down = Spread(gds_s, r["gdl_s"], r["gdown"], FS)
    down.x_out(r["gdx_s"])
    ph.combine()
    lax.fori_loop(0, GROUPS, y_part, 0)
    py = Reduce(lambda i: py_s.at[i], r["yr_s"])
    py.send_diag()
    py.send_sib()
    lax.fori_loop(0, D // 256, up_grad, 0)
    grad_two = ph.finish()
    gu_s = r["gu_s"]
    up_back = [
        wires.send(
            gus_s.at[pl.ds(pl.multiple_of(flip(w, k) * S, S), S)],
            gu_s.at[pl.ds(pl.multiple_of(w * S, S), S)],
            wdev(flip(w, k)),
        )
        for k in (2, 3, 1)
    ]

    dz_s, dos_s, dor_s = r["dz_s"], r["dos_s"], r["dor_s"]
    unit_two, scale_two = unit_rows(x1_s[...])
    top = r["dy_s"][w].astype(F32)
    grad_middle = top + unit_rows_back(grad_two, unit_two, scale_two, gain_two)
    dz = grad_middle.astype(BF)
    dz_s[...] = grad_middle
    do_turn = Turn(dos_s, dor_s)

    def out_back(step, carry):
        block = by_distance(step)
        dos_s[block] = dot_nt(dz, wo_s[block]).astype(BF)

        @pl.when(step < last)
        def _():
            do_turn.message(block).start()

        return carry

    lax.fori_loop(0, GROUPS, out_back, 0)
    dor_s[hg] = dos_s[hg]
    early = r["early_s"]
    W_EARLY = 4 * D + 4 * LANES + FS
    early[c, :, 0:D] = rows_sum(dz.astype(F32))
    early[c, :, D : 2 * D] = rows_sum(grad_two * unit_two)
    early[c, :, 2 * D : 3 * D] = rows_sum(grad_two)
    early[c, :, 3 * D : 4 * D] = rows_sum(top)
    early[c, :, 4 * D + 4 * LANES :] = rows_sum(da_s[...].reshape(half, FS).astype(F32))

    gos_s, gor_s = r["gos_s"], r["gor_s"]
    for i in range(GROUPS):
        piece = dot_tn(or_s[i], dz)
        gos_s[i, 0:LANES, :] = piece[0:LANES, :].astype(BF)
        gos_s[i, LANES:S, :] = piece[S:, :].astype(BF)
    go = Reduce(lambda i: gos_s.at[i], gor_s)
    go.send_diag()
    go.send_sib()

    dkv_s, dq_s, dqkv_s = r["dkv_s"], r["dq_s"], r["dqkv_s"]
    dkv_s[...] = jnp.zeros(dkv_s.shape, F32)

    def back_block(block, side):
        outs = dor_s[block].astype(F32)
        kept = oa_s[block]
        grads_q = []
        for h in range(3):
            tile = 0 if h < 2 else LANES
            keep = low_half if h == 0 else jnp.logical_not(low_half)
            scaled = jnp.where(keep, outs[:, tile : tile + LANES], 0.0) * li_s[h, block]
            delta = jnp.sum(scaled * kept[:, tile : tile + LANES], axis=-1, keepdims=True)
            rounded = scaled.astype(BF)
            grad_prob = dot_nt(rounded, kv_s[side, :, VT[h] : VT[h] + LANES])
            weights = e_s[h, block, side]
            grad_score = (weights.astype(F32) * (grad_prob - delta)).astype(BF)
            grads_q.append(dot_nn(grad_score, kv_s[side, :, KT[h] : KT[h] + LANES]))
            dkv_s[side, :, KT[h] : KT[h] + LANES] += dot_tn(grad_score, q_s[h, block])
            dkv_s[side, :, VT[h] : VT[h] + LANES] += dot_tn(weights, rounded)
        first = jnp.where(low_half, grads_q[0], grads_q[1]) * 0.125
        final = jnp.where(low_half, grads_q[2], 0.0) * 0.125
        if side == 1:
            dq_s[block, :, :LANES] = first
            dq_s[block, :, LANES:] = final
        else:
            rows = pl.ds(pl.multiple_of(block * R, R), R)
            dqkv_s[rows, :LANES] = (dq_s[block, :, :LANES] + first).astype(BF)
            dqkv_s[rows, LANES : 2 * LANES] = (dq_s[block, :, LANES:] + final).astype(BF)

    def nearest(step):
        return by_distance(last - step)

    def back_other(step, carry):
        block = nearest(step)

        @pl.when(step > 0)
        def _():
            do_turn.arrived(block)

        back_block(block, 1)

        @pl.when(step == 2)
        def _():
            down.x_in()

        @pl.when(step == 3)
        def _():
            go.combine_now()

        return carry

    def combine_now():
        go.a.wait_recv()
        go.recv[3] = sum_bf(go.part(w2)[...], go.recv[0])
        go.c.start()

    go.combine_now = combine_now
    go.c = wires.copy(wires.take(), gor_s.at[3], gor_s.at[2], across)
    lax.fori_loop(0, GROUPS, back_other, 0)
    wires.later(go.c)
    kvt_s, kvr_s = r["kvt_s"], r["kvr_s"]
    kvt_s[...] = dkv_s[1].astype(BF)
    kv_back = wires.send(kvt_s, kvr_s, xdev)

    def back_own(step, carry):
        back_block(nearest(step), 0)

        @pl.when(step == 1)
        def _():
            down.second()

        return carry

    lax.fori_loop(0, GROUPS, back_own, 0)
    down.third()
    for one in up_back:
        one.wait_recv()
    gu_s[own_w, :] = gus_s[own_w, :]
    gu_s[D : D + S, :] = go.finish().astype(BF)
    py.combine()
    kv_back.wait_recv()
    dqkv_s[:, 2 * LANES :] = sum_bf(dkv_s[0], kvr_s[...])
    up = Spread(gu_s, r["gul_s"], r["gup"], D + S)
    up.x_out(r["gux_s"])

    ph1_s = r["ph1_s"]
    h1_sum = LineSum(lambda b: ph1_s.at[b], r["h1r_s"])

    def h1_part(step, carry):
        block = by_distance(step)
        rows = pl.ds(pl.multiple_of(block * R, R), R)
        ph1_s[block] = dot_nt(dqkv_s[rows, :], wq_s[...]).astype(BF)
        h1_sum.ends_block(block)
        return carry

    lax.fori_loop(0, GROUPS, h1_part, 0)

    gqs_s = r["gqs_s"]

    def qkv_grad(i, carry):
        at = pl.ds(pl.multiple_of(i * 256, 256), 256)
        gqs_s[at, :] = dot_tn(h1_s[:, :, at].reshape(half, 256), dqkv_s[...]).astype(BF)
        return carry

    lax.fori_loop(0, D // 256, qkv_grad, 0)
    gq = Reduce(lambda i: gqs_s.at[pl.ds(pl.multiple_of(i * S, S), S)], r["gqr_s"])
    gq.send_diag()
    gq.send_sib()
    early[c, :, 4 * D : 4 * D + 2 * LANES] = rows_sum(dqkv_s[:, : 2 * LANES].astype(F32))
    early[c, :, 4 * D + 2 * LANES : 4 * D + 4 * LANES] = rows_sum(
        dqkv_s[:, 3 * LANES :].astype(F32)
    )

    class Share:
        def __init__(self, rows):
            self.rows = rows
            self.at = wires.take(n_ctx)
            for i in range(1, n_ctx):
                one = wires.copy(self.at + i, rows.at[c], rows.at[c], ctx_peers[i - 1])
                one.start()
                wires.later(one)

        def total(self):
            for i in range(1, n_ctx):
                wires.copy(self.at + i, self.rows.at[c], self.rows.at[c], left).wait_recv()
            return sum([self.rows[i] for i in range(n_ctx)])

    early_all = Share(early)
    gq.combine()
    h1_sum.second()
    down.turn()
    h1_sum.third()
    gqc_s, gqx_s, gqkv = r["gqc_s"], r["gqx_s"], r["gqkv"]
    gqc_s[...] = gq.finish().astype(BF)
    n = S // 2
    mine = pl.ds(pl.multiple_of(px * n, 8), n)
    qx = wires.send(gqc_s.at[pl.ds(pl.multiple_of((1 - px) * n, 8), n)], gqx_s, xdev)
    down.step(1)
    up.x_in()
    late = r["late_s"]

    def put_h1(grad_one):
        unit_one, scale_one = unit_rows(x_s[hg].astype(F32))
        grad_in = dz_s[...] + unit_rows_back(grad_one, unit_one, scale_one, gain_one)
        r["dx"][...] = grad_in.astype(BF)
        late[c, :, 0:D] = rows_sum(grad_one * unit_one)
        late[c, :, D : 2 * D] = rows_sum(grad_one)

    df_s = r["df_s"]

    def keep_h1(total):
        df_s[...] = total

    h1_sum.final(keep_h1)
    put_h1(df_s[...])
    late_all = Share(late)
    qx.wait_recv()
    gqkv[hg, mine, :] = sum_bf(gqc_s[mine, :], gqx_s[...])
    q_line = LineGather(lambda b: gqkv.at[b, mine], True)
    q_line.start()
    down.step(2)
    up.second()
    q_line.step(1)
    up.third()
    down.step(3)
    q_line.step(2)
    up.turn()
    r["y"][...] = (x1_s[...] + py.finish() + down_b).astype(BF)
    ones = early_all.total()
    twos = late_all.total()
    bq_all, bv_all = [], []
    for g in range(GROUPS):
        group_sum = sum([early[g * G + i] for i in range(G)])
        bq_all.append(group_sum[:, 4 * D : 4 * D + S])
        v_end = pltpu.roll(
            group_sum[:, 4 * D + 2 * LANES : 4 * D + 3 * LANES], LANES // 2, 1
        )[:, : S - LANES]
        bv_all.append(
            jnp.concatenate([group_sum[:, 4 * D + 3 * LANES : 4 * D + 4 * LANES], v_end], axis=1)
        )
    vectors = [twos[:, 0:D], twos[:, D:]] + [ones[:, i * D : (i + 1) * D] for i in range(4)]
    vecs, vecr = r["vecs_s"], r["vecr_s"]
    for i in range(GROUPS):
        for j, one in enumerate(vectors):
            vecs[i, :, j * 256 : j * 256 + S] = one[:, i * S : (i + 1) * S]
        vecs[i, :, 6 * 256 : 6 * 256 + S] = bq_all[i]
        vecs[i, :, 7 * 256 : 7 * 256 + S] = bv_all[i]
    vec_sends = [wires.send(vecs.at[flip(w, k)], vecr.at[k - 1], wdev(flip(w, k))) for k in (1, 2, 3)]
    up.step(1)
    q_line.step(3)
    for one in vec_sends:
        one.wait_recv()
    r["vec"][:, 0 : 8 * 256] = vecs[w] + vecr[0] + vecr[1] + vecr[2]
    r["vec"][:, 8 * 256 :] = ones[:, 4 * D + 4 * LANES :]
    up.step(2)
    up.step(3)
    down.done()
    q_line.done()
    up.done()
    wires.drain()


def widen_kernel(S, FS, y, dx, down, up, out, qkv, y_out, dx_out, down_out, up_out, out_out, q_out, k_out, v_out):
    y_out[...] = y[...]
    dx_out[...] = dx[...]
    down_out[...] = down[...].astype(F32)
    up_out[...] = up[...].astype(F32)
    out_out[...] = out[...].astype(F32)

    def heads(pieces):
        return jnp.concatenate(
            [qkv[i, :, a:b].astype(F32) for i in range(GROUPS) for a, b in pieces], axis=1
        )

    q_out[...] = heads([(0, S)])
    k_out[...] = heads([(2 * LANES, 2 * LANES + S)])
    v_out[...] = heads([(4 * LANES, 5 * LANES), (2 * LANES + S, 4 * LANES)])


SEMS = 160


def fast_device(mesh_sizes, *arrays):
    (tokens, doc_lengths, out_grad, norm1_gain, norm1_bias, w_query, b_query, w_key, w_value,
     b_value, w_out, b_out, norm2_gain, norm2_bias, w_up, b_up, w_down, b_down) = arrays
    n_ctx, n_wsh = mesh_sizes
    R, D = tokens.shape[1], tokens.shape[2]
    S, FS, n_doc = D // GROUPS, w_down.shape[0], doc_lengths.shape[1]
    half, QW = GROUPS * R, 5 * LANES

    smem = pl.BlockSpec(memory_space=pltpu.SMEM)
    vmem = pl.BlockSpec(memory_space=pltpu.VMEM)
    anywhere = pl.BlockSpec(memory_space=pl.ANY)
    inputs = [
        ("doc", doc_lengths, smem),
        ("tok", tokens[0], anywhere),
        ("dy", out_grad[0], anywhere),
        ("wq", w_query, anywhere),
        ("wk", w_key, anywhere),
        ("wv", w_value, anywhere),
        ("wout", w_out, anywhere),
        ("wup", w_up, anywhere),
        ("wdown", w_down, anywhere),
        ("n1g", norm1_gain[None], vmem),
        ("n1b", norm1_bias[None], vmem),
        ("bq", b_query[None], vmem),
        ("bv", b_value[None], vmem),
        ("bo", b_out[None], vmem),
        ("n2g", norm2_gain[None], vmem),
        ("n2b", norm2_bias[None], vmem),
        ("bd", b_down[None], vmem),
        ("bup", b_up[None], vmem),
    ]
    outputs = [
        ("y", (R, D), BF),
        ("dx", (R, D), BF),
        ("gdown", (FS, D), BF),
        ("gup", (D + S, FS), BF),
        ("gqkv", (GROUPS, S, QW), BF),
        ("vec", (1, 8 * 256 + FS), F32),
    ]
    scratch = [
        ("x_s", (GROUPS, R, D), BF),
        ("h1_s", (GROUPS, R, D), BF),
        ("win_s", (3, S, D), BF),
        ("wq_s", (D, QW), BF),
        ("par_s", (GROUPS, 8, 2 * LANES), F32),
        ("q_s", (3, GROUPS, R, LANES), BF),
        ("kv_s", (2, half, 3 * LANES), BF),
        ("e_s", (3, GROUPS, 2, R, half), BF),
        ("li_s", (3, GROUPS, R, LANES), F32),
        ("oa_s", (GROUPS, R, 2 * LANES), F32),
        ("os_s", (GROUPS, R, 2 * LANES), BF),
        ("or_s", (GROUPS, R, 2 * LANES), BF),
        ("wo_s", (GROUPS, 2 * LANES, D), BF),
        ("wu_s", (GROUPS, S, FS), BF),
        ("wd_s", (FS, D), BF),
        ("dy_s", (GROUPS, R, D), BF),
        ("x1_s", (R, D), F32),
        ("h2_s", (GROUPS, R, D), BF),
        ("g_s", (GROUPS, R, FS), BF),
        ("da_s", (GROUPS, R, FS), BF),
        ("ph_s", (GROUPS, R, D), BF),
        ("hr_s", (4, R, D), BF),
        ("py_s", (GROUPS, R, D), BF),
        ("yr_s", (4, R, D), BF),
        ("dz_s", (R, D), F32),
        ("dos_s", (GROUPS, R, 2 * LANES), BF),
        ("dor_s", (GROUPS, R, 2 * LANES), BF),
        ("dkv_s", (2, half, 3 * LANES), F32),
        ("kvt_s", (half, 3 * LANES), BF),
        ("kvr_s", (half, 3 * LANES), BF),
        ("dq_s", (GROUPS, R, 2 * LANES), F32),
        ("dqkv_s", (half, QW), BF),
        ("ph1_s", (GROUPS, R, D), BF),
        ("h1r_s", (6, R, D), BF),
        ("df_s", (R, D), F32),
        ("gds_s", (FS, D), BF),
        ("gdx_s", (FS // 2, D), BF),
        ("gdl_s", (6, FS // 8, D), BF),
        ("gus_s", (D, FS), BF),
        ("gu_s", (D + S, FS), BF),
        ("gux_s", ((D + S) // 2, FS), BF),
        ("gul_s", (6, (D + S) // 8, FS), BF),
        ("gos_s", (GROUPS, S, D), BF),
        ("gor_s", (4, S, D), BF),
        ("gqs_s", (D, QW), BF),
        ("gqr_s", (4, S, QW), BF),
        ("gqc_s", (S, QW), BF),
        ("gqx_s", (S // 2, QW), BF),
        ("early_s", (n_ctx, 1, 4 * D + 4 * LANES + FS), F32),
        ("late_s", (n_ctx, 1, 2 * D), F32),
        ("vecs_s", (GROUPS, 1, 8 * 256), F32),
        ("vecr_s", (3, 1, 8 * 256), F32),
    ]
    sems = [("send_sems", SEMS), ("recv_sems", SEMS), ("local_sems", 9)]
    names = [one[0] for one in inputs + outputs + scratch + sems]
    y, dx, g_down, g_up, g_qkv, vec = pl.pallas_call(
        partial(layer_kernel, (n_ctx, n_doc, R, D, S, FS), names),
        out_shape=[jax.ShapeDtypeStruct(shape, dtype) for name, shape, dtype in outputs],
        in_specs=[spec for name, value, spec in inputs],
        out_specs=[vmem] * len(outputs),
        scratch_shapes=[pltpu.VMEM(shape, dtype) for name, shape, dtype in scratch]
        + [pltpu.SemaphoreType.DMA((count,)) for name, count in sems],
        compiler_params=pltpu.CompilerParams(
            collective_id=0, has_side_effects=True, vmem_limit_bytes=67043328
        ),
        name="layer",
    )(*[value for name, value, spec in inputs])

    n = 4
    row = lambda i: (i, 0)
    y, dx, down, up, out, q, k, v = pl.pallas_call(
        partial(widen_kernel, S, FS),
        grid=(n,),
        in_specs=[
            pl.BlockSpec((R // n, D), row),
            pl.BlockSpec((R // n, D), row),
            pl.BlockSpec((FS // n, D), row),
            pl.BlockSpec((S, FS), row),
            pl.BlockSpec((S // n, D), lambda i: (D // (S // n) + i, 0)),
            pl.BlockSpec((GROUPS, S // n, QW), lambda i: (0, i, 0)),
        ],
        out_specs=[
            pl.BlockSpec((R // n, D), row),
            pl.BlockSpec((R // n, D), row),
            pl.BlockSpec((FS // n, D), row),
            pl.BlockSpec((S, FS), lambda i: (0, i)),
        ]
        + [pl.BlockSpec((S // n, D), row)] * 4,
        out_shape=[
            jax.ShapeDtypeStruct((R, D), BF),
            jax.ShapeDtypeStruct((R, D), BF),
            jax.ShapeDtypeStruct((FS, D), F32),
            jax.ShapeDtypeStruct((S, GROUPS * FS), F32),
        ]
        + [jax.ShapeDtypeStruct((S, D), F32)] * 4,
        name="widen",
    )(y, dx, g_down, g_up, g_up, g_qkv)

    def vector(i, size=S):
        return vec[0, i * 256 : i * 256 + size]

    return (
        y[None],
        dx[None],
        vector(0),
        vector(1),
        q,
        vector(6),
        k,
        v,
        vector(7),
        out,
        vector(2),
        vector(3),
        vector(4),
        up,
        vector(8, FS),
        down,
        vector(5),
    )


def solution(mesh):
    in_specs = (
        P("wsh", "ctx", None),
        P("wsh", None),
        P("wsh", "ctx", None),
        P("wsh"),
        P("wsh"),
        P("wsh", None),
        P("wsh"),
        P("wsh", None),
        P("wsh", None),
        P("wsh"),
        P("wsh", None),
        P("wsh"),
        P("wsh"),
        P("wsh"),
        P("wsh", None),
        P("wsh"),
        P("wsh", None),
        P("wsh"),
    )
    out_specs = (
        P("wsh", "ctx", None),
        P("wsh", "ctx", None),
        P("wsh"),
        P("wsh"),
        P("wsh", None),
        P("wsh"),
        P("wsh", None),
        P("wsh", None),
        P("wsh"),
        P("wsh", None),
        P("wsh"),
        P("wsh"),
        P("wsh"),
        P("wsh", None),
        P("wsh"),
        P("wsh", None),
        P("wsh"),
    )
    sizes = (mesh.shape["ctx"], mesh.shape["wsh"])
    body = partial(fast_device, sizes) if sizes == (2 * GROUPS, GROUPS) else per_device
    return jax.shard_map(
        body, mesh=mesh, in_specs=in_specs, out_specs=out_specs, check_vma=False
    )
```

```python
from functools import partial
import math

import jax
import jax.numpy as jnp
from jax import lax
from jax.experimental import pallas as pl
from jax.experimental.pallas import tpu as pltpu
from jax.sharding import PartitionSpec as P

HEADS = 12


EPS = 1e-06
NEG_START = -1e30


def norm_rows(inputs, norm_gain, norm_bias):
    row_mean = jnp.mean(inputs, axis=-1, keepdims=True)
    centred = inputs - row_mean
    variance = jnp.mean(centred * centred, axis=-1, keepdims=True)
    return centred * lax.rsqrt(variance + EPS) * norm_gain + norm_bias


def doc_of(positions, doc_ends):
    return jnp.sum((positions[:, None] >= doc_ends[None, :]).astype(jnp.int32), axis=1)


def dot_plain(left, right):
    return jnp.dot(left, right, preferred_element_type=jnp.float32)


def dot_left(left, right):
    return lax.dot_general(
        left, right, (((0,), (0,)), ((), ())), preferred_element_type=jnp.float32
    )


def dot_right(left, right):
    return lax.dot_general(
        left, right, (((1,), (1,)), ((), ())), preferred_element_type=jnp.float32
    )


def masked_scores(query_heads, key_heads, query_ids, key_ids, score_scale):
    raw_scores = (
        jnp.einsum("qhd,khd->hqk", query_heads, key_heads, preferred_element_type=jnp.float32)
        * score_scale
    )
    same_doc = (query_ids[:, None] == key_ids[None, :])[None]
    return jnp.where(same_doc, raw_scores, -jnp.inf)


def per_device(
    tokens,
    doc_lengths,
    out_grad,
    norm1_gain,
    norm1_bias,
    w_query,
    b_query,
    w_key,
    w_value,
    b_value,
    w_out,
    b_out,
    norm2_gain,
    norm2_bias,
    w_up,
    b_up,
    w_down,
    b_down,
):
    (
        gain_one,
        bias_one,
        query_w,
        query_b,
        key_w,
        value_w,
        value_b,
        out_w,
        out_b,
        gain_two,
        bias_two,
        up_w,
        up_b,
        down_w,
        down_b,
    ) = (
        lax.all_gather(norm1_gain, "wsh", axis=0, tiled=True),
        lax.all_gather(norm1_bias, "wsh", axis=0, tiled=True),
        lax.all_gather(w_query, "wsh", axis=0, tiled=True),
        lax.all_gather(b_query, "wsh", axis=0, tiled=True),
        lax.all_gather(w_key, "wsh", axis=0, tiled=True),
        lax.all_gather(w_value, "wsh", axis=0, tiled=True),
        lax.all_gather(b_value, "wsh", axis=0, tiled=True),
        lax.all_gather(w_out, "wsh", axis=0, tiled=True),
        lax.all_gather(b_out, "wsh", axis=0, tiled=True),
        lax.all_gather(norm2_gain, "wsh", axis=0, tiled=True),
        lax.all_gather(norm2_bias, "wsh", axis=0, tiled=True),
        lax.all_gather(w_up, "wsh", axis=0, tiled=True),
        lax.all_gather(b_up, "wsh", axis=0, tiled=True),
        lax.all_gather(w_down, "wsh", axis=0, tiled=True),
        lax.all_gather(b_down, "wsh", axis=0, tiled=True),
    )
    row_count = tokens.shape[1]
    model_width = tokens.shape[2]
    head_dim = model_width // HEADS
    score_scale = head_dim ** (-0.5)
    first_gain = gain_one.astype(jnp.float32)
    first_bias = bias_one.astype(jnp.float32)
    second_gain = gain_two.astype(jnp.float32)
    second_bias = bias_two.astype(jnp.float32)
    inputs = tokens[0].astype(jnp.float32)
    doc_ends = jnp.cumsum(doc_lengths[0])
    own_ids = doc_of(
        lax.axis_index("ctx") * row_count + jnp.arange(row_count, dtype=jnp.int32), doc_ends
    )
    normed_one = norm_rows(inputs, first_gain, first_bias).astype(jnp.bfloat16)
    queries = (dot_plain(normed_one, query_w) + query_b.astype(jnp.float32)).astype(jnp.bfloat16)
    key_rows = dot_plain(normed_one, key_w).astype(jnp.bfloat16)
    values = (dot_plain(normed_one, value_w) + value_b.astype(jnp.float32)).astype(jnp.bfloat16)
    key_all, value_all = (
        lax.all_gather(key_rows, "ctx", axis=0, tiled=True),
        lax.all_gather(values, "ctx", axis=0, tiled=True),
    )
    total_rows = key_all.shape[0]
    key_block = math.gcd(total_rows, 2048)
    block_count = total_rows // key_block
    key_stack = key_all.reshape(block_count, key_block, HEADS, head_dim)
    value_stack = value_all.reshape(block_count, key_block, HEADS, head_dim)
    id_stack = doc_of(jnp.arange(total_rows, dtype=jnp.int32), doc_ends).reshape(
        block_count, key_block
    )
    query_heads = queries.reshape(row_count, HEADS, head_dim)

    def lse_step(running, block_in):
        run_max, run_sum = running
        key_heads, key_ids = block_in
        scores = masked_scores(query_heads, key_heads, own_ids, key_ids, score_scale)
        new_max = jnp.maximum(run_max, jnp.max(scores, axis=-1))
        new_sum = run_sum * jnp.exp(run_max - new_max) + jnp.sum(
            jnp.exp(scores - new_max[:, :, None]), axis=-1
        )
        return ((new_max, new_sum), None)

    start_max = jnp.full((HEADS, row_count), NEG_START, jnp.float32)
    (final_max, final_sum), unused = lax.scan(
        lse_step, (start_max, jnp.zeros_like(start_max)), (key_stack, id_stack)
    )
    log_total = final_max + jnp.log(final_sum)

    def out_step(running, block_in):
        key_heads, value_heads, key_ids = block_in
        scores = masked_scores(query_heads, key_heads, own_ids, key_ids, score_scale)
        attn_prob = jnp.exp(scores - log_total[:, :, None]).astype(jnp.bfloat16)
        return (
            running
            + jnp.einsum(
                "hqk,khd->qhd", attn_prob, value_heads, preferred_element_type=jnp.float32
            ),
            None,
        )

    attn_sum, unused = lax.scan(
        out_step,
        jnp.zeros((row_count, HEADS, head_dim), jnp.float32),
        (key_stack, value_stack, id_stack),
    )
    attended = attn_sum.reshape(row_count, model_width).astype(jnp.bfloat16)
    middle = inputs + dot_plain(attended, out_w) + out_b.astype(jnp.float32)
    normed_two = norm_rows(middle, second_gain, second_bias).astype(jnp.bfloat16)
    hidden = dot_plain(normed_two, up_w) + up_b.astype(jnp.float32)
    active = jax.nn.gelu(hidden, approximate=True).astype(jnp.bfloat16)
    output = middle + dot_plain(active, down_w) + down_b.astype(jnp.float32)
    top_grad = out_grad[0]
    top_float = top_grad.astype(jnp.float32)
    grad_down_w = dot_left(active, top_grad)
    grad_down_b = jnp.sum(top_float, axis=0)
    grad_active = dot_right(top_grad, down_w)
    unused, gelu_pull = jax.vjp(partial(jax.nn.gelu, approximate=True), hidden)
    grad_hidden = gelu_pull(grad_active)[0].astype(jnp.bfloat16)
    grad_up_w = dot_left(normed_two, grad_hidden)
    grad_up_b = jnp.sum(grad_hidden.astype(jnp.float32), axis=0)
    grad_normed_two = dot_right(grad_hidden, up_w)
    unused, second_pull = jax.vjp(norm_rows, middle, second_gain, second_bias)
    grad_middle, grad_gain_two, grad_bias_two = second_pull(grad_normed_two)
    grad_middle = grad_middle + top_float
    grad_branch = grad_middle.astype(jnp.bfloat16)
    grad_out_w = dot_left(attended, grad_branch)
    grad_out_b = jnp.sum(grad_branch.astype(jnp.float32), axis=0)
    grad_attended = dot_right(grad_branch, out_w).astype(jnp.bfloat16)
    grad_heads = grad_attended.reshape(row_count, HEADS, head_dim)
    row_delta = jnp.sum(grad_heads.astype(jnp.float32) * attn_sum, axis=-1)
    head_delta = row_delta.T
    query_start = jnp.zeros((row_count, HEADS, head_dim), jnp.float32)

    def full_step(grad_query, block_in):
        key_heads, value_heads, key_ids = block_in
        scores = masked_scores(query_heads, key_heads, own_ids, key_ids, score_scale)
        attn_prob = jnp.exp(scores - log_total[:, :, None])
        grad_prob = jnp.einsum(
            "qhd,khd->hqk", grad_heads, value_heads, preferred_element_type=jnp.float32
        )
        grad_score = (attn_prob * (grad_prob - head_delta[:, :, None])).astype(jnp.bfloat16)
        grad_query = grad_query + jnp.einsum(
            "hqk,khd->qhd", grad_score, key_heads, preferred_element_type=jnp.float32
        )
        grad_key = (
            jnp.einsum("hqk,qhd->khd", grad_score, query_heads, preferred_element_type=jnp.float32)
            * score_scale
        )
        grad_value = jnp.einsum(
            "hqk,qhd->khd",
            attn_prob.astype(jnp.bfloat16),
            grad_heads,
            preferred_element_type=jnp.float32,
        )
        return (
            grad_query,
            (grad_key.reshape(key_block, model_width), grad_value.reshape(key_block, model_width)),
        )

    grad_query, key_terms = lax.scan(full_step, query_start, (key_stack, value_stack, id_stack))
    key_grad, value_grad = (
        lax.psum_scatter(
            key_terms[0].reshape(total_rows, model_width), "ctx", scatter_dimension=0, tiled=True
        ),
        lax.psum_scatter(
            key_terms[1].reshape(total_rows, model_width), "ctx", scatter_dimension=0, tiled=True
        ),
    )
    grad_query_rows = (
        (grad_query * score_scale).reshape(row_count, model_width).astype(jnp.bfloat16)
    )
    grad_key_rows = key_grad.astype(jnp.bfloat16)
    grad_value_rows = value_grad.astype(jnp.bfloat16)
    grad_query_w = dot_left(normed_one, grad_query_rows)
    grad_query_b = jnp.sum(grad_query_rows.astype(jnp.float32), axis=0)
    grad_key_w = dot_left(normed_one, grad_key_rows)
    grad_value_w = dot_left(normed_one, grad_value_rows)
    grad_value_b = jnp.sum(grad_value_rows.astype(jnp.float32), axis=0)
    grad_normed_one = (
        dot_right(grad_query_rows, query_w)
        + dot_right(grad_key_rows, key_w)
        + dot_right(grad_value_rows, value_w)
    )
    unused, first_pull = jax.vjp(norm_rows, inputs, first_gain, first_bias)
    grad_inputs, grad_gain_one, grad_bias_one = first_pull(grad_normed_one)
    grad_inputs = grad_inputs + grad_middle
    (
        share_gain_one,
        share_bias_one,
        share_query_w,
        share_query_b,
        share_key_w,
        share_value_w,
        share_value_b,
        share_out_w,
        share_out_b,
        share_gain_two,
        share_bias_two,
        share_up_w,
        share_up_b,
        share_down_w,
        share_down_b,
    ) = (
        lax.psum_scatter(
            grad_gain_one.astype(jnp.bfloat16), "wsh", scatter_dimension=0, tiled=True
        ).astype(jnp.float32),
        lax.psum_scatter(
            grad_bias_one.astype(jnp.bfloat16), "wsh", scatter_dimension=0, tiled=True
        ).astype(jnp.float32),
        lax.psum_scatter(
            grad_query_w.astype(jnp.bfloat16), "wsh", scatter_dimension=0, tiled=True
        ).astype(jnp.float32),
        lax.psum_scatter(
            grad_query_b.astype(jnp.bfloat16), "wsh", scatter_dimension=0, tiled=True
        ).astype(jnp.float32),
        lax.psum_scatter(
            grad_key_w.astype(jnp.bfloat16), "wsh", scatter_dimension=0, tiled=True
        ).astype(jnp.float32),
        lax.psum_scatter(
            grad_value_w.astype(jnp.bfloat16), "wsh", scatter_dimension=0, tiled=True
        ).astype(jnp.float32),
        lax.psum_scatter(
            grad_value_b.astype(jnp.bfloat16), "wsh", scatter_dimension=0, tiled=True
        ).astype(jnp.float32),
        lax.psum_scatter(
            grad_out_w.astype(jnp.bfloat16), "wsh", scatter_dimension=0, tiled=True
        ).astype(jnp.float32),
        lax.psum_scatter(
            grad_out_b.astype(jnp.bfloat16), "wsh", scatter_dimension=0, tiled=True
        ).astype(jnp.float32),
        lax.psum_scatter(
            grad_gain_two.astype(jnp.bfloat16), "wsh", scatter_dimension=0, tiled=True
        ).astype(jnp.float32),
        lax.psum_scatter(
            grad_bias_two.astype(jnp.bfloat16), "wsh", scatter_dimension=0, tiled=True
        ).astype(jnp.float32),
        lax.psum_scatter(
            grad_up_w.astype(jnp.bfloat16), "wsh", scatter_dimension=0, tiled=True
        ).astype(jnp.float32),
        lax.psum_scatter(
            grad_up_b.astype(jnp.bfloat16), "wsh", scatter_dimension=0, tiled=True
        ).astype(jnp.float32),
        lax.psum_scatter(
            grad_down_w.astype(jnp.bfloat16), "wsh", scatter_dimension=0, tiled=True
        ).astype(jnp.float32),
        lax.psum_scatter(
            grad_down_b.astype(jnp.bfloat16), "wsh", scatter_dimension=0, tiled=True
        ).astype(jnp.float32),
    )
    totals = lax.psum(
        (
            share_gain_one,
            share_bias_one,
            share_query_w,
            share_query_b,
            share_key_w,
            share_value_w,
            share_value_b,
            share_out_w,
            share_out_b,
            share_gain_two,
            share_bias_two,
            share_up_w,
            share_up_b,
            share_down_w,
            share_down_b,
        ),
        "ctx",
    )
    return (
        output.astype(jnp.bfloat16)[None],
        grad_inputs.astype(jnp.bfloat16)[None],
        totals[0],
        totals[1],
        totals[2],
        totals[3],
        totals[4],
        totals[5],
        totals[6],
        totals[7],
        totals[8],
        totals[9],
        totals[10],
        totals[11],
        totals[12],
        totals[13],
        totals[14],
    )


MESH = pl.DeviceIdType.MESH
F32 = jnp.float32
BF = jnp.bfloat16
GROUPS = 4
LANES = 128


def flip(value, mask):
    return ((value // 2 + mask // 2) % 2) * 2 + (value + mask) % 2


def dot_nn(left, right):
    return lax.dot_general(left, right, (((1,), (0,)), ((), ())), preferred_element_type=F32)


def dot_nt(left, right):
    return lax.dot_general(left, right, (((1,), (1,)), ((), ())), preferred_element_type=F32)


def dot_tn(left, right):
    return lax.dot_general(left, right, (((0,), (0,)), ((), ())), preferred_element_type=F32)


def unit_rows(inputs):
    row_mean = jnp.mean(inputs, axis=-1, keepdims=True)
    centred = inputs - row_mean
    variance = jnp.mean(centred * centred, axis=-1, keepdims=True)
    scale = lax.rsqrt(variance + EPS)
    return centred * scale, scale


def unit_rows_back(grad_normed, unit, scale, gain):
    grad_unit = grad_normed * gain
    return scale * (
        grad_unit
        - jnp.mean(grad_unit, axis=-1, keepdims=True)
        - unit * jnp.mean(grad_unit * unit, axis=-1, keepdims=True)
    )


def rows_sum(values):
    return jnp.sum(values, axis=0, keepdims=True)


def sum_bf(*values):
    return sum([one.astype(F32) for one in values]).astype(BF)


class Wires:
    def __init__(self, send_sems, recv_sems):
        self.send_sems, self.recv_sems, self.used, self.started = send_sems, recv_sems, 0, []

    def take(self, count=1):
        first = self.used
        self.used += count
        return first

    def copy(self, index, source, target, device):
        return pltpu.make_async_remote_copy(
            src_ref=source,
            dst_ref=target,
            send_sem=self.send_sems.at[index],
            recv_sem=self.recv_sems.at[index],
            device_id=device,
            device_id_type=MESH,
        )

    def send(self, source, target, device):
        one = self.copy(self.take(), source, target, device)
        one.start()
        self.started.append((one, None))
        return one

    def later(self, one, when=None):
        self.started.append((one, when))
        return one

    def plan(self, source, target, device):
        return self.later(self.copy(self.take(), source, target, device))

    def drain(self):
        for one, when in self.started:
            if when is None:
                one.wait_send()
            else:
                pl.when(when)(one.wait_send)


ORDER = (
    "up_grad", "ph_combine", "down_grad", "y_part", "wait_ph", "ln2", "D_xout", "sums", "up_xin",
    "out_grad", "py_combine", "bo0", "bo1", "up_in", "bo2", "bo3", "D_in", "kv_out", "go_combine",
    "U2a", "U2b", "bw0", "U3", "bw1", "go_out", "D2a", "U_turn", "bw2", "D2b", "bw3", "D3", "kv_in",
    "qkv_grad", "early", "U_i1", "go_in", "gq_comb", "D_turn", "U_o1", "go_turn", "h1_part",
    "gq_fin", "D_o1", "D_i1", "U_i2", "q_start", "go_done", "layer_out", "D_i2", "H2a", "U_i3",
    "q_i1", "early2", "D_i3", "q_o1", "h1_e2", "H2b", "H3", "go_fin", "q_i2", "h1_fin", "q_i3",
    "small", "fin",
)


def layer_kernel(sizes, names, *refs):
    n_ctx, n_doc, R, D, S, FS = sizes
    r = dict(zip(names, refs, strict=True))
    G = n_ctx // GROUPS
    last = GROUPS - 1
    half = GROUPS * R
    c = lax.axis_index("ctx")
    w = lax.axis_index("wsh")
    hg, px = c // G, c % G

    def zdev(group):
        return {"ctx": group * G + px, "wsh": w}

    def wdev(index):
        return {"ctx": c, "wsh": index}

    xdev = {"ctx": hg * G + 1 - px, "wsh": w}
    left, right = zdev((hg + last) % GROUPS), zdev((hg + 1) % GROUPS)
    w1, w2, w3 = flip(w, 1), flip(w, 2), flip(w, 3)
    sib, across, diag = wdev(w1), wdev(w2), wdev(w3)
    wires = Wires(r["send_sems"], r["recv_sems"])
    lane = lax.broadcasted_iota(jnp.int32, (1, LANES), 1)
    low_half = lane < LANES // 2

    def pick(table):
        return sum([jnp.where(hg == i, one, 0) for i, one in enumerate(table)])

    def by_distance(step):
        return (
            jnp.where(step == 0, pick((3, 3, 0, 0)), 0)
            + jnp.where(step == 1, pick((2, 0, 3, 1)), 0)
            + jnp.where(step == 2, pick((1, 2, 1, 2)), 0)
            + jnp.where(step == 3, hg, 0)
        )

    local = r["local_sems"]

    def fetch(index, source, target):
        one = pltpu.make_async_copy(source, target, local.at[index])
        one.start()
        return one

    tok_in = fetch(0, r["tok"], r["x_s"].at[hg])
    qkv_in = [fetch(1 + i, r[name], r["win_s"].at[i]) for i, name in enumerate(("wq", "wk", "wv"))]
    dy_in = fetch(4, r["dy"], r["dy_s"].at[w])
    wo_in = [
        fetch(5, r["wout"].at[pl.ds(0, LANES)], r["wo_s"].at[w, pl.ds(0, LANES)]),
        fetch(6, r["wout"].at[pl.ds(LANES, S - LANES)], r["wo_s"].at[w, pl.ds(S, S - LANES)]),
    ]
    wu_in = fetch(7, r["wup"].at[:, pl.ds(pl.multiple_of(w * FS, FS), FS)], r["wu_s"].at[w])
    wd_in = fetch(8, r["wdown"], r["wd_s"])

    barrier = pltpu.get_barrier_semaphore()
    ctx_peers = [{"ctx": (c + i) % n_ctx, "wsh": w} for i in range(1, n_ctx)]
    partners = ctx_peers + [sib, across, diag]
    for partner in partners:
        pl.semaphore_signal(barrier, inc=1, device_id=partner, device_id_type=MESH)

    for one in qkv_in:
        one.wait()
    own_w = pl.ds(pl.multiple_of(w * S, S), S)
    win, wq_s = r["win_s"], r["wq_s"]
    for g in range(GROUPS):

        @pl.when(hg == g)
        def _():
            a = g * S
            wq_s[own_w, 0:S] = win[0, :, a : a + S]
            wq_s[own_w, S : 2 * LANES] = jnp.zeros((S, 2 * LANES - S), BF)
            wq_s[own_w, 2 * LANES : 2 * LANES + S] = win[1, :, a : a + S]
            wq_s[own_w, 2 * LANES + S : 4 * LANES] = win[2, :, a + LANES : a + S]
            wq_s[own_w, 4 * LANES : 5 * LANES] = win[2, :, a : a + LANES]

    par_s = r["par_s"]
    par_s[w] = jnp.zeros((8, 2 * LANES), F32)
    for i, name in enumerate(("n1g", "n1b", "bq", "bv", "bo", "n2g", "n2b", "bd")):
        par_s[w, i : i + 1, 0:S] = r[name][...].astype(F32)[None, :]
    r["wo_s"][:, LANES:S, :] = jnp.zeros((GROUPS, S - LANES, D), BF)
    tok_in.wait()
    pl.semaphore_wait(barrier, len(partners))

    class Gather:
        def __init__(self, slot):
            self.slot = slot
            self.to_across = wires.send(slot(w), slot(w), across)
            self.to_sib = wires.send(slot(w), slot(w), sib)

        def relay(self):
            self.to_across.wait_recv()
            self.on = wires.send(self.slot(w2), self.slot(w2), sib)

        def finish(self):
            self.to_sib.wait_recv()
            self.on.wait_recv()

    class Reduce:
        def __init__(self, part, recv):
            self.part, self.recv = part, recv
            self.a = wires.plan(part(w3), recv.at[0], sib)
            self.b = wires.plan(part(w1), recv.at[1], sib)
            self.c = wires.plan(recv.at[3], recv.at[2], across)

        def start(self):
            self.a.start()
            self.b.start()

        def combine(self):
            self.a.wait_recv()
            self.recv[3] = sum_bf(self.part(w2)[...], self.recv[0])
            self.c.start()

        def finish(self):
            self.b.wait_recv()
            self.c.wait_recv()
            return (
                self.part(w)[...].astype(F32)
                + self.recv[1].astype(F32)
                + self.recv[2].astype(F32)
            )

    class LineSum:
        def __init__(self, part, recv):
            self.part, self.recv = part, recv
            self.first_at = wires.take(6)
            for i in range(3):
                wires.later(self.message(i, True), hg > i)
                wires.later(self.message(i, False), hg < last - i)

        def message(self, i, leftward):
            block, slot = (i, i) if leftward else (last - i, 3 + i)
            return wires.copy(
                self.first_at + slot, self.part(block), self.recv.at[slot], left if leftward else right
            )

        def ends_block(self, block):
            for i in range(2):

                @pl.when((hg == last) & (block == i))
                def _():
                    self.message(i, True).start()

                @pl.when((hg == 0) & (block == last - i))
                def _():
                    self.message(i, False).start()

        def ends(self, which=(0, 1, 2)):
            for i in which:

                @pl.when(hg == last)
                def _():
                    self.message(i, True).start()

                @pl.when(hg == 0)
                def _():
                    self.message(i, False).start()

        def pass_on(self, position, i, leftward):
            @pl.when(hg == position)
            def _():
                one = self.message(i, leftward)
                one.wait_recv()
                block, slot = (i, i) if leftward else (last - i, 3 + i)
                self.part(block)[...] = sum_bf(self.part(block)[...], self.recv[slot])
                one.start()

        def second(self, which=(0, 1)):
            for i in which:
                self.pass_on(2, i, True)
                self.pass_on(1, i, False)

        def third(self):
            self.pass_on(1, 0, True)
            self.pass_on(2, 0, False)

        def final(self, put):
            for position in range(GROUPS):

                @pl.when(hg == position)
                def _():
                    total = self.part(position)[...].astype(F32)
                    if position < last:
                        self.message(position, True).wait_recv()
                        total = total + self.recv[position].astype(F32)
                    if position > 0:
                        self.message(last - position, False).wait_recv()
                        total = total + self.recv[3 + last - position].astype(F32)
                    put(total)

    class LineGather:
        def __init__(self, slot, to_x):
            self.slot, self.to_x = slot, to_x
            self.first_at = wires.take(6)
            self.x_at = wires.take(GROUPS) if to_x else None
            for d in (1, 2, 3):
                wires.later(self.message(d, 0), (hg >= d - 1) & (hg < last))
                wires.later(self.message(d, 1), (hg + d - 1 <= last) & (hg > 0))
            if to_x:
                for b in range(GROUPS):
                    wires.later(self.x_message(b))

        def message(self, d, side):
            block = (hg + GROUPS + (1 - d) * (1 - 2 * side)) % GROUPS
            device = zdev((hg + GROUPS + 1 - 2 * side) % GROUPS)
            return wires.copy(
                self.first_at + 3 * side + d - 1, self.slot(block), self.slot(block), device
            )

        def x_message(self, block):
            return wires.copy(self.x_at + block, self.slot(block), self.slot(block), xdev)

        def start(self):
            pl.when(hg < last)(self.message(1, 0).start)
            pl.when(hg > 0)(self.message(1, 1).start)
            if self.to_x:
                self.x_message(hg).start()

        def arrived(self, d, side, then=None):
            block = (hg + GROUPS - d * (1 - 2 * side)) % GROUPS
            here = jnp.where(side == 0, (hg >= d).astype(jnp.int32), (hg + d <= last).astype(jnp.int32))
            onward = here * jnp.where(side == 0, (hg < last).astype(jnp.int32), (hg > 0).astype(jnp.int32))

            @pl.when(here == 1)
            def _():
                wires.copy(
                    self.first_at + 3 * side + d - 1, self.slot(block), self.slot(block), left
                ).wait_recv()

            @pl.when(onward == 1)
            def _():
                self.message(d + 1, side).start()

            @pl.when(here == 1)
            def _():
                if self.to_x:
                    self.x_message(block).start()
                if then is not None:
                    then(block)

        def inner(self, d):
            self.arrived(d, jnp.where(hg < 2, 1, 0))

        def outer(self, d):
            self.arrived(d, jnp.where(hg < 2, 0, 1))

        def done(self):
            for b in range(GROUPS):
                self.x_message(b).wait_recv()

    x_s, h1_s, q_s, kv_s = r["x_s"], r["h1_s"], r["q_s"], r["kv_s"]
    rows_two = R // 2
    tokens = [
        LineGather(lambda b, j=j: x_s.at[b, pl.ds(j * rows_two, rows_two)], False) for j in (0, 1)
    ]
    for one in tokens:
        one.start()
    ws_all = Gather(lambda i: wq_s.at[pl.ds(pl.multiple_of(i * S, S), S)])
    par_all = Gather(lambda i: par_s.at[i])
    par_all.relay()
    ws_all.relay()
    par_all.finish()

    pars = jnp.concatenate([par_s[i][:, :S] for i in range(GROUPS)], axis=1)
    gain_one, bias_one, out_b, gain_two, bias_two, down_b = [
        pars[i : i + 1] for i in (0, 1, 4, 5, 6, 7)
    ]
    up_b = r["bup"][...].astype(F32)[None, :]
    own_par = par_s[hg]
    v_tile, v_last = own_par[3:4, :LANES], own_par[3:4, LANES:]
    qkv_b = jnp.concatenate(
        [own_par[2:3, :], jnp.zeros((1, LANES), F32), pltpu.roll(v_last, LANES // 2, 1), v_tile],
        axis=1,
    )

    def norm_block(block):
        unit, unused = unit_rows(x_s[block].astype(F32))
        h1_s[block] = (unit * gain_one + bias_one).astype(BF)

    norm_block(hg)
    ws_all.finish()
    for one in wo_in:
        one.wait()
    dy_in.wait()
    wo_s, dy_s, wu_s = r["wo_s"], r["dy_s"], r["wu_s"]
    wo_top = Gather(lambda i: wo_s.at[i, pl.ds(0, LANES)])
    wo_low = Gather(lambda i: wo_s.at[i, pl.ds(S, S - LANES)])
    dy_all = Gather(lambda i: dy_s.at[i])

    kv_first = wires.take(GROUPS)

    def kv_copy(block):
        rows = pl.ds(pl.multiple_of(block * R, R), R)
        return wires.copy(kv_first + block, kv_s.at[0, rows], kv_s.at[1, rows], xdev)

    def project(block):
        qkv = dot_nn(h1_s[block], wq_s[...]) + qkv_b
        queries = qkv[:, : 2 * LANES].astype(BF).astype(F32) * 0.125
        q_s[0, block] = jnp.where(low_half, queries[:, :LANES], 0.0).astype(BF)
        q_s[1, block] = jnp.where(low_half, 0.0, queries[:, :LANES]).astype(BF)
        q_s[2, block] = queries[:, LANES:].astype(BF)
        kv_s[0, pl.ds(pl.multiple_of(block * R, R), R), :] = qkv[:, 2 * LANES :].astype(BF)
        kv_copy(block).start()

    def norm_project(block):
        norm_block(block)
        project(block)

    project(hg)

    inner_side = jnp.where(hg < 2, 1, 0)

    def token_step(i, carry):
        d = i + 1
        for one in tokens:
            one.arrived(d, inner_side)
            one.arrived(d, 1 - inner_side)

        def side_block(side, present):
            step = d * (1 - 2 * side)

            @pl.when(present)
            def _():
                norm_project((hg + GROUPS - step) % GROUPS)

        lower = (hg >= d).astype(jnp.int32)
        upper = (hg + d <= last).astype(jnp.int32)
        side_block(inner_side, jnp.where(hg < 2, upper, lower) == 1)
        side_block(1 - inner_side, jnp.where(hg < 2, lower, upper) == 1)
        return carry

    lax.fori_loop(0, 3, token_step, 0)
    wo_top.relay()
    wo_low.relay()
    dy_all.relay()
    up_sends = [
        wires.send(
            r["wup"].at[:, pl.ds(pl.multiple_of(flip(w, k) * FS, FS), FS)],
            wu_s.at[w],
            wdev(flip(w, k)),
        )
        for k in (2, 3, 1)
    ]
    for b in range(GROUPS):
        kv_copy(b).wait_recv()
        wires.later(kv_copy(b))

    doc_ends = []
    for i in range(n_doc):
        doc_ends.append(r["doc"][0, i] + (doc_ends[-1] if i else 0))

    def doc_ids(positions):
        return sum([(positions >= end).astype(jnp.int32) for end in doc_ends])

    key_at = lax.broadcasted_iota(jnp.int32, (1, half), 1)
    key_block = sum([(key_at >= i * R).astype(jnp.int32) for i in range(1, GROUPS)])
    key_base = key_at + key_block * (R * (G - 1))
    key_ids = [doc_ids(key_base + px * R), doc_ids(key_base + (1 - px) * R)]
    KT, VT = (0, 0, LANES), (2 * LANES, 2 * LANES, LANES)
    e_s, li_s, oa_s, os_s, or_s = r["e_s"], r["li_s"], r["oa_s"], r["os_s"], r["or_s"]

    class Turn:
        def __init__(self, source, target):
            self.source, self.target = source, target
            self.first_at = wires.take(GROUPS)
            for i in (1, 2, 3):
                wires.later(self.message((hg + i) % GROUPS))

        def message(self, block):
            index = self.first_at + (block - hg + GROUPS) % GROUPS
            return wires.copy(index, self.source.at[block], self.target.at[hg], zdev(block))

        def arrived(self, block):
            index = self.first_at + (hg - block + GROUPS) % GROUPS
            wires.copy(index, self.target.at[block], self.target.at[block], left).wait_recv()

    o_turn = Turn(os_s, or_s)

    def attend(step, carry):
        block = by_distance(step)
        row_at = (block * G + px) * R + lax.broadcasted_iota(jnp.int32, (R, 1), 0)
        row_ids = doc_ids(row_at)
        outs = []
        for h in range(3):
            queries = q_s[h, block]
            scores = [
                jnp.where(
                    row_ids == key_ids[side],
                    dot_nt(queries, kv_s[side, :, KT[h] : KT[h] + LANES]),
                    NEG_START,
                )
                for side in (0, 1)
            ]
            top = jnp.maximum(
                jnp.max(scores[0], axis=-1, keepdims=True), jnp.max(scores[1], axis=-1, keepdims=True)
            )
            weights = [jnp.exp(one - top) for one in scores]
            total = jnp.sum(weights[0], axis=-1, keepdims=True) + jnp.sum(
                weights[1], axis=-1, keepdims=True
            )
            inverse = 1.0 / total
            mixed = jnp.zeros((R, LANES), F32)
            for side in (0, 1):
                rounded = weights[side].astype(BF)
                e_s[h, block, side] = rounded
                mixed += dot_nn(rounded, kv_s[side, :, VT[h] : VT[h] + LANES])
            li_s[h, block] = jnp.broadcast_to(inverse, (R, LANES))
            outs.append(mixed * inverse)
        first = jnp.where(low_half, outs[0], outs[1])
        final = jnp.where(low_half, 0.0, outs[2])
        oa_s[block, :, :LANES] = first
        oa_s[block, :, LANES:] = final
        os_s[block, :, :LANES] = first.astype(BF)
        os_s[block, :, LANES:] = final.astype(BF)

        @pl.when(step < last)
        def _():
            o_turn.message(block).start()

        return carry

    lax.fori_loop(0, GROUPS, attend, 0)
    or_s[hg] = os_s[hg]
    wo_top.finish()
    wo_low.finish()
    for i in (1, 2, 3):
        o_turn.arrived((hg + i) % GROUPS)

    middle = x_s[hg].astype(F32) + out_b
    for i in range(GROUPS):
        middle += dot_nn(or_s[i], wo_s[i])
    x1_s, h2_s, g_s, da_s = r["x1_s"], r["h2_s"], r["g_s"], r["da_s"]
    x1_s[...] = middle
    unit_two, scale_two = unit_rows(middle)
    h2_s[w] = (unit_two * gain_two + bias_two).astype(BF)
    h2_all = Gather(lambda i: h2_s.at[i])
    dy_all.finish()
    wu_in.wait()
    wd_in.wait()
    for one in up_sends:
        one.wait_recv()
    ph_s, hr_s, wd_s = r["ph_s"], r["hr_s"], r["wd_s"]
    ph = Reduce(lambda i: ph_s.at[i], hr_s)

    def up_and_back(slot):
        hidden = dot_nn(h2_s[slot], wu_s[...].reshape(D, FS)) + up_b
        square = hidden * hidden
        inner = math.sqrt(2.0 / math.pi) * (hidden + 0.044715 * (square * hidden))
        bent = jnp.tanh(inner)
        g_s[slot] = (0.5 * hidden * (1.0 + bent)).astype(BF)
        slope = 0.5 * (1.0 + bent) + 0.5 * hidden * (1.0 - bent * bent) * (
            math.sqrt(2.0 / math.pi) * (1.0 + 3.0 * 0.044715 * square)
        )
        grad_active = dot_nt(dy_s[slot], wd_s[...])
        grad_hidden = (grad_active * slope).astype(BF)
        da_s[slot] = grad_hidden
        ph_s[slot] = dot_nt(grad_hidden, wu_s[...].reshape(D, FS)).astype(BF)

    on_copy = wires.copy(wires.take(), h2_s.at[w2], h2_s.at[w2], sib)

    def mlp_step(j, carry):
        @pl.when(j == 1)
        def _():
            h2_all.to_sib.wait_recv()

        @pl.when(j == 2)
        def _():
            h2_all.to_across.wait_recv()
            on_copy.start()

        @pl.when(j == 3)
        def _():
            on_copy.wait_recv()

        up_and_back(flip(w, j))

        @pl.when(j == 1)
        def _():
            ph.b.start()

        @pl.when(j == 3)
        def _():
            ph.a.start()

        return carry

    lax.fori_loop(0, GROUPS, mlp_step, 0)
    wires.later(on_copy)

    gus_s, gds_s, py_s = r["gus_s"], r["gds_s"], r["py_s"]

    def up_grad(i, carry):
        at = pl.ds(pl.multiple_of(i * 2 * S, 2 * S), 2 * S)
        gus_s[pl.ds(2 * i, 2)] = (
            dot_tn(h2_s[:, :, at].reshape(half, 2 * S), da_s[...].reshape(half, FS))
            .astype(BF)
            .reshape(2, 2, S // 2, FS)
        )
        return carry

    def down_grad(i, carry):
        at = pl.ds(pl.multiple_of(i * 256, 256), 256)
        gds_s[at, :] = dot_tn(
            g_s[:, :, at].reshape(half, 256), dy_s[...].reshape(half, D)
        ).astype(BF)
        return carry

    def y_part(j, carry):
        py_s[j] = dot_nn(g_s[j], wd_s[...]).astype(BF)
        return carry

    class Spread:
        def __init__(self, part, recv, slot, to_x):
            self.sum = LineSum(part, recv)
            self.gather = LineGather(slot, to_x)

        def turn(self):
            def put(total):
                self.gather.slot(hg)[...] = total.astype(BF)

            self.sum.final(put)
            self.gather.start()

    class Share:
        def __init__(self, rows):
            self.rows = rows
            self.at = wires.take(n_ctx)
            for i in range(1, n_ctx):
                wires.later(self.message(i))

        def message(self, i):
            return wires.copy(self.at + i, self.rows.at[c], self.rows.at[c], ctx_peers[i - 1])

        def start(self):
            for i in range(1, n_ctx):
                self.message(i).start()

        def total(self):
            for i in range(1, n_ctx):
                wires.copy(self.at + i, self.rows.at[c], self.rows.at[c], left).wait_recv()
            return sum([self.rows[i] for i in range(n_ctx)])

    n = S // 2
    n_down = FS // 8
    quarter = n // GROUPS
    gd_s, gu_s, up_f = r["gd_s"], r["gu_s"], r["gup_s"]
    mine = pl.ds(pl.multiple_of(px * n, 8), n)
    theirs = pl.ds(pl.multiple_of((1 - px) * n, 8), n)

    def down_rows(b):
        return pl.ds(pl.multiple_of(px * (4 * n_down) + b * n_down, 8), n_down)

    down_here = pl.ds(pl.multiple_of(px * (4 * n_down), 8), 4 * n_down)
    down_there = pl.ds(pl.multiple_of((1 - px) * (4 * n_down), 8), 4 * n_down)
    py = Reduce(lambda i: py_s.at[i], r["yr_s"])
    up_x = wires.plan(gus_s.at[:, 1 - px], r["gux_s"], xdev)
    up_y_first = wires.take(GROUPS)

    def up_y(k, out):
        to = flip(w, k)
        return wires.copy(
            up_y_first + k, gus_s.at[to, px], gu_s.at[w if out else to], wdev(to)
        )

    for k in (1, 2, 3):
        wires.later(up_y(k, True))
    up = Spread(lambda b: gu_s.at[b], r["gul_s"], lambda b: up_f.at[b, px], True)
    down_x = wires.plan(gds_s.at[down_there], r["gdx_s"], xdev)
    down = Spread(
        lambda b: gds_s.at[down_rows(b)], r["gdl_s"], lambda b: gd_s.at[down_rows(b)], True
    )
    dz_s, dos_s, dor_s = r["dz_s"], r["dos_s"], r["dor_s"]
    do_turn = Turn(dos_s, dor_s)
    early, early_x_s, early_z_s = r["early_s"], r["early_x_s"], r["early_z_s"]
    late = r["late_s"]
    early_x = wires.plan(early, early_x_s, xdev)
    early_first = wires.take(GROUPS)

    def early_z(i):
        return wires.copy(
            early_first + i, early_z_s.at[hg], early_z_s.at[hg], zdev((hg + i) % GROUPS)
        )

    for i in (1, 2, 3):
        wires.later(early_z(i))
    late_all = Share(late)
    gos_s, gor_s = r["gos_s"], r["gor_s"]
    go_s, gox_s, gop_s, gon_s, go_f = r["go_s"], r["gox_s"], r["gop_s"], r["gon_s"], r["gout_s"]
    go = Reduce(lambda i: gos_s.at[i], gor_s)
    go_x = wires.plan(go_s.at[theirs], gox_s, xdev)
    go_turn = Turn(gop_s, gon_s)
    go_first = wires.take(GROUPS)

    def go_back(i):
        piece = go_f.at[px, hg]
        return wires.copy(go_first + i, piece, piece, zdev((hg + i) % GROUPS))

    for i in (1, 2, 3):
        wires.later(go_back(i))
    go_x2 = wires.plan(go_f.at[px], go_f.at[px], xdev)
    kvt_s, kvr_s, ph1_s, gqs_s = r["kvt_s"], r["kvr_s"], r["ph1_s"], r["gqs_s"]
    kv_back = wires.plan(kvt_s, kvr_s, xdev)
    h1_sum = LineSum(lambda b: ph1_s.at[b], r["h1r_s"])
    gq = Reduce(lambda i: gqs_s.at[pl.ds(pl.multiple_of(i * S, S), S)], r["gqr_s"])
    gqc_s, gqx_s, gqkv = r["gqc_s"], r["gqx_s"], r["gq_s"]
    qx = wires.plan(gqc_s.at[theirs], gqx_s, xdev)
    q_line = LineGather(lambda b: gqkv.at[b, mine], True)
    vecs, vecr = r["vecs_s"], r["vecr_s"]
    vec_first = wires.take(GROUPS)

    def vec_send(k):
        return wires.copy(
            vec_first + k, vecs.at[flip(w, k)], vecr.at[k - 1], wdev(flip(w, k))
        )

    for k in (1, 2, 3):
        wires.later(vec_send(k))
    dkv_s, dq_s, dqkv_s, df_s = r["dkv_s"], r["dq_s"], r["dqkv_s"], r["df_s"]

    steps = {}

    def step_of(name):
        def keep(body):
            steps[name] = body
            return body

        return keep

    @step_of("up_xin")
    def _():
        up_x.wait_recv()
        here = gus_s.at[:, px]
        here[...] = sum_bf(here[...], r["gux_s"][...])
        gu_s[w] = gus_s[w, px]
        for k in (2, 3, 1):
            up_y(k, True).start()

    @step_of("up_in")
    def _():
        for k in (1, 2, 3):
            up_y(k, False).wait_recv()
        up.sum.ends()

    @step_of("D_in")
    def _():
        down_x.wait_recv()
        gds_s[down_here, :] = sum_bf(gds_s[down_here, :], r["gdx_s"][...])
        down.sum.ends()

    steps["D_xout"] = down_x.start
    for name, chain in (("U", up), ("D", down)):
        steps[name + "2a"] = partial(chain.sum.second, (0,))
        steps[name + "2b"] = partial(chain.sum.second, (1,))
        steps[name + "3"] = chain.sum.third
        steps[name + "_turn"] = chain.turn
    for name, line in (("U", up.gather), ("D", down.gather), ("q", q_line)):
        steps[name + "_i1"] = partial(line.inner, 1)
        steps[name + "_o1"] = partial(line.outer, 1)
        steps[name + "_i2"] = partial(line.inner, 2)
        steps[name + "_i3"] = partial(line.inner, 3)
    steps["H2a"] = partial(h1_sum.second, (0,))
    steps["H2b"] = partial(h1_sum.second, (1,))
    steps["H3"] = h1_sum.third
    steps["h1_e2"] = partial(h1_sum.ends, (2,))
    steps["go_combine"] = go.combine
    steps["py_combine"] = py.combine
    steps["gq_comb"] = gq.combine

    @step_of("go_out")
    def _():
        go_s[...] = go.finish().astype(BF)
        go_x.start()

    @step_of("go_in")
    def _():
        go_x.wait_recv()
        go_half = go_s[mine, :].astype(F32) + gox_s[...].astype(F32)
        for b in range(GROUPS):
            gop_s[b] = go_half[b * quarter : (b + 1) * quarter].astype(BF)
        for i in (2, 1, 3):
            go_turn.message((hg + i) % GROUPS).start()

    @step_of("go_turn")
    def _():
        for i in (1, 2, 3):
            go_turn.arrived((hg + i) % GROUPS)
        go_total = gop_s[hg].astype(F32)
        for i in (1, 2, 3):
            go_total = go_total + gon_s[(hg + i) % GROUPS].astype(F32)
        go_f[px, hg] = go_total.astype(BF)
        for i in (2, 1, 3):
            go_back(i).start()

    @step_of("go_done")
    def _():
        for i in (1, 2, 3):
            go_back(i).wait_recv()
        go_x2.start()

    @step_of("go_fin")
    def _():
        go_x2.wait_recv()

    steps["early"] = early_x.start

    @step_of("early2")
    def _():
        early_x.wait_recv()
        early_z_s[hg] = early[...] + early_x_s[...]
        for i in (1, 2, 3):
            early_z(i).start()

    @step_of("kv_in")
    def _():
        kv_back.wait_recv()
        dqkv_s[:, 2 * LANES :] = sum_bf(dkv_s[0], kvr_s[...])

    @step_of("h1_part")
    def _():
        def h1_part(step, carry):
            block = by_distance(step)
            rows = pl.ds(pl.multiple_of(block * R, R), R)
            ph1_s[block] = dot_nt(dqkv_s[rows, :], wq_s[...]).astype(BF)
            h1_sum.ends_block(block)
            return carry

        lax.fori_loop(0, GROUPS, h1_part, 0)

    @step_of("qkv_grad")
    def _():
        def qkv_grad(i, carry):
            at = pl.ds(pl.multiple_of(i * 256, 256), 256)
            gqs_s[at, :] = dot_tn(h1_s[:, :, at].reshape(half, 256), dqkv_s[...]).astype(BF)
            return carry

        lax.fori_loop(0, D // 256, qkv_grad, 0)
        gq.start()
        late[c, :, 2 * D : 2 * D + 2 * LANES] = rows_sum(dqkv_s[:, : 2 * LANES].astype(F32))
        late[c, :, 2 * D + 2 * LANES :] = rows_sum(dqkv_s[:, 3 * LANES :].astype(F32))

    @step_of("gq_fin")
    def _():
        gqc_s[...] = gq.finish().astype(BF)
        qx.start()

    @step_of("q_start")
    def _():
        qx.wait_recv()
        gqkv[hg, mine, :] = sum_bf(gqc_s[mine, :], gqx_s[...])
        q_line.start()

    @step_of("h1_fin")
    def _():
        def keep_h1(total):
            df_s[...] = total

        h1_sum.final(keep_h1)
        grad_one = df_s[...]
        unit_one, scale_one = unit_rows(x_s[hg].astype(F32))
        grad_in = dz_s[...] + unit_rows_back(grad_one, unit_one, scale_one, gain_one)
        r["dx_s"][...] = grad_in.astype(BF)
        late[c, :, 0:D] = rows_sum(grad_one * unit_one)
        late[c, :, D : 2 * D] = rows_sum(grad_one)
        late_all.start()

    @step_of("layer_out")
    def _():
        r["y_s"][...] = (x1_s[...] + py.finish() + down_b).astype(BF)

    @step_of("small")
    def _():
        for i in (1, 2, 3):
            there = (hg + i) % GROUPS
            wires.copy(early_first + GROUPS - i, early_z_s.at[there], early_z_s.at[there], left).wait_recv()
        ones = sum([early_z_s[i] for i in range(GROUPS)])
        twos = late_all.total()
        bq_all, bv_all = [], []
        for g in range(GROUPS):
            group_sum = sum([late[g * G + i][:, 2 * D :] for i in range(G)])
            bq_all.append(group_sum[:, :S])
            v_end = pltpu.roll(group_sum[:, 2 * LANES : 3 * LANES], LANES // 2, 1)[:, : S - LANES]
            bv_all.append(jnp.concatenate([group_sum[:, 3 * LANES :], v_end], axis=1))
        vectors = [twos[:, 0:D], twos[:, D : 2 * D]] + [
            ones[:, i * D : (i + 1) * D] for i in range(4)
        ]
        for i in range(GROUPS):
            for j, one in enumerate(vectors):
                vecs[i, :, j * 256 : j * 256 + S] = one[:, i * S : (i + 1) * S]
            vecs[i, :, 6 * 256 : 6 * 256 + S] = bq_all[i]
            vecs[i, :, 7 * 256 : 7 * 256 + S] = bv_all[i]
        r["vec"][:, 8 * 256 :] = ones[:, 4 * D :]
        for k in (1, 2, 3):
            vec_send(k).start()

    carried = {}

    @step_of("up_grad")
    def _():
        lax.fori_loop(0, 2, up_grad, 0)
        up_x.start()

    steps["ph_combine"] = ph.combine

    @step_of("down_grad")
    def _():
        lax.fori_loop(0, FS // 256, down_grad, 0)

    @step_of("y_part")
    def _():
        lax.fori_loop(0, GROUPS, y_part, 0)
        py.start()

    @step_of("wait_ph")
    def _():
        carried["two"] = ph.finish()

    @step_of("ln2")
    def _():
        grad_two = carried["two"]
        unit_two, scale_two = unit_rows(x1_s[...])
        top = r["dy_s"][w].astype(F32)
        grad_middle = top + unit_rows_back(grad_two, unit_two, scale_two, gain_two)
        dz = grad_middle.astype(BF)
        dz_s[...] = grad_middle
        carried["dz"], carried["unit"], carried["top"] = dz, unit_two, top

        def out_back(step, carry):
            block = by_distance(step)
            dos_s[block] = dot_nt(dz, wo_s[block]).astype(BF)

            @pl.when(step < last)
            def _():
                do_turn.message(block).start()

            return carry

        lax.fori_loop(0, GROUPS, out_back, 0)

    @step_of("sums")
    def _():
        dor_s[hg] = dos_s[hg]
        early[:, 0:D] = rows_sum(carried["dz"].astype(F32))
        early[:, D : 2 * D] = rows_sum(carried["two"] * carried["unit"])
        early[:, 2 * D : 3 * D] = rows_sum(carried["two"])
        early[:, 3 * D : 4 * D] = rows_sum(carried["top"])
        early[:, 4 * D :] = rows_sum(da_s[...].reshape(half, FS).astype(F32))

    @step_of("out_grad")
    def _():
        for i in range(GROUPS):
            piece = dot_tn(or_s[i], carried["dz"])
            gos_s[i, 0:LANES, :] = piece[0:LANES, :].astype(BF)
            gos_s[i, LANES:S, :] = piece[S:, :].astype(BF)
        go.start()
        dkv_s[...] = jnp.zeros(dkv_s.shape, F32)

    def back_block(block, side):
        outs = dor_s[block].astype(F32)
        kept = oa_s[block]
        grads_q = []
        for h in range(3):
            tile = 0 if h < 2 else LANES
            keep = low_half if h == 0 else jnp.logical_not(low_half)
            scaled = jnp.where(keep, outs[:, tile : tile + LANES], 0.0) * li_s[h, block]
            delta = jnp.sum(scaled * kept[:, tile : tile + LANES], axis=-1, keepdims=True)
            rounded = scaled.astype(BF)
            grad_prob = dot_nt(rounded, kv_s[side, :, VT[h] : VT[h] + LANES])
            weights = e_s[h, block, side]
            grad_score = (weights.astype(F32) * (grad_prob - delta)).astype(BF)
            grads_q.append(dot_nn(grad_score, kv_s[side, :, KT[h] : KT[h] + LANES]))
            dkv_s[side, :, KT[h] : KT[h] + LANES] += dot_tn(grad_score, q_s[h, block])
            dkv_s[side, :, VT[h] : VT[h] + LANES] += dot_tn(weights, rounded)
        first = jnp.where(low_half, grads_q[0], grads_q[1]) * 0.125
        final = jnp.where(low_half, grads_q[2], 0.0) * 0.125
        if side == 1:
            dq_s[block, :, :LANES] = first
            dq_s[block, :, LANES:] = final
        else:
            rows = pl.ds(pl.multiple_of(block * R, R), R)
            dqkv_s[rows, :LANES] = (dq_s[block, :, :LANES] + first).astype(BF)
            dqkv_s[rows, LANES : 2 * LANES] = (dq_s[block, :, LANES:] + final).astype(BF)

    def nearest(step):
        return by_distance(last - step)

    @step_of("kv_out")
    def _():
        kvt_s[...] = dkv_s[1].astype(BF)
        kv_back.start()

    @step_of("fin")
    def _():
        for k in (1, 2, 3):
            vec_send(k).wait_recv()
        r["vec"][:, 0 : 8 * 256] = vecs[w] + vecr[0] + vecr[1] + vecr[2]
        outs = [fetch(0, r["y_s"], r["y"]), fetch(1, r["dx_s"], r["dx"]), fetch(5, go_f, r["gout"])]
        down.gather.done()
        outs.append(fetch(2, gd_s, r["gdown"]))
        up.gather.done()
        outs.append(fetch(3, up_f, r["gup"]))
        q_line.done()
        outs.append(fetch(4, gqkv, r["gqkv"]))
        for one in outs:
            one.wait()

    def attention_back(side, plans):
        def body(step, carry):
            block = nearest(step)
            if side == 1:

                @pl.when(step > 0)
                def _():
                    do_turn.arrived(block)

            back_block(block, side)
            for k, names in enumerate(plans):
                if names:

                    @pl.when(step == k)
                    def _():
                        for name in names:
                            steps[name]()

            return carry

        lax.fori_loop(0, GROUPS, body, 0)

    at = 0
    order = ORDER
    while at < len(order):
        name = order[at]
        at += 1
        if name in ("bo0", "bw0"):
            plans, kind = [[]], name[:2]
            while at < len(order) and (order[at][:2] == kind or len(plans) < GROUPS):
                if order[at][:2] == kind:
                    plans.append([])
                else:
                    plans[-1].append(order[at])
                at += 1
            attention_back(1 if kind == "bo" else 0, plans)
        else:
            steps[name]()
    wires.drain()


def widen_kernel(S, y, dx, down, up, out, qkv, vec, y_out, dx_out, down_out, up_out, out_out, q_out, k_out, v_out, *vec_outs):
    y_out[...] = y[...]
    dx_out[...] = dx[...]
    down_out[...] = down[...].astype(F32)
    n = S // 2
    for i in (0, 1):
        up_out[i * n : (i + 1) * n, :] = up[0, i].astype(F32)
    out_out[...] = out[...].astype(F32)
    at = 0
    for one in vec_outs:
        one[...] = vec[0, at : at + one.shape[0]]
        at += max(one.shape[0], 256)

    def heads(pieces):
        return jnp.concatenate(
            [qkv[i, :, a:b].astype(F32) for i in range(GROUPS) for a, b in pieces], axis=1
        )

    q_out[...] = heads([(0, S)])
    k_out[...] = heads([(2 * LANES, 2 * LANES + S)])
    v_out[...] = heads([(4 * LANES, 5 * LANES), (2 * LANES + S, 4 * LANES)])


SEMS = 176


def fast_device(mesh_sizes, *arrays):
    (tokens, doc_lengths, out_grad, norm1_gain, norm1_bias, w_query, b_query, w_key, w_value,
     b_value, w_out, b_out, norm2_gain, norm2_bias, w_up, b_up, w_down, b_down) = arrays
    n_ctx, n_wsh = mesh_sizes
    R, D = tokens.shape[1], tokens.shape[2]
    S, FS, n_doc = D // GROUPS, w_down.shape[0], doc_lengths.shape[1]
    half, QW = GROUPS * R, 5 * LANES

    smem = pl.BlockSpec(memory_space=pltpu.SMEM)
    vmem = pl.BlockSpec(memory_space=pltpu.VMEM)
    anywhere = pl.BlockSpec(memory_space=pl.ANY)
    inputs = [
        ("doc", doc_lengths, smem),
        ("tok", tokens[0], anywhere),
        ("dy", out_grad[0], anywhere),
        ("wq", w_query, anywhere),
        ("wk", w_key, anywhere),
        ("wv", w_value, anywhere),
        ("wout", w_out, anywhere),
        ("wup", w_up, anywhere),
        ("wdown", w_down, anywhere),
        ("n1g", norm1_gain, vmem),
        ("n1b", norm1_bias, vmem),
        ("bq", b_query, vmem),
        ("bv", b_value, vmem),
        ("bo", b_out, vmem),
        ("n2g", norm2_gain, vmem),
        ("n2b", norm2_bias, vmem),
        ("bd", b_down, vmem),
        ("bup", b_up, vmem),
    ]
    n_up = S // 2
    outputs = [
        ("y", (R, D), BF, anywhere),
        ("dx", (R, D), BF, anywhere),
        ("gdown", (FS, D), BF, anywhere),
        ("gup", (GROUPS, 2, n_up, FS), BF, anywhere),
        ("gout", (2, GROUPS, S // 8, D), BF, anywhere),
        ("gqkv", (GROUPS, S, QW), BF, anywhere),
        ("vec", (1, 8 * 256 + FS), F32, vmem),
    ]
    scratch = [
        ("x_s", (GROUPS, R, D), BF),
        ("h1_s", (GROUPS, R, D), BF),
        ("win_s", (3, S, D), BF),
        ("wq_s", (D, QW), BF),
        ("par_s", (GROUPS, 8, 2 * LANES), F32),
        ("q_s", (3, GROUPS, R, LANES), BF),
        ("kv_s", (2, half, 3 * LANES), BF),
        ("e_s", (3, GROUPS, 2, R, half), BF),
        ("li_s", (3, GROUPS, R, LANES), F32),
        ("oa_s", (GROUPS, R, 2 * LANES), F32),
        ("os_s", (GROUPS, R, 2 * LANES), BF),
        ("or_s", (GROUPS, R, 2 * LANES), BF),
        ("wo_s", (GROUPS, 2 * LANES, D), BF),
        ("wu_s", (GROUPS, S, FS), BF),
        ("wd_s", (FS, D), BF),
        ("dy_s", (GROUPS, R, D), BF),
        ("x1_s", (R, D), F32),
        ("h2_s", (GROUPS, R, D), BF),
        ("g_s", (GROUPS, R, FS), BF),
        ("da_s", (GROUPS, R, FS), BF),
        ("ph_s", (GROUPS, R, D), BF),
        ("hr_s", (4, R, D), BF),
        ("py_s", (GROUPS, R, D), BF),
        ("yr_s", (4, R, D), BF),
        ("dz_s", (R, D), F32),
        ("dos_s", (GROUPS, R, 2 * LANES), BF),
        ("dor_s", (GROUPS, R, 2 * LANES), BF),
        ("dkv_s", (2, half, 3 * LANES), F32),
        ("kvt_s", (half, 3 * LANES), BF),
        ("kvr_s", (half, 3 * LANES), BF),
        ("dq_s", (GROUPS, R, 2 * LANES), F32),
        ("dqkv_s", (half, QW), BF),
        ("ph1_s", (GROUPS, R, D), BF),
        ("h1r_s", (6, R, D), BF),
        ("df_s", (R, D), F32),
        ("gds_s", (FS, D), BF),
        ("gdx_s", (FS // 2, D), BF),
        ("gdl_s", (6, FS // 8, D), BF),
        ("gd_s", (FS, D), BF),
        ("gus_s", (GROUPS, 2, S // 2, FS), BF),
        ("gu_s", (GROUPS, n_up, FS), BF),
        ("gux_s", (GROUPS, S // 2, FS), BF),
        ("gul_s", (6, n_up, FS), BF),
        ("gup_s", (GROUPS, 2, n_up, FS), BF),
        ("go_s", (S, D), BF),
        ("gox_s", (S // 2, D), BF),
        ("gop_s", (GROUPS, S // 8, D), BF),
        ("gon_s", (GROUPS, S // 8, D), BF),
        ("gout_s", (2, GROUPS, S // 8, D), BF),
        ("gq_s", (GROUPS, S, QW), BF),
        ("y_s", (R, D), BF),
        ("dx_s", (R, D), BF),
        ("gos_s", (GROUPS, S, D), BF),
        ("gor_s", (4, S, D), BF),
        ("gqs_s", (D, QW), BF),
        ("gqr_s", (4, S, QW), BF),
        ("gqc_s", (S, QW), BF),
        ("gqx_s", (S // 2, QW), BF),
        ("early_s", (1, 4 * D + FS), F32),
        ("early_x_s", (1, 4 * D + FS), F32),
        ("early_z_s", (GROUPS, 1, 4 * D + FS), F32),
        ("late_s", (n_ctx, 1, 2 * D + 4 * LANES), F32),
        ("vecs_s", (GROUPS, 1, 8 * 256), F32),
        ("vecr_s", (3, 1, 8 * 256), F32),
    ]
    sems = [("send_sems", SEMS), ("recv_sems", SEMS), ("local_sems", 9)]
    names = [one[0] for one in inputs + outputs + scratch + sems]
    y, dx, g_down, g_up, g_out, g_qkv, vec = pl.pallas_call(
        partial(layer_kernel, (n_ctx, n_doc, R, D, S, FS), names),
        out_shape=[jax.ShapeDtypeStruct(shape, dtype) for name, shape, dtype, spec in outputs],
        in_specs=[spec for name, value, spec in inputs],
        out_specs=[spec for name, shape, dtype, spec in outputs],
        scratch_shapes=[pltpu.VMEM(shape, dtype) for name, shape, dtype in scratch]
        + [pltpu.SemaphoreType.DMA((count,)) for name, count in sems],
        compiler_params=pltpu.CompilerParams(
            collective_id=0, has_side_effects=True, vmem_limit_bytes=67043328
        ),
        name="layer",
    )(*[value for name, value, spec in inputs])

    n = GROUPS
    row = lambda i: (i, 0)
    whole = lambda i: (0,)
    sizes = [S] * 8 + [FS]
    wide = pl.pallas_call(
        partial(widen_kernel, S),
        grid=(n,),
        in_specs=[
            pl.BlockSpec((R // n, D), row),
            pl.BlockSpec((R // n, D), row),
            pl.BlockSpec((FS // n, D), row),
            pl.BlockSpec((1, 2, n_up, FS), lambda i: (i, 0, 0, 0)),
            pl.BlockSpec((2, 1, S // 8, D), lambda i: (0, i, 0, 0)),
            pl.BlockSpec((GROUPS, S // n, QW), lambda i: (0, i, 0)),
            pl.BlockSpec((1, 8 * 256 + FS), lambda i: (0, 0)),
        ],
        out_specs=[
            pl.BlockSpec((R // n, D), row),
            pl.BlockSpec((R // n, D), row),
            pl.BlockSpec((FS // n, D), row),
            pl.BlockSpec((S, FS), lambda i: (0, i)),
            pl.BlockSpec((2, 1, S // 8, D), lambda i: (0, i, 0, 0)),
        ]
        + [pl.BlockSpec((S // n, D), row)] * 3
        + [pl.BlockSpec((size,), whole) for size in sizes],
        out_shape=[
            jax.ShapeDtypeStruct((R, D), BF),
            jax.ShapeDtypeStruct((R, D), BF),
            jax.ShapeDtypeStruct((FS, D), F32),
            jax.ShapeDtypeStruct((S, GROUPS * FS), F32),
            jax.ShapeDtypeStruct((2, GROUPS, S // 8, D), F32),
        ]
        + [jax.ShapeDtypeStruct((S, D), F32)] * 3
        + [jax.ShapeDtypeStruct((size,), F32) for size in sizes],
        name="widen",
    )(y, dx, g_down, g_up, g_out, g_qkv, vec)
    y, dx, down, up, out, q, k, v, n1g, n1b, bo, n2g, n2b, bd, bq, bv, bup = wide
    return (
        y[None], dx[None], n1g, n1b, q, bq, k, v, bv, out.reshape(S, D), bo, n2g, n2b, up, bup, down, bd,
    )


def solution(mesh):
    in_specs = (
        P("wsh", "ctx", None),
        P("wsh", None),
        P("wsh", "ctx", None),
        P("wsh"),
        P("wsh"),
        P("wsh", None),
        P("wsh"),
        P("wsh", None),
        P("wsh", None),
        P("wsh"),
        P("wsh", None),
        P("wsh"),
        P("wsh"),
        P("wsh"),
        P("wsh", None),
        P("wsh"),
        P("wsh", None),
        P("wsh"),
    )
    out_specs = (
        P("wsh", "ctx", None),
        P("wsh", "ctx", None),
        P("wsh"),
        P("wsh"),
        P("wsh", None),
        P("wsh"),
        P("wsh", None),
        P("wsh", None),
        P("wsh"),
        P("wsh", None),
        P("wsh"),
        P("wsh"),
        P("wsh"),
        P("wsh", None),
        P("wsh"),
        P("wsh", None),
        P("wsh"),
    )
    sizes = (mesh.shape["ctx"], mesh.shape["wsh"])
    body = partial(fast_device, sizes) if sizes == (2 * GROUPS, GROUPS) else per_device
    return jax.shard_map(
        body, mesh=mesh, in_specs=in_specs, out_specs=out_specs, check_vma=False
    )
```

```python
from functools import partial
import math

import jax
import jax.numpy as jnp
from jax import lax
from jax.experimental import pallas as pl
from jax.experimental.pallas import tpu as pltpu
from jax.sharding import PartitionSpec as P

HEADS = 12


EPS = 1e-06
NEG_START = -1e30


def norm_rows(inputs, norm_gain, norm_bias):
    row_mean = jnp.mean(inputs, axis=-1, keepdims=True)
    centred = inputs - row_mean
    variance = jnp.mean(centred * centred, axis=-1, keepdims=True)
    return centred * lax.rsqrt(variance + EPS) * norm_gain + norm_bias


def doc_of(positions, doc_ends):
    return jnp.sum((positions[:, None] >= doc_ends[None, :]).astype(jnp.int32), axis=1)


def dot_plain(left, right):
    return jnp.dot(left, right, preferred_element_type=jnp.float32)


def dot_left(left, right):
    return lax.dot_general(
        left, right, (((0,), (0,)), ((), ())), preferred_element_type=jnp.float32
    )


def dot_right(left, right):
    return lax.dot_general(
        left, right, (((1,), (1,)), ((), ())), preferred_element_type=jnp.float32
    )


def masked_scores(query_heads, key_heads, query_ids, key_ids, score_scale):
    raw_scores = (
        jnp.einsum("qhd,khd->hqk", query_heads, key_heads, preferred_element_type=jnp.float32)
        * score_scale
    )
    same_doc = (query_ids[:, None] == key_ids[None, :])[None]
    return jnp.where(same_doc, raw_scores, -jnp.inf)


def per_device(
    tokens,
    doc_lengths,
    out_grad,
    norm1_gain,
    norm1_bias,
    w_query,
    b_query,
    w_key,
    w_value,
    b_value,
    w_out,
    b_out,
    norm2_gain,
    norm2_bias,
    w_up,
    b_up,
    w_down,
    b_down,
):
    (
        gain_one,
        bias_one,
        query_w,
        query_b,
        key_w,
        value_w,
        value_b,
        out_w,
        out_b,
        gain_two,
        bias_two,
        up_w,
        up_b,
        down_w,
        down_b,
    ) = (
        lax.all_gather(norm1_gain, "wsh", axis=0, tiled=True),
        lax.all_gather(norm1_bias, "wsh", axis=0, tiled=True),
        lax.all_gather(w_query, "wsh", axis=0, tiled=True),
        lax.all_gather(b_query, "wsh", axis=0, tiled=True),
        lax.all_gather(w_key, "wsh", axis=0, tiled=True),
        lax.all_gather(w_value, "wsh", axis=0, tiled=True),
        lax.all_gather(b_value, "wsh", axis=0, tiled=True),
        lax.all_gather(w_out, "wsh", axis=0, tiled=True),
        lax.all_gather(b_out, "wsh", axis=0, tiled=True),
        lax.all_gather(norm2_gain, "wsh", axis=0, tiled=True),
        lax.all_gather(norm2_bias, "wsh", axis=0, tiled=True),
        lax.all_gather(w_up, "wsh", axis=0, tiled=True),
        lax.all_gather(b_up, "wsh", axis=0, tiled=True),
        lax.all_gather(w_down, "wsh", axis=0, tiled=True),
        lax.all_gather(b_down, "wsh", axis=0, tiled=True),
    )
    row_count = tokens.shape[1]
    model_width = tokens.shape[2]
    head_dim = model_width // HEADS
    score_scale = head_dim ** (-0.5)
    first_gain = gain_one.astype(jnp.float32)
    first_bias = bias_one.astype(jnp.float32)
    second_gain = gain_two.astype(jnp.float32)
    second_bias = bias_two.astype(jnp.float32)
    inputs = tokens[0].astype(jnp.float32)
    doc_ends = jnp.cumsum(doc_lengths[0])
    own_ids = doc_of(
        lax.axis_index("ctx") * row_count + jnp.arange(row_count, dtype=jnp.int32), doc_ends
    )
    normed_one = norm_rows(inputs, first_gain, first_bias).astype(jnp.bfloat16)
    queries = (dot_plain(normed_one, query_w) + query_b.astype(jnp.float32)).astype(jnp.bfloat16)
    key_rows = dot_plain(normed_one, key_w).astype(jnp.bfloat16)
    values = (dot_plain(normed_one, value_w) + value_b.astype(jnp.float32)).astype(jnp.bfloat16)
    key_all, value_all = (
        lax.all_gather(key_rows, "ctx", axis=0, tiled=True),
        lax.all_gather(values, "ctx", axis=0, tiled=True),
    )
    total_rows = key_all.shape[0]
    key_block = math.gcd(total_rows, 2048)
    block_count = total_rows // key_block
    key_stack = key_all.reshape(block_count, key_block, HEADS, head_dim)
    value_stack = value_all.reshape(block_count, key_block, HEADS, head_dim)
    id_stack = doc_of(jnp.arange(total_rows, dtype=jnp.int32), doc_ends).reshape(
        block_count, key_block
    )
    query_heads = queries.reshape(row_count, HEADS, head_dim)

    def lse_step(running, block_in):
        run_max, run_sum = running
        key_heads, key_ids = block_in
        scores = masked_scores(query_heads, key_heads, own_ids, key_ids, score_scale)
        new_max = jnp.maximum(run_max, jnp.max(scores, axis=-1))
        new_sum = run_sum * jnp.exp(run_max - new_max) + jnp.sum(
            jnp.exp(scores - new_max[:, :, None]), axis=-1
        )
        return ((new_max, new_sum), None)

    start_max = jnp.full((HEADS, row_count), NEG_START, jnp.float32)
    (final_max, final_sum), unused = lax.scan(
        lse_step, (start_max, jnp.zeros_like(start_max)), (key_stack, id_stack)
    )
    log_total = final_max + jnp.log(final_sum)

    def out_step(running, block_in):
        key_heads, value_heads, key_ids = block_in
        scores = masked_scores(query_heads, key_heads, own_ids, key_ids, score_scale)
        attn_prob = jnp.exp(scores - log_total[:, :, None]).astype(jnp.bfloat16)
        return (
            running
            + jnp.einsum(
                "hqk,khd->qhd", attn_prob, value_heads, preferred_element_type=jnp.float32
            ),
            None,
        )

    attn_sum, unused = lax.scan(
        out_step,
        jnp.zeros((row_count, HEADS, head_dim), jnp.float32),
        (key_stack, value_stack, id_stack),
    )
    attended = attn_sum.reshape(row_count, model_width).astype(jnp.bfloat16)
    middle = inputs + dot_plain(attended, out_w) + out_b.astype(jnp.float32)
    normed_two = norm_rows(middle, second_gain, second_bias).astype(jnp.bfloat16)
    hidden = dot_plain(normed_two, up_w) + up_b.astype(jnp.float32)
    active = jax.nn.gelu(hidden, approximate=True).astype(jnp.bfloat16)
    output = middle + dot_plain(active, down_w) + down_b.astype(jnp.float32)
    top_grad = out_grad[0]
    top_float = top_grad.astype(jnp.float32)
    grad_down_w = dot_left(active, top_grad)
    grad_down_b = jnp.sum(top_float, axis=0)
    grad_active = dot_right(top_grad, down_w)
    unused, gelu_pull = jax.vjp(partial(jax.nn.gelu, approximate=True), hidden)
    grad_hidden = gelu_pull(grad_active)[0].astype(jnp.bfloat16)
    grad_up_w = dot_left(normed_two, grad_hidden)
    grad_up_b = jnp.sum(grad_hidden.astype(jnp.float32), axis=0)
    grad_normed_two = dot_right(grad_hidden, up_w)
    unused, second_pull = jax.vjp(norm_rows, middle, second_gain, second_bias)
    grad_middle, grad_gain_two, grad_bias_two = second_pull(grad_normed_two)
    grad_middle = grad_middle + top_float
    grad_branch = grad_middle.astype(jnp.bfloat16)
    grad_out_w = dot_left(attended, grad_branch)
    grad_out_b = jnp.sum(grad_branch.astype(jnp.float32), axis=0)
    grad_attended = dot_right(grad_branch, out_w).astype(jnp.bfloat16)
    grad_heads = grad_attended.reshape(row_count, HEADS, head_dim)
    row_delta = jnp.sum(grad_heads.astype(jnp.float32) * attn_sum, axis=-1)
    head_delta = row_delta.T
    query_start = jnp.zeros((row_count, HEADS, head_dim), jnp.float32)

    def full_step(grad_query, block_in):
        key_heads, value_heads, key_ids = block_in
        scores = masked_scores(query_heads, key_heads, own_ids, key_ids, score_scale)
        attn_prob = jnp.exp(scores - log_total[:, :, None])
        grad_prob = jnp.einsum(
            "qhd,khd->hqk", grad_heads, value_heads, preferred_element_type=jnp.float32
        )
        grad_score = (attn_prob * (grad_prob - head_delta[:, :, None])).astype(jnp.bfloat16)
        grad_query = grad_query + jnp.einsum(
            "hqk,khd->qhd", grad_score, key_heads, preferred_element_type=jnp.float32
        )
        grad_key = (
            jnp.einsum("hqk,qhd->khd", grad_score, query_heads, preferred_element_type=jnp.float32)
            * score_scale
        )
        grad_value = jnp.einsum(
            "hqk,qhd->khd",
            attn_prob.astype(jnp.bfloat16),
            grad_heads,
            preferred_element_type=jnp.float32,
        )
        return (
            grad_query,
            (grad_key.reshape(key_block, model_width), grad_value.reshape(key_block, model_width)),
        )

    grad_query, key_terms = lax.scan(full_step, query_start, (key_stack, value_stack, id_stack))
    key_grad, value_grad = (
        lax.psum_scatter(
            key_terms[0].reshape(total_rows, model_width), "ctx", scatter_dimension=0, tiled=True
        ),
        lax.psum_scatter(
            key_terms[1].reshape(total_rows, model_width), "ctx", scatter_dimension=0, tiled=True
        ),
    )
    grad_query_rows = (
        (grad_query * score_scale).reshape(row_count, model_width).astype(jnp.bfloat16)
    )
    grad_key_rows = key_grad.astype(jnp.bfloat16)
    grad_value_rows = value_grad.astype(jnp.bfloat16)
    grad_query_w = dot_left(normed_one, grad_query_rows)
    grad_query_b = jnp.sum(grad_query_rows.astype(jnp.float32), axis=0)
    grad_key_w = dot_left(normed_one, grad_key_rows)
    grad_value_w = dot_left(normed_one, grad_value_rows)
    grad_value_b = jnp.sum(grad_value_rows.astype(jnp.float32), axis=0)
    grad_normed_one = (
        dot_right(grad_query_rows, query_w)
        + dot_right(grad_key_rows, key_w)
        + dot_right(grad_value_rows, value_w)
    )
    unused, first_pull = jax.vjp(norm_rows, inputs, first_gain, first_bias)
    grad_inputs, grad_gain_one, grad_bias_one = first_pull(grad_normed_one)
    grad_inputs = grad_inputs + grad_middle
    (
        share_gain_one,
        share_bias_one,
        share_query_w,
        share_query_b,
        share_key_w,
        share_value_w,
        share_value_b,
        share_out_w,
        share_out_b,
        share_gain_two,
        share_bias_two,
        share_up_w,
        share_up_b,
        share_down_w,
        share_down_b,
    ) = (
        lax.psum_scatter(
            grad_gain_one.astype(jnp.bfloat16), "wsh", scatter_dimension=0, tiled=True
        ).astype(jnp.float32),
        lax.psum_scatter(
            grad_bias_one.astype(jnp.bfloat16), "wsh", scatter_dimension=0, tiled=True
        ).astype(jnp.float32),
        lax.psum_scatter(
            grad_query_w.astype(jnp.bfloat16), "wsh", scatter_dimension=0, tiled=True
        ).astype(jnp.float32),
        lax.psum_scatter(
            grad_query_b.astype(jnp.bfloat16), "wsh", scatter_dimension=0, tiled=True
        ).astype(jnp.float32),
        lax.psum_scatter(
            grad_key_w.astype(jnp.bfloat16), "wsh", scatter_dimension=0, tiled=True
        ).astype(jnp.float32),
        lax.psum_scatter(
            grad_value_w.astype(jnp.bfloat16), "wsh", scatter_dimension=0, tiled=True
        ).astype(jnp.float32),
        lax.psum_scatter(
            grad_value_b.astype(jnp.bfloat16), "wsh", scatter_dimension=0, tiled=True
        ).astype(jnp.float32),
        lax.psum_scatter(
            grad_out_w.astype(jnp.bfloat16), "wsh", scatter_dimension=0, tiled=True
        ).astype(jnp.float32),
        lax.psum_scatter(
            grad_out_b.astype(jnp.bfloat16), "wsh", scatter_dimension=0, tiled=True
        ).astype(jnp.float32),
        lax.psum_scatter(
            grad_gain_two.astype(jnp.bfloat16), "wsh", scatter_dimension=0, tiled=True
        ).astype(jnp.float32),
        lax.psum_scatter(
            grad_bias_two.astype(jnp.bfloat16), "wsh", scatter_dimension=0, tiled=True
        ).astype(jnp.float32),
        lax.psum_scatter(
            grad_up_w.astype(jnp.bfloat16), "wsh", scatter_dimension=0, tiled=True
        ).astype(jnp.float32),
        lax.psum_scatter(
            grad_up_b.astype(jnp.bfloat16), "wsh", scatter_dimension=0, tiled=True
        ).astype(jnp.float32),
        lax.psum_scatter(
            grad_down_w.astype(jnp.bfloat16), "wsh", scatter_dimension=0, tiled=True
        ).astype(jnp.float32),
        lax.psum_scatter(
            grad_down_b.astype(jnp.bfloat16), "wsh", scatter_dimension=0, tiled=True
        ).astype(jnp.float32),
    )
    totals = lax.psum(
        (
            share_gain_one,
            share_bias_one,
            share_query_w,
            share_query_b,
            share_key_w,
            share_value_w,
            share_value_b,
            share_out_w,
            share_out_b,
            share_gain_two,
            share_bias_two,
            share_up_w,
            share_up_b,
            share_down_w,
            share_down_b,
        ),
        "ctx",
    )
    return (
        output.astype(jnp.bfloat16)[None],
        grad_inputs.astype(jnp.bfloat16)[None],
        totals[0],
        totals[1],
        totals[2],
        totals[3],
        totals[4],
        totals[5],
        totals[6],
        totals[7],
        totals[8],
        totals[9],
        totals[10],
        totals[11],
        totals[12],
        totals[13],
        totals[14],
    )


MESH = pl.DeviceIdType.MESH
F32 = jnp.float32
BF = jnp.bfloat16
GROUPS = 4
LANES = 128


def flip(value, mask):
    return ((value // 2 + mask // 2) % 2) * 2 + (value + mask) % 2


def dot_nn(left, right):
    return lax.dot_general(left, right, (((1,), (0,)), ((), ())), preferred_element_type=F32)


def dot_nt(left, right):
    return lax.dot_general(left, right, (((1,), (1,)), ((), ())), preferred_element_type=F32)


def dot_tn(left, right):
    return lax.dot_general(left, right, (((0,), (0,)), ((), ())), preferred_element_type=F32)


def unit_rows(inputs):
    row_mean = jnp.mean(inputs, axis=-1, keepdims=True)
    centred = inputs - row_mean
    variance = jnp.mean(centred * centred, axis=-1, keepdims=True)
    scale = lax.rsqrt(variance + EPS)
    return centred * scale, scale


def unit_rows_back(grad_normed, unit, scale, gain):
    grad_unit = grad_normed * gain
    return scale * (
        grad_unit
        - jnp.mean(grad_unit, axis=-1, keepdims=True)
        - unit * jnp.mean(grad_unit * unit, axis=-1, keepdims=True)
    )


def rows_sum(values):
    return jnp.sum(values, axis=0, keepdims=True)


def sum_bf(*values):
    return sum([one.astype(F32) for one in values]).astype(BF)


class Wires:
    def __init__(self, send_sems, recv_sems):
        self.send_sems, self.recv_sems, self.used, self.started = send_sems, recv_sems, 0, []

    def take(self, count=1):
        first = self.used
        self.used += count
        return first

    def copy(self, index, source, target, device):
        return pltpu.make_async_remote_copy(
            src_ref=source,
            dst_ref=target,
            send_sem=self.send_sems.at[index],
            recv_sem=self.recv_sems.at[index],
            device_id=device,
            device_id_type=MESH,
        )

    def send(self, source, target, device):
        one = self.copy(self.take(), source, target, device)
        one.start()
        self.started.append((one, None))
        return one

    def later(self, one, when=None):
        self.started.append((one, when))
        return one

    def plan(self, source, target, device):
        return self.later(self.copy(self.take(), source, target, device))

    def drain(self):
        for one, when in self.started:
            if when is None:
                one.wait_send()
            else:
                pl.when(when)(one.wait_send)


ORDER = (
    "up_grad", "ph_combine", "down_grad", "y_part", "wait_ph", "ln2", "D_xout", "sums", "up_xin",
    "out_grad", "bo0", "py_combine", "bo1", "up_in", "bo2", "bo3", "D_in", "kv_out", "go_combine",
    "U2a", "U2b", "bw0", "bw1", "U3", "go_out", "D2a", "U_turn", "bw2", "D2b", "bw3", "D3", "kv_in",
    "qkv_grad", "early", "U_i1", "go_in", "gq_comb", "D_turn", "U_o1", "go_turn", "h1_part",
    "gq_fin", "D_o1", "D_i1", "U_i2", "q_start", "go_done", "layer_out", "D_i2", "H2a", "U_i3",
    "q_i1", "early2", "D_i3", "q_o1", "h1_e2", "H2b", "H3", "go_fin", "q_i2", "h1_fin", "q_i3",
    "small", "fin",
)


def layer_kernel(sizes, names, *refs):
    n_ctx, n_doc, R, D, S, FS = sizes
    r = dict(zip(names, refs, strict=True))
    G = n_ctx // GROUPS
    last = GROUPS - 1
    half = GROUPS * R
    c = lax.axis_index("ctx")
    w = lax.axis_index("wsh")
    hg, px = c // G, c % G

    def zdev(group):
        return {"ctx": group * G + px, "wsh": w}

    def wdev(index):
        return {"ctx": c, "wsh": index}

    xdev = {"ctx": hg * G + 1 - px, "wsh": w}
    left, right = zdev((hg + last) % GROUPS), zdev((hg + 1) % GROUPS)
    w1, w2, w3 = flip(w, 1), flip(w, 2), flip(w, 3)
    sib, across, diag = wdev(w1), wdev(w2), wdev(w3)
    wires = Wires(r["send_sems"], r["recv_sems"])
    lane = lax.broadcasted_iota(jnp.int32, (1, LANES), 1)
    low_half = lane < LANES // 2

    def pick(table):
        return sum([jnp.where(hg == i, one, 0) for i, one in enumerate(table)])

    def by_distance(step):
        return (
            jnp.where(step == 0, pick((3, 3, 0, 0)), 0)
            + jnp.where(step == 1, pick((2, 0, 3, 1)), 0)
            + jnp.where(step == 2, pick((1, 2, 1, 2)), 0)
            + jnp.where(step == 3, hg, 0)
        )

    local = r["local_sems"]

    def fetch(index, source, target):
        one = pltpu.make_async_copy(source, target, local.at[index])
        one.start()
        return one

    tok_in = fetch(0, r["tok"], r["x_s"].at[hg])
    qkv_in = [fetch(1 + i, r[name], r["win_s"].at[i]) for i, name in enumerate(("wq", "wk", "wv"))]
    dy_in = fetch(4, r["dy"], r["dy_s"].at[w])
    wo_in = [
        fetch(5, r["wout"].at[pl.ds(0, LANES)], r["wo_s"].at[w, pl.ds(0, LANES)]),
        fetch(6, r["wout"].at[pl.ds(LANES, S - LANES)], r["wo_s"].at[w, pl.ds(S, S - LANES)]),
    ]
    wu_in = fetch(7, r["wup"].at[:, pl.ds(pl.multiple_of(w * FS, FS), FS)], r["wu_s"].at[w])
    wd_in = fetch(8, r["wdown"], r["wd_s"])

    barrier = pltpu.get_barrier_semaphore()
    ctx_peers = [{"ctx": (c + i) % n_ctx, "wsh": w} for i in range(1, n_ctx)]
    partners = ctx_peers + [sib, across, diag]
    for partner in partners:
        pl.semaphore_signal(barrier, inc=1, device_id=partner, device_id_type=MESH)

    for one in qkv_in:
        one.wait()
    own_w = pl.ds(pl.multiple_of(w * S, S), S)
    win, wq_s = r["win_s"], r["wq_s"]
    for g in range(GROUPS):

        @pl.when(hg == g)
        def _():
            a = g * S
            wq_s[own_w, 0:S] = win[0, :, a : a + S]
            wq_s[own_w, S : 2 * LANES] = jnp.zeros((S, 2 * LANES - S), BF)
            wq_s[own_w, 2 * LANES : 2 * LANES + S] = win[1, :, a : a + S]
            wq_s[own_w, 2 * LANES + S : 4 * LANES] = win[2, :, a + LANES : a + S]
            wq_s[own_w, 4 * LANES : 5 * LANES] = win[2, :, a : a + LANES]

    par_s = r["par_s"]
    par_s[w] = jnp.zeros((8, 2 * LANES), F32)
    for i, name in enumerate(("n1g", "n1b", "bq", "bv", "bo", "n2g", "n2b", "bd")):
        par_s[w, i : i + 1, 0:S] = r[name][...].astype(F32)[None, :]
    r["wo_s"][:, LANES:S, :] = jnp.zeros((GROUPS, S - LANES, D), BF)
    tok_in.wait()
    pl.semaphore_wait(barrier, len(partners))

    class Gather:
        def __init__(self, slot):
            self.slot = slot
            self.to_across = wires.send(slot(w), slot(w), across)
            self.to_sib = wires.send(slot(w), slot(w), sib)

        def relay(self):
            self.to_across.wait_recv()
            self.on = wires.send(self.slot(w2), self.slot(w2), sib)

        def finish(self):
            self.to_sib.wait_recv()
            self.on.wait_recv()

    class Reduce:
        def __init__(self, part, recv):
            self.part, self.recv = part, recv
            self.a = wires.plan(part(w3), recv.at[0], sib)
            self.b = wires.plan(part(w1), recv.at[1], sib)
            self.c = wires.plan(recv.at[3], recv.at[2], across)

        def start(self):
            self.a.start()
            self.b.start()

        def combine(self):
            self.a.wait_recv()
            self.recv[3] = sum_bf(self.part(w2)[...], self.recv[0])
            self.c.start()

        def finish(self):
            self.b.wait_recv()
            self.c.wait_recv()
            return (
                self.part(w)[...].astype(F32)
                + self.recv[1].astype(F32)
                + self.recv[2].astype(F32)
            )

    class LineSum:
        def __init__(self, part, recv):
            self.part, self.recv = part, recv
            self.first_at = wires.take(6)
            for i in range(3):
                wires.later(self.message(i, True), hg > i)
                wires.later(self.message(i, False), hg < last - i)

        def message(self, i, leftward):
            block, slot = (i, i) if leftward else (last - i, 3 + i)
            return wires.copy(
                self.first_at + slot, self.part(block), self.recv.at[slot], left if leftward else right
            )

        def ends_block(self, block):
            for i in range(2):

                @pl.when((hg == last) & (block == i))
                def _():
                    self.message(i, True).start()

                @pl.when((hg == 0) & (block == last - i))
                def _():
                    self.message(i, False).start()

        def ends(self, which=(0, 1, 2)):
            for i in which:

                @pl.when(hg == last)
                def _():
                    self.message(i, True).start()

                @pl.when(hg == 0)
                def _():
                    self.message(i, False).start()

        def pass_on(self, position, i, leftward):
            @pl.when(hg == position)
            def _():
                one = self.message(i, leftward)
                one.wait_recv()
                block, slot = (i, i) if leftward else (last - i, 3 + i)
                self.part(block)[...] = sum_bf(self.part(block)[...], self.recv[slot])
                one.start()

        def second(self, which=(0, 1)):
            for i in which:
                self.pass_on(2, i, True)
                self.pass_on(1, i, False)

        def third(self):
            self.pass_on(1, 0, True)
            self.pass_on(2, 0, False)

        def final(self, put):
            for position in range(GROUPS):

                @pl.when(hg == position)
                def _():
                    total = self.part(position)[...].astype(F32)
                    if position < last:
                        self.message(position, True).wait_recv()
                        total = total + self.recv[position].astype(F32)
                    if position > 0:
                        self.message(last - position, False).wait_recv()
                        total = total + self.recv[3 + last - position].astype(F32)
                    put(total)

    class LineGather:
        def __init__(self, slot, to_x):
            self.slot, self.to_x = slot, to_x
            self.first_at = wires.take(6)
            self.x_at = wires.take(GROUPS) if to_x else None
            for d in (1, 2, 3):
                wires.later(self.message(d, 0), (hg >= d - 1) & (hg < last))
                wires.later(self.message(d, 1), (hg + d - 1 <= last) & (hg > 0))
            if to_x:
                for b in range(GROUPS):
                    wires.later(self.x_message(b))

        def message(self, d, side):
            block = (hg + GROUPS + (1 - d) * (1 - 2 * side)) % GROUPS
            device = zdev((hg + GROUPS + 1 - 2 * side) % GROUPS)
            return wires.copy(
                self.first_at + 3 * side + d - 1, self.slot(block), self.slot(block), device
            )

        def x_message(self, block):
            return wires.copy(self.x_at + block, self.slot(block), self.slot(block), xdev)

        def start(self):
            pl.when(hg < last)(self.message(1, 0).start)
            pl.when(hg > 0)(self.message(1, 1).start)
            if self.to_x:
                self.x_message(hg).start()

        def arrived(self, d, side, then=None):
            block = (hg + GROUPS - d * (1 - 2 * side)) % GROUPS
            here = jnp.where(side == 0, (hg >= d).astype(jnp.int32), (hg + d <= last).astype(jnp.int32))
            onward = here * jnp.where(side == 0, (hg < last).astype(jnp.int32), (hg > 0).astype(jnp.int32))

            @pl.when(here == 1)
            def _():
                wires.copy(
                    self.first_at + 3 * side + d - 1, self.slot(block), self.slot(block), left
                ).wait_recv()

            @pl.when(onward == 1)
            def _():
                self.message(d + 1, side).start()

            @pl.when(here == 1)
            def _():
                if self.to_x:
                    self.x_message(block).start()
                if then is not None:
                    then(block)

        def inner(self, d):
            self.arrived(d, jnp.where(hg < 2, 1, 0))

        def outer(self, d):
            self.arrived(d, jnp.where(hg < 2, 0, 1))

        def done(self):
            for b in range(GROUPS):
                self.x_message(b).wait_recv()

    x_s, h1_s, q_s, kv_s = r["x_s"], r["h1_s"], r["q_s"], r["kv_s"]
    rows_two = R // 2
    tokens = [
        LineGather(lambda b, j=j: x_s.at[b, pl.ds(j * rows_two, rows_two)], False) for j in (0, 1)
    ]
    for one in tokens:
        one.start()
    ws_all = Gather(lambda i: wq_s.at[pl.ds(pl.multiple_of(i * S, S), S)])
    par_all = Gather(lambda i: par_s.at[i])
    par_all.relay()
    ws_all.relay()
    par_all.finish()

    pars = jnp.concatenate([par_s[i][:, :S] for i in range(GROUPS)], axis=1)
    gain_one, bias_one, out_b, gain_two, bias_two, down_b = [
        pars[i : i + 1] for i in (0, 1, 4, 5, 6, 7)
    ]
    up_b = r["bup"][...].astype(F32)[None, :]
    own_par = par_s[hg]
    v_tile, v_last = own_par[3:4, :LANES], own_par[3:4, LANES:]
    qkv_b = jnp.concatenate(
        [own_par[2:3, :], jnp.zeros((1, LANES), F32), pltpu.roll(v_last, LANES // 2, 1), v_tile],
        axis=1,
    )

    def norm_block(block):
        unit, unused = unit_rows(x_s[block].astype(F32))
        h1_s[block] = (unit * gain_one + bias_one).astype(BF)

    norm_block(hg)
    ws_all.finish()
    for one in wo_in:
        one.wait()
    dy_in.wait()
    wo_s, dy_s, wu_s = r["wo_s"], r["dy_s"], r["wu_s"]
    wo_top = Gather(lambda i: wo_s.at[i, pl.ds(0, LANES)])
    wo_low = Gather(lambda i: wo_s.at[i, pl.ds(S, S - LANES)])
    dy_all = Gather(lambda i: dy_s.at[i])

    kv_first = wires.take(GROUPS)

    def kv_copy(block):
        rows = pl.ds(pl.multiple_of(block * R, R), R)
        return wires.copy(kv_first + block, kv_s.at[0, rows], kv_s.at[1, rows], xdev)

    def project(block):
        qkv = dot_nn(h1_s[block], wq_s[...]) + qkv_b
        queries = qkv[:, : 2 * LANES].astype(BF).astype(F32) * 0.125
        q_s[0, block] = jnp.where(low_half, queries[:, :LANES], 0.0).astype(BF)
        q_s[1, block] = jnp.where(low_half, 0.0, queries[:, :LANES]).astype(BF)
        q_s[2, block] = queries[:, LANES:].astype(BF)
        kv_s[0, pl.ds(pl.multiple_of(block * R, R), R), :] = qkv[:, 2 * LANES :].astype(BF)
        kv_copy(block).start()

    def norm_project(block):
        norm_block(block)
        project(block)

    project(hg)

    inner_side = jnp.where(hg < 2, 1, 0)

    def token_step(i, carry):
        d = i + 1
        for one in tokens:
            one.arrived(d, inner_side)
            one.arrived(d, 1 - inner_side)

        def side_block(side, present):
            step = d * (1 - 2 * side)

            @pl.when(present)
            def _():
                norm_project((hg + GROUPS - step) % GROUPS)

        lower = (hg >= d).astype(jnp.int32)
        upper = (hg + d <= last).astype(jnp.int32)
        side_block(inner_side, jnp.where(hg < 2, upper, lower) == 1)
        side_block(1 - inner_side, jnp.where(hg < 2, lower, upper) == 1)
        return carry

    lax.fori_loop(0, 3, token_step, 0)
    wo_top.relay()
    wo_low.relay()
    dy_all.relay()
    up_sends = [
        wires.send(
            r["wup"].at[:, pl.ds(pl.multiple_of(flip(w, k) * FS, FS), FS)],
            wu_s.at[w],
            wdev(flip(w, k)),
        )
        for k in (2, 3, 1)
    ]
    for b in range(GROUPS):
        kv_copy(b).wait_recv()
        wires.later(kv_copy(b))

    doc_ends = []
    for i in range(n_doc):
        doc_ends.append(r["doc"][0, i] + (doc_ends[-1] if i else 0))

    def doc_ids(positions):
        return sum([(positions >= end).astype(jnp.int32) for end in doc_ends])

    key_at = lax.broadcasted_iota(jnp.int32, (1, half), 1)
    key_block = sum([(key_at >= i * R).astype(jnp.int32) for i in range(1, GROUPS)])
    key_base = key_at + key_block * (R * (G - 1))
    key_ids = [doc_ids(key_base + px * R), doc_ids(key_base + (1 - px) * R)]
    KT, VT = (0, 0, LANES), (2 * LANES, 2 * LANES, LANES)
    e_s, li_s, oa_s, os_s, or_s = r["e_s"], r["li_s"], r["oa_s"], r["os_s"], r["or_s"]

    class Turn:
        def __init__(self, source, target):
            self.source, self.target = source, target
            self.first_at = wires.take(GROUPS)
            for i in (1, 2, 3):
                wires.later(self.message((hg + i) % GROUPS))

        def message(self, block):
            index = self.first_at + (block - hg + GROUPS) % GROUPS
            return wires.copy(index, self.source.at[block], self.target.at[hg], zdev(block))

        def arrived(self, block):
            index = self.first_at + (hg - block + GROUPS) % GROUPS
            wires.copy(index, self.target.at[block], self.target.at[block], left).wait_recv()

    o_turn = Turn(os_s, or_s)

    def attend(step, carry):
        block = by_distance(step)
        row_at = (block * G + px) * R + lax.broadcasted_iota(jnp.int32, (R, 1), 0)
        row_ids = doc_ids(row_at)
        outs = []
        for h in range(3):
            queries = q_s[h, block]
            scores = [
                jnp.where(
                    row_ids == key_ids[side],
                    dot_nt(queries, kv_s[side, :, KT[h] : KT[h] + LANES]),
                    NEG_START,
                )
                for side in (0, 1)
            ]
            top = jnp.maximum(
                jnp.max(scores[0], axis=-1, keepdims=True), jnp.max(scores[1], axis=-1, keepdims=True)
            )
            weights = [jnp.exp(one - top) for one in scores]
            total = jnp.sum(weights[0], axis=-1, keepdims=True) + jnp.sum(
                weights[1], axis=-1, keepdims=True
            )
            inverse = 1.0 / total
            mixed = jnp.zeros((R, LANES), F32)
            for side in (0, 1):
                rounded = weights[side].astype(BF)
                e_s[h, block, side] = rounded
                mixed += dot_nn(rounded, kv_s[side, :, VT[h] : VT[h] + LANES])
            li_s[h, block] = jnp.broadcast_to(inverse, (R, LANES))
            outs.append(mixed * inverse)
        first = jnp.where(low_half, outs[0], outs[1])
        final = jnp.where(low_half, 0.0, outs[2])
        oa_s[block, :, :LANES] = first
        oa_s[block, :, LANES:] = final
        os_s[block, :, :LANES] = first.astype(BF)
        os_s[block, :, LANES:] = final.astype(BF)

        @pl.when(step < last)
        def _():
            o_turn.message(block).start()

        return carry

    lax.fori_loop(0, GROUPS, attend, 0)
    or_s[hg] = os_s[hg]
    wo_top.finish()
    wo_low.finish()
    for i in (1, 2, 3):
        o_turn.arrived((hg + i) % GROUPS)

    middle = x_s[hg].astype(F32) + out_b
    for i in range(GROUPS):
        middle += dot_nn(or_s[i], wo_s[i])
    x1_s, h2_s, g_s, da_s = r["x1_s"], r["h2_s"], r["g_s"], r["da_s"]
    x1_s[...] = middle
    unit_two, scale_two = unit_rows(middle)
    h2_s[w] = (unit_two * gain_two + bias_two).astype(BF)
    h2_all = Gather(lambda i: h2_s.at[i])
    dy_all.finish()
    wu_in.wait()
    wd_in.wait()
    for one in up_sends:
        one.wait_recv()
    ph_s, hr_s, wd_s = r["ph_s"], r["hr_s"], r["wd_s"]
    ph = Reduce(lambda i: ph_s.at[i], hr_s)

    def up_and_back(slot):
        hidden = dot_nn(h2_s[slot], wu_s[...].reshape(D, FS)) + up_b
        square = hidden * hidden
        inner = math.sqrt(2.0 / math.pi) * (hidden + 0.044715 * (square * hidden))
        bent = jnp.tanh(inner)
        g_s[slot] = (0.5 * hidden * (1.0 + bent)).astype(BF)
        slope = 0.5 * (1.0 + bent) + 0.5 * hidden * (1.0 - bent * bent) * (
            math.sqrt(2.0 / math.pi) * (1.0 + 3.0 * 0.044715 * square)
        )
        grad_active = dot_nt(dy_s[slot], wd_s[...])
        grad_hidden = (grad_active * slope).astype(BF)
        da_s[slot] = grad_hidden
        ph_s[slot] = dot_nt(grad_hidden, wu_s[...].reshape(D, FS)).astype(BF)

    on_copy = wires.copy(wires.take(), h2_s.at[w2], h2_s.at[w2], sib)

    def mlp_step(j, carry):
        @pl.when(j == 1)
        def _():
            h2_all.to_sib.wait_recv()

        @pl.when(j == 2)
        def _():
            h2_all.to_across.wait_recv()
            on_copy.start()

        @pl.when(j == 3)
        def _():
            on_copy.wait_recv()

        up_and_back(flip(w, j))

        @pl.when(j == 1)
        def _():
            ph.b.start()

        @pl.when(j == 3)
        def _():
            ph.a.start()

        return carry

    lax.fori_loop(0, GROUPS, mlp_step, 0)
    wires.later(on_copy)

    gus_s, gds_s, py_s = r["gus_s"], r["gds_s"], r["py_s"]

    def up_grad(i, carry):
        at = pl.ds(pl.multiple_of(i * 2 * S, 2 * S), 2 * S)
        gus_s[pl.ds(2 * i, 2)] = (
            dot_tn(h2_s[:, :, at].reshape(half, 2 * S), da_s[...].reshape(half, FS))
            .astype(BF)
            .reshape(2, 2, S // 2, FS)
        )
        return carry

    def down_grad(i, carry):
        at = pl.ds(pl.multiple_of(i * 256, 256), 256)
        gds_s[at, :] = dot_tn(
            g_s[:, :, at].reshape(half, 256), dy_s[...].reshape(half, D)
        ).astype(BF)
        return carry

    def y_part(j, carry):
        py_s[j] = dot_nn(g_s[j], wd_s[...]).astype(BF)
        return carry

    class Spread:
        def __init__(self, part, recv, slot, to_x):
            self.sum = LineSum(part, recv)
            self.gather = LineGather(slot, to_x)

        def turn(self):
            def put(total):
                self.gather.slot(hg)[...] = total.astype(BF)

            self.sum.final(put)
            self.gather.start()

    class Share:
        def __init__(self, rows):
            self.rows = rows
            self.at = wires.take(n_ctx)
            for i in range(1, n_ctx):
                wires.later(self.message(i))

        def message(self, i):
            return wires.copy(self.at + i, self.rows.at[c], self.rows.at[c], ctx_peers[i - 1])

        def start(self):
            for i in range(1, n_ctx):
                self.message(i).start()

        def total(self):
            for i in range(1, n_ctx):
                wires.copy(self.at + i, self.rows.at[c], self.rows.at[c], left).wait_recv()
            return sum([self.rows[i] for i in range(n_ctx)])

    n = S // 2
    n_down = FS // 8
    quarter = n // GROUPS
    gd_s, gu_s, up_f = r["gdown"], r["gu_s"], r["gup"]
    mine = pl.ds(pl.multiple_of(px * n, 8), n)
    theirs = pl.ds(pl.multiple_of((1 - px) * n, 8), n)

    def down_rows(b):
        return pl.ds(pl.multiple_of(px * (4 * n_down) + b * n_down, 8), n_down)

    down_here = pl.ds(pl.multiple_of(px * (4 * n_down), 8), 4 * n_down)
    down_there = pl.ds(pl.multiple_of((1 - px) * (4 * n_down), 8), 4 * n_down)
    py = Reduce(lambda i: py_s.at[i], r["yr_s"])
    up_x = wires.plan(gus_s.at[:, 1 - px], r["gux_s"], xdev)
    up_y_first = wires.take(GROUPS)

    def up_y(k, out):
        to = flip(w, k)
        return wires.copy(
            up_y_first + k, gus_s.at[to, px], gu_s.at[w if out else to], wdev(to)
        )

    for k in (1, 2, 3):
        wires.later(up_y(k, True))
    up = Spread(lambda b: gu_s.at[b], r["gul_s"], lambda b: up_f.at[b, px], True)
    down_x = wires.plan(gds_s.at[down_there], r["gdx_s"], xdev)
    down = Spread(
        lambda b: gds_s.at[down_rows(b)], r["gdl_s"], lambda b: gd_s.at[down_rows(b)], True
    )
    dz_s, dos_s, dor_s = r["dz_s"], r["dos_s"], r["dor_s"]
    do_turn = Turn(dos_s, dor_s)
    early, early_x_s, early_z_s = r["early_s"], r["early_x_s"], r["early_z_s"]
    late = r["late_s"]
    early_x = wires.plan(early, early_x_s, xdev)
    early_first = wires.take(GROUPS)

    def early_z(i):
        return wires.copy(
            early_first + i, early_z_s.at[hg], early_z_s.at[hg], zdev((hg + i) % GROUPS)
        )

    for i in (1, 2, 3):
        wires.later(early_z(i))
    late_all = Share(late)
    gos_s, gor_s = r["gos_s"], r["gor_s"]
    go_s, gox_s, gop_s, gon_s, go_f = r["go_s"], r["gox_s"], r["gop_s"], r["gon_s"], r["gout"]
    go = Reduce(lambda i: gos_s.at[i], gor_s)
    go_x = wires.plan(go_s.at[theirs], gox_s, xdev)
    go_turn = Turn(gop_s, gon_s)
    go_first = wires.take(GROUPS)

    def go_back(i):
        piece = go_f.at[px, hg]
        return wires.copy(go_first + i, piece, piece, zdev((hg + i) % GROUPS))

    for i in (1, 2, 3):
        wires.later(go_back(i))
    go_x2 = wires.plan(go_f.at[px], go_f.at[px], xdev)
    kvt_s, kvr_s, ph1_s, gqs_s = r["kvt_s"], r["kvr_s"], r["ph1_s"], r["gqs_s"]
    kv_back = wires.plan(kvt_s, kvr_s, xdev)
    h1_sum = LineSum(lambda b: ph1_s.at[b], r["h1r_s"])
    gq = Reduce(lambda i: gqs_s.at[pl.ds(pl.multiple_of(i * S, S), S)], r["gqr_s"])
    gqc_s, gqx_s, gqkv = r["gqc_s"], r["gqx_s"], r["gqkv"]
    qx = wires.plan(gqc_s.at[theirs], gqx_s, xdev)
    q_line = LineGather(lambda b: gqkv.at[b, mine], True)
    vecs, vecr = r["vecs_s"], r["vecr_s"]
    vec_first = wires.take(GROUPS)

    def vec_send(k):
        return wires.copy(
            vec_first + k, vecs.at[flip(w, k)], vecr.at[k - 1], wdev(flip(w, k))
        )

    for k in (1, 2, 3):
        wires.later(vec_send(k))
    dkv_s, dq_s, dqkv_s, df_s = r["dkv_s"], r["dq_s"], r["dqkv_s"], r["df_s"]

    steps = {}

    def step_of(name):
        def keep(body):
            steps[name] = body
            return body

        return keep

    @step_of("up_xin")
    def _():
        up_x.wait_recv()
        here = gus_s.at[:, px]
        here[...] = sum_bf(here[...], r["gux_s"][...])
        gu_s[w] = gus_s[w, px]
        for k in (2, 3, 1):
            up_y(k, True).start()

    @step_of("up_in")
    def _():
        for k in (1, 2, 3):
            up_y(k, False).wait_recv()
        up.sum.ends()

    @step_of("D_in")
    def _():
        down_x.wait_recv()
        gds_s[down_here, :] = sum_bf(gds_s[down_here, :], r["gdx_s"][...])
        down.sum.ends()

    steps["D_xout"] = down_x.start
    for name, chain in (("U", up), ("D", down)):
        steps[name + "2a"] = partial(chain.sum.second, (0,))
        steps[name + "2b"] = partial(chain.sum.second, (1,))
        steps[name + "3"] = chain.sum.third
        steps[name + "_turn"] = chain.turn
    for name, line in (("U", up.gather), ("D", down.gather), ("q", q_line)):
        steps[name + "_i1"] = partial(line.inner, 1)
        steps[name + "_o1"] = partial(line.outer, 1)
        steps[name + "_i2"] = partial(line.inner, 2)
        steps[name + "_i3"] = partial(line.inner, 3)
    steps["H2a"] = partial(h1_sum.second, (0,))
    steps["H2b"] = partial(h1_sum.second, (1,))
    steps["H3"] = h1_sum.third
    steps["h1_e2"] = partial(h1_sum.ends, (2,))
    steps["go_combine"] = go.combine
    steps["py_combine"] = py.combine
    steps["gq_comb"] = gq.combine

    @step_of("go_out")
    def _():
        go_s[...] = go.finish().astype(BF)
        go_x.start()

    @step_of("go_in")
    def _():
        go_x.wait_recv()
        go_half = go_s[mine, :].astype(F32) + gox_s[...].astype(F32)
        for b in range(GROUPS):
            gop_s[b] = go_half[b * quarter : (b + 1) * quarter].astype(BF)
        for i in (2, 1, 3):
            go_turn.message((hg + i) % GROUPS).start()

    @step_of("go_turn")
    def _():
        for i in (1, 2, 3):
            go_turn.arrived((hg + i) % GROUPS)
        go_total = gop_s[hg].astype(F32)
        for i in (1, 2, 3):
            go_total = go_total + gon_s[(hg + i) % GROUPS].astype(F32)
        go_f[px, hg] = go_total.astype(BF)
        for i in (2, 1, 3):
            go_back(i).start()

    @step_of("go_done")
    def _():
        for i in (1, 2, 3):
            go_back(i).wait_recv()
        go_x2.start()

    @step_of("go_fin")
    def _():
        go_x2.wait_recv()

    steps["early"] = early_x.start

    @step_of("early2")
    def _():
        early_x.wait_recv()
        early_z_s[hg] = early[...] + early_x_s[...]
        for i in (1, 2, 3):
            early_z(i).start()

    @step_of("kv_in")
    def _():
        kv_back.wait_recv()
        dqkv_s[:, 2 * LANES :] = sum_bf(dkv_s[0], kvr_s[...])

    @step_of("h1_part")
    def _():
        def h1_part(step, carry):
            block = by_distance(step)
            rows = pl.ds(pl.multiple_of(block * R, R), R)
            ph1_s[block] = dot_nt(dqkv_s[rows, :], wq_s[...]).astype(BF)
            h1_sum.ends_block(block)
            return carry

        lax.fori_loop(0, GROUPS, h1_part, 0)

    @step_of("qkv_grad")
    def _():
        def qkv_grad(i, carry):
            at = pl.ds(pl.multiple_of(i * 256, 256), 256)
            gqs_s[at, :] = dot_tn(h1_s[:, :, at].reshape(half, 256), dqkv_s[...]).astype(BF)
            return carry

        lax.fori_loop(0, D // 256, qkv_grad, 0)
        gq.start()
        late[c, :, 2 * D : 2 * D + 2 * LANES] = rows_sum(dqkv_s[:, : 2 * LANES].astype(F32))
        late[c, :, 2 * D + 2 * LANES :] = rows_sum(dqkv_s[:, 3 * LANES :].astype(F32))

    @step_of("gq_fin")
    def _():
        gqc_s[...] = gq.finish().astype(BF)
        qx.start()

    @step_of("q_start")
    def _():
        qx.wait_recv()
        gqkv[hg, mine, :] = sum_bf(gqc_s[mine, :], gqx_s[...])
        q_line.start()

    @step_of("h1_fin")
    def _():
        def keep_h1(total):
            df_s[...] = total

        h1_sum.final(keep_h1)
        grad_one = df_s[...]
        unit_one, scale_one = unit_rows(x_s[hg].astype(F32))
        grad_in = dz_s[...] + unit_rows_back(grad_one, unit_one, scale_one, gain_one)
        r["dx"][...] = grad_in.astype(BF)
        late[c, :, 0:D] = rows_sum(grad_one * unit_one)
        late[c, :, D : 2 * D] = rows_sum(grad_one)
        late_all.start()

    @step_of("layer_out")
    def _():
        r["y"][...] = (x1_s[...] + py.finish() + down_b).astype(BF)

    @step_of("small")
    def _():
        for i in (1, 2, 3):
            there = (hg + i) % GROUPS
            wires.copy(early_first + GROUPS - i, early_z_s.at[there], early_z_s.at[there], left).wait_recv()
        ones = sum([early_z_s[i] for i in range(GROUPS)])
        twos = late_all.total()
        bq_all, bv_all = [], []
        for g in range(GROUPS):
            group_sum = sum([late[g * G + i][:, 2 * D :] for i in range(G)])
            bq_all.append(group_sum[:, :S])
            v_end = pltpu.roll(group_sum[:, 2 * LANES : 3 * LANES], LANES // 2, 1)[:, : S - LANES]
            bv_all.append(jnp.concatenate([group_sum[:, 3 * LANES :], v_end], axis=1))
        vectors = [twos[:, 0:D], twos[:, D : 2 * D]] + [
            ones[:, i * D : (i + 1) * D] for i in range(4)
        ]
        for i in range(GROUPS):
            for j, one in enumerate(vectors):
                vecs[i, :, j * 256 : j * 256 + S] = one[:, i * S : (i + 1) * S]
            vecs[i, :, 6 * 256 : 6 * 256 + S] = bq_all[i]
            vecs[i, :, 7 * 256 : 7 * 256 + S] = bv_all[i]
        r["vec"][:, 8 * 256 :] = ones[:, 4 * D :]
        for k in (1, 2, 3):
            vec_send(k).start()

    carried = {}

    @step_of("up_grad")
    def _():
        lax.fori_loop(0, 2, up_grad, 0)
        up_x.start()

    steps["ph_combine"] = ph.combine

    @step_of("down_grad")
    def _():
        lax.fori_loop(0, FS // 256, down_grad, 0)

    @step_of("y_part")
    def _():
        lax.fori_loop(0, GROUPS, y_part, 0)
        py.start()

    @step_of("wait_ph")
    def _():
        carried["two"] = ph.finish()

    @step_of("ln2")
    def _():
        grad_two = carried["two"]
        unit_two, scale_two = unit_rows(x1_s[...])
        top = r["dy_s"][w].astype(F32)
        grad_middle = top + unit_rows_back(grad_two, unit_two, scale_two, gain_two)
        dz = grad_middle.astype(BF)
        dz_s[...] = grad_middle
        carried["dz"], carried["unit"], carried["top"] = dz, unit_two, top

        def out_back(step, carry):
            block = by_distance(step)
            dos_s[block] = dot_nt(dz, wo_s[block]).astype(BF)

            @pl.when(step < last)
            def _():
                do_turn.message(block).start()

            return carry

        lax.fori_loop(0, GROUPS, out_back, 0)

    @step_of("sums")
    def _():
        dor_s[hg] = dos_s[hg]
        early[:, 0:D] = rows_sum(carried["dz"].astype(F32))
        early[:, D : 2 * D] = rows_sum(carried["two"] * carried["unit"])
        early[:, 2 * D : 3 * D] = rows_sum(carried["two"])
        early[:, 3 * D : 4 * D] = rows_sum(carried["top"])
        early[:, 4 * D :] = rows_sum(da_s[...].reshape(half, FS).astype(F32))

    @step_of("out_grad")
    def _():
        for i in range(GROUPS):
            piece = dot_tn(or_s[i], carried["dz"])
            gos_s[i, 0:LANES, :] = piece[0:LANES, :].astype(BF)
            gos_s[i, LANES:S, :] = piece[S:, :].astype(BF)
        go.start()
        dkv_s[...] = jnp.zeros(dkv_s.shape, F32)

    def back_block(block, side):
        outs = dor_s[block].astype(F32)
        kept = oa_s[block]
        grads_q = []
        for h in range(3):
            tile = 0 if h < 2 else LANES
            keep = low_half if h == 0 else jnp.logical_not(low_half)
            scaled = jnp.where(keep, outs[:, tile : tile + LANES], 0.0) * li_s[h, block]
            delta = jnp.sum(scaled * kept[:, tile : tile + LANES], axis=-1, keepdims=True)
            rounded = scaled.astype(BF)
            grad_prob = dot_nt(rounded, kv_s[side, :, VT[h] : VT[h] + LANES])
            weights = e_s[h, block, side]
            grad_score = (weights.astype(F32) * (grad_prob - delta)).astype(BF)
            grads_q.append(dot_nn(grad_score, kv_s[side, :, KT[h] : KT[h] + LANES]))
            dkv_s[side, :, KT[h] : KT[h] + LANES] += dot_tn(grad_score, q_s[h, block])
            dkv_s[side, :, VT[h] : VT[h] + LANES] += dot_tn(weights, rounded)
        first = jnp.where(low_half, grads_q[0], grads_q[1]) * 0.125
        final = jnp.where(low_half, grads_q[2], 0.0) * 0.125
        if side == 1:
            dq_s[block, :, :LANES] = first
            dq_s[block, :, LANES:] = final
        else:
            rows = pl.ds(pl.multiple_of(block * R, R), R)
            dqkv_s[rows, :LANES] = (dq_s[block, :, :LANES] + first).astype(BF)
            dqkv_s[rows, LANES : 2 * LANES] = (dq_s[block, :, LANES:] + final).astype(BF)

    def nearest(step):
        return by_distance(last - step)

    @step_of("kv_out")
    def _():
        kvt_s[...] = dkv_s[1].astype(BF)
        kv_back.start()

    @step_of("fin")
    def _():
        for k in (1, 2, 3):
            vec_send(k).wait_recv()
        r["vec"][:, 0 : 8 * 256] = vecs[w] + vecr[0] + vecr[1] + vecr[2]
        down.gather.done()
        up.gather.done()
        q_line.done()

    def attention_back(side, plans):
        def body(step, carry):
            block = nearest(step)
            if side == 1:

                @pl.when(step > 0)
                def _():
                    do_turn.arrived(block)

            back_block(block, side)
            for k, names in enumerate(plans):
                if names:

                    @pl.when(step == k)
                    def _():
                        for name in names:
                            steps[name]()

            return carry

        lax.fori_loop(0, GROUPS, body, 0)

    at = 0
    order = ORDER
    while at < len(order):
        name = order[at]
        at += 1
        if name in ("bo0", "bw0"):
            plans, kind = [[]], name[:2]
            while at < len(order) and (order[at][:2] == kind or len(plans) < GROUPS):
                if order[at][:2] == kind:
                    plans.append([])
                else:
                    plans[-1].append(order[at])
                at += 1
            attention_back(1 if kind == "bo" else 0, plans)
        else:
            steps[name]()
    wires.drain()


def widen_kernel(S, names, *refs):
    r = dict(zip(names, refs, strict=True))
    n = S // 2
    started = []

    def send(source, target):
        one = pltpu.make_async_copy(source, target, r["sems"].at[len(started)])
        one.start()
        started.append(one)

    def put(name, at, value):
        r[name + "_b"][at] = value
        send(r[name + "_b"].at[at], r[name + "_o"].at[at])

    send(r["y"], r["y_o"])
    send(r["dx"], r["dx_o"])
    FS = r["up"].shape[3]
    for i in range(GROUPS):
        rows = slice(i * S, (i + 1) * S)
        put("down", (rows, slice(None)), r["down"][rows, :].astype(F32))
        for j in (0, 1):
            at = (slice(j * n, (j + 1) * n), slice(i * FS, (i + 1) * FS))
            put("up", at, r["up"][i, j].astype(F32))
    put("out", (slice(None),), r["out"][...].astype(F32))

    def heads(pieces):
        return jnp.concatenate(
            [r["qkv"][i, :, a:b].astype(F32) for i in range(GROUPS) for a, b in pieces], axis=1
        )

    put("q", (slice(None),), heads([(0, S)]))
    put("k", (slice(None),), heads([(2 * LANES, 2 * LANES + S)]))
    put("v", (slice(None),), heads([(4 * LANES, 5 * LANES), (2 * LANES + S, 4 * LANES)]))
    at = 0
    for i in range(9):
        one = r["vec%d" % i]
        one[...] = r["vec"][0, at : at + one.shape[0]]
        at += max(one.shape[0], 256)
    for one in started:
        one.wait()


SEMS = 140


def fast_device(mesh_sizes, *arrays):
    (tokens, doc_lengths, out_grad, norm1_gain, norm1_bias, w_query, b_query, w_key, w_value,
     b_value, w_out, b_out, norm2_gain, norm2_bias, w_up, b_up, w_down, b_down) = arrays
    n_ctx, n_wsh = mesh_sizes
    R, D = tokens.shape[1], tokens.shape[2]
    S, FS, n_doc = D // GROUPS, w_down.shape[0], doc_lengths.shape[1]
    half, QW = GROUPS * R, 5 * LANES

    smem = pl.BlockSpec(memory_space=pltpu.SMEM)
    vmem = pl.BlockSpec(memory_space=pltpu.VMEM)
    anywhere = pl.BlockSpec(memory_space=pl.ANY)
    inputs = [
        ("doc", doc_lengths, smem),
        ("tok", tokens[0], anywhere),
        ("dy", out_grad[0], anywhere),
        ("wq", w_query, anywhere),
        ("wk", w_key, anywhere),
        ("wv", w_value, anywhere),
        ("wout", w_out, anywhere),
        ("wup", w_up, anywhere),
        ("wdown", w_down, anywhere),
        ("n1g", norm1_gain, vmem),
        ("n1b", norm1_bias, vmem),
        ("bq", b_query, vmem),
        ("bv", b_value, vmem),
        ("bo", b_out, vmem),
        ("n2g", norm2_gain, vmem),
        ("n2b", norm2_bias, vmem),
        ("bd", b_down, vmem),
        ("bup", b_up, vmem),
    ]
    n_up = S // 2
    outputs = [
        ("y", (R, D), BF),
        ("dx", (R, D), BF),
        ("gdown", (FS, D), BF),
        ("gup", (GROUPS, 2, n_up, FS), BF),
        ("gout", (2, GROUPS, S // 8, D), BF),
        ("gqkv", (GROUPS, S, QW), BF),
        ("vec", (1, 8 * 256 + FS), F32),
    ]
    scratch = [
        ("x_s", (GROUPS, R, D), BF),
        ("h1_s", (GROUPS, R, D), BF),
        ("win_s", (3, S, D), BF),
        ("wq_s", (D, QW), BF),
        ("par_s", (GROUPS, 8, 2 * LANES), F32),
        ("q_s", (3, GROUPS, R, LANES), BF),
        ("kv_s", (2, half, 3 * LANES), BF),
        ("e_s", (3, GROUPS, 2, R, half), BF),
        ("li_s", (3, GROUPS, R, LANES), F32),
        ("oa_s", (GROUPS, R, 2 * LANES), F32),
        ("os_s", (GROUPS, R, 2 * LANES), BF),
        ("or_s", (GROUPS, R, 2 * LANES), BF),
        ("wo_s", (GROUPS, 2 * LANES, D), BF),
        ("wu_s", (GROUPS, S, FS), BF),
        ("wd_s", (FS, D), BF),
        ("dy_s", (GROUPS, R, D), BF),
        ("x1_s", (R, D), F32),
        ("h2_s", (GROUPS, R, D), BF),
        ("g_s", (GROUPS, R, FS), BF),
        ("da_s", (GROUPS, R, FS), BF),
        ("ph_s", (GROUPS, R, D), BF),
        ("hr_s", (4, R, D), BF),
        ("py_s", (GROUPS, R, D), BF),
        ("yr_s", (4, R, D), BF),
        ("dz_s", (R, D), F32),
        ("dos_s", (GROUPS, R, 2 * LANES), BF),
        ("dor_s", (GROUPS, R, 2 * LANES), BF),
        ("dkv_s", (2, half, 3 * LANES), F32),
        ("kvt_s", (half, 3 * LANES), BF),
        ("kvr_s", (half, 3 * LANES), BF),
        ("dq_s", (GROUPS, R, 2 * LANES), F32),
        ("dqkv_s", (half, QW), BF),
        ("ph1_s", (GROUPS, R, D), BF),
        ("h1r_s", (6, R, D), BF),
        ("df_s", (R, D), F32),
        ("gds_s", (FS, D), BF),
        ("gdx_s", (FS // 2, D), BF),
        ("gdl_s", (6, FS // 8, D), BF),
        ("gus_s", (GROUPS, 2, S // 2, FS), BF),
        ("gu_s", (GROUPS, n_up, FS), BF),
        ("gux_s", (GROUPS, S // 2, FS), BF),
        ("gul_s", (6, n_up, FS), BF),
        ("go_s", (S, D), BF),
        ("gox_s", (S // 2, D), BF),
        ("gop_s", (GROUPS, S // 8, D), BF),
        ("gon_s", (GROUPS, S // 8, D), BF),
        ("gos_s", (GROUPS, S, D), BF),
        ("gor_s", (4, S, D), BF),
        ("gqs_s", (D, QW), BF),
        ("gqr_s", (4, S, QW), BF),
        ("gqc_s", (S, QW), BF),
        ("gqx_s", (S // 2, QW), BF),
        ("early_s", (1, 4 * D + FS), F32),
        ("early_x_s", (1, 4 * D + FS), F32),
        ("early_z_s", (GROUPS, 1, 4 * D + FS), F32),
        ("late_s", (n_ctx, 1, 2 * D + 4 * LANES), F32),
        ("vecs_s", (GROUPS, 1, 8 * 256), F32),
        ("vecr_s", (3, 1, 8 * 256), F32),
    ]
    sems = [("send_sems", SEMS), ("recv_sems", SEMS), ("local_sems", 9)]
    names = [one[0] for one in inputs + outputs + scratch + sems]
    y, dx, g_down, g_up, g_out, g_qkv, vec = pl.pallas_call(
        partial(layer_kernel, (n_ctx, n_doc, R, D, S, FS), names),
        out_shape=[pltpu.VMEM(shape, dtype) for name, shape, dtype in outputs],
        in_specs=[spec for name, value, spec in inputs],
        out_specs=[vmem] * len(outputs),
        scratch_shapes=[pltpu.VMEM(shape, dtype) for name, shape, dtype in scratch]
        + [pltpu.SemaphoreType.DMA((count,)) for name, count in sems],
        compiler_params=pltpu.CompilerParams(
            collective_id=0, has_side_effects=True, vmem_limit_bytes=62000000
        ),
        name="layer",
    )(*[value for name, value, spec in inputs])

    big = [
        ("y", (R, D), BF),
        ("dx", (R, D), BF),
        ("down", (FS, D), F32),
        ("up", (S, GROUPS * FS), F32),
        ("out", (2, GROUPS, S // 8, D), F32),
        ("q", (S, D), F32),
        ("k", (S, D), F32),
        ("v", (S, D), F32),
    ]
    vectors = [("vec%d" % i, size) for i, size in enumerate([S] * 8 + [FS])]
    names = ["y", "dx", "down", "up", "out", "qkv", "vec"]
    names += [name + "_o" for name, shape, dtype in big] + [name for name, size in vectors]
    names += [name + "_b" for name, shape, dtype in big[2:]] + ["sems"]
    wide = pl.pallas_call(
        partial(widen_kernel, S, names),
        in_specs=[vmem] * 7,
        out_specs=[anywhere] * len(big) + [vmem] * len(vectors),
        out_shape=[jax.ShapeDtypeStruct(shape, dtype) for name, shape, dtype in big]
        + [jax.ShapeDtypeStruct((size,), F32) for name, size in vectors],
        scratch_shapes=[pltpu.VMEM(shape, dtype) for name, shape, dtype in big[2:]]
        + [pltpu.SemaphoreType.DMA((18,))],
        compiler_params=pltpu.CompilerParams(vmem_limit_bytes=24000000),
        name="widen",
    )(y, dx, g_down, g_up, g_out, g_qkv, vec)
    y, dx, down, up, out, q, k, v, n1g, n1b, bo, n2g, n2b, bd, bq, bv, bup = wide
    return (
        y[None], dx[None], n1g, n1b, q, bq, k, v, bv, out.reshape(S, D), bo, n2g, n2b, up, bup, down, bd,
    )


def solution(mesh):
    in_specs = (
        P("wsh", "ctx", None),
        P("wsh", None),
        P("wsh", "ctx", None),
        P("wsh"),
        P("wsh"),
        P("wsh", None),
        P("wsh"),
        P("wsh", None),
        P("wsh", None),
        P("wsh"),
        P("wsh", None),
        P("wsh"),
        P("wsh"),
        P("wsh"),
        P("wsh", None),
        P("wsh"),
        P("wsh", None),
        P("wsh"),
    )
    out_specs = (
        P("wsh", "ctx", None),
        P("wsh", "ctx", None),
        P("wsh"),
        P("wsh"),
        P("wsh", None),
        P("wsh"),
        P("wsh", None),
        P("wsh", None),
        P("wsh"),
        P("wsh", None),
        P("wsh"),
        P("wsh"),
        P("wsh"),
        P("wsh", None),
        P("wsh"),
        P("wsh", None),
        P("wsh"),
    )
    sizes = (mesh.shape["ctx"], mesh.shape["wsh"])
    body = partial(fast_device, sizes) if sizes == (2 * GROUPS, GROUPS) else per_device
    return jax.shard_map(
        body, mesh=mesh, in_specs=in_specs, out_specs=out_specs, check_vma=False
    )
```

```python
from functools import partial
import math

import jax
import jax.numpy as jnp
from jax import lax
from jax.experimental import pallas as pl
from jax.experimental.pallas import tpu as pltpu
from jax.sharding import PartitionSpec as P

HEADS = 12


EPS = 1e-06
NEG_START = -1e30


def norm_rows(inputs, norm_gain, norm_bias):
    row_mean = jnp.mean(inputs, axis=-1, keepdims=True)
    centred = inputs - row_mean
    variance = jnp.mean(centred * centred, axis=-1, keepdims=True)
    return centred * lax.rsqrt(variance + EPS) * norm_gain + norm_bias


def doc_of(positions, doc_ends):
    return jnp.sum((positions[:, None] >= doc_ends[None, :]).astype(jnp.int32), axis=1)


def dot_plain(left, right):
    return jnp.dot(left, right, preferred_element_type=jnp.float32)


def dot_left(left, right):
    return lax.dot_general(
        left, right, (((0,), (0,)), ((), ())), preferred_element_type=jnp.float32
    )


def dot_right(left, right):
    return lax.dot_general(
        left, right, (((1,), (1,)), ((), ())), preferred_element_type=jnp.float32
    )


def masked_scores(query_heads, key_heads, query_ids, key_ids, score_scale):
    raw_scores = (
        jnp.einsum("qhd,khd->hqk", query_heads, key_heads, preferred_element_type=jnp.float32)
        * score_scale
    )
    same_doc = (query_ids[:, None] == key_ids[None, :])[None]
    return jnp.where(same_doc, raw_scores, -jnp.inf)


def per_device(
    tokens,
    doc_lengths,
    out_grad,
    norm1_gain,
    norm1_bias,
    w_query,
    b_query,
    w_key,
    w_value,
    b_value,
    w_out,
    b_out,
    norm2_gain,
    norm2_bias,
    w_up,
    b_up,
    w_down,
    b_down,
):
    (
        gain_one,
        bias_one,
        query_w,
        query_b,
        key_w,
        value_w,
        value_b,
        out_w,
        out_b,
        gain_two,
        bias_two,
        up_w,
        up_b,
        down_w,
        down_b,
    ) = (
        lax.all_gather(norm1_gain, "wsh", axis=0, tiled=True),
        lax.all_gather(norm1_bias, "wsh", axis=0, tiled=True),
        lax.all_gather(w_query, "wsh", axis=0, tiled=True),
        lax.all_gather(b_query, "wsh", axis=0, tiled=True),
        lax.all_gather(w_key, "wsh", axis=0, tiled=True),
        lax.all_gather(w_value, "wsh", axis=0, tiled=True),
        lax.all_gather(b_value, "wsh", axis=0, tiled=True),
        lax.all_gather(w_out, "wsh", axis=0, tiled=True),
        lax.all_gather(b_out, "wsh", axis=0, tiled=True),
        lax.all_gather(norm2_gain, "wsh", axis=0, tiled=True),
        lax.all_gather(norm2_bias, "wsh", axis=0, tiled=True),
        lax.all_gather(w_up, "wsh", axis=0, tiled=True),
        lax.all_gather(b_up, "wsh", axis=0, tiled=True),
        lax.all_gather(w_down, "wsh", axis=0, tiled=True),
        lax.all_gather(b_down, "wsh", axis=0, tiled=True),
    )
    row_count = tokens.shape[1]
    model_width = tokens.shape[2]
    head_dim = model_width // HEADS
    score_scale = head_dim ** (-0.5)
    first_gain = gain_one.astype(jnp.float32)
    first_bias = bias_one.astype(jnp.float32)
    second_gain = gain_two.astype(jnp.float32)
    second_bias = bias_two.astype(jnp.float32)
    inputs = tokens[0].astype(jnp.float32)
    doc_ends = jnp.cumsum(doc_lengths[0])
    own_ids = doc_of(
        lax.axis_index("ctx") * row_count + jnp.arange(row_count, dtype=jnp.int32), doc_ends
    )
    normed_one = norm_rows(inputs, first_gain, first_bias).astype(jnp.bfloat16)
    queries = (dot_plain(normed_one, query_w) + query_b.astype(jnp.float32)).astype(jnp.bfloat16)
    key_rows = dot_plain(normed_one, key_w).astype(jnp.bfloat16)
    values = (dot_plain(normed_one, value_w) + value_b.astype(jnp.float32)).astype(jnp.bfloat16)
    key_all, value_all = (
        lax.all_gather(key_rows, "ctx", axis=0, tiled=True),
        lax.all_gather(values, "ctx", axis=0, tiled=True),
    )
    total_rows = key_all.shape[0]
    key_block = math.gcd(total_rows, 2048)
    block_count = total_rows // key_block
    key_stack = key_all.reshape(block_count, key_block, HEADS, head_dim)
    value_stack = value_all.reshape(block_count, key_block, HEADS, head_dim)
    id_stack = doc_of(jnp.arange(total_rows, dtype=jnp.int32), doc_ends).reshape(
        block_count, key_block
    )
    query_heads = queries.reshape(row_count, HEADS, head_dim)

    def lse_step(running, block_in):
        run_max, run_sum = running
        key_heads, key_ids = block_in
        scores = masked_scores(query_heads, key_heads, own_ids, key_ids, score_scale)
        new_max = jnp.maximum(run_max, jnp.max(scores, axis=-1))
        new_sum = run_sum * jnp.exp(run_max - new_max) + jnp.sum(
            jnp.exp(scores - new_max[:, :, None]), axis=-1
        )
        return ((new_max, new_sum), None)

    start_max = jnp.full((HEADS, row_count), NEG_START, jnp.float32)
    (final_max, final_sum), unused = lax.scan(
        lse_step, (start_max, jnp.zeros_like(start_max)), (key_stack, id_stack)
    )
    log_total = final_max + jnp.log(final_sum)

    def out_step(running, block_in):
        key_heads, value_heads, key_ids = block_in
        scores = masked_scores(query_heads, key_heads, own_ids, key_ids, score_scale)
        attn_prob = jnp.exp(scores - log_total[:, :, None]).astype(jnp.bfloat16)
        return (
            running
            + jnp.einsum(
                "hqk,khd->qhd", attn_prob, value_heads, preferred_element_type=jnp.float32
            ),
            None,
        )

    attn_sum, unused = lax.scan(
        out_step,
        jnp.zeros((row_count, HEADS, head_dim), jnp.float32),
        (key_stack, value_stack, id_stack),
    )
    attended = attn_sum.reshape(row_count, model_width).astype(jnp.bfloat16)
    middle = inputs + dot_plain(attended, out_w) + out_b.astype(jnp.float32)
    normed_two = norm_rows(middle, second_gain, second_bias).astype(jnp.bfloat16)
    hidden = dot_plain(normed_two, up_w) + up_b.astype(jnp.float32)
    active = jax.nn.gelu(hidden, approximate=True).astype(jnp.bfloat16)
    output = middle + dot_plain(active, down_w) + down_b.astype(jnp.float32)
    top_grad = out_grad[0]
    top_float = top_grad.astype(jnp.float32)
    grad_down_w = dot_left(active, top_grad)
    grad_down_b = jnp.sum(top_float, axis=0)
    grad_active = dot_right(top_grad, down_w)
    unused, gelu_pull = jax.vjp(partial(jax.nn.gelu, approximate=True), hidden)
    grad_hidden = gelu_pull(grad_active)[0].astype(jnp.bfloat16)
    grad_up_w = dot_left(normed_two, grad_hidden)
    grad_up_b = jnp.sum(grad_hidden.astype(jnp.float32), axis=0)
    grad_normed_two = dot_right(grad_hidden, up_w)
    unused, second_pull = jax.vjp(norm_rows, middle, second_gain, second_bias)
    grad_middle, grad_gain_two, grad_bias_two = second_pull(grad_normed_two)
    grad_middle = grad_middle + top_float
    grad_branch = grad_middle.astype(jnp.bfloat16)
    grad_out_w = dot_left(attended, grad_branch)
    grad_out_b = jnp.sum(grad_branch.astype(jnp.float32), axis=0)
    grad_attended = dot_right(grad_branch, out_w).astype(jnp.bfloat16)
    grad_heads = grad_attended.reshape(row_count, HEADS, head_dim)
    row_delta = jnp.sum(grad_heads.astype(jnp.float32) * attn_sum, axis=-1)
    head_delta = row_delta.T
    query_start = jnp.zeros((row_count, HEADS, head_dim), jnp.float32)

    def full_step(grad_query, block_in):
        key_heads, value_heads, key_ids = block_in
        scores = masked_scores(query_heads, key_heads, own_ids, key_ids, score_scale)
        attn_prob = jnp.exp(scores - log_total[:, :, None])
        grad_prob = jnp.einsum(
            "qhd,khd->hqk", grad_heads, value_heads, preferred_element_type=jnp.float32
        )
        grad_score = (attn_prob * (grad_prob - head_delta[:, :, None])).astype(jnp.bfloat16)
        grad_query = grad_query + jnp.einsum(
            "hqk,khd->qhd", grad_score, key_heads, preferred_element_type=jnp.float32
        )
        grad_key = (
            jnp.einsum("hqk,qhd->khd", grad_score, query_heads, preferred_element_type=jnp.float32)
            * score_scale
        )
        grad_value = jnp.einsum(
            "hqk,qhd->khd",
            attn_prob.astype(jnp.bfloat16),
            grad_heads,
            preferred_element_type=jnp.float32,
        )
        return (
            grad_query,
            (grad_key.reshape(key_block, model_width), grad_value.reshape(key_block, model_width)),
        )

    grad_query, key_terms = lax.scan(full_step, query_start, (key_stack, value_stack, id_stack))
    key_grad, value_grad = (
        lax.psum_scatter(
            key_terms[0].reshape(total_rows, model_width), "ctx", scatter_dimension=0, tiled=True
        ),
        lax.psum_scatter(
            key_terms[1].reshape(total_rows, model_width), "ctx", scatter_dimension=0, tiled=True
        ),
    )
    grad_query_rows = (
        (grad_query * score_scale).reshape(row_count, model_width).astype(jnp.bfloat16)
    )
    grad_key_rows = key_grad.astype(jnp.bfloat16)
    grad_value_rows = value_grad.astype(jnp.bfloat16)
    grad_query_w = dot_left(normed_one, grad_query_rows)
    grad_query_b = jnp.sum(grad_query_rows.astype(jnp.float32), axis=0)
    grad_key_w = dot_left(normed_one, grad_key_rows)
    grad_value_w = dot_left(normed_one, grad_value_rows)
    grad_value_b = jnp.sum(grad_value_rows.astype(jnp.float32), axis=0)
    grad_normed_one = (
        dot_right(grad_query_rows, query_w)
        + dot_right(grad_key_rows, key_w)
        + dot_right(grad_value_rows, value_w)
    )
    unused, first_pull = jax.vjp(norm_rows, inputs, first_gain, first_bias)
    grad_inputs, grad_gain_one, grad_bias_one = first_pull(grad_normed_one)
    grad_inputs = grad_inputs + grad_middle
    (
        share_gain_one,
        share_bias_one,
        share_query_w,
        share_query_b,
        share_key_w,
        share_value_w,
        share_value_b,
        share_out_w,
        share_out_b,
        share_gain_two,
        share_bias_two,
        share_up_w,
        share_up_b,
        share_down_w,
        share_down_b,
    ) = (
        lax.psum_scatter(
            grad_gain_one.astype(jnp.bfloat16), "wsh", scatter_dimension=0, tiled=True
        ).astype(jnp.float32),
        lax.psum_scatter(
            grad_bias_one.astype(jnp.bfloat16), "wsh", scatter_dimension=0, tiled=True
        ).astype(jnp.float32),
        lax.psum_scatter(
            grad_query_w.astype(jnp.bfloat16), "wsh", scatter_dimension=0, tiled=True
        ).astype(jnp.float32),
        lax.psum_scatter(
            grad_query_b.astype(jnp.bfloat16), "wsh", scatter_dimension=0, tiled=True
        ).astype(jnp.float32),
        lax.psum_scatter(
            grad_key_w.astype(jnp.bfloat16), "wsh", scatter_dimension=0, tiled=True
        ).astype(jnp.float32),
        lax.psum_scatter(
            grad_value_w.astype(jnp.bfloat16), "wsh", scatter_dimension=0, tiled=True
        ).astype(jnp.float32),
        lax.psum_scatter(
            grad_value_b.astype(jnp.bfloat16), "wsh", scatter_dimension=0, tiled=True
        ).astype(jnp.float32),
        lax.psum_scatter(
            grad_out_w.astype(jnp.bfloat16), "wsh", scatter_dimension=0, tiled=True
        ).astype(jnp.float32),
        lax.psum_scatter(
            grad_out_b.astype(jnp.bfloat16), "wsh", scatter_dimension=0, tiled=True
        ).astype(jnp.float32),
        lax.psum_scatter(
            grad_gain_two.astype(jnp.bfloat16), "wsh", scatter_dimension=0, tiled=True
        ).astype(jnp.float32),
        lax.psum_scatter(
            grad_bias_two.astype(jnp.bfloat16), "wsh", scatter_dimension=0, tiled=True
        ).astype(jnp.float32),
        lax.psum_scatter(
            grad_up_w.astype(jnp.bfloat16), "wsh", scatter_dimension=0, tiled=True
        ).astype(jnp.float32),
        lax.psum_scatter(
            grad_up_b.astype(jnp.bfloat16), "wsh", scatter_dimension=0, tiled=True
        ).astype(jnp.float32),
        lax.psum_scatter(
            grad_down_w.astype(jnp.bfloat16), "wsh", scatter_dimension=0, tiled=True
        ).astype(jnp.float32),
        lax.psum_scatter(
            grad_down_b.astype(jnp.bfloat16), "wsh", scatter_dimension=0, tiled=True
        ).astype(jnp.float32),
    )
    totals = lax.psum(
        (
            share_gain_one,
            share_bias_one,
            share_query_w,
            share_query_b,
            share_key_w,
            share_value_w,
            share_value_b,
            share_out_w,
            share_out_b,
            share_gain_two,
            share_bias_two,
            share_up_w,
            share_up_b,
            share_down_w,
            share_down_b,
        ),
        "ctx",
    )
    return (
        output.astype(jnp.bfloat16)[None],
        grad_inputs.astype(jnp.bfloat16)[None],
        totals[0],
        totals[1],
        totals[2],
        totals[3],
        totals[4],
        totals[5],
        totals[6],
        totals[7],
        totals[8],
        totals[9],
        totals[10],
        totals[11],
        totals[12],
        totals[13],
        totals[14],
    )


MESH = pl.DeviceIdType.MESH
F32 = jnp.float32
BF = jnp.bfloat16
GROUPS = 4
LANES = 128


def flip(value, mask):
    return ((value // 2 + mask // 2) % 2) * 2 + (value + mask) % 2


def dot_nn(left, right):
    return lax.dot_general(left, right, (((1,), (0,)), ((), ())), preferred_element_type=F32)


def dot_nt(left, right):
    return lax.dot_general(left, right, (((1,), (1,)), ((), ())), preferred_element_type=F32)


def dot_tn(left, right):
    return lax.dot_general(left, right, (((0,), (0,)), ((), ())), preferred_element_type=F32)


def unit_rows(inputs):
    row_mean = jnp.mean(inputs, axis=-1, keepdims=True)
    centred = inputs - row_mean
    variance = jnp.mean(centred * centred, axis=-1, keepdims=True)
    scale = lax.rsqrt(variance + EPS)
    return centred * scale, scale


def unit_rows_back(grad_normed, unit, scale, gain):
    grad_unit = grad_normed * gain
    return scale * (
        grad_unit
        - jnp.mean(grad_unit, axis=-1, keepdims=True)
        - unit * jnp.mean(grad_unit * unit, axis=-1, keepdims=True)
    )


def rows_sum(values):
    return jnp.sum(values, axis=0, keepdims=True)


def sum_bf(*values):
    return sum([one.astype(F32) for one in values]).astype(BF)


class Wires:
    def __init__(self, send_sems, recv_sems):
        self.send_sems, self.recv_sems, self.used, self.started = send_sems, recv_sems, 0, []

    def take(self, count=1):
        first = self.used
        self.used += count
        return first

    def copy(self, index, source, target, device):
        return pltpu.make_async_remote_copy(
            src_ref=source,
            dst_ref=target,
            send_sem=self.send_sems.at[index],
            recv_sem=self.recv_sems.at[index],
            device_id=device,
            device_id_type=MESH,
        )

    def send(self, source, target, device):
        one = self.copy(self.take(), source, target, device)
        one.start()
        self.started.append((one, None))
        return one

    def later(self, one, when=None):
        self.started.append((one, when))
        return one

    def plan(self, source, target, device):
        return self.later(self.copy(self.take(), source, target, device))

    def drain(self):
        for one, when in self.started:
            if when is None:
                one.wait_send()
            else:
                pl.when(when)(one.wait_send)


ORDER = (
    "up_grad", "ph_combine", "down_grad", "A_e0", "y_part", "A_e1", "wait_ph", "D_xout", "ln2",
    "sums", "out_grad", "up_xin", "bo0", "A_e2", "A2a", "A2b", "early", "bo1", "bo2", "bo3",
    "kv_out", "D_in", "go_combine", "bw0", "D2a", "up_in", "bw1", "D3", "D2b", "A3", "U2a", "bw2",
    "U2b", "go_out", "D_turn", "U3", "bw3", "kv_in", "qkv_grad", "go_in", "A_out", "gq_comb",
    "U_turn", "A_turn", "go_turn", "U_i1", "gq_fin", "A_o1", "A_i1", "U_o1", "h1_part", "go_done",
    "D_i1", "q_start", "U_i2", "H2a", "py_combine", "q_i1", "A_i2", "A_i3", "h1_e2", "early2",
    "U_i3", "D_o1", "q_o1", "H2b", "H3", "go_fin", "D_i2", "q_i2", "h1_fin", "D_i3", "q_i3",
    "layer_out", "small", "fin",
)


def layer_kernel(sizes, names, *refs):
    n_ctx, n_doc, R, D, S, FS = sizes
    r = dict(zip(names, refs, strict=True))
    G = n_ctx // GROUPS
    last = GROUPS - 1
    half = GROUPS * R
    c = lax.axis_index("ctx")
    w = lax.axis_index("wsh")
    hg, px = c // G, c % G

    def zdev(group):
        return {"ctx": group * G + px, "wsh": w}

    def wdev(index):
        return {"ctx": c, "wsh": index}

    xdev = {"ctx": hg * G + 1 - px, "wsh": w}
    left, right = zdev((hg + last) % GROUPS), zdev((hg + 1) % GROUPS)
    w1, w2, w3 = flip(w, 1), flip(w, 2), flip(w, 3)
    sib, across, diag = wdev(w1), wdev(w2), wdev(w3)
    wires = Wires(r["send_sems"], r["recv_sems"])
    lane = lax.broadcasted_iota(jnp.int32, (1, LANES), 1)
    low_half = lane < LANES // 2

    def pick(table):
        return sum([jnp.where(hg == i, one, 0) for i, one in enumerate(table)])

    def by_distance(step):
        return (
            jnp.where(step == 0, pick((3, 3, 0, 0)), 0)
            + jnp.where(step == 1, pick((2, 0, 3, 1)), 0)
            + jnp.where(step == 2, pick((1, 2, 1, 2)), 0)
            + jnp.where(step == 3, hg, 0)
        )

    local = r["local_sems"]

    def fetch(index, source, target):
        one = pltpu.make_async_copy(source, target, local.at[index])
        one.start()
        return one

    tok_in = fetch(0, r["tok"], r["x_s"].at[hg])
    qkv_in = [fetch(1 + i, r[name], r["win_s"].at[i]) for i, name in enumerate(("wq", "wk", "wv"))]
    dy_in = fetch(4, r["dy"], r["dy_s"].at[w])
    wo_in = [
        fetch(5, r["wout"].at[pl.ds(0, LANES)], r["wo_s"].at[w, pl.ds(0, LANES)]),
        fetch(6, r["wout"].at[pl.ds(LANES, S - LANES)], r["wo_s"].at[w, pl.ds(S, S - LANES)]),
    ]
    wu_in = fetch(7, r["wup"].at[:, pl.ds(pl.multiple_of(w * FS, FS), FS)], r["wu_s"].at[w])
    wd_in = fetch(8, r["wdown"], r["wd_s"])

    barrier = pltpu.get_barrier_semaphore()
    ctx_peers = [{"ctx": (c + i) % n_ctx, "wsh": w} for i in range(1, n_ctx)]
    partners = ctx_peers + [sib, across, diag]
    for partner in partners:
        pl.semaphore_signal(barrier, inc=1, device_id=partner, device_id_type=MESH)

    for one in qkv_in:
        one.wait()
    own_w = pl.ds(pl.multiple_of(w * S, S), S)
    win, wq_s = r["win_s"], r["wq_s"]
    for g in range(GROUPS):

        @pl.when(hg == g)
        def _():
            a = g * S
            wq_s[own_w, 0:S] = win[0, :, a : a + S]
            wq_s[own_w, S : 2 * LANES] = jnp.zeros((S, 2 * LANES - S), BF)
            wq_s[own_w, 2 * LANES : 2 * LANES + S] = win[1, :, a : a + S]
            wq_s[own_w, 2 * LANES + S : 4 * LANES] = win[2, :, a + LANES : a + S]
            wq_s[own_w, 4 * LANES : 5 * LANES] = win[2, :, a : a + LANES]

    par_s = r["par_s"]
    par_s[w] = jnp.zeros((8, 2 * LANES), F32)
    for i, name in enumerate(("n1g", "n1b", "bq", "bv", "bo", "n2g", "n2b", "bd")):
        par_s[w, i : i + 1, 0:S] = r[name][...].astype(F32)[None, :]
    r["wo_s"][:, LANES:S, :] = jnp.zeros((GROUPS, S - LANES, D), BF)
    tok_in.wait()
    pl.semaphore_wait(barrier, len(partners))

    class Gather:
        def __init__(self, slot):
            self.slot = slot
            self.to_across = wires.send(slot(w), slot(w), across)
            self.to_sib = wires.send(slot(w), slot(w), sib)

        def relay(self):
            self.to_across.wait_recv()
            self.on = wires.send(self.slot(w2), self.slot(w2), sib)

        def finish(self):
            self.to_sib.wait_recv()
            self.on.wait_recv()

    class Reduce:
        def __init__(self, part, recv):
            self.part, self.recv = part, recv
            self.a = wires.plan(part(w3), recv.at[0], sib)
            self.b = wires.plan(part(w1), recv.at[1], sib)
            self.c = wires.plan(recv.at[3], recv.at[2], across)

        def start(self):
            self.a.start()
            self.b.start()

        def combine(self):
            self.a.wait_recv()
            self.recv[3] = sum_bf(self.part(w2)[...], self.recv[0])
            self.c.start()

        def finish(self):
            self.b.wait_recv()
            self.c.wait_recv()
            return (
                self.part(w)[...].astype(F32)
                + self.recv[1].astype(F32)
                + self.recv[2].astype(F32)
            )

    class LineSum:
        def __init__(self, part, recv):
            self.part, self.recv = part, recv
            self.first_at = wires.take(6)
            for i in range(3):
                wires.later(self.message(i, True), hg > i)
                wires.later(self.message(i, False), hg < last - i)

        def message(self, i, leftward):
            block, slot = (i, i) if leftward else (last - i, 3 + i)
            return wires.copy(
                self.first_at + slot, self.part(block), self.recv.at[slot], left if leftward else right
            )

        def ends_block(self, block):
            for i in range(2):

                @pl.when((hg == last) & (block == i))
                def _():
                    self.message(i, True).start()

                @pl.when((hg == 0) & (block == last - i))
                def _():
                    self.message(i, False).start()

        def ends(self, which=(0, 1, 2)):
            for i in which:

                @pl.when(hg == last)
                def _():
                    self.message(i, True).start()

                @pl.when(hg == 0)
                def _():
                    self.message(i, False).start()

        def pass_on(self, position, i, leftward):
            @pl.when(hg == position)
            def _():
                one = self.message(i, leftward)
                one.wait_recv()
                block, slot = (i, i) if leftward else (last - i, 3 + i)
                self.part(block)[...] = sum_bf(self.part(block)[...], self.recv[slot])
                one.start()

        def second(self, which=(0, 1)):
            for i in which:
                self.pass_on(2, i, True)
                self.pass_on(1, i, False)

        def third(self):
            self.pass_on(1, 0, True)
            self.pass_on(2, 0, False)

        def final(self, put):
            for position in range(GROUPS):

                @pl.when(hg == position)
                def _():
                    total = self.part(position)[...].astype(F32)
                    if position < last:
                        self.message(position, True).wait_recv()
                        total = total + self.recv[position].astype(F32)
                    if position > 0:
                        self.message(last - position, False).wait_recv()
                        total = total + self.recv[3 + last - position].astype(F32)
                    put(total)

    class LineGather:
        def __init__(self, slot, to_x):
            self.slot, self.to_x = slot, to_x
            self.first_at = wires.take(6)
            self.x_at = wires.take(GROUPS) if to_x else None
            for d in (1, 2, 3):
                wires.later(self.message(d, 0), (hg >= d - 1) & (hg < last))
                wires.later(self.message(d, 1), (hg + d - 1 <= last) & (hg > 0))
            if to_x:
                for b in range(GROUPS):
                    wires.later(self.x_message(b))

        def message(self, d, side):
            block = (hg + GROUPS + (1 - d) * (1 - 2 * side)) % GROUPS
            device = zdev((hg + GROUPS + 1 - 2 * side) % GROUPS)
            return wires.copy(
                self.first_at + 3 * side + d - 1, self.slot(block), self.slot(block), device
            )

        def x_message(self, block):
            return wires.copy(self.x_at + block, self.slot(block), self.slot(block), xdev)

        def start(self):
            pl.when(hg < last)(self.message(1, 0).start)
            pl.when(hg > 0)(self.message(1, 1).start)
            if self.to_x:
                self.x_message(hg).start()

        def arrived(self, d, side, then=None):
            block = (hg + GROUPS - d * (1 - 2 * side)) % GROUPS
            here = jnp.where(side == 0, (hg >= d).astype(jnp.int32), (hg + d <= last).astype(jnp.int32))
            onward = here * jnp.where(side == 0, (hg < last).astype(jnp.int32), (hg > 0).astype(jnp.int32))

            @pl.when(here == 1)
            def _():
                wires.copy(
                    self.first_at + 3 * side + d - 1, self.slot(block), self.slot(block), left
                ).wait_recv()

            @pl.when(onward == 1)
            def _():
                self.message(d + 1, side).start()

            @pl.when(here == 1)
            def _():
                if self.to_x:
                    self.x_message(block).start()
                if then is not None:
                    then(block)

        def inner(self, d):
            self.arrived(d, jnp.where(hg < 2, 1, 0))

        def outer(self, d):
            self.arrived(d, jnp.where(hg < 2, 0, 1))

        def done(self):
            for b in range(GROUPS):
                self.x_message(b).wait_recv()

    x_s, h1_s, q_s, kv_s = r["x_s"], r["h1_s"], r["q_s"], r["kv_s"]
    rows_two = R // 2
    tokens = [
        LineGather(lambda b, j=j: x_s.at[b, pl.ds(j * rows_two, rows_two)], False) for j in (0, 1)
    ]
    for one in tokens:
        one.start()
    ws_all = Gather(lambda i: wq_s.at[pl.ds(pl.multiple_of(i * S, S), S)])
    par_all = Gather(lambda i: par_s.at[i])
    for one in wo_in:
        one.wait()
    dy_in.wait()
    wo_s, dy_s, wu_s = r["wo_s"], r["dy_s"], r["wu_s"]
    wo_top = Gather(lambda i: wo_s.at[i, pl.ds(0, LANES)])
    wo_low = Gather(lambda i: wo_s.at[i, pl.ds(S, S - LANES)])
    dy_all = Gather(lambda i: dy_s.at[i])
    up_sends = [
        wires.send(
            r["wup"].at[:, pl.ds(pl.multiple_of(flip(w, k) * FS, FS), FS)],
            wu_s.at[w],
            wdev(flip(w, k)),
        )
        for k in (2, 3, 1)
    ]
    inner_side = jnp.where(hg < 2, 1, 0)
    tokens[0].arrived(1, inner_side)
    tokens[0].arrived(1, 1 - inner_side)
    par_all.relay()
    ws_all.relay()
    tokens[1].arrived(1, inner_side)
    tokens[1].arrived(1, 1 - inner_side)
    par_all.finish()

    pars = jnp.concatenate([par_s[i][:, :S] for i in range(GROUPS)], axis=1)
    gain_one, bias_one, out_b, gain_two, bias_two, down_b = [
        pars[i : i + 1] for i in (0, 1, 4, 5, 6, 7)
    ]
    up_b = r["bup"][...].astype(F32)[None, :]
    own_par = par_s[hg]
    v_tile, v_last = own_par[3:4, :LANES], own_par[3:4, LANES:]
    qkv_b = jnp.concatenate(
        [own_par[2:3, :], jnp.zeros((1, LANES), F32), pltpu.roll(v_last, LANES // 2, 1), v_tile],
        axis=1,
    )
    ws_all.finish()

    kv_first = wires.take(2 * GROUPS)

    def kv_copy(block, j):
        rows = pl.ds(pl.multiple_of(block * R + j * rows_two, rows_two), rows_two)
        return wires.copy(
            kv_first + 2 * block + j, kv_s.at[0, rows], kv_s.at[1, rows], xdev
        )

    def project(block, j):
        rows = pl.ds(pl.multiple_of(j * rows_two, rows_two), rows_two)
        unit, unused = unit_rows(x_s[block, rows, :].astype(F32))
        normed = (unit * gain_one + bias_one).astype(BF)
        h1_s[block, rows, :] = normed
        qkv = dot_nn(normed, wq_s[...]) + qkv_b
        queries = qkv[:, : 2 * LANES].astype(BF).astype(F32) * 0.125
        q_s[0, block, rows, :] = jnp.where(low_half, queries[:, :LANES], 0.0).astype(BF)
        q_s[1, block, rows, :] = jnp.where(low_half, 0.0, queries[:, :LANES]).astype(BF)
        q_s[2, block, rows, :] = queries[:, LANES:].astype(BF)
        kv_rows = pl.ds(pl.multiple_of(block * R + j * rows_two, rows_two), rows_two)
        kv_s[0, kv_rows, :] = qkv[:, 2 * LANES :].astype(BF)
        kv_copy(block, j).start()

    def near_project(i, carry):
        away = jnp.where(i < 2, 0, jnp.where(i < 4, 1, 3)) * (1 - 2 * (1 - inner_side))
        block = (hg + 2 * GROUPS + jnp.where(i < 4, away, (1 - 2 * inner_side))) % GROUPS

        @pl.when((i < 4) | ((hg > 0) & (hg < last)))
        def _():
            project(block, i % 2)

        return carry

    lax.fori_loop(0, 6, near_project, 0)

    def far_project(i, carry):
        d = i + 2
        block = (hg + GROUPS - d * (1 - 2 * inner_side)) % GROUPS
        for j, one in enumerate(tokens):
            one.arrived(d, inner_side)

            @pl.when(jnp.where(hg < 2, hg + d <= last, hg >= d))
            def _():
                project(block, j)

        return carry

    lax.fori_loop(0, 2, far_project, 0)
    wo_top.relay()
    wo_low.relay()
    dy_all.relay()
    doc_ends = []
    for i in range(n_doc):
        doc_ends.append(r["doc"][0, i] + (doc_ends[-1] if i else 0))

    def doc_ids(positions):
        return sum([(positions >= end).astype(jnp.int32) for end in doc_ends])

    key_at = lax.broadcasted_iota(jnp.int32, (1, half), 1)
    key_block = sum([(key_at >= i * R).astype(jnp.int32) for i in range(1, GROUPS)])
    key_base = key_at + key_block * (R * (G - 1))
    key_ids = [doc_ids(key_base + px * R), doc_ids(key_base + (1 - px) * R)]
    KT, VT, KO = (0, 0, LANES), (2 * LANES, 2 * LANES, LANES), (0, 0, LANES)
    e_s, li_s, oa_s, os_s, or_s = r["e_s"], r["li_s"], r["oa_s"], r["os_s"], r["or_s"]
    of_s = r["of_s"]

    def pack(target, first, final):
        target[0:R, :] = first.astype(BF)
        turned = pltpu.roll(final[rows_two:, :], LANES // 2, 1)
        target[R : R + rows_two, :] = jnp.where(low_half, turned, final[:rows_two, :]).astype(BF)

    def unpack(source, target):
        target[:, :LANES] = source[0:R, :]
        both = source[R : R + rows_two, :].astype(F32)
        target[0:rows_two, LANES:] = jnp.where(low_half, 0.0, both).astype(BF)
        turned = pltpu.roll(both, LANES // 2, 1)
        target[rows_two:, LANES:] = jnp.where(low_half, 0.0, turned).astype(BF)

    class Turn:
        def __init__(self, source, target):
            self.source, self.target = source, target
            self.first_at = wires.take(GROUPS)
            for i in (1, 2, 3):
                wires.later(self.message((hg + i) % GROUPS))

        def message(self, block):
            index = self.first_at + (block - hg + GROUPS) % GROUPS
            return wires.copy(index, self.source.at[block], self.target.at[hg], zdev(block))

        def arrived(self, block):
            index = self.first_at + (hg - block + GROUPS) % GROUPS
            wires.copy(index, self.target.at[block], self.target.at[block], left).wait_recv()

    on_s = r["on_s"]
    o_turn = Turn(os_s, on_s)

    def row_ids_of(block):
        row_at = (block * G + px) * R + lax.broadcasted_iota(jnp.int32, (R, 1), 0)
        return doc_ids(row_at)

    def attend_side(block, side):
        row_ids = row_ids_of(block)
        same = row_ids == key_ids[side]
        scores = [
            jnp.where(
                same, dot_nt(q_s[h, block], kv_s[side, :, KT[h] : KT[h] + LANES]), NEG_START
            )
            for h in range(3)
        ]
        tops = [jnp.max(one, axis=-1, keepdims=True) for one in scores]
        weights = [jnp.exp(one - top) for one, top in zip(scores, tops, strict=True)]
        mixed = []
        for h in range(3):
            rounded = weights[h].astype(BF)
            e_s[h, block, side] = rounded
            mixed.append(dot_nn(rounded, kv_s[side, :, VT[h] : VT[h] + LANES]))
        totals = [jnp.sum(one, axis=-1, keepdims=True) for one in weights]
        return tops, totals, mixed

    def attend_own(block, carry):
        tops, totals, mixed = attend_side(block, 0)
        for h in range(3):
            li_s[0, h, block] = jnp.broadcast_to(tops[h], (R, LANES))
            li_s[1, h, block] = jnp.broadcast_to(totals[h], (R, LANES))
            of_s[h, block] = mixed[h]
        return carry

    lax.fori_loop(0, GROUPS, attend_own, 0)
    for b in range(GROUPS):
        for j in (0, 1):
            kv_copy(b, j).wait_recv()
            wires.later(kv_copy(b, j))

    def attend(step, carry):
        block = by_distance(step)
        tops, totals, mixed = attend_side(block, 1)
        outs = []
        for h in range(3):
            top, total = tops[h], totals[h]
            own_top = li_s[0, h, block]
            both_top = jnp.maximum(own_top, top)
            own_part, part = jnp.exp(own_top - both_top), jnp.exp(top - both_top)
            inverse = 1.0 / (li_s[1, h, block] * own_part + total * part)
            own_part, part = own_part * inverse, part * inverse
            li_s[0, h, block] = own_part
            li_s[1, h, block] = part
            outs.append(of_s[h, block] * own_part + mixed[h] * part)
        first = jnp.where(low_half, outs[0], outs[1])
        final = jnp.where(low_half, 0.0, outs[2])
        oa_s[block, :, :LANES] = first
        oa_s[block, :, LANES:] = final
        pack(os_s.at[block], first, final)

        @pl.when(step < last)
        def _():
            o_turn.message(block).start()

        return carry

    lax.fori_loop(0, GROUPS, attend, 0)
    unpack(os_s.at[hg], or_s.at[hg])
    wo_top.finish()
    wo_low.finish()
    for i in (1, 2, 3):
        there = (hg + i) % GROUPS
        o_turn.arrived(there)
        unpack(on_s.at[there], or_s.at[there])

    middle = x_s[hg].astype(F32) + out_b
    for i in range(GROUPS):
        middle += dot_nn(or_s[i], wo_s[i])
    x1_s, h2_s, g_s, da_s = r["x1_s"], r["h2_s"], r["g_s"], r["da_s"]
    x1_s[...] = middle
    unit_two, scale_two = unit_rows(middle)
    h2_s[w] = (unit_two * gain_two + bias_two).astype(BF)
    h2_all = Gather(lambda i: h2_s.at[i])
    dy_all.finish()
    wu_in.wait()
    wd_in.wait()
    for one in up_sends:
        one.wait_recv()
    ph_s, hr_s, wd_s = r["ph_s"], r["hr_s"], r["wd_s"]
    ph = Reduce(lambda i: ph_s.at[i], hr_s)

    def up_and_back(slot):
        hidden = dot_nn(h2_s[slot], wu_s[...].reshape(D, FS)) + up_b
        square = hidden * hidden
        inner = math.sqrt(2.0 / math.pi) * (hidden + 0.044715 * (square * hidden))
        bent = jnp.tanh(inner)
        g_s[slot] = (0.5 * hidden * (1.0 + bent)).astype(BF)
        slope = 0.5 * (1.0 + bent) + 0.5 * hidden * (1.0 - bent * bent) * (
            math.sqrt(2.0 / math.pi) * (1.0 + 3.0 * 0.044715 * square)
        )
        grad_active = dot_nt(dy_s[slot], wd_s[...])
        grad_hidden = (grad_active * slope).astype(BF)
        da_s[slot] = grad_hidden
        ph_s[slot] = dot_nt(grad_hidden, wu_s[...].reshape(D, FS)).astype(BF)

    on_copy = wires.copy(wires.take(), h2_s.at[w2], h2_s.at[w2], sib)

    def mlp_step(j, carry):
        @pl.when(j == 1)
        def _():
            h2_all.to_sib.wait_recv()

        @pl.when(j == 2)
        def _():
            h2_all.to_across.wait_recv()
            on_copy.start()

        @pl.when(j == 3)
        def _():
            on_copy.wait_recv()

        up_and_back(flip(w, j))

        @pl.when(j == 1)
        def _():
            ph.b.start()

        @pl.when(j == 3)
        def _():
            ph.a.start()

        return carry

    lax.fori_loop(0, GROUPS, mlp_step, 0)
    wires.later(on_copy)

    gus_s, gas_s, gds_s, py_s = r["gus_s"], r["gas_s"], r["gds_s"], r["py_s"]
    cols = gas_s.shape[1]

    def up_grad(i, carry):
        at = pl.ds(pl.multiple_of(i * 2 * S, 2 * S), 2 * S)
        gus_s[pl.ds(2 * i, 2)] = (
            dot_tn(h2_s[:, :, at].reshape(half, 2 * S), da_s[...].reshape(half, FS))
            .astype(BF)
            .reshape(2, 2, S // 2, FS)
        )
        return carry

    def down_grad(i, carry):
        at = pl.ds(pl.multiple_of(i * 256, 256), 256)
        both = dot_tn(g_s[:, :, at].reshape(half, 256), dy_s[...].reshape(half, D)).astype(BF)
        gas_s[at, :] = both[:, :cols]
        gds_s[at, :] = both[:, cols:]
        return carry

    def y_part(j, carry):
        py_s[j] = dot_nn(g_s[j], wd_s[...]).astype(BF)
        return carry

    class Spread:
        def __init__(self, part, recv, slot, to_x):
            self.sum = LineSum(part, recv)
            self.gather = LineGather(slot, to_x)

        def turn(self):
            def put(total):
                self.gather.slot(hg)[...] = total.astype(BF)

            self.sum.final(put)
            self.gather.start()

    class Share:
        def __init__(self, rows):
            self.rows = rows
            self.at = wires.take(n_ctx)
            for i in range(1, n_ctx):
                wires.later(self.message(i))

        def message(self, i):
            return wires.copy(self.at + i, self.rows.at[c], self.rows.at[c], ctx_peers[i - 1])

        def start(self):
            for i in range(1, n_ctx):
                self.message(i).start()

        def total(self):
            for i in range(1, n_ctx):
                wires.copy(self.at + i, self.rows.at[c], self.rows.at[c], left).wait_recv()
            return sum([self.rows[i] for i in range(n_ctx)])

    n = S // 2
    n_down = FS // 8
    quarter = n // GROUPS
    ga_f, gd_f, gu_s, up_f = r["gda"], r["gdb"], r["gu_s"], r["gup"]
    mine = pl.ds(pl.multiple_of(px * n, 8), n)
    theirs = pl.ds(pl.multiple_of((1 - px) * n, 8), n)

    def down_rows(b):
        return pl.ds(pl.multiple_of(px * (4 * n_down) + b * n_down, 8), n_down)

    down_here = pl.ds(pl.multiple_of(px * (4 * n_down), 8), 4 * n_down)
    down_there = pl.ds(pl.multiple_of((1 - px) * (4 * n_down), 8), 4 * n_down)
    py = Reduce(lambda i: py_s.at[i], r["yr_s"])
    up_x = wires.plan(gus_s.at[:, 1 - px], r["gux_s"], xdev)
    up_y_first = wires.take(GROUPS)

    def up_y(k, out):
        to = flip(w, k)
        return wires.copy(
            up_y_first + k, gus_s.at[to, px], gu_s.at[w if out else to], wdev(to)
        )

    for k in (1, 2, 3):
        wires.later(up_y(k, True))
    up = Spread(lambda b: gu_s.at[b], r["gul_s"], lambda b: up_f.at[b, px], True)
    down_x = wires.plan(gds_s.at[down_there], r["gdx_s"], xdev)
    down = Spread(
        lambda b: gds_s.at[down_rows(b)], r["gdl_s"], lambda b: gd_f.at[down_rows(b)], True
    )
    gat_s, gax_s = r["gat_s"], r["gax_s"]

    def across_rows(b):
        return pl.ds(pl.multiple_of(b * 2 * n_down + px * n_down, 8), n_down)

    most = Spread(
        lambda b: gas_s.at[pl.ds(pl.multiple_of(b * 2 * n_down, 8), 2 * n_down)],
        r["gal_s"],
        lambda b: ga_f.at[across_rows(b)],
        True,
    )
    most_x = wires.plan(gat_s.at[1 - px], gax_s, xdev)
    dz_s, dos_s, dor_s = r["dz_s"], r["dos_s"], r["dor_s"]
    don_s = r["don_s"]
    do_turn = Turn(dos_s, don_s)
    early, early_x_s, early_z_s = r["early_s"], r["early_x_s"], r["early_z_s"]
    late = r["late_s"]
    early_x = wires.plan(early, early_x_s, xdev)
    early_first = wires.take(GROUPS)

    def early_z(i):
        return wires.copy(
            early_first + i, early_z_s.at[hg], early_z_s.at[hg], zdev((hg + i) % GROUPS)
        )

    for i in (1, 2, 3):
        wires.later(early_z(i))
    late_all = Share(late)
    gos_s, gor_s = r["gos_s"], r["gor_s"]
    go_s, gox_s, gop_s, gon_s, go_f = r["go_s"], r["gox_s"], r["gop_s"], r["gon_s"], r["gout"]
    go = Reduce(lambda i: gos_s.at[i], gor_s)
    go_x = wires.plan(go_s.at[theirs], gox_s, xdev)
    go_turn = Turn(gop_s, gon_s)
    go_first = wires.take(GROUPS)

    def go_back(i):
        piece = go_f.at[px, hg]
        return wires.copy(go_first + i, piece, piece, zdev((hg + i) % GROUPS))

    for i in (1, 2, 3):
        wires.later(go_back(i))
    go_x2 = wires.plan(go_f.at[px], go_f.at[px], xdev)
    kvt_s, kvr_s, ph1_s, gqs_s = r["kvt_s"], r["kvr_s"], r["ph1_s"], r["gqs_s"]
    kv_back = wires.plan(kvt_s, kvr_s, xdev)
    h1_sum = LineSum(lambda b: ph1_s.at[b], r["h1r_s"])
    gq = Reduce(lambda i: gqs_s.at[pl.ds(pl.multiple_of(i * S, S), S)], r["gqr_s"])
    gqc_s, gqx_s, gqkv = r["gqc_s"], r["gqx_s"], r["gqkv"]
    qx = wires.plan(gqc_s.at[theirs], gqx_s, xdev)
    q_line = LineGather(lambda b: gqkv.at[b, mine], True)
    vecs, vecr = r["vecs_s"], r["vecr_s"]
    vec_first = wires.take(GROUPS)

    def vec_send(k):
        return wires.copy(
            vec_first + k, vecs.at[flip(w, k)], vecr.at[k - 1], wdev(flip(w, k))
        )

    for k in (1, 2, 3):
        wires.later(vec_send(k))
    dkv_s, dq_s, dqkv_s, df_s = r["dkv_s"], r["dq_s"], r["dqkv_s"], r["df_s"]

    steps = {}

    def step_of(name):
        def keep(body):
            steps[name] = body
            return body

        return keep

    @step_of("up_xin")
    def _():
        up_x.wait_recv()
        here = gus_s.at[:, px]
        here[...] = sum_bf(here[...], r["gux_s"][...])
        gu_s[w] = gus_s[w, px]
        for k in (2, 3, 1):
            up_y(k, True).start()

    @step_of("up_in")
    def _():
        for k in (1, 2, 3):
            up_y(k, False).wait_recv()
        up.sum.ends()

    @step_of("D_in")
    def _():
        down_x.wait_recv()
        gds_s[down_here, :] = sum_bf(gds_s[down_here, :], r["gdx_s"][...])
        down.sum.ends()

    steps["D_xout"] = down_x.start
    for i in range(3):
        steps["A_e%d" % i] = partial(most.sum.ends, (i,))
    steps["A2a"] = partial(most.sum.second, (0,))
    steps["A2b"] = partial(most.sum.second, (1,))
    steps["A3"] = most.sum.third

    @step_of("A_out")
    def _():
        def put(total):
            gat_s[...] = total.astype(BF).reshape(2, n_down, cols)

        most.sum.final(put)
        most_x.start()

    @step_of("A_turn")
    def _():
        most_x.wait_recv()
        ga_f[across_rows(hg), :] = sum_bf(gat_s[px], gax_s[...])
        most.gather.start()

    for name, chain in (("U", up), ("D", down)):
        steps[name + "2a"] = partial(chain.sum.second, (0,))
        steps[name + "2b"] = partial(chain.sum.second, (1,))
        steps[name + "3"] = chain.sum.third
        steps[name + "_turn"] = chain.turn
    for name, line in (("U", up.gather), ("D", down.gather), ("A", most.gather), ("q", q_line)):
        steps[name + "_i1"] = partial(line.inner, 1)
        steps[name + "_o1"] = partial(line.outer, 1)
        steps[name + "_i2"] = partial(line.inner, 2)
        steps[name + "_i3"] = partial(line.inner, 3)
    steps["H2a"] = partial(h1_sum.second, (0,))
    steps["H2b"] = partial(h1_sum.second, (1,))
    steps["H3"] = h1_sum.third
    steps["h1_e2"] = partial(h1_sum.ends, (2,))
    steps["go_combine"] = go.combine
    steps["py_combine"] = py.combine
    steps["gq_comb"] = gq.combine

    @step_of("go_out")
    def _():
        go_s[...] = go.finish().astype(BF)
        go_x.start()

    @step_of("go_in")
    def _():
        go_x.wait_recv()
        go_half = go_s[mine, :].astype(F32) + gox_s[...].astype(F32)
        for b in range(GROUPS):
            gop_s[b] = go_half[b * quarter : (b + 1) * quarter].astype(BF)
        for i in (2, 1, 3):
            go_turn.message((hg + i) % GROUPS).start()

    @step_of("go_turn")
    def _():
        for i in (1, 2, 3):
            go_turn.arrived((hg + i) % GROUPS)
        go_total = gop_s[hg].astype(F32)
        for i in (1, 2, 3):
            go_total = go_total + gon_s[(hg + i) % GROUPS].astype(F32)
        go_f[px, hg] = go_total.astype(BF)
        for i in (2, 1, 3):
            go_back(i).start()

    @step_of("go_done")
    def _():
        for i in (1, 2, 3):
            go_back(i).wait_recv()
        go_x2.start()

    @step_of("go_fin")
    def _():
        go_x2.wait_recv()

    steps["early"] = early_x.start

    @step_of("early2")
    def _():
        early_x.wait_recv()
        early_z_s[hg] = early[...] + early_x_s[...]
        for i in (1, 2, 3):
            early_z(i).start()

    @step_of("kv_in")
    def _():
        kv_back.wait_recv()
        dqkv_s[:, 2 * LANES :] = jnp.transpose(sum_bf(dkv_s[0], kvr_s[...]))

    @step_of("h1_part")
    def _():
        def h1_part(step, carry):
            block = by_distance(step)
            rows = pl.ds(pl.multiple_of(block * R, R), R)
            ph1_s[block] = dot_nt(dqkv_s[rows, :], wq_s[...]).astype(BF)
            h1_sum.ends_block(block)
            return carry

        lax.fori_loop(0, GROUPS, h1_part, 0)

    @step_of("qkv_grad")
    def _():
        def qkv_grad(i, carry):
            at = pl.ds(pl.multiple_of(i * 256, 256), 256)
            gqs_s[at, :] = dot_tn(h1_s[:, :, at].reshape(half, 256), dqkv_s[...]).astype(BF)
            return carry

        lax.fori_loop(0, D // 256, qkv_grad, 0)
        gq.start()
        late[c, :, 2 * D : 2 * D + 2 * LANES] = rows_sum(dqkv_s[:, : 2 * LANES].astype(F32))
        late[c, :, 2 * D + 2 * LANES :] = rows_sum(dqkv_s[:, 3 * LANES :].astype(F32))

    @step_of("gq_fin")
    def _():
        gqc_s[...] = gq.finish().astype(BF)
        qx.start()

    @step_of("q_start")
    def _():
        qx.wait_recv()
        gqkv[hg, mine, :] = sum_bf(gqc_s[mine, :], gqx_s[...])
        q_line.start()

    @step_of("h1_fin")
    def _():
        def keep_h1(total):
            df_s[...] = total

        h1_sum.final(keep_h1)
        grad_one = df_s[...]
        unit_one, scale_one = unit_rows(x_s[hg].astype(F32))
        grad_in = dz_s[...] + unit_rows_back(grad_one, unit_one, scale_one, gain_one)
        r["dx"][...] = grad_in.astype(BF)
        late[c, :, 0:D] = rows_sum(grad_one * unit_one)
        late[c, :, D : 2 * D] = rows_sum(grad_one)
        late_all.start()

    @step_of("layer_out")
    def _():
        r["y"][...] = (x1_s[...] + py.finish() + down_b).astype(BF)

    @step_of("small")
    def _():
        for i in (1, 2, 3):
            there = (hg + i) % GROUPS
            wires.copy(early_first + GROUPS - i, early_z_s.at[there], early_z_s.at[there], left).wait_recv()
        ones = sum([early_z_s[i] for i in range(GROUPS)])
        twos = late_all.total()
        bq_all, bv_all = [], []
        for g in range(GROUPS):
            group_sum = sum([late[g * G + i][:, 2 * D :] for i in range(G)])
            bq_all.append(group_sum[:, :S])
            v_end = pltpu.roll(group_sum[:, 2 * LANES : 3 * LANES], LANES // 2, 1)[:, : S - LANES]
            bv_all.append(jnp.concatenate([group_sum[:, 3 * LANES :], v_end], axis=1))
        vectors = [twos[:, 0:D], twos[:, D : 2 * D]] + [
            ones[:, i * D : (i + 1) * D] for i in range(4)
        ]
        for i in range(GROUPS):
            for j, one in enumerate(vectors):
                vecs[i, :, j * 256 : j * 256 + S] = one[:, i * S : (i + 1) * S]
            vecs[i, :, 6 * 256 : 6 * 256 + S] = bq_all[i]
            vecs[i, :, 7 * 256 : 7 * 256 + S] = bv_all[i]
        r["vec"][:, 8 * 256 :] = ones[:, 4 * D :]
        for k in (1, 2, 3):
            vec_send(k).start()

    carried = {}

    @step_of("up_grad")
    def _():
        lax.fori_loop(0, 2, up_grad, 0)
        up_x.start()

    steps["ph_combine"] = ph.combine

    @step_of("down_grad")
    def _():
        lax.fori_loop(0, FS // 256, down_grad, 0)

    @step_of("y_part")
    def _():
        lax.fori_loop(0, GROUPS, y_part, 0)
        py.start()

    @step_of("wait_ph")
    def _():
        carried["two"] = ph.finish()

    @step_of("ln2")
    def _():
        grad_two = carried["two"]
        unit_two, scale_two = unit_rows(x1_s[...])
        top = r["dy_s"][w].astype(F32)
        grad_middle = top + unit_rows_back(grad_two, unit_two, scale_two, gain_two)
        dz = grad_middle.astype(BF)
        dz_s[...] = grad_middle
        carried["dz"], carried["unit"], carried["top"] = dz, unit_two, top

        def out_back(step, carry):
            block = by_distance(step)
            grad_o = dot_nt(dz, wo_s[block])
            pack(dos_s.at[block], grad_o[:, :LANES], grad_o[:, LANES:])

            @pl.when(step < last)
            def _():
                do_turn.message(block).start()

            return carry

        lax.fori_loop(0, GROUPS, out_back, 0)

    @step_of("sums")
    def _():
        unpack(dos_s.at[hg], dor_s.at[hg])
        early[:, 0:D] = rows_sum(carried["dz"].astype(F32))
        early[:, D : 2 * D] = rows_sum(carried["two"] * carried["unit"])
        early[:, 2 * D : 3 * D] = rows_sum(carried["two"])
        early[:, 3 * D : 4 * D] = rows_sum(carried["top"])
        early[:, 4 * D :] = rows_sum(da_s[...].reshape(half, FS).astype(F32))

    @step_of("out_grad")
    def _():
        for i in range(GROUPS):
            piece = dot_tn(or_s[i], carried["dz"])
            gos_s[i, 0:LANES, :] = piece[0:LANES, :].astype(BF)
            gos_s[i, LANES:S, :] = piece[S:, :].astype(BF)
        go.start()
        dkv_s[...] = jnp.zeros(dkv_s.shape, F32)

    def back_block(block, side):
        outs = dor_s[block].astype(F32)
        kept = oa_s[block]
        scaled = []
        for h in range(3):
            tile = 0 if h < 2 else LANES
            keep = low_half if h == 0 else jnp.logical_not(low_half)
            scaled.append(
                jnp.where(keep, outs[:, tile : tile + LANES], 0.0) * li_s[side, h, block]
            )
        deltas = [
            jnp.sum(
                scaled[h] * kept[:, KO[h] : KO[h] + LANES], axis=-1, keepdims=True
            )
            for h in range(3)
        ]
        rounded = [one.astype(BF) for one in scaled]
        grad_probs = [
            dot_nt(rounded[h], kv_s[side, :, VT[h] : VT[h] + LANES]) for h in range(3)
        ]
        grad_scores = [
            (e_s[h, block, side].astype(F32) * (grad_probs[h] - deltas[h])).astype(BF)
            for h in range(3)
        ]
        grads_q = [
            dot_nn(grad_scores[h], kv_s[side, :, KT[h] : KT[h] + LANES]) for h in range(3)
        ]
        for h in range(3):
            dkv_s[side, KT[h] : KT[h] + LANES, :] += dot_tn(q_s[h, block], grad_scores[h])
            dkv_s[side, VT[h] : VT[h] + LANES, :] += dot_tn(rounded[h], e_s[h, block, side])
        first = jnp.where(low_half, grads_q[0], grads_q[1]) * 0.125
        final = jnp.where(low_half, grads_q[2], 0.0) * 0.125
        if side == 1:
            dq_s[block, :, :LANES] = first
            dq_s[block, :, LANES:] = final
        else:
            rows = pl.ds(pl.multiple_of(block * R, R), R)
            dqkv_s[rows, :LANES] = (dq_s[block, :, :LANES] + first).astype(BF)
            dqkv_s[rows, LANES : 2 * LANES] = (dq_s[block, :, LANES:] + final).astype(BF)

    def nearest(step):
        return by_distance(last - step)

    @step_of("kv_out")
    def _():
        kvt_s[...] = dkv_s[1].astype(BF)
        kv_back.start()

    @step_of("fin")
    def _():
        for k in (1, 2, 3):
            vec_send(k).wait_recv()
        r["vec"][:, 0 : 8 * 256] = vecs[w] + vecr[0] + vecr[1] + vecr[2]
        down.gather.done()
        most.gather.done()
        up.gather.done()
        q_line.done()

    def attention_back(side, plans):
        def body(step, carry):
            block = nearest(step)
            if side == 1:

                @pl.when(step > 0)
                def _():
                    do_turn.arrived(block)
                    unpack(don_s.at[block], dor_s.at[block])

            back_block(block, side)
            for k, names in enumerate(plans):
                if names:

                    @pl.when(step == k)
                    def _():
                        for name in names:
                            steps[name]()

            return carry

        lax.fori_loop(0, GROUPS, body, 0)

    at = 0
    order = ORDER
    while at < len(order):
        name = order[at]
        at += 1
        if name in ("bo0", "bw0"):
            plans, kind = [[]], name[:2]
            while at < len(order) and (order[at][:2] == kind or len(plans) < GROUPS):
                if order[at][:2] == kind:
                    plans.append([])
                else:
                    plans[-1].append(order[at])
                at += 1
            attention_back(1 if kind == "bo" else 0, plans)
        else:
            steps[name]()
    assert wires.used == SEMS
    wires.drain()


def widen_kernel(S, names, *refs):
    r = dict(zip(names, refs, strict=True))
    n = S // 2
    started = []

    def send(source, target):
        one = pltpu.make_async_copy(source, target, r["sems"].at[len(started)])
        one.start()
        started.append(one)

    def put(name, at, value):
        r[name + "_b"][at] = value
        send(r[name + "_b"].at[at], r[name + "_o"].at[at])

    send(r["y"], r["y_o"])
    send(r["dx"], r["dx_o"])
    FS = r["up"].shape[3]
    for i in range(GROUPS):
        rows = slice(i * S, (i + 1) * S)
        both = [r[name][rows, :].astype(F32) for name in ("da", "db")]
        put("down", (rows, slice(None)), jnp.concatenate(both, axis=1))
        for j in (0, 1):
            at = (slice(j * n, (j + 1) * n), slice(i * FS, (i + 1) * FS))
            put("up", at, r["up"][i, j].astype(F32))
    put("out", (slice(None),), r["out"][...].astype(F32))

    def heads(pieces):
        return jnp.concatenate(
            [r["qkv"][i, :, a:b].astype(F32) for i in range(GROUPS) for a, b in pieces], axis=1
        )

    put("q", (slice(None),), heads([(0, S)]))
    put("k", (slice(None),), heads([(2 * LANES, 2 * LANES + S)]))
    put("v", (slice(None),), heads([(4 * LANES, 5 * LANES), (2 * LANES + S, 4 * LANES)]))
    at = 0
    for i in range(9):
        one = r["vec%d" % i]
        one[...] = r["vec"][0, at : at + one.shape[0]]
        at += max(one.shape[0], 256)
    for one in started:
        one.wait()


SEMS = 161


def fast_device(mesh_sizes, *arrays):
    (tokens, doc_lengths, out_grad, norm1_gain, norm1_bias, w_query, b_query, w_key, w_value,
     b_value, w_out, b_out, norm2_gain, norm2_bias, w_up, b_up, w_down, b_down) = arrays
    n_ctx, n_wsh = mesh_sizes
    R, D = tokens.shape[1], tokens.shape[2]
    S, FS, n_doc = D // GROUPS, w_down.shape[0], doc_lengths.shape[1]
    half, QW = GROUPS * R, 5 * LANES

    smem = pl.BlockSpec(memory_space=pltpu.SMEM)
    vmem = pl.BlockSpec(memory_space=pltpu.VMEM)
    anywhere = pl.BlockSpec(memory_space=pl.ANY)
    inputs = [
        ("doc", doc_lengths, smem),
        ("tok", tokens[0], anywhere),
        ("dy", out_grad[0], anywhere),
        ("wq", w_query, anywhere),
        ("wk", w_key, anywhere),
        ("wv", w_value, anywhere),
        ("wout", w_out, anywhere),
        ("wup", w_up, anywhere),
        ("wdown", w_down, anywhere),
        ("n1g", norm1_gain, vmem),
        ("n1b", norm1_bias, vmem),
        ("bq", b_query, vmem),
        ("bv", b_value, vmem),
        ("bo", b_out, vmem),
        ("n2g", norm2_gain, vmem),
        ("n2b", norm2_bias, vmem),
        ("bd", b_down, vmem),
        ("bup", b_up, vmem),
    ]
    n_up = S // 2
    outputs = [
        ("y", (R, D), BF),
        ("dx", (R, D), BF),
        ("gda", (FS, 2 * D // 3), BF),
        ("gdb", (FS, D // 3), BF),
        ("gup", (GROUPS, 2, n_up, FS), BF),
        ("gout", (2, GROUPS, S // 8, D), BF),
        ("gqkv", (GROUPS, S, QW), BF),
        ("vec", (1, 8 * 256 + FS), F32),
    ]
    scratch = [
        ("x_s", (GROUPS, R, D), BF),
        ("h1_s", (GROUPS, R, D), BF),
        ("win_s", (3, S, D), BF),
        ("wq_s", (D, QW), BF),
        ("par_s", (GROUPS, 8, 2 * LANES), F32),
        ("q_s", (3, GROUPS, R, LANES), BF),
        ("kv_s", (2, half, 3 * LANES), BF),
        ("e_s", (3, GROUPS, 2, R, half), BF),
        ("li_s", (2, 3, GROUPS, R, LANES), F32),
        ("of_s", (3, GROUPS, R, LANES), F32),
        ("oa_s", (GROUPS, R, 2 * LANES), F32),
        ("os_s", (GROUPS, R + R // 2, LANES), BF),
        ("on_s", (GROUPS, R + R // 2, LANES), BF),
        ("or_s", (GROUPS, R, 2 * LANES), BF),
        ("wo_s", (GROUPS, 2 * LANES, D), BF),
        ("wu_s", (GROUPS, S, FS), BF),
        ("wd_s", (FS, D), BF),
        ("dy_s", (GROUPS, R, D), BF),
        ("x1_s", (R, D), F32),
        ("h2_s", (GROUPS, R, D), BF),
        ("g_s", (GROUPS, R, FS), BF),
        ("da_s", (GROUPS, R, FS), BF),
        ("ph_s", (GROUPS, R, D), BF),
        ("hr_s", (4, R, D), BF),
        ("py_s", (GROUPS, R, D), BF),
        ("yr_s", (4, R, D), BF),
        ("dz_s", (R, D), F32),
        ("dos_s", (GROUPS, R + R // 2, LANES), BF),
        ("don_s", (GROUPS, R + R // 2, LANES), BF),
        ("dor_s", (GROUPS, R, 2 * LANES), BF),
        ("dkv_s", (2, 3 * LANES, half), F32),
        ("kvt_s", (3 * LANES, half), BF),
        ("kvr_s", (3 * LANES, half), BF),
        ("dq_s", (GROUPS, R, 2 * LANES), F32),
        ("dqkv_s", (half, QW), BF),
        ("ph1_s", (GROUPS, R, D), BF),
        ("h1r_s", (6, R, D), BF),
        ("df_s", (R, D), F32),
        ("gas_s", (FS, 2 * D // 3), BF),
        ("gal_s", (6, FS // 4, 2 * D // 3), BF),
        ("gat_s", (2, FS // 8, 2 * D // 3), BF),
        ("gax_s", (FS // 8, 2 * D // 3), BF),
        ("gds_s", (FS, D // 3), BF),
        ("gdx_s", (FS // 2, D // 3), BF),
        ("gdl_s", (6, FS // 8, D // 3), BF),
        ("gus_s", (GROUPS, 2, S // 2, FS), BF),
        ("gu_s", (GROUPS, n_up, FS), BF),
        ("gux_s", (GROUPS, S // 2, FS), BF),
        ("gul_s", (6, n_up, FS), BF),
        ("go_s", (S, D), BF),
        ("gox_s", (S // 2, D), BF),
        ("gop_s", (GROUPS, S // 8, D), BF),
        ("gon_s", (GROUPS, S // 8, D), BF),
        ("gos_s", (GROUPS, S, D), BF),
        ("gor_s", (4, S, D), BF),
        ("gqs_s", (D, QW), BF),
        ("gqr_s", (4, S, QW), BF),
        ("gqc_s", (S, QW), BF),
        ("gqx_s", (S // 2, QW), BF),
        ("early_s", (1, 4 * D + FS), F32),
        ("early_x_s", (1, 4 * D + FS), F32),
        ("early_z_s", (GROUPS, 1, 4 * D + FS), F32),
        ("late_s", (n_ctx, 1, 2 * D + 4 * LANES), F32),
        ("vecs_s", (GROUPS, 1, 8 * 256), F32),
        ("vecr_s", (3, 1, 8 * 256), F32),
    ]
    sems = [("send_sems", SEMS), ("recv_sems", SEMS), ("local_sems", 9)]
    names = [one[0] for one in inputs + outputs + scratch + sems]
    y, dx, g_da, g_db, g_up, g_out, g_qkv, vec = pl.pallas_call(
        partial(layer_kernel, (n_ctx, n_doc, R, D, S, FS), names),
        out_shape=[pltpu.VMEM(shape, dtype) for name, shape, dtype in outputs],
        in_specs=[spec for name, value, spec in inputs],
        out_specs=[vmem] * len(outputs),
        scratch_shapes=[pltpu.VMEM(shape, dtype) for name, shape, dtype in scratch]
        + [pltpu.SemaphoreType.DMA((count,)) for name, count in sems],
        compiler_params=pltpu.CompilerParams(
            collective_id=0, has_side_effects=True, vmem_limit_bytes=62000000
        ),
        name="layer",
    )(*[value for name, value, spec in inputs])

    big = [
        ("y", (R, D), BF),
        ("dx", (R, D), BF),
        ("down", (FS, D), F32),
        ("up", (S, GROUPS * FS), F32),
        ("out", (2, GROUPS, S // 8, D), F32),
        ("q", (S, D), F32),
        ("k", (S, D), F32),
        ("v", (S, D), F32),
    ]
    vectors = [("vec%d" % i, size) for i, size in enumerate([S] * 8 + [FS])]
    names = ["y", "dx", "da", "db", "up", "out", "qkv", "vec"]
    names += [name + "_o" for name, shape, dtype in big] + [name for name, size in vectors]
    names += [name + "_b" for name, shape, dtype in big[2:]] + ["sems"]
    wide = pl.pallas_call(
        partial(widen_kernel, S, names),
        in_specs=[vmem] * 8,
        out_specs=[anywhere] * len(big) + [vmem] * len(vectors),
        out_shape=[jax.ShapeDtypeStruct(shape, dtype) for name, shape, dtype in big]
        + [jax.ShapeDtypeStruct((size,), F32) for name, size in vectors],
        scratch_shapes=[pltpu.VMEM(shape, dtype) for name, shape, dtype in big[2:]]
        + [pltpu.SemaphoreType.DMA((18,))],
        compiler_params=pltpu.CompilerParams(vmem_limit_bytes=24000000),
        name="widen",
    )(y, dx, g_da, g_db, g_up, g_out, g_qkv, vec)
    y, dx, down, up, out, q, k, v, n1g, n1b, bo, n2g, n2b, bd, bq, bv, bup = wide
    return (
        y[None], dx[None], n1g, n1b, q, bq, k, v, bv, out.reshape(S, D), bo, n2g, n2b, up, bup, down, bd,
    )


def solution(mesh):
    in_specs = (
        P("wsh", "ctx", None),
        P("wsh", None),
        P("wsh", "ctx", None),
        P("wsh"),
        P("wsh"),
        P("wsh", None),
        P("wsh"),
        P("wsh", None),
        P("wsh", None),
        P("wsh"),
        P("wsh", None),
        P("wsh"),
        P("wsh"),
        P("wsh"),
        P("wsh", None),
        P("wsh"),
        P("wsh", None),
        P("wsh"),
    )
    out_specs = (
        P("wsh", "ctx", None),
        P("wsh", "ctx", None),
        P("wsh"),
        P("wsh"),
        P("wsh", None),
        P("wsh"),
        P("wsh", None),
        P("wsh", None),
        P("wsh"),
        P("wsh", None),
        P("wsh"),
        P("wsh"),
        P("wsh"),
        P("wsh", None),
        P("wsh"),
        P("wsh", None),
        P("wsh"),
    )
    sizes = (mesh.shape["ctx"], mesh.shape["wsh"])
    body = partial(fast_device, sizes) if sizes == (2 * GROUPS, GROUPS) else per_device
    return jax.shard_map(
        body, mesh=mesh, in_specs=in_specs, out_specs=out_specs, check_vma=False
    )
```

```python
from functools import partial
import math

import jax
import jax.numpy as jnp
from jax import lax
from jax.experimental import pallas as pl
from jax.experimental.pallas import tpu as pltpu
from jax.sharding import PartitionSpec as P

HEADS = 12


EPS = 1e-06
NEG_START = -1e30


def norm_rows(inputs, norm_gain, norm_bias):
    row_mean = jnp.mean(inputs, axis=-1, keepdims=True)
    centred = inputs - row_mean
    variance = jnp.mean(centred * centred, axis=-1, keepdims=True)
    return centred * lax.rsqrt(variance + EPS) * norm_gain + norm_bias


def doc_of(positions, doc_ends):
    return jnp.sum((positions[:, None] >= doc_ends[None, :]).astype(jnp.int32), axis=1)


def dot_plain(left, right):
    return jnp.dot(left, right, preferred_element_type=jnp.float32)


def dot_left(left, right):
    return lax.dot_general(
        left, right, (((0,), (0,)), ((), ())), preferred_element_type=jnp.float32
    )


def dot_right(left, right):
    return lax.dot_general(
        left, right, (((1,), (1,)), ((), ())), preferred_element_type=jnp.float32
    )


def masked_scores(query_heads, key_heads, query_ids, key_ids, score_scale):
    raw_scores = (
        jnp.einsum("qhd,khd->hqk", query_heads, key_heads, preferred_element_type=jnp.float32)
        * score_scale
    )
    same_doc = (query_ids[:, None] == key_ids[None, :])[None]
    return jnp.where(same_doc, raw_scores, -jnp.inf)


def per_device(
    tokens,
    doc_lengths,
    out_grad,
    norm1_gain,
    norm1_bias,
    w_query,
    b_query,
    w_key,
    w_value,
    b_value,
    w_out,
    b_out,
    norm2_gain,
    norm2_bias,
    w_up,
    b_up,
    w_down,
    b_down,
):
    (
        gain_one,
        bias_one,
        query_w,
        query_b,
        key_w,
        value_w,
        value_b,
        out_w,
        out_b,
        gain_two,
        bias_two,
        up_w,
        up_b,
        down_w,
        down_b,
    ) = (
        lax.all_gather(norm1_gain, "wsh", axis=0, tiled=True),
        lax.all_gather(norm1_bias, "wsh", axis=0, tiled=True),
        lax.all_gather(w_query, "wsh", axis=0, tiled=True),
        lax.all_gather(b_query, "wsh", axis=0, tiled=True),
        lax.all_gather(w_key, "wsh", axis=0, tiled=True),
        lax.all_gather(w_value, "wsh", axis=0, tiled=True),
        lax.all_gather(b_value, "wsh", axis=0, tiled=True),
        lax.all_gather(w_out, "wsh", axis=0, tiled=True),
        lax.all_gather(b_out, "wsh", axis=0, tiled=True),
        lax.all_gather(norm2_gain, "wsh", axis=0, tiled=True),
        lax.all_gather(norm2_bias, "wsh", axis=0, tiled=True),
        lax.all_gather(w_up, "wsh", axis=0, tiled=True),
        lax.all_gather(b_up, "wsh", axis=0, tiled=True),
        lax.all_gather(w_down, "wsh", axis=0, tiled=True),
        lax.all_gather(b_down, "wsh", axis=0, tiled=True),
    )
    row_count = tokens.shape[1]
    model_width = tokens.shape[2]
    head_dim = model_width // HEADS
    score_scale = head_dim ** (-0.5)
    first_gain = gain_one.astype(jnp.float32)
    first_bias = bias_one.astype(jnp.float32)
    second_gain = gain_two.astype(jnp.float32)
    second_bias = bias_two.astype(jnp.float32)
    inputs = tokens[0].astype(jnp.float32)
    doc_ends = jnp.cumsum(doc_lengths[0])
    own_ids = doc_of(
        lax.axis_index("ctx") * row_count + jnp.arange(row_count, dtype=jnp.int32), doc_ends
    )
    normed_one = norm_rows(inputs, first_gain, first_bias).astype(jnp.bfloat16)
    queries = (dot_plain(normed_one, query_w) + query_b.astype(jnp.float32)).astype(jnp.bfloat16)
    key_rows = dot_plain(normed_one, key_w).astype(jnp.bfloat16)
    values = (dot_plain(normed_one, value_w) + value_b.astype(jnp.float32)).astype(jnp.bfloat16)
    key_all, value_all = (
        lax.all_gather(key_rows, "ctx", axis=0, tiled=True),
        lax.all_gather(values, "ctx", axis=0, tiled=True),
    )
    total_rows = key_all.shape[0]
    key_block = math.gcd(total_rows, 2048)
    block_count = total_rows // key_block
    key_stack = key_all.reshape(block_count, key_block, HEADS, head_dim)
    value_stack = value_all.reshape(block_count, key_block, HEADS, head_dim)
    id_stack = doc_of(jnp.arange(total_rows, dtype=jnp.int32), doc_ends).reshape(
        block_count, key_block
    )
    query_heads = queries.reshape(row_count, HEADS, head_dim)

    def lse_step(running, block_in):
        run_max, run_sum = running
        key_heads, key_ids = block_in
        scores = masked_scores(query_heads, key_heads, own_ids, key_ids, score_scale)
        new_max = jnp.maximum(run_max, jnp.max(scores, axis=-1))
        new_sum = run_sum * jnp.exp(run_max - new_max) + jnp.sum(
            jnp.exp(scores - new_max[:, :, None]), axis=-1
        )
        return ((new_max, new_sum), None)

    start_max = jnp.full((HEADS, row_count), NEG_START, jnp.float32)
    (final_max, final_sum), unused = lax.scan(
        lse_step, (start_max, jnp.zeros_like(start_max)), (key_stack, id_stack)
    )
    log_total = final_max + jnp.log(final_sum)

    def out_step(running, block_in):
        key_heads, value_heads, key_ids = block_in
        scores = masked_scores(query_heads, key_heads, own_ids, key_ids, score_scale)
        attn_prob = jnp.exp(scores - log_total[:, :, None]).astype(jnp.bfloat16)
        return (
            running
            + jnp.einsum(
                "hqk,khd->qhd", attn_prob, value_heads, preferred_element_type=jnp.float32
            ),
            None,
        )

    attn_sum, unused = lax.scan(
        out_step,
        jnp.zeros((row_count, HEADS, head_dim), jnp.float32),
        (key_stack, value_stack, id_stack),
    )
    attended = attn_sum.reshape(row_count, model_width).astype(jnp.bfloat16)
    middle = inputs + dot_plain(attended, out_w) + out_b.astype(jnp.float32)
    normed_two = norm_rows(middle, second_gain, second_bias).astype(jnp.bfloat16)
    hidden = dot_plain(normed_two, up_w) + up_b.astype(jnp.float32)
    active = jax.nn.gelu(hidden, approximate=True).astype(jnp.bfloat16)
    output = middle + dot_plain(active, down_w) + down_b.astype(jnp.float32)
    top_grad = out_grad[0]
    top_float = top_grad.astype(jnp.float32)
    grad_down_w = dot_left(active, top_grad)
    grad_down_b = jnp.sum(top_float, axis=0)
    grad_active = dot_right(top_grad, down_w)
    unused, gelu_pull = jax.vjp(partial(jax.nn.gelu, approximate=True), hidden)
    grad_hidden = gelu_pull(grad_active)[0].astype(jnp.bfloat16)
    grad_up_w = dot_left(normed_two, grad_hidden)
    grad_up_b = jnp.sum(grad_hidden.astype(jnp.float32), axis=0)
    grad_normed_two = dot_right(grad_hidden, up_w)
    unused, second_pull = jax.vjp(norm_rows, middle, second_gain, second_bias)
    grad_middle, grad_gain_two, grad_bias_two = second_pull(grad_normed_two)
    grad_middle = grad_middle + top_float
    grad_branch = grad_middle.astype(jnp.bfloat16)
    grad_out_w = dot_left(attended, grad_branch)
    grad_out_b = jnp.sum(grad_branch.astype(jnp.float32), axis=0)
    grad_attended = dot_right(grad_branch, out_w).astype(jnp.bfloat16)
    grad_heads = grad_attended.reshape(row_count, HEADS, head_dim)
    row_delta = jnp.sum(grad_heads.astype(jnp.float32) * attn_sum, axis=-1)
    head_delta = row_delta.T
    query_start = jnp.zeros((row_count, HEADS, head_dim), jnp.float32)

    def full_step(grad_query, block_in):
        key_heads, value_heads, key_ids = block_in
        scores = masked_scores(query_heads, key_heads, own_ids, key_ids, score_scale)
        attn_prob = jnp.exp(scores - log_total[:, :, None])
        grad_prob = jnp.einsum(
            "qhd,khd->hqk", grad_heads, value_heads, preferred_element_type=jnp.float32
        )
        grad_score = (attn_prob * (grad_prob - head_delta[:, :, None])).astype(jnp.bfloat16)
        grad_query = grad_query + jnp.einsum(
            "hqk,khd->qhd", grad_score, key_heads, preferred_element_type=jnp.float32
        )
        grad_key = (
            jnp.einsum("hqk,qhd->khd", grad_score, query_heads, preferred_element_type=jnp.float32)
            * score_scale
        )
        grad_value = jnp.einsum(
            "hqk,qhd->khd",
            attn_prob.astype(jnp.bfloat16),
            grad_heads,
            preferred_element_type=jnp.float32,
        )
        return (
            grad_query,
            (grad_key.reshape(key_block, model_width), grad_value.reshape(key_block, model_width)),
        )

    grad_query, key_terms = lax.scan(full_step, query_start, (key_stack, value_stack, id_stack))
    key_grad, value_grad = (
        lax.psum_scatter(
            key_terms[0].reshape(total_rows, model_width), "ctx", scatter_dimension=0, tiled=True
        ),
        lax.psum_scatter(
            key_terms[1].reshape(total_rows, model_width), "ctx", scatter_dimension=0, tiled=True
        ),
    )
    grad_query_rows = (
        (grad_query * score_scale).reshape(row_count, model_width).astype(jnp.bfloat16)
    )
    grad_key_rows = key_grad.astype(jnp.bfloat16)
    grad_value_rows = value_grad.astype(jnp.bfloat16)
    grad_query_w = dot_left(normed_one, grad_query_rows)
    grad_query_b = jnp.sum(grad_query_rows.astype(jnp.float32), axis=0)
    grad_key_w = dot_left(normed_one, grad_key_rows)
    grad_value_w = dot_left(normed_one, grad_value_rows)
    grad_value_b = jnp.sum(grad_value_rows.astype(jnp.float32), axis=0)
    grad_normed_one = (
        dot_right(grad_query_rows, query_w)
        + dot_right(grad_key_rows, key_w)
        + dot_right(grad_value_rows, value_w)
    )
    unused, first_pull = jax.vjp(norm_rows, inputs, first_gain, first_bias)
    grad_inputs, grad_gain_one, grad_bias_one = first_pull(grad_normed_one)
    grad_inputs = grad_inputs + grad_middle
    (
        share_gain_one,
        share_bias_one,
        share_query_w,
        share_query_b,
        share_key_w,
        share_value_w,
        share_value_b,
        share_out_w,
        share_out_b,
        share_gain_two,
        share_bias_two,
        share_up_w,
        share_up_b,
        share_down_w,
        share_down_b,
    ) = (
        lax.psum_scatter(
            grad_gain_one.astype(jnp.bfloat16), "wsh", scatter_dimension=0, tiled=True
        ).astype(jnp.float32),
        lax.psum_scatter(
            grad_bias_one.astype(jnp.bfloat16), "wsh", scatter_dimension=0, tiled=True
        ).astype(jnp.float32),
        lax.psum_scatter(
            grad_query_w.astype(jnp.bfloat16), "wsh", scatter_dimension=0, tiled=True
        ).astype(jnp.float32),
        lax.psum_scatter(
            grad_query_b.astype(jnp.bfloat16), "wsh", scatter_dimension=0, tiled=True
        ).astype(jnp.float32),
        lax.psum_scatter(
            grad_key_w.astype(jnp.bfloat16), "wsh", scatter_dimension=0, tiled=True
        ).astype(jnp.float32),
        lax.psum_scatter(
            grad_value_w.astype(jnp.bfloat16), "wsh", scatter_dimension=0, tiled=True
        ).astype(jnp.float32),
        lax.psum_scatter(
            grad_value_b.astype(jnp.bfloat16), "wsh", scatter_dimension=0, tiled=True
        ).astype(jnp.float32),
        lax.psum_scatter(
            grad_out_w.astype(jnp.bfloat16), "wsh", scatter_dimension=0, tiled=True
        ).astype(jnp.float32),
        lax.psum_scatter(
            grad_out_b.astype(jnp.bfloat16), "wsh", scatter_dimension=0, tiled=True
        ).astype(jnp.float32),
        lax.psum_scatter(
            grad_gain_two.astype(jnp.bfloat16), "wsh", scatter_dimension=0, tiled=True
        ).astype(jnp.float32),
        lax.psum_scatter(
            grad_bias_two.astype(jnp.bfloat16), "wsh", scatter_dimension=0, tiled=True
        ).astype(jnp.float32),
        lax.psum_scatter(
            grad_up_w.astype(jnp.bfloat16), "wsh", scatter_dimension=0, tiled=True
        ).astype(jnp.float32),
        lax.psum_scatter(
            grad_up_b.astype(jnp.bfloat16), "wsh", scatter_dimension=0, tiled=True
        ).astype(jnp.float32),
        lax.psum_scatter(
            grad_down_w.astype(jnp.bfloat16), "wsh", scatter_dimension=0, tiled=True
        ).astype(jnp.float32),
        lax.psum_scatter(
            grad_down_b.astype(jnp.bfloat16), "wsh", scatter_dimension=0, tiled=True
        ).astype(jnp.float32),
    )
    totals = lax.psum(
        (
            share_gain_one,
            share_bias_one,
            share_query_w,
            share_query_b,
            share_key_w,
            share_value_w,
            share_value_b,
            share_out_w,
            share_out_b,
            share_gain_two,
            share_bias_two,
            share_up_w,
            share_up_b,
            share_down_w,
            share_down_b,
        ),
        "ctx",
    )
    return (
        output.astype(jnp.bfloat16)[None],
        grad_inputs.astype(jnp.bfloat16)[None],
        totals[0],
        totals[1],
        totals[2],
        totals[3],
        totals[4],
        totals[5],
        totals[6],
        totals[7],
        totals[8],
        totals[9],
        totals[10],
        totals[11],
        totals[12],
        totals[13],
        totals[14],
    )


MESH = pl.DeviceIdType.MESH
F32 = jnp.float32
BF = jnp.bfloat16
GROUPS = 4
LANES = 128


def flip(value, mask):
    return ((value // 2 + mask // 2) % 2) * 2 + (value + mask) % 2


def dot_nn(left, right):
    return lax.dot_general(left, right, (((1,), (0,)), ((), ())), preferred_element_type=F32)


def dot_nt(left, right):
    return lax.dot_general(left, right, (((1,), (1,)), ((), ())), preferred_element_type=F32)


def dot_tn(left, right):
    return lax.dot_general(left, right, (((0,), (0,)), ((), ())), preferred_element_type=F32)


def unit_rows(inputs):
    row_mean = jnp.mean(inputs, axis=-1, keepdims=True)
    centred = inputs - row_mean
    variance = jnp.mean(centred * centred, axis=-1, keepdims=True)
    scale = lax.rsqrt(variance + EPS)
    return centred * scale, scale


def unit_rows_back(grad_normed, unit, scale, gain):
    grad_unit = grad_normed * gain
    return scale * (
        grad_unit
        - jnp.mean(grad_unit, axis=-1, keepdims=True)
        - unit * jnp.mean(grad_unit * unit, axis=-1, keepdims=True)
    )


def rows_sum(values):
    return jnp.sum(values, axis=0, keepdims=True)


def sum_bf(*values):
    return sum([one.astype(F32) for one in values]).astype(BF)


class Wires:
    def __init__(self, send_sems, recv_sems):
        self.send_sems, self.recv_sems, self.used, self.started = send_sems, recv_sems, 0, []

    def take(self, count=1):
        first = self.used
        self.used += count
        return first

    def copy(self, index, source, target, device):
        return pltpu.make_async_remote_copy(
            src_ref=source,
            dst_ref=target,
            send_sem=self.send_sems.at[index],
            recv_sem=self.recv_sems.at[index],
            device_id=device,
            device_id_type=MESH,
        )

    def send(self, source, target, device):
        one = self.copy(self.take(), source, target, device)
        one.start()
        self.started.append((one, None))
        return one

    def later(self, one, when=None):
        self.started.append((one, when))
        return one

    def plan(self, source, target, device):
        return self.later(self.copy(self.take(), source, target, device))

    def drain(self):
        for one, when in self.started:
            if when is None:
                one.wait_send()
            else:
                pl.when(when)(one.wait_send)


ORDER = (
    "up_grad", "ph_combine", "down_grad", "A_e0", "y_part", "wait_ph", "D_xout", "ln2", "sums",
    "out_grad", "A_e1", "bo0", "bo1", "bo2", "A_e2", "A2a", "up_xin", "bo3", "kv_out", "go_combine",
    "bw0", "bw1", "D_in", "A2b", "D2a", "py_combine", "A3", "bw2", "up_in", "A_out", "D2b", "bw3",
    "U2a", "go_out", "D3", "D_turn", "kv_in", "U2b", "U3", "qkv_grad", "A_turn", "go_in", "early",
    "D_o1", "D_i1", "gq_comb", "U_turn", "h1_part", "gq_fin", "A_i1", "U_o1", "U_i1", "go_turn",
    "A_o1", "q_start", "U_i2", "H2a", "q_i1", "D_i2", "A_i2", "q_o1", "go_done", "D_i3",
    "layer_out", "H3", "h1_e2", "H2b", "A_i3", "U_i3", "q_i2", "early2", "h1_fin", "q_i3", "small",
    "go_fin", "fin",
)


def layer_kernel(sizes, names, *refs):
    n_ctx, n_doc, R, D, S, FS = sizes
    r = dict(zip(names, refs, strict=True))
    G = n_ctx // GROUPS
    last = GROUPS - 1
    half = GROUPS * R
    c = lax.axis_index("ctx")
    w = lax.axis_index("wsh")
    hg, px = c // G, c % G

    def zdev(group):
        return {"ctx": group * G + px, "wsh": w}

    def wdev(index):
        return {"ctx": c, "wsh": index}

    xdev = {"ctx": hg * G + 1 - px, "wsh": w}
    left, right = zdev((hg + last) % GROUPS), zdev((hg + 1) % GROUPS)
    w1, w2, w3 = flip(w, 1), flip(w, 2), flip(w, 3)
    sib, across, diag = wdev(w1), wdev(w2), wdev(w3)
    wires = Wires(r["send_sems"], r["recv_sems"])
    lane = lax.broadcasted_iota(jnp.int32, (1, LANES), 1)
    low_half = lane < LANES // 2

    def pick(table):
        return sum([jnp.where(hg == i, one, 0) for i, one in enumerate(table)])

    def by_distance(step):
        return (
            jnp.where(step == 0, pick((3, 3, 0, 0)), 0)
            + jnp.where(step == 1, pick((2, 0, 3, 1)), 0)
            + jnp.where(step == 2, pick((1, 2, 1, 2)), 0)
            + jnp.where(step == 3, hg, 0)
        )

    local = r["local_sems"]

    def fetch(index, source, target):
        one = pltpu.make_async_copy(source, target, local.at[index])
        one.start()
        return one

    tok_in = fetch(0, r["tok"], r["x_s"].at[hg])
    qkv_in = [fetch(1 + i, r[name], r["win_s"].at[i]) for i, name in enumerate(("wq", "wk", "wv"))]
    dy_in = fetch(4, r["dy"], r["dy_s"].at[w])
    wo_in = [
        fetch(5, r["wout"].at[pl.ds(0, LANES)], r["wo_s"].at[w, pl.ds(0, LANES)]),
        fetch(6, r["wout"].at[pl.ds(LANES, S - LANES)], r["wo_s"].at[w, pl.ds(S, S - LANES)]),
    ]
    wu_in = fetch(7, r["wup"].at[:, pl.ds(pl.multiple_of(w * FS, FS), FS)], r["wu_s"].at[w])
    wd_in = fetch(8, r["wdown"], r["wd_s"])

    barrier = pltpu.get_barrier_semaphore()
    ctx_peers = [{"ctx": (c + i) % n_ctx, "wsh": w} for i in range(1, n_ctx)]
    partners = ctx_peers + [sib, across, diag]
    for partner in partners:
        pl.semaphore_signal(barrier, inc=1, device_id=partner, device_id_type=MESH)

    pl.semaphore_wait(barrier, len(partners))

    class Gather:
        def __init__(self, slot):
            self.slot = slot
            self.to_across = wires.send(slot(w), slot(w), across)
            self.to_sib = wires.send(slot(w), slot(w), sib)

        def relay(self):
            self.to_across.wait_recv()
            self.on = wires.send(self.slot(w2), self.slot(w2), sib)

        def finish(self):
            self.to_sib.wait_recv()
            self.on.wait_recv()

    class Reduce:
        def __init__(self, part, recv):
            self.part, self.recv = part, recv
            self.a = wires.plan(part(w3), recv.at[0], sib)
            self.b = wires.plan(part(w1), recv.at[1], sib)
            self.c = wires.plan(recv.at[3], recv.at[2], across)

        def start(self):
            self.a.start()
            self.b.start()

        def combine(self):
            self.a.wait_recv()
            self.recv[3] = sum_bf(self.part(w2)[...], self.recv[0])
            self.c.start()

        def finish(self):
            self.b.wait_recv()
            self.c.wait_recv()
            return (
                self.part(w)[...].astype(F32)
                + self.recv[1].astype(F32)
                + self.recv[2].astype(F32)
            )

    class LineSum:
        def __init__(self, part, recv):
            self.part, self.recv = part, recv
            self.first_at = wires.take(6)
            for i in range(3):
                wires.later(self.message(i, True), hg > i)
                wires.later(self.message(i, False), hg < last - i)

        def message(self, i, leftward):
            block, slot = (i, i) if leftward else (last - i, 3 + i)
            return wires.copy(
                self.first_at + slot, self.part(block), self.recv.at[slot], left if leftward else right
            )

        def ends_block(self, block):
            for i in range(2):

                @pl.when((hg == last) & (block == i))
                def _():
                    self.message(i, True).start()

                @pl.when((hg == 0) & (block == last - i))
                def _():
                    self.message(i, False).start()

        def ends(self, which=(0, 1, 2)):
            for i in which:

                @pl.when(hg == last)
                def _():
                    self.message(i, True).start()

                @pl.when(hg == 0)
                def _():
                    self.message(i, False).start()

        def pass_on(self, position, i, leftward):
            @pl.when(hg == position)
            def _():
                one = self.message(i, leftward)
                one.wait_recv()
                block, slot = (i, i) if leftward else (last - i, 3 + i)
                self.part(block)[...] = sum_bf(self.part(block)[...], self.recv[slot])
                one.start()

        def second(self, which=(0, 1)):
            for i in which:
                self.pass_on(2, i, True)
                self.pass_on(1, i, False)

        def third(self):
            self.pass_on(1, 0, True)
            self.pass_on(2, 0, False)

        def final(self, put):
            for position in range(GROUPS):

                @pl.when(hg == position)
                def _():
                    total = self.part(position)[...].astype(F32)
                    if position < last:
                        self.message(position, True).wait_recv()
                        total = total + self.recv[position].astype(F32)
                    if position > 0:
                        self.message(last - position, False).wait_recv()
                        total = total + self.recv[3 + last - position].astype(F32)
                    put(total)

    class LineGather:
        def __init__(self, slot, to_x, own=None):
            self.slot, self.to_x, self.own = slot, to_x, own
            self.first_at = wires.take(6)
            self.x_at = wires.take(GROUPS) if to_x else None
            for d in (1, 2, 3):
                wires.later(self.message(d, 0), (hg >= d - 1) & (hg < last))
                wires.later(self.message(d, 1), (hg + d - 1 <= last) & (hg > 0))
            if to_x:
                for b in range(GROUPS):
                    wires.later(self.x_message(b))

        def message(self, d, side):
            block = (hg + GROUPS + (1 - d) * (1 - 2 * side)) % GROUPS
            device = zdev((hg + GROUPS + 1 - 2 * side) % GROUPS)
            first = self.own is not None and isinstance(d, int) and d == 1
            source = self.own if first else self.slot(block)
            return wires.copy(self.first_at + 3 * side + d - 1, source, self.slot(block), device)

        def x_message(self, block):
            return wires.copy(self.x_at + block, self.slot(block), self.slot(block), xdev)

        def start(self):
            pl.when(hg < last)(self.message(1, 0).start)
            pl.when(hg > 0)(self.message(1, 1).start)
            if self.to_x:
                self.x_message(hg).start()

        def arrived(self, d, side, then=None):
            block = (hg + GROUPS - d * (1 - 2 * side)) % GROUPS
            here = jnp.where(side == 0, (hg >= d).astype(jnp.int32), (hg + d <= last).astype(jnp.int32))
            onward = here * jnp.where(side == 0, (hg < last).astype(jnp.int32), (hg > 0).astype(jnp.int32))

            @pl.when(here == 1)
            def _():
                wires.copy(
                    self.first_at + 3 * side + d - 1, self.slot(block), self.slot(block), left
                ).wait_recv()

            @pl.when(onward == 1)
            def _():
                self.message(d + 1, side).start()

            @pl.when(here == 1)
            def _():
                if self.to_x:
                    self.x_message(block).start()
                if then is not None:
                    then(block)

        def inner(self, d):
            self.arrived(d, jnp.where(hg < 2, 1, 0))

        def outer(self, d):
            self.arrived(d, jnp.where(hg < 2, 0, 1))

        def done(self):
            for b in range(GROUPS):
                self.x_message(b).wait_recv()

    x_s, h1_s, q_s, kv_s = r["x_s"], r["h1_s"], r["q_s"], r["kv_s"]
    rows_two = R // 2
    tokens = [
        LineGather(
            lambda b, j=j: x_s.at[b, pl.ds(j * rows_two, rows_two)],
            False,
            r["tok"].at[pl.ds(j * rows_two, rows_two)],
        )
        for j in (0, 1)
    ]
    for one in tokens:
        one.start()
    for one in qkv_in:
        one.wait()
    own_w = pl.ds(pl.multiple_of(w * S, S), S)
    win, wq_s = r["win_s"], r["wq_s"]
    for g in range(GROUPS):

        @pl.when(hg == g)
        def _():
            a = g * S
            wq_s[own_w, 0:S] = win[0, :, a : a + S]
            wq_s[own_w, S : 2 * LANES] = jnp.zeros((S, 2 * LANES - S), BF)
            wq_s[own_w, 2 * LANES : 2 * LANES + S] = win[1, :, a : a + S]
            wq_s[own_w, 2 * LANES + S : 4 * LANES] = win[2, :, a + LANES : a + S]
            wq_s[own_w, 4 * LANES : 5 * LANES] = win[2, :, a : a + LANES]

    par_s = r["par_s"]
    par_s[w] = jnp.zeros((8, 2 * LANES), F32)
    for i, name in enumerate(("n1g", "n1b", "bq", "bv", "bo", "n2g", "n2b", "bd")):
        par_s[w, i : i + 1, 0:S] = r[name][...].astype(F32)[None, :]
    r["wo_s"][:, LANES:S, :] = jnp.zeros((GROUPS, S - LANES, D), BF)
    ws_all = Gather(lambda i: wq_s.at[pl.ds(pl.multiple_of(i * S, S), S)])
    par_all = Gather(lambda i: par_s.at[i])
    for one in wo_in:
        one.wait()
    dy_in.wait()
    wo_s, dy_s, wu_s = r["wo_s"], r["dy_s"], r["wu_s"]
    wo_top = Gather(lambda i: wo_s.at[i, pl.ds(0, LANES)])
    wo_low = Gather(lambda i: wo_s.at[i, pl.ds(S, S - LANES)])
    dy_all = Gather(lambda i: dy_s.at[i])
    up_sends = [
        wires.send(
            r["wup"].at[:, pl.ds(pl.multiple_of(flip(w, k) * FS, FS), FS)],
            wu_s.at[w],
            wdev(flip(w, k)),
        )
        for k in (2, 3, 1)
    ]
    inner_side = jnp.where(hg < 2, 1, 0)
    tokens[0].arrived(1, inner_side)
    tokens[0].arrived(1, 1 - inner_side)
    par_all.relay()
    ws_all.relay()
    tokens[1].arrived(1, inner_side)
    tokens[1].arrived(1, 1 - inner_side)
    par_all.finish()

    pars = jnp.concatenate([par_s[i][:, :S] for i in range(GROUPS)], axis=1)
    gain_one, bias_one, out_b, gain_two, bias_two, down_b = [
        pars[i : i + 1] for i in (0, 1, 4, 5, 6, 7)
    ]
    up_b = r["bup"][...].astype(F32)[None, :]
    own_par = par_s[hg]
    v_tile, v_last = own_par[3:4, :LANES], own_par[3:4, LANES:]
    qkv_b = jnp.concatenate(
        [own_par[2:3, :], jnp.zeros((1, LANES), F32), pltpu.roll(v_last, LANES // 2, 1), v_tile],
        axis=1,
    )
    ws_all.finish()
    tok_in.wait()

    kv_first = wires.take(2 * GROUPS)

    def kv_copy(block, j):
        rows = pl.ds(pl.multiple_of(block * R + j * rows_two, rows_two), rows_two)
        return wires.copy(
            kv_first + 2 * block + j, kv_s.at[0, rows], kv_s.at[1, rows], xdev
        )

    def project(block, j):
        rows = pl.ds(pl.multiple_of(j * rows_two, rows_two), rows_two)
        unit, unused = unit_rows(x_s[block, rows, :].astype(F32))
        normed = (unit * gain_one + bias_one).astype(BF)
        h1_s[block, rows, :] = normed
        qkv = dot_nn(normed, wq_s[...]) + qkv_b
        queries = qkv[:, : 2 * LANES].astype(BF).astype(F32) * 0.125
        q_s[0, block, rows, :] = jnp.where(low_half, queries[:, :LANES], 0.0).astype(BF)
        q_s[1, block, rows, :] = jnp.where(low_half, 0.0, queries[:, :LANES]).astype(BF)
        q_s[2, block, rows, :] = queries[:, LANES:].astype(BF)
        kv_rows = pl.ds(pl.multiple_of(block * R + j * rows_two, rows_two), rows_two)
        kv_s[0, kv_rows, :] = qkv[:, 2 * LANES :].astype(BF)
        kv_copy(block, j).start()

    def near_project(i, carry):
        away = jnp.where(i < 2, 0, jnp.where(i < 4, 1, 3)) * (1 - 2 * (1 - inner_side))
        block = (hg + 2 * GROUPS + jnp.where(i < 4, away, (1 - 2 * inner_side))) % GROUPS

        @pl.when((i < 4) | ((hg > 0) & (hg < last)))
        def _():
            project(block, i % 2)

        return carry

    lax.fori_loop(0, 6, near_project, 0)

    def far_project(i, carry):
        d = i + 2
        block = (hg + GROUPS - d * (1 - 2 * inner_side)) % GROUPS
        for j, one in enumerate(tokens):
            one.arrived(d, inner_side)

            @pl.when(jnp.where(hg < 2, hg + d <= last, hg >= d))
            def _():
                project(block, j)

        return carry

    lax.fori_loop(0, 2, far_project, 0)
    wo_top.relay()
    wo_low.relay()
    doc_ends = []
    for i in range(n_doc):
        doc_ends.append(r["doc"][0, i] + (doc_ends[-1] if i else 0))

    def doc_ids(positions):
        return sum([(positions >= end).astype(jnp.int32) for end in doc_ends])

    key_at = lax.broadcasted_iota(jnp.int32, (1, half), 1)
    key_block = sum([(key_at >= i * R).astype(jnp.int32) for i in range(1, GROUPS)])
    key_base = key_at + key_block * (R * (G - 1))
    key_ids = [doc_ids(key_base + px * R), doc_ids(key_base + (1 - px) * R)]
    KT, VT, KO = (0, 0, LANES), (2 * LANES, 2 * LANES, LANES), (0, 0, LANES)
    e_s, li_s, oa_s, os_s, or_s = r["e_s"], r["li_s"], r["oa_s"], r["os_s"], r["or_s"]
    of_s = r["of_s"]

    def pack(target, first, final):
        target[0:R, :] = first.astype(BF)
        turned = pltpu.roll(final[rows_two:, :], LANES // 2, 1)
        target[R : R + rows_two, :] = jnp.where(low_half, turned, final[:rows_two, :]).astype(BF)

    def unpack(source, target):
        target[:, :LANES] = source[0:R, :]
        both = source[R : R + rows_two, :].astype(F32)
        target[0:rows_two, LANES:] = jnp.where(low_half, 0.0, both).astype(BF)
        turned = pltpu.roll(both, LANES // 2, 1)
        target[rows_two:, LANES:] = jnp.where(low_half, 0.0, turned).astype(BF)

    class Turn:
        def __init__(self, source, target):
            self.source, self.target = source, target
            self.first_at = wires.take(GROUPS)
            for i in (1, 2, 3):
                wires.later(self.message((hg + i) % GROUPS))

        def message(self, block):
            index = self.first_at + (block - hg + GROUPS) % GROUPS
            return wires.copy(index, self.source.at[block], self.target.at[hg], zdev(block))

        def arrived(self, block):
            index = self.first_at + (hg - block + GROUPS) % GROUPS
            wires.copy(index, self.target.at[block], self.target.at[block], left).wait_recv()

    on_s = r["on_s"]
    o_turn = Turn(os_s, on_s)

    def row_ids_of(block):
        row_at = (block * G + px) * R + lax.broadcasted_iota(jnp.int32, (R, 1), 0)
        return doc_ids(row_at)

    def attend_side(block, side):
        row_ids = row_ids_of(block)
        same = row_ids == key_ids[side]
        scores = [
            jnp.where(
                same, dot_nt(q_s[h, block], kv_s[side, :, KT[h] : KT[h] + LANES]), NEG_START
            )
            for h in range(3)
        ]
        tops = [jnp.max(one, axis=-1, keepdims=True) for one in scores]
        weights = [jnp.exp(one - top) for one, top in zip(scores, tops, strict=True)]
        mixed = []
        for h in range(3):
            rounded = weights[h].astype(BF)
            e_s[h, block, side] = rounded
            mixed.append(dot_nn(rounded, kv_s[side, :, VT[h] : VT[h] + LANES]))
        totals = [jnp.sum(one, axis=-1, keepdims=True) for one in weights]
        return tops, totals, mixed

    def attend_own(block, carry):
        tops, totals, mixed = attend_side(block, 0)
        for h in range(3):
            li_s[0, h, block] = jnp.broadcast_to(tops[h], (R, LANES))
            li_s[1, h, block] = jnp.broadcast_to(totals[h], (R, LANES))
            of_s[h, block] = mixed[h]
        return carry

    lax.fori_loop(0, GROUPS, attend_own, 0)
    dy_all.relay()
    for b in range(GROUPS):
        for j in (0, 1):
            kv_copy(b, j).wait_recv()
            wires.later(kv_copy(b, j))

    def attend(step, carry):
        block = by_distance(step)
        tops, totals, mixed = attend_side(block, 1)
        outs = []
        for h in range(3):
            top, total = tops[h], totals[h]
            own_top = li_s[0, h, block]
            both_top = jnp.maximum(own_top, top)
            own_part, part = jnp.exp(own_top - both_top), jnp.exp(top - both_top)
            inverse = 1.0 / (li_s[1, h, block] * own_part + total * part)
            own_part, part = own_part * inverse, part * inverse
            li_s[0, h, block] = own_part
            li_s[1, h, block] = part
            outs.append(of_s[h, block] * own_part + mixed[h] * part)
        first = jnp.where(low_half, outs[0], outs[1])
        final = jnp.where(low_half, 0.0, outs[2])
        oa_s[block, :, :LANES] = first
        oa_s[block, :, LANES:] = final
        pack(os_s.at[block], first, final)

        @pl.when(step < last)
        def _():
            o_turn.message(block).start()

        return carry

    lax.fori_loop(0, GROUPS, attend, 0)
    unpack(os_s.at[hg], or_s.at[hg])
    dy_all.finish()
    wd_in.wait()
    wd_s, dkv_s = r["wd_s"], r["dkv_s"]

    def top_rows(slot):
        return slot // 2, pl.ds(pl.multiple_of((slot % 2) * R, R), R)

    def top_part(slot, carry):
        dkv_s[top_rows(slot)] = dot_nt(dy_s[slot], wd_s[...])
        return carry

    lax.fori_loop(0, GROUPS, top_part, 0)
    wo_top.finish()
    wo_low.finish()
    for i in (1, 2, 3):
        there = (hg + i) % GROUPS
        o_turn.arrived(there)
        unpack(on_s.at[there], or_s.at[there])

    middle = x_s[hg].astype(F32) + out_b
    for i in range(GROUPS):
        middle += dot_nn(or_s[i], wo_s[i])
    x1_s, h2_s, g_s, da_s = r["x1_s"], r["h2_s"], r["g_s"], r["da_s"]
    x1_s[...] = middle
    unit_two, scale_two = unit_rows(middle)
    h2_s[w] = (unit_two * gain_two + bias_two).astype(BF)
    halves = [pl.ds(0, rows_two), pl.ds(rows_two, rows_two)]
    h2_all = [Gather(lambda i, part=part: h2_s.at[i, part]) for part in halves]
    wu_in.wait()
    for one in up_sends:
        one.wait_recv()
    ph_s, hr_s = r["ph_s"], r["hr_s"]
    ph = [
        Reduce(lambda i, part=part: ph_s.at[i, part], hr_s.at[k]) for k, part in enumerate(halves)
    ]

    def up_and_back(slot, start, count):
        rows = pl.ds(start, count)
        hidden = dot_nn(h2_s[slot, rows, :], wu_s[...].reshape(D, FS)) + up_b
        square = hidden * hidden
        inner = math.sqrt(2.0 / math.pi) * (hidden + 0.044715 * (square * hidden))
        bent = jnp.tanh(inner)
        g_s[slot, rows, :] = (0.5 * hidden * (1.0 + bent)).astype(BF)
        slope = 0.5 * (1.0 + bent) + 0.5 * hidden * (1.0 - bent * bent) * (
            math.sqrt(2.0 / math.pi) * (1.0 + 3.0 * 0.044715 * square)
        )
        top_at = pl.ds(pl.multiple_of((slot % 2) * R + start, rows_two), count)
        grad_hidden = (dkv_s[slot // 2, top_at, :] * slope).astype(BF)
        da_s[slot, rows, :] = grad_hidden
        ph_s[slot, rows, :] = dot_nt(grad_hidden, wu_s[...].reshape(D, FS)).astype(BF)

    def mlp_near(j, carry):
        @pl.when(j == 1)
        def _():
            for one in h2_all:
                one.to_sib.wait_recv()

        up_and_back(flip(w, j), 0, R)
        return carry

    lax.fori_loop(0, 2, mlp_near, 0)
    for one in ph:
        one.b.start()
    on_copies = [
        wires.plan(h2_s.at[w2, part], h2_s.at[w2, part], sib) for part in halves
    ]
    for k in (0, 1):
        h2_all[k].to_across.wait_recv()
        on_copies[k].start()
        up_and_back(w2, k * rows_two, rows_two)
        if k == 1:
            ph[0].combine()
        on_copies[k].wait_recv()
        up_and_back(w3, k * rows_two, rows_two)
        ph[k].a.start()

    gus_s, gas_s, gds_s, py_s = r["gus_s"], r["gas_s"], r["gds_s"], r["py_s"]
    cols = gas_s.shape[1]

    def up_grad(i, carry):
        at = pl.ds(pl.multiple_of(i * 2 * S, 2 * S), 2 * S)
        gus_s[pl.ds(2 * i, 2)] = (
            dot_tn(h2_s[:, :, at].reshape(half, 2 * S), da_s[...].reshape(half, FS))
            .astype(BF)
            .reshape(2, 2, S // 2, FS)
        )
        return carry

    def down_grad(i, carry):
        at = pl.ds(pl.multiple_of(i * 256, 256), 256)
        both = dot_tn(g_s[:, :, at].reshape(half, 256), dy_s[...].reshape(half, D)).astype(BF)
        gas_s[at, :] = both[:, :cols]
        gds_s[at, :] = both[:, cols:]
        return carry

    def y_part(j, carry):
        py_s[j] = dot_nn(g_s[j], wd_s[...]).astype(BF)
        return carry

    class Spread:
        def __init__(self, part, recv, slot, to_x):
            self.sum = LineSum(part, recv)
            self.gather = LineGather(slot, to_x)

        def turn(self):
            def put(total):
                self.gather.slot(hg)[...] = total.astype(BF)

            self.sum.final(put)
            self.gather.start()

    class Share:
        def __init__(self, rows):
            self.rows = rows
            self.at = wires.take(n_ctx)
            for i in range(1, n_ctx):
                wires.later(self.message(i))

        def message(self, i):
            return wires.copy(self.at + i, self.rows.at[c], self.rows.at[c], ctx_peers[i - 1])

        def start(self):
            for i in range(1, n_ctx):
                self.message(i).start()

        def total(self):
            for i in range(1, n_ctx):
                wires.copy(self.at + i, self.rows.at[c], self.rows.at[c], left).wait_recv()
            return sum([self.rows[i] for i in range(n_ctx)])

    n = S // 2
    n_down = FS // 8
    quarter = n // GROUPS
    ga_f, gd_f, gu_s, up_f = r["gda"], r["gdb"], r["gu_s"], r["gup"]
    mine = pl.ds(pl.multiple_of(px * n, 8), n)
    theirs = pl.ds(pl.multiple_of((1 - px) * n, 8), n)

    def down_rows(b):
        return pl.ds(pl.multiple_of(px * (4 * n_down) + b * n_down, 8), n_down)

    down_here = pl.ds(pl.multiple_of(px * (4 * n_down), 8), 4 * n_down)
    down_there = pl.ds(pl.multiple_of((1 - px) * (4 * n_down), 8), 4 * n_down)
    py = Reduce(lambda i: py_s.at[i], r["yr_s"])
    up_x = wires.plan(gus_s.at[:, 1 - px], r["gux_s"], xdev)
    up_y_first = wires.take(GROUPS)

    def up_y(k, out):
        to = flip(w, k)
        return wires.copy(
            up_y_first + k, gus_s.at[to, px], gu_s.at[w if out else to], wdev(to)
        )

    for k in (1, 2, 3):
        wires.later(up_y(k, True))
    up = Spread(lambda b: gu_s.at[b], r["gul_s"], lambda b: up_f.at[b, px], True)
    down_x = wires.plan(gds_s.at[down_there], r["gdx_s"], xdev)
    down = Spread(
        lambda b: gds_s.at[down_rows(b)], r["gdl_s"], lambda b: gd_f.at[down_rows(b)], True
    )
    gat_s, gax_s = r["gat_s"], r["gax_s"]

    def across_rows(b):
        return pl.ds(pl.multiple_of(b * 2 * n_down + px * n_down, 8), n_down)

    most = Spread(
        lambda b: gas_s.at[pl.ds(pl.multiple_of(b * 2 * n_down, 8), 2 * n_down)],
        r["gal_s"],
        lambda b: ga_f.at[across_rows(b)],
        True,
    )
    most_x = wires.plan(gat_s.at[1 - px], gax_s, xdev)
    dz_s, dos_s, dor_s = r["dz_s"], r["dos_s"], r["dor_s"]
    don_s = r["don_s"]
    do_turn = Turn(dos_s, don_s)
    early, early_x_s, early_z_s = r["early_s"], r["early_x_s"], r["early_z_s"]
    late = r["late_s"]
    early_x = wires.plan(early, early_x_s, xdev)
    early_first = wires.take(GROUPS)

    def early_z(i):
        return wires.copy(
            early_first + i, early_z_s.at[hg], early_z_s.at[hg], zdev((hg + i) % GROUPS)
        )

    for i in (1, 2, 3):
        wires.later(early_z(i))
    late_all = Share(late)
    gos_s, gor_s = r["gos_s"], r["gor_s"]
    go_s, gox_s, gop_s, gon_s, go_f = r["go_s"], r["gox_s"], r["gop_s"], r["gon_s"], r["gout"]
    go = Reduce(lambda i: gos_s.at[i], gor_s)
    go_x = wires.plan(go_s.at[theirs], gox_s, xdev)
    go_turn = Turn(gop_s, gon_s)
    go_first = wires.take(GROUPS)

    def go_back(i):
        piece = go_f.at[px, hg]
        return wires.copy(go_first + i, piece, piece, zdev((hg + i) % GROUPS))

    for i in (1, 2, 3):
        wires.later(go_back(i))
    go_x2 = wires.plan(go_f.at[px], go_f.at[px], xdev)
    kvt_s, kvr_s, ph1_s, gqs_s = r["kvt_s"], r["kvr_s"], r["ph1_s"], r["gqs_s"]
    kv_back = wires.plan(kvt_s, kvr_s, xdev)
    h1_sum = LineSum(lambda b: ph1_s.at[b], r["h1r_s"])
    gq = Reduce(lambda i: gqs_s.at[pl.ds(pl.multiple_of(i * S, S), S)], r["gqr_s"])
    gqc_s, gqx_s, gqkv = r["gqc_s"], r["gqx_s"], r["gqkv"]
    qx = wires.plan(gqc_s.at[theirs], gqx_s, xdev)
    q_line = LineGather(lambda b: gqkv.at[b, mine], True)
    vecs, vecr = r["vecs_s"], r["vecr_s"]
    vec_first = wires.take(GROUPS)

    def vec_send(k):
        return wires.copy(
            vec_first + k, vecs.at[flip(w, k)], vecr.at[k - 1], wdev(flip(w, k))
        )

    for k in (1, 2, 3):
        wires.later(vec_send(k))
    dq_s, dqkv_s, df_s = r["dq_s"], r["dqkv_s"], r["df_s"]

    steps = {}

    def step_of(name):
        def keep(body):
            steps[name] = body
            return body

        return keep

    @step_of("up_xin")
    def _():
        up_x.wait_recv()
        here = gus_s.at[:, px]
        here[...] = sum_bf(here[...], r["gux_s"][...])
        gu_s[w] = gus_s[w, px]
        for k in (2, 3, 1):
            up_y(k, True).start()

    @step_of("up_in")
    def _():
        for k in (1, 2, 3):
            up_y(k, False).wait_recv()
        up.sum.ends()

    @step_of("D_in")
    def _():
        down_x.wait_recv()
        gds_s[down_here, :] = sum_bf(gds_s[down_here, :], r["gdx_s"][...])
        down.sum.ends()

    steps["D_xout"] = down_x.start
    for i in range(3):
        steps["A_e%d" % i] = partial(most.sum.ends, (i,))
    steps["A2a"] = partial(most.sum.second, (0,))
    steps["A2b"] = partial(most.sum.second, (1,))
    steps["A3"] = most.sum.third

    @step_of("A_out")
    def _():
        def put(total):
            gat_s[...] = total.astype(BF).reshape(2, n_down, cols)

        most.sum.final(put)
        most_x.start()

    @step_of("A_turn")
    def _():
        most_x.wait_recv()
        ga_f[across_rows(hg), :] = sum_bf(gat_s[px], gax_s[...])
        most.gather.start()

    for name, chain in (("U", up), ("D", down)):
        steps[name + "2a"] = partial(chain.sum.second, (0,))
        steps[name + "2b"] = partial(chain.sum.second, (1,))
        steps[name + "3"] = chain.sum.third
        steps[name + "_turn"] = chain.turn
    for name, line in (("U", up.gather), ("D", down.gather), ("A", most.gather), ("q", q_line)):
        steps[name + "_i1"] = partial(line.inner, 1)
        steps[name + "_o1"] = partial(line.outer, 1)
        steps[name + "_i2"] = partial(line.inner, 2)
        steps[name + "_i3"] = partial(line.inner, 3)
    steps["H2a"] = partial(h1_sum.second, (0,))
    steps["H2b"] = partial(h1_sum.second, (1,))
    steps["H3"] = h1_sum.third
    steps["h1_e2"] = partial(h1_sum.ends, (2,))
    steps["go_combine"] = go.combine
    steps["py_combine"] = py.combine
    steps["gq_comb"] = gq.combine

    @step_of("go_out")
    def _():
        go_s[...] = go.finish().astype(BF)
        go_x.start()

    @step_of("go_in")
    def _():
        go_x.wait_recv()
        go_half = go_s[mine, :].astype(F32) + gox_s[...].astype(F32)
        for b in range(GROUPS):
            gop_s[b] = go_half[b * quarter : (b + 1) * quarter].astype(BF)
        for i in (2, 1, 3):
            go_turn.message((hg + i) % GROUPS).start()

    @step_of("go_turn")
    def _():
        for i in (1, 2, 3):
            go_turn.arrived((hg + i) % GROUPS)
        go_total = gop_s[hg].astype(F32)
        for i in (1, 2, 3):
            go_total = go_total + gon_s[(hg + i) % GROUPS].astype(F32)
        go_f[px, hg] = go_total.astype(BF)
        for i in (2, 1, 3):
            go_back(i).start()

    @step_of("go_done")
    def _():
        for i in (1, 2, 3):
            go_back(i).wait_recv()
        go_x2.start()

    @step_of("go_fin")
    def _():
        go_x2.wait_recv()

    steps["early"] = early_x.start

    @step_of("early2")
    def _():
        early_x.wait_recv()
        early_z_s[hg] = early[...] + early_x_s[...]
        for i in (1, 2, 3):
            early_z(i).start()

    @step_of("kv_in")
    def _():
        kv_back.wait_recv()
        dqkv_s[:, 2 * LANES :] = jnp.transpose(sum_bf(dkv_s[0], kvr_s[...]))

    @step_of("h1_part")
    def _():
        def h1_part(step, carry):
            block = by_distance(step)
            rows = pl.ds(pl.multiple_of(block * R, R), R)
            ph1_s[block] = dot_nt(dqkv_s[rows, :], wq_s[...]).astype(BF)
            h1_sum.ends_block(block)
            return carry

        lax.fori_loop(0, GROUPS, h1_part, 0)

    @step_of("qkv_grad")
    def _():
        def qkv_grad(i, carry):
            at = pl.ds(pl.multiple_of(i * 256, 256), 256)
            gqs_s[at, :] = dot_tn(h1_s[:, :, at].reshape(half, 256), dqkv_s[...]).astype(BF)
            return carry

        lax.fori_loop(0, D // 256, qkv_grad, 0)
        gq.start()
        late[c, :, 2 * D : 2 * D + 2 * LANES] = rows_sum(dqkv_s[:, : 2 * LANES].astype(F32))
        late[c, :, 2 * D + 2 * LANES :] = rows_sum(dqkv_s[:, 3 * LANES :].astype(F32))

    @step_of("gq_fin")
    def _():
        gqc_s[...] = gq.finish().astype(BF)
        qx.start()

    @step_of("q_start")
    def _():
        qx.wait_recv()
        gqkv[hg, mine, :] = sum_bf(gqc_s[mine, :], gqx_s[...])
        q_line.start()

    @step_of("h1_fin")
    def _():
        def keep_h1(total):
            df_s[...] = total

        h1_sum.final(keep_h1)
        grad_one = df_s[...]
        unit_one, scale_one = unit_rows(x_s[hg].astype(F32))
        grad_in = dz_s[...] + unit_rows_back(grad_one, unit_one, scale_one, gain_one)
        r["dx"][...] = grad_in.astype(BF)
        late[c, :, 0:D] = rows_sum(grad_one * unit_one)
        late[c, :, D : 2 * D] = rows_sum(grad_one)
        late_all.start()

    @step_of("layer_out")
    def _():
        r["y"][...] = (x1_s[...] + py.finish() + down_b).astype(BF)

    @step_of("small")
    def _():
        for i in (1, 2, 3):
            there = (hg + i) % GROUPS
            wires.copy(early_first + GROUPS - i, early_z_s.at[there], early_z_s.at[there], left).wait_recv()
        ones = sum([early_z_s[i] for i in range(GROUPS)])
        twos = late_all.total()
        bq_all, bv_all = [], []
        for g in range(GROUPS):
            group_sum = sum([late[g * G + i][:, 2 * D :] for i in range(G)])
            bq_all.append(group_sum[:, :S])
            v_end = pltpu.roll(group_sum[:, 2 * LANES : 3 * LANES], LANES // 2, 1)[:, : S - LANES]
            bv_all.append(jnp.concatenate([group_sum[:, 3 * LANES :], v_end], axis=1))
        vectors = [twos[:, 0:D], twos[:, D : 2 * D]] + [
            ones[:, i * D : (i + 1) * D] for i in range(4)
        ]
        for i in range(GROUPS):
            for j, one in enumerate(vectors):
                vecs[i, :, j * 256 : j * 256 + S] = one[:, i * S : (i + 1) * S]
            vecs[i, :, 6 * 256 : 6 * 256 + S] = bq_all[i]
            vecs[i, :, 7 * 256 : 7 * 256 + S] = bv_all[i]
        r["vec"][:, 8 * 256 :] = ones[:, 4 * D :]
        for k in (1, 2, 3):
            vec_send(k).start()

    carried = {}

    @step_of("up_grad")
    def _():
        lax.fori_loop(0, 2, up_grad, 0)
        up_x.start()

    steps["ph_combine"] = ph[1].combine

    @step_of("down_grad")
    def _():
        lax.fori_loop(0, FS // 256, down_grad, 0)

    @step_of("y_part")
    def _():
        lax.fori_loop(0, GROUPS, y_part, 0)
        py.start()

    @step_of("wait_ph")
    def _():
        carried["two"] = jnp.concatenate([one.finish() for one in ph], axis=0)

    @step_of("ln2")
    def _():
        grad_two = carried["two"]
        unit_two, scale_two = unit_rows(x1_s[...])
        top = r["dy_s"][w].astype(F32)
        grad_middle = top + unit_rows_back(grad_two, unit_two, scale_two, gain_two)
        dz = grad_middle.astype(BF)
        dz_s[...] = grad_middle
        carried["dz"], carried["unit"], carried["top"] = dz, unit_two, top

        def out_back(step, carry):
            block = by_distance(step)
            grad_o = dot_nt(dz, wo_s[block])
            pack(dos_s.at[block], grad_o[:, :LANES], grad_o[:, LANES:])

            @pl.when(step < last)
            def _():
                do_turn.message(block).start()

            return carry

        lax.fori_loop(0, GROUPS, out_back, 0)

    @step_of("sums")
    def _():
        unpack(dos_s.at[hg], dor_s.at[hg])
        early[:, 0:D] = rows_sum(carried["dz"].astype(F32))
        early[:, D : 2 * D] = rows_sum(carried["two"] * carried["unit"])
        early[:, 2 * D : 3 * D] = rows_sum(carried["two"])
        early[:, 3 * D : 4 * D] = rows_sum(carried["top"])
        early[:, 4 * D :] = rows_sum(da_s[...].reshape(half, FS).astype(F32))

    @step_of("out_grad")
    def _():
        for i in range(GROUPS):
            piece = dot_tn(or_s[i], carried["dz"])
            gos_s[i, 0:LANES, :] = piece[0:LANES, :].astype(BF)
            gos_s[i, LANES:S, :] = piece[S:, :].astype(BF)
        go.start()
        dkv_s[...] = jnp.zeros(dkv_s.shape, F32)

    def back_block(block, side):
        outs = dor_s[block].astype(F32)
        kept = oa_s[block]
        scaled = []
        for h in range(3):
            tile = 0 if h < 2 else LANES
            keep = low_half if h == 0 else jnp.logical_not(low_half)
            scaled.append(
                jnp.where(keep, outs[:, tile : tile + LANES], 0.0) * li_s[side, h, block]
            )
        deltas = [
            jnp.sum(
                scaled[h] * kept[:, KO[h] : KO[h] + LANES], axis=-1, keepdims=True
            )
            for h in range(3)
        ]
        rounded = [one.astype(BF) for one in scaled]
        grad_probs = [
            dot_nt(rounded[h], kv_s[side, :, VT[h] : VT[h] + LANES]) for h in range(3)
        ]
        grad_scores = [
            (e_s[h, block, side].astype(F32) * (grad_probs[h] - deltas[h])).astype(BF)
            for h in range(3)
        ]
        grads_q = [
            dot_nn(grad_scores[h], kv_s[side, :, KT[h] : KT[h] + LANES]) for h in range(3)
        ]
        for h in range(3):
            dkv_s[side, KT[h] : KT[h] + LANES, :] += dot_tn(q_s[h, block], grad_scores[h])
            dkv_s[side, VT[h] : VT[h] + LANES, :] += dot_tn(rounded[h], e_s[h, block, side])
        first = jnp.where(low_half, grads_q[0], grads_q[1]) * 0.125
        final = jnp.where(low_half, grads_q[2], 0.0) * 0.125
        if side == 1:
            dq_s[block, :, :LANES] = first
            dq_s[block, :, LANES:] = final
        else:
            rows = pl.ds(pl.multiple_of(block * R, R), R)
            dqkv_s[rows, :LANES] = (dq_s[block, :, :LANES] + first).astype(BF)
            dqkv_s[rows, LANES : 2 * LANES] = (dq_s[block, :, LANES:] + final).astype(BF)

    def nearest(step):
        return by_distance(last - step)

    @step_of("kv_out")
    def _():
        kvt_s[...] = dkv_s[1].astype(BF)
        kv_back.start()

    @step_of("fin")
    def _():
        for k in (1, 2, 3):
            vec_send(k).wait_recv()
        r["vec"][:, 0 : 8 * 256] = vecs[w] + vecr[0] + vecr[1] + vecr[2]
        down.gather.done()
        most.gather.done()
        up.gather.done()
        q_line.done()

    def attention_back(side, plans):
        def body(step, carry):
            block = nearest(step)
            if side == 1:

                @pl.when(step > 0)
                def _():
                    do_turn.arrived(block)
                    unpack(don_s.at[block], dor_s.at[block])

            back_block(block, side)
            for k, names in enumerate(plans):
                if names:

                    @pl.when(step == k)
                    def _():
                        for name in names:
                            steps[name]()

            return carry

        lax.fori_loop(0, GROUPS, body, 0)

    at = 0
    order = ORDER
    while at < len(order):
        name = order[at]
        at += 1
        if name in ("bo0", "bw0"):
            plans, kind = [[]], name[:2]
            while at < len(order) and (order[at][:2] == kind or len(plans) < GROUPS):
                if order[at][:2] == kind:
                    plans.append([])
                else:
                    plans[-1].append(order[at])
                at += 1
            attention_back(1 if kind == "bo" else 0, plans)
        else:
            steps[name]()
    assert wires.used == SEMS
    wires.drain()


def widen_kernel(S, names, *refs):
    r = dict(zip(names, refs, strict=True))
    n = S // 2
    started = []

    def send(source, target):
        one = pltpu.make_async_copy(source, target, r["sems"].at[len(started)])
        one.start()
        started.append(one)

    def put(name, at, value):
        r[name + "_b"][at] = value
        send(r[name + "_b"].at[at], r[name + "_o"].at[at])

    send(r["y"], r["y_o"])
    send(r["dx"], r["dx_o"])
    put("out", (slice(None),), r["out"][...].astype(F32))

    def heads(pieces):
        return jnp.concatenate(
            [r["qkv"][i, :, a:b].astype(F32) for i in range(GROUPS) for a, b in pieces], axis=1
        )

    put("q", (slice(None),), heads([(0, S)]))
    put("k", (slice(None),), heads([(2 * LANES, 2 * LANES + S)]))
    put("v", (slice(None),), heads([(4 * LANES, 5 * LANES), (2 * LANES + S, 4 * LANES)]))
    FS = r["up"].shape[3]
    for i in range(GROUPS):
        rows = slice(i * S, (i + 1) * S)
        both = [r[name][rows, :].astype(F32) for name in ("da", "db")]
        put("down", (rows, slice(None)), jnp.concatenate(both, axis=1))
        for j in (0, 1):
            at = (slice(j * n, (j + 1) * n), slice(i * FS, (i + 1) * FS))
            put("up", at, r["up"][i, j].astype(F32))
    at = 0
    for i in range(9):
        one = r["vec%d" % i]
        one[...] = r["vec"][0, at : at + one.shape[0]]
        at += max(one.shape[0], 256)
    for one in started:
        one.wait()


SEMS = 167


def fast_device(mesh_sizes, *arrays):
    (tokens, doc_lengths, out_grad, norm1_gain, norm1_bias, w_query, b_query, w_key, w_value,
     b_value, w_out, b_out, norm2_gain, norm2_bias, w_up, b_up, w_down, b_down) = arrays
    n_ctx, n_wsh = mesh_sizes
    R, D = tokens.shape[1], tokens.shape[2]
    S, FS, n_doc = D // GROUPS, w_down.shape[0], doc_lengths.shape[1]
    half, QW = GROUPS * R, 5 * LANES

    smem = pl.BlockSpec(memory_space=pltpu.SMEM)
    vmem = pl.BlockSpec(memory_space=pltpu.VMEM)
    anywhere = pl.BlockSpec(memory_space=pl.ANY)
    inputs = [
        ("doc", doc_lengths, smem),
        ("tok", tokens[0], anywhere),
        ("dy", out_grad[0], anywhere),
        ("wq", w_query, anywhere),
        ("wk", w_key, anywhere),
        ("wv", w_value, anywhere),
        ("wout", w_out, anywhere),
        ("wup", w_up, anywhere),
        ("wdown", w_down, anywhere),
        ("n1g", norm1_gain, vmem),
        ("n1b", norm1_bias, vmem),
        ("bq", b_query, vmem),
        ("bv", b_value, vmem),
        ("bo", b_out, vmem),
        ("n2g", norm2_gain, vmem),
        ("n2b", norm2_bias, vmem),
        ("bd", b_down, vmem),
        ("bup", b_up, vmem),
    ]
    n_up = S // 2
    outputs = [
        ("y", (R, D), BF),
        ("dx", (R, D), BF),
        ("gda", (FS, 2 * D // 3), BF),
        ("gdb", (FS, D // 3), BF),
        ("gup", (GROUPS, 2, n_up, FS), BF),
        ("gout", (2, GROUPS, S // 8, D), BF),
        ("gqkv", (GROUPS, S, QW), BF),
        ("vec", (1, 8 * 256 + FS), F32),
    ]
    scratch = [
        ("x_s", (GROUPS, R, D), BF),
        ("h1_s", (GROUPS, R, D), BF),
        ("win_s", (3, S, D), BF),
        ("wq_s", (D, QW), BF),
        ("par_s", (GROUPS, 8, 2 * LANES), F32),
        ("q_s", (3, GROUPS, R, LANES), BF),
        ("kv_s", (2, half, 3 * LANES), BF),
        ("e_s", (3, GROUPS, 2, R, half), BF),
        ("li_s", (2, 3, GROUPS, R, LANES), F32),
        ("of_s", (3, GROUPS, R, LANES), F32),
        ("oa_s", (GROUPS, R, 2 * LANES), F32),
        ("os_s", (GROUPS, R + R // 2, LANES), BF),
        ("on_s", (GROUPS, R + R // 2, LANES), BF),
        ("or_s", (GROUPS, R, 2 * LANES), BF),
        ("wo_s", (GROUPS, 2 * LANES, D), BF),
        ("wu_s", (GROUPS, S, FS), BF),
        ("wd_s", (FS, D), BF),
        ("dy_s", (GROUPS, R, D), BF),
        ("x1_s", (R, D), F32),
        ("h2_s", (GROUPS, R, D), BF),
        ("g_s", (GROUPS, R, FS), BF),
        ("da_s", (GROUPS, R, FS), BF),
        ("ph_s", (GROUPS, R, D), BF),
        ("hr_s", (2, 4, R // 2, D), BF),
        ("py_s", (GROUPS, R, D), BF),
        ("yr_s", (4, R, D), BF),
        ("dz_s", (R, D), F32),
        ("dos_s", (GROUPS, R + R // 2, LANES), BF),
        ("don_s", (GROUPS, R + R // 2, LANES), BF),
        ("dor_s", (GROUPS, R, 2 * LANES), BF),
        ("dkv_s", (2, 3 * LANES, half), F32),
        ("kvt_s", (3 * LANES, half), BF),
        ("kvr_s", (3 * LANES, half), BF),
        ("dq_s", (GROUPS, R, 2 * LANES), F32),
        ("dqkv_s", (half, QW), BF),
        ("ph1_s", (GROUPS, R, D), BF),
        ("h1r_s", (6, R, D), BF),
        ("df_s", (R, D), F32),
        ("gas_s", (FS, 2 * D // 3), BF),
        ("gal_s", (6, FS // 4, 2 * D // 3), BF),
        ("gat_s", (2, FS // 8, 2 * D // 3), BF),
        ("gax_s", (FS // 8, 2 * D // 3), BF),
        ("gds_s", (FS, D // 3), BF),
        ("gdx_s", (FS // 2, D // 3), BF),
        ("gdl_s", (6, FS // 8, D // 3), BF),
        ("gus_s", (GROUPS, 2, S // 2, FS), BF),
        ("gu_s", (GROUPS, n_up, FS), BF),
        ("gux_s", (GROUPS, S // 2, FS), BF),
        ("gul_s", (6, n_up, FS), BF),
        ("go_s", (S, D), BF),
        ("gox_s", (S // 2, D), BF),
        ("gop_s", (GROUPS, S // 8, D), BF),
        ("gon_s", (GROUPS, S // 8, D), BF),
        ("gos_s", (GROUPS, S, D), BF),
        ("gor_s", (4, S, D), BF),
        ("gqs_s", (D, QW), BF),
        ("gqr_s", (4, S, QW), BF),
        ("gqc_s", (S, QW), BF),
        ("gqx_s", (S // 2, QW), BF),
        ("early_s", (1, 4 * D + FS), F32),
        ("early_x_s", (1, 4 * D + FS), F32),
        ("early_z_s", (GROUPS, 1, 4 * D + FS), F32),
        ("late_s", (n_ctx, 1, 2 * D + 4 * LANES), F32),
        ("vecs_s", (GROUPS, 1, 8 * 256), F32),
        ("vecr_s", (3, 1, 8 * 256), F32),
    ]
    sems = [("send_sems", SEMS), ("recv_sems", SEMS), ("local_sems", 9)]
    names = [one[0] for one in inputs + outputs + scratch + sems]
    y, dx, g_da, g_db, g_up, g_out, g_qkv, vec = pl.pallas_call(
        partial(layer_kernel, (n_ctx, n_doc, R, D, S, FS), names),
        out_shape=[pltpu.VMEM(shape, dtype) for name, shape, dtype in outputs],
        in_specs=[spec for name, value, spec in inputs],
        out_specs=[vmem] * len(outputs),
        scratch_shapes=[pltpu.VMEM(shape, dtype) for name, shape, dtype in scratch]
        + [pltpu.SemaphoreType.DMA((count,)) for name, count in sems],
        compiler_params=pltpu.CompilerParams(
            collective_id=0, has_side_effects=True, vmem_limit_bytes=62000000
        ),
        name="layer",
    )(*[value for name, value, spec in inputs])

    big = [
        ("y", (R, D), BF),
        ("dx", (R, D), BF),
        ("down", (FS, D), F32),
        ("up", (S, GROUPS * FS), F32),
        ("out", (2, GROUPS, S // 8, D), F32),
        ("q", (S, D), F32),
        ("k", (S, D), F32),
        ("v", (S, D), F32),
    ]
    vectors = [("vec%d" % i, size) for i, size in enumerate([S] * 8 + [FS])]
    names = ["y", "dx", "da", "db", "up", "out", "qkv", "vec"]
    names += [name + "_o" for name, shape, dtype in big] + [name for name, size in vectors]
    names += [name + "_b" for name, shape, dtype in big[2:]] + ["sems"]
    wide = pl.pallas_call(
        partial(widen_kernel, S, names),
        in_specs=[vmem] * 8,
        out_specs=[anywhere] * len(big) + [vmem] * len(vectors),
        out_shape=[jax.ShapeDtypeStruct(shape, dtype) for name, shape, dtype in big]
        + [jax.ShapeDtypeStruct((size,), F32) for name, size in vectors],
        scratch_shapes=[pltpu.VMEM(shape, dtype) for name, shape, dtype in big[2:]]
        + [pltpu.SemaphoreType.DMA((18,))],
        compiler_params=pltpu.CompilerParams(vmem_limit_bytes=24000000),
        name="widen",
    )(y, dx, g_da, g_db, g_up, g_out, g_qkv, vec)
    y, dx, down, up, out, q, k, v, n1g, n1b, bo, n2g, n2b, bd, bq, bv, bup = wide
    return (
        y[None], dx[None], n1g, n1b, q, bq, k, v, bv, out.reshape(S, D), bo, n2g, n2b, up, bup, down, bd,
    )


def solution(mesh):
    in_specs = (
        P("wsh", "ctx", None),
        P("wsh", None),
        P("wsh", "ctx", None),
        P("wsh"),
        P("wsh"),
        P("wsh", None),
        P("wsh"),
        P("wsh", None),
        P("wsh", None),
        P("wsh"),
        P("wsh", None),
        P("wsh"),
        P("wsh"),
        P("wsh"),
        P("wsh", None),
        P("wsh"),
        P("wsh", None),
        P("wsh"),
    )
    out_specs = (
        P("wsh", "ctx", None),
        P("wsh", "ctx", None),
        P("wsh"),
        P("wsh"),
        P("wsh", None),
        P("wsh"),
        P("wsh", None),
        P("wsh", None),
        P("wsh"),
        P("wsh", None),
        P("wsh"),
        P("wsh"),
        P("wsh"),
        P("wsh", None),
        P("wsh"),
        P("wsh", None),
        P("wsh"),
    )
    sizes = (mesh.shape["ctx"], mesh.shape["wsh"])
    body = partial(fast_device, sizes) if sizes == (2 * GROUPS, GROUPS) else per_device
    return jax.shard_map(
        body, mesh=mesh, in_specs=in_specs, out_specs=out_specs, check_vma=False
    )
```

```python
from functools import partial
import math

import jax
import jax.numpy as jnp
from jax import lax
from jax.experimental import pallas as pl
from jax.experimental.pallas import tpu as pltpu
from jax.sharding import PartitionSpec as P

HEADS = 12


EPS = 1e-06
NEG_START = -1e30


def norm_rows(inputs, norm_gain, norm_bias):
    row_mean = jnp.mean(inputs, axis=-1, keepdims=True)
    centred = inputs - row_mean
    variance = jnp.mean(centred * centred, axis=-1, keepdims=True)
    return centred * lax.rsqrt(variance + EPS) * norm_gain + norm_bias


def doc_of(positions, doc_ends):
    return jnp.sum((positions[:, None] >= doc_ends[None, :]).astype(jnp.int32), axis=1)


def dot_plain(left, right):
    return jnp.dot(left, right, preferred_element_type=jnp.float32)


def dot_left(left, right):
    return lax.dot_general(
        left, right, (((0,), (0,)), ((), ())), preferred_element_type=jnp.float32
    )


def dot_right(left, right):
    return lax.dot_general(
        left, right, (((1,), (1,)), ((), ())), preferred_element_type=jnp.float32
    )


def masked_scores(query_heads, key_heads, query_ids, key_ids, score_scale):
    raw_scores = (
        jnp.einsum("qhd,khd->hqk", query_heads, key_heads, preferred_element_type=jnp.float32)
        * score_scale
    )
    same_doc = (query_ids[:, None] == key_ids[None, :])[None]
    return jnp.where(same_doc, raw_scores, -jnp.inf)


def per_device(
    tokens,
    doc_lengths,
    out_grad,
    norm1_gain,
    norm1_bias,
    w_query,
    b_query,
    w_key,
    w_value,
    b_value,
    w_out,
    b_out,
    norm2_gain,
    norm2_bias,
    w_up,
    b_up,
    w_down,
    b_down,
):
    (
        gain_one,
        bias_one,
        query_w,
        query_b,
        key_w,
        value_w,
        value_b,
        out_w,
        out_b,
        gain_two,
        bias_two,
        up_w,
        up_b,
        down_w,
        down_b,
    ) = (
        lax.all_gather(norm1_gain, "wsh", axis=0, tiled=True),
        lax.all_gather(norm1_bias, "wsh", axis=0, tiled=True),
        lax.all_gather(w_query, "wsh", axis=0, tiled=True),
        lax.all_gather(b_query, "wsh", axis=0, tiled=True),
        lax.all_gather(w_key, "wsh", axis=0, tiled=True),
        lax.all_gather(w_value, "wsh", axis=0, tiled=True),
        lax.all_gather(b_value, "wsh", axis=0, tiled=True),
        lax.all_gather(w_out, "wsh", axis=0, tiled=True),
        lax.all_gather(b_out, "wsh", axis=0, tiled=True),
        lax.all_gather(norm2_gain, "wsh", axis=0, tiled=True),
        lax.all_gather(norm2_bias, "wsh", axis=0, tiled=True),
        lax.all_gather(w_up, "wsh", axis=0, tiled=True),
        lax.all_gather(b_up, "wsh", axis=0, tiled=True),
        lax.all_gather(w_down, "wsh", axis=0, tiled=True),
        lax.all_gather(b_down, "wsh", axis=0, tiled=True),
    )
    row_count = tokens.shape[1]
    model_width = tokens.shape[2]
    head_dim = model_width // HEADS
    score_scale = head_dim ** (-0.5)
    first_gain = gain_one.astype(jnp.float32)
    first_bias = bias_one.astype(jnp.float32)
    second_gain = gain_two.astype(jnp.float32)
    second_bias = bias_two.astype(jnp.float32)
    inputs = tokens[0].astype(jnp.float32)
    doc_ends = jnp.cumsum(doc_lengths[0])
    own_ids = doc_of(
        lax.axis_index("ctx") * row_count + jnp.arange(row_count, dtype=jnp.int32), doc_ends
    )
    normed_one = norm_rows(inputs, first_gain, first_bias).astype(jnp.bfloat16)
    queries = (dot_plain(normed_one, query_w) + query_b.astype(jnp.float32)).astype(jnp.bfloat16)
    key_rows = dot_plain(normed_one, key_w).astype(jnp.bfloat16)
    values = (dot_plain(normed_one, value_w) + value_b.astype(jnp.float32)).astype(jnp.bfloat16)
    key_all, value_all = (
        lax.all_gather(key_rows, "ctx", axis=0, tiled=True),
        lax.all_gather(values, "ctx", axis=0, tiled=True),
    )
    total_rows = key_all.shape[0]
    key_block = math.gcd(total_rows, 2048)
    block_count = total_rows // key_block
    key_stack = key_all.reshape(block_count, key_block, HEADS, head_dim)
    value_stack = value_all.reshape(block_count, key_block, HEADS, head_dim)
    id_stack = doc_of(jnp.arange(total_rows, dtype=jnp.int32), doc_ends).reshape(
        block_count, key_block
    )
    query_heads = queries.reshape(row_count, HEADS, head_dim)

    def lse_step(running, block_in):
        run_max, run_sum = running
        key_heads, key_ids = block_in
        scores = masked_scores(query_heads, key_heads, own_ids, key_ids, score_scale)
        new_max = jnp.maximum(run_max, jnp.max(scores, axis=-1))
        new_sum = run_sum * jnp.exp(run_max - new_max) + jnp.sum(
            jnp.exp(scores - new_max[:, :, None]), axis=-1
        )
        return ((new_max, new_sum), None)

    start_max = jnp.full((HEADS, row_count), NEG_START, jnp.float32)
    (final_max, final_sum), unused = lax.scan(
        lse_step, (start_max, jnp.zeros_like(start_max)), (key_stack, id_stack)
    )
    log_total = final_max + jnp.log(final_sum)

    def out_step(running, block_in):
        key_heads, value_heads, key_ids = block_in
        scores = masked_scores(query_heads, key_heads, own_ids, key_ids, score_scale)
        attn_prob = jnp.exp(scores - log_total[:, :, None]).astype(jnp.bfloat16)
        return (
            running
            + jnp.einsum(
                "hqk,khd->qhd", attn_prob, value_heads, preferred_element_type=jnp.float32
            ),
            None,
        )

    attn_sum, unused = lax.scan(
        out_step,
        jnp.zeros((row_count, HEADS, head_dim), jnp.float32),
        (key_stack, value_stack, id_stack),
    )
    attended = attn_sum.reshape(row_count, model_width).astype(jnp.bfloat16)
    middle = inputs + dot_plain(attended, out_w) + out_b.astype(jnp.float32)
    normed_two = norm_rows(middle, second_gain, second_bias).astype(jnp.bfloat16)
    hidden = dot_plain(normed_two, up_w) + up_b.astype(jnp.float32)
    active = jax.nn.gelu(hidden, approximate=True).astype(jnp.bfloat16)
    output = middle + dot_plain(active, down_w) + down_b.astype(jnp.float32)
    top_grad = out_grad[0]
    top_float = top_grad.astype(jnp.float32)
    grad_down_w = dot_left(active, top_grad)
    grad_down_b = jnp.sum(top_float, axis=0)
    grad_active = dot_right(top_grad, down_w)
    unused, gelu_pull = jax.vjp(partial(jax.nn.gelu, approximate=True), hidden)
    grad_hidden = gelu_pull(grad_active)[0].astype(jnp.bfloat16)
    grad_up_w = dot_left(normed_two, grad_hidden)
    grad_up_b = jnp.sum(grad_hidden.astype(jnp.float32), axis=0)
    grad_normed_two = dot_right(grad_hidden, up_w)
    unused, second_pull = jax.vjp(norm_rows, middle, second_gain, second_bias)
    grad_middle, grad_gain_two, grad_bias_two = second_pull(grad_normed_two)
    grad_middle = grad_middle + top_float
    grad_branch = grad_middle.astype(jnp.bfloat16)
    grad_out_w = dot_left(attended, grad_branch)
    grad_out_b = jnp.sum(grad_branch.astype(jnp.float32), axis=0)
    grad_attended = dot_right(grad_branch, out_w).astype(jnp.bfloat16)
    grad_heads = grad_attended.reshape(row_count, HEADS, head_dim)
    row_delta = jnp.sum(grad_heads.astype(jnp.float32) * attn_sum, axis=-1)
    head_delta = row_delta.T
    query_start = jnp.zeros((row_count, HEADS, head_dim), jnp.float32)

    def full_step(grad_query, block_in):
        key_heads, value_heads, key_ids = block_in
        scores = masked_scores(query_heads, key_heads, own_ids, key_ids, score_scale)
        attn_prob = jnp.exp(scores - log_total[:, :, None])
        grad_prob = jnp.einsum(
            "qhd,khd->hqk", grad_heads, value_heads, preferred_element_type=jnp.float32
        )
        grad_score = (attn_prob * (grad_prob - head_delta[:, :, None])).astype(jnp.bfloat16)
        grad_query = grad_query + jnp.einsum(
            "hqk,khd->qhd", grad_score, key_heads, preferred_element_type=jnp.float32
        )
        grad_key = (
            jnp.einsum("hqk,qhd->khd", grad_score, query_heads, preferred_element_type=jnp.float32)
            * score_scale
        )
        grad_value = jnp.einsum(
            "hqk,qhd->khd",
            attn_prob.astype(jnp.bfloat16),
            grad_heads,
            preferred_element_type=jnp.float32,
        )
        return (
            grad_query,
            (grad_key.reshape(key_block, model_width), grad_value.reshape(key_block, model_width)),
        )

    grad_query, key_terms = lax.scan(full_step, query_start, (key_stack, value_stack, id_stack))
    key_grad, value_grad = (
        lax.psum_scatter(
            key_terms[0].reshape(total_rows, model_width), "ctx", scatter_dimension=0, tiled=True
        ),
        lax.psum_scatter(
            key_terms[1].reshape(total_rows, model_width), "ctx", scatter_dimension=0, tiled=True
        ),
    )
    grad_query_rows = (
        (grad_query * score_scale).reshape(row_count, model_width).astype(jnp.bfloat16)
    )
    grad_key_rows = key_grad.astype(jnp.bfloat16)
    grad_value_rows = value_grad.astype(jnp.bfloat16)
    grad_query_w = dot_left(normed_one, grad_query_rows)
    grad_query_b = jnp.sum(grad_query_rows.astype(jnp.float32), axis=0)
    grad_key_w = dot_left(normed_one, grad_key_rows)
    grad_value_w = dot_left(normed_one, grad_value_rows)
    grad_value_b = jnp.sum(grad_value_rows.astype(jnp.float32), axis=0)
    grad_normed_one = (
        dot_right(grad_query_rows, query_w)
        + dot_right(grad_key_rows, key_w)
        + dot_right(grad_value_rows, value_w)
    )
    unused, first_pull = jax.vjp(norm_rows, inputs, first_gain, first_bias)
    grad_inputs, grad_gain_one, grad_bias_one = first_pull(grad_normed_one)
    grad_inputs = grad_inputs + grad_middle
    (
        share_gain_one,
        share_bias_one,
        share_query_w,
        share_query_b,
        share_key_w,
        share_value_w,
        share_value_b,
        share_out_w,
        share_out_b,
        share_gain_two,
        share_bias_two,
        share_up_w,
        share_up_b,
        share_down_w,
        share_down_b,
    ) = (
        lax.psum_scatter(
            grad_gain_one.astype(jnp.bfloat16), "wsh", scatter_dimension=0, tiled=True
        ).astype(jnp.float32),
        lax.psum_scatter(
            grad_bias_one.astype(jnp.bfloat16), "wsh", scatter_dimension=0, tiled=True
        ).astype(jnp.float32),
        lax.psum_scatter(
            grad_query_w.astype(jnp.bfloat16), "wsh", scatter_dimension=0, tiled=True
        ).astype(jnp.float32),
        lax.psum_scatter(
            grad_query_b.astype(jnp.bfloat16), "wsh", scatter_dimension=0, tiled=True
        ).astype(jnp.float32),
        lax.psum_scatter(
            grad_key_w.astype(jnp.bfloat16), "wsh", scatter_dimension=0, tiled=True
        ).astype(jnp.float32),
        lax.psum_scatter(
            grad_value_w.astype(jnp.bfloat16), "wsh", scatter_dimension=0, tiled=True
        ).astype(jnp.float32),
        lax.psum_scatter(
            grad_value_b.astype(jnp.bfloat16), "wsh", scatter_dimension=0, tiled=True
        ).astype(jnp.float32),
        lax.psum_scatter(
            grad_out_w.astype(jnp.bfloat16), "wsh", scatter_dimension=0, tiled=True
        ).astype(jnp.float32),
        lax.psum_scatter(
            grad_out_b.astype(jnp.bfloat16), "wsh", scatter_dimension=0, tiled=True
        ).astype(jnp.float32),
        lax.psum_scatter(
            grad_gain_two.astype(jnp.bfloat16), "wsh", scatter_dimension=0, tiled=True
        ).astype(jnp.float32),
        lax.psum_scatter(
            grad_bias_two.astype(jnp.bfloat16), "wsh", scatter_dimension=0, tiled=True
        ).astype(jnp.float32),
        lax.psum_scatter(
            grad_up_w.astype(jnp.bfloat16), "wsh", scatter_dimension=0, tiled=True
        ).astype(jnp.float32),
        lax.psum_scatter(
            grad_up_b.astype(jnp.bfloat16), "wsh", scatter_dimension=0, tiled=True
        ).astype(jnp.float32),
        lax.psum_scatter(
            grad_down_w.astype(jnp.bfloat16), "wsh", scatter_dimension=0, tiled=True
        ).astype(jnp.float32),
        lax.psum_scatter(
            grad_down_b.astype(jnp.bfloat16), "wsh", scatter_dimension=0, tiled=True
        ).astype(jnp.float32),
    )
    totals = lax.psum(
        (
            share_gain_one,
            share_bias_one,
            share_query_w,
            share_query_b,
            share_key_w,
            share_value_w,
            share_value_b,
            share_out_w,
            share_out_b,
            share_gain_two,
            share_bias_two,
            share_up_w,
            share_up_b,
            share_down_w,
            share_down_b,
        ),
        "ctx",
    )
    return (
        output.astype(jnp.bfloat16)[None],
        grad_inputs.astype(jnp.bfloat16)[None],
        totals[0],
        totals[1],
        totals[2],
        totals[3],
        totals[4],
        totals[5],
        totals[6],
        totals[7],
        totals[8],
        totals[9],
        totals[10],
        totals[11],
        totals[12],
        totals[13],
        totals[14],
    )


MESH = pl.DeviceIdType.MESH
F32 = jnp.float32
BF = jnp.bfloat16
GROUPS = 4
LANES = 128


def flip(value, mask):
    return ((value // 2 + mask // 2) % 2) * 2 + (value + mask) % 2


def dot_nn(left, right):
    return lax.dot_general(left, right, (((1,), (0,)), ((), ())), preferred_element_type=F32)


def dot_nt(left, right):
    return lax.dot_general(left, right, (((1,), (1,)), ((), ())), preferred_element_type=F32)


def dot_tn(left, right):
    return lax.dot_general(left, right, (((0,), (0,)), ((), ())), preferred_element_type=F32)


def unit_rows(inputs):
    row_mean = jnp.mean(inputs, axis=-1, keepdims=True)
    centred = inputs - row_mean
    variance = jnp.mean(centred * centred, axis=-1, keepdims=True)
    scale = lax.rsqrt(variance + EPS)
    return centred * scale, scale


def unit_rows_back(grad_normed, unit, scale, gain):
    grad_unit = grad_normed * gain
    return scale * (
        grad_unit
        - jnp.mean(grad_unit, axis=-1, keepdims=True)
        - unit * jnp.mean(grad_unit * unit, axis=-1, keepdims=True)
    )


def rows_sum(values):
    return jnp.sum(values, axis=0, keepdims=True)


def sum_bf(*values):
    return sum([one.astype(F32) for one in values]).astype(BF)


class Wires:
    def __init__(self, send_sems, recv_sems):
        self.send_sems, self.recv_sems, self.used, self.started = send_sems, recv_sems, 0, []

    def take(self, count=1):
        first = self.used
        self.used += count
        return first

    def copy(self, index, source, target, device):
        return pltpu.make_async_remote_copy(
            src_ref=source,
            dst_ref=target,
            send_sem=self.send_sems.at[index % SEND_SEMS],
            recv_sem=self.recv_sems.at[index],
            device_id=device,
            device_id_type=MESH,
        )

    def send(self, source, target, device):
        one = self.copy(self.take(), source, target, device)
        one.start()
        self.started.append((one, None))
        return one

    def later(self, one, when=None):
        self.started.append((one, when))
        return one

    def plan(self, source, target, device):
        return self.later(self.copy(self.take(), source, target, device))

    def drain(self):
        for one, when in self.started:
            if when is None:
                one.wait_send()
            else:
                pl.when(when)(one.wait_send)


ORDER = (
    "up_grad", "ph_combine", "down_grad", "A_e0", "D_xout", "A_e1", "y_part", "wait_ph", "ln2",
    "sums", "out_grad", "bo0", "bo1", "up_xin", "A_e2", "A2a", "A2b", "go_combine", "bo2", "bo3",
    "kv_out", "D_in", "py_combine", "bw0", "A3", "up_in", "bw1", "bw2", "D2a", "D2b", "A_out",
    "U2a", "early", "bw3", "go_out", "D3", "U2b", "D_turn", "U3", "kv_in", "qkv_grad", "A_turn",
    "gq_comb", "U_turn", "go_in", "D_i1", "D_o1", "gq_fin", "U_i1", "U_o1", "A_i1", "A_o1",
    "h1_part", "q_start", "U_i2", "H2a", "layer_out", "U_i3", "A_i2", "q_i1", "D_i2", "go_turn",
    "q_o1", "D_i3", "h1_e2", "H2b", "A_i3", "go_done", "H3", "q_i2", "early2", "h1_fin", "q_i3",
    "small", "go_fin", "fin",
)


def layer_kernel(sizes, names, *refs):
    n_ctx, n_doc, R, D, S, FS = sizes
    r = dict(zip(names, refs, strict=True))
    G = n_ctx // GROUPS
    last = GROUPS - 1
    half = GROUPS * R
    c = lax.axis_index("ctx")
    w = lax.axis_index("wsh")
    hg, px = c // G, c % G

    def zdev(group):
        return {"ctx": group * G + px, "wsh": w}

    def wdev(index):
        return {"ctx": c, "wsh": index}

    xdev = {"ctx": hg * G + 1 - px, "wsh": w}
    left, right = zdev((hg + last) % GROUPS), zdev((hg + 1) % GROUPS)
    w1, w2, w3 = flip(w, 1), flip(w, 2), flip(w, 3)
    sib, across, diag = wdev(w1), wdev(w2), wdev(w3)
    wires = Wires(r["send_sems"], r["recv_sems"])
    lane = lax.broadcasted_iota(jnp.int32, (1, LANES), 1)
    low_half = lane < LANES // 2

    def pick(table):
        return sum([jnp.where(hg == i, one, 0) for i, one in enumerate(table)])

    def by_distance(step):
        return (
            jnp.where(step == 0, pick((3, 3, 0, 0)), 0)
            + jnp.where(step == 1, pick((2, 0, 3, 1)), 0)
            + jnp.where(step == 2, pick((1, 2, 1, 2)), 0)
            + jnp.where(step == 3, hg, 0)
        )

    local = r["local_sems"]

    def fetch(index, source, target):
        one = pltpu.make_async_copy(source, target, local.at[index])
        one.start()
        return one

    tok_in = fetch(0, r["tok"], r["x_s"].at[hg])
    qkv_in = [fetch(1 + i, r[name], r["win_s"].at[i]) for i, name in enumerate(("wq", "wk", "wv"))]
    dy_in = fetch(4, r["dy"], r["dy_s"].at[w])
    wo_in = [
        fetch(5, r["wout"].at[pl.ds(0, LANES)], r["wo_s"].at[w, pl.ds(0, LANES)]),
        fetch(6, r["wout"].at[pl.ds(LANES, S - LANES)], r["wo_s"].at[w, pl.ds(S, S - LANES)]),
    ]
    wu_in = fetch(7, r["wup"].at[:, pl.ds(pl.multiple_of(w * FS, FS), FS)], r["wu_s"].at[w])
    wd_in = fetch(8, r["wdown"], r["wd_s"])

    barrier = pltpu.get_barrier_semaphore()
    ctx_peers = [{"ctx": (c + i) % n_ctx, "wsh": w} for i in range(1, n_ctx)]
    partners = ctx_peers + [sib, across, diag]
    for partner in partners:
        pl.semaphore_signal(barrier, inc=1, device_id=partner, device_id_type=MESH)

    pl.semaphore_wait(barrier, len(partners))

    class Gather:
        def __init__(self, slot):
            self.slot = slot
            self.to_across = wires.send(slot(w), slot(w), across)
            self.to_sib = wires.send(slot(w), slot(w), sib)

        def relay(self):
            self.to_across.wait_recv()
            self.on = wires.send(self.slot(w2), self.slot(w2), sib)

        def finish(self):
            self.to_sib.wait_recv()
            self.on.wait_recv()

    class Reduce:
        def __init__(self, part, recv):
            self.part, self.recv = part, recv
            self.a = wires.plan(part(w3), recv.at[0], sib)
            self.b = wires.plan(part(w1), recv.at[1], sib)
            self.c = wires.plan(recv.at[3], recv.at[2], across)

        def start(self):
            self.a.start()
            self.b.start()

        def combine(self):
            self.a.wait_recv()
            self.recv[3] = sum_bf(self.part(w2)[...], self.recv[0])
            self.c.start()

        def finish(self):
            self.b.wait_recv()
            self.c.wait_recv()
            return (
                self.part(w)[...].astype(F32)
                + self.recv[1].astype(F32)
                + self.recv[2].astype(F32)
            )

    class LineSum:
        def __init__(self, part, recv):
            self.part, self.recv = part, recv
            self.first_at = wires.take(6)
            for i in range(3):
                wires.later(self.message(i, True), hg > i)
                wires.later(self.message(i, False), hg < last - i)

        def message(self, i, leftward):
            block, slot = (i, i) if leftward else (last - i, 3 + i)
            return wires.copy(
                self.first_at + slot, self.part(block), self.recv.at[slot], left if leftward else right
            )

        def ends_block(self, block):
            for i in range(2):

                @pl.when((hg == last) & (block == i))
                def _():
                    self.message(i, True).start()

                @pl.when((hg == 0) & (block == last - i))
                def _():
                    self.message(i, False).start()

        def ends(self, which=(0, 1, 2)):
            for i in which:

                @pl.when(hg == last)
                def _():
                    self.message(i, True).start()

                @pl.when(hg == 0)
                def _():
                    self.message(i, False).start()

        def pass_on(self, position, i, leftward):
            @pl.when(hg == position)
            def _():
                one = self.message(i, leftward)
                one.wait_recv()
                block, slot = (i, i) if leftward else (last - i, 3 + i)
                self.part(block)[...] = sum_bf(self.part(block)[...], self.recv[slot])
                one.start()

        def second(self, which=(0, 1)):
            for i in which:
                self.pass_on(2, i, True)
                self.pass_on(1, i, False)

        def third(self):
            self.pass_on(1, 0, True)
            self.pass_on(2, 0, False)

        def final(self, put):
            for position in range(GROUPS):

                @pl.when(hg == position)
                def _():
                    total = self.part(position)[...].astype(F32)
                    if position < last:
                        self.message(position, True).wait_recv()
                        total = total + self.recv[position].astype(F32)
                    if position > 0:
                        self.message(last - position, False).wait_recv()
                        total = total + self.recv[3 + last - position].astype(F32)
                    put(total)

    class LineGather:
        def __init__(self, slot, to_x, own=None):
            self.slot, self.to_x, self.own = slot, to_x, own
            self.first_at = wires.take(6)
            self.x_at = wires.take(GROUPS) if to_x else None
            for d in (1, 2, 3):
                wires.later(self.message(d, 0), (hg >= d - 1) & (hg < last))
                wires.later(self.message(d, 1), (hg + d - 1 <= last) & (hg > 0))
            if to_x:
                for b in range(GROUPS):
                    wires.later(self.x_message(b))

        def message(self, d, side):
            block = (hg + GROUPS + (1 - d) * (1 - 2 * side)) % GROUPS
            device = zdev((hg + GROUPS + 1 - 2 * side) % GROUPS)
            first = self.own is not None and isinstance(d, int) and d == 1
            source = self.own if first else self.slot(block)
            return wires.copy(self.first_at + 3 * side + d - 1, source, self.slot(block), device)

        def x_message(self, block):
            return wires.copy(self.x_at + block, self.slot(block), self.slot(block), xdev)

        def start(self):
            pl.when(hg < last)(self.message(1, 0).start)
            pl.when(hg > 0)(self.message(1, 1).start)
            if self.to_x:
                self.x_message(hg).start()

        def arrived(self, d, side, then=None):
            block = (hg + GROUPS - d * (1 - 2 * side)) % GROUPS
            here = jnp.where(side == 0, (hg >= d).astype(jnp.int32), (hg + d <= last).astype(jnp.int32))
            onward = here * jnp.where(side == 0, (hg < last).astype(jnp.int32), (hg > 0).astype(jnp.int32))

            @pl.when(here == 1)
            def _():
                wires.copy(
                    self.first_at + 3 * side + d - 1, self.slot(block), self.slot(block), left
                ).wait_recv()

            @pl.when(onward == 1)
            def _():
                self.message(d + 1, side).start()

            @pl.when(here == 1)
            def _():
                if self.to_x:
                    self.x_message(block).start()
                if then is not None:
                    then(block)

        def inner(self, d):
            self.arrived(d, jnp.where(hg < 2, 1, 0))

        def outer(self, d):
            self.arrived(d, jnp.where(hg < 2, 0, 1))

        def done(self):
            for b in range(GROUPS):
                self.x_message(b).wait_recv()

    x_s, h1_s, q_s, kv_s = r["x_s"], r["h1_s"], r["q_s"], r["kv_s"]
    rows_two = R // 2
    tokens = [
        LineGather(
            lambda b, j=j: x_s.at[b, pl.ds(j * rows_two, rows_two)],
            False,
            r["tok"].at[pl.ds(j * rows_two, rows_two)],
        )
        for j in (0, 1)
    ]
    for one in tokens:
        one.start()
    for one in qkv_in:
        one.wait()
    own_w = pl.ds(pl.multiple_of(w * S, S), S)
    win, wq_s = r["win_s"], r["wq_s"]
    for g in range(GROUPS):

        @pl.when(hg == g)
        def _():
            a = g * S
            wq_s[own_w, 0:S] = win[0, :, a : a + S]
            wq_s[own_w, S : 2 * LANES] = jnp.zeros((S, 2 * LANES - S), BF)
            wq_s[own_w, 2 * LANES : 2 * LANES + S] = win[1, :, a : a + S]
            wq_s[own_w, 2 * LANES + S : 4 * LANES] = win[2, :, a + LANES : a + S]
            wq_s[own_w, 4 * LANES : 5 * LANES] = win[2, :, a : a + LANES]

    par_s = r["par_s"]
    par_s[w] = jnp.zeros((8, 2 * LANES), F32)
    for i, name in enumerate(("n1g", "n1b", "bq", "bv", "bo", "n2g", "n2b", "bd")):
        par_s[w, i : i + 1, 0:S] = r[name][...].astype(F32)[None, :]
    r["wo_s"][:, LANES:S, :] = jnp.zeros((GROUPS, S - LANES, D), BF)
    ws_all = Gather(lambda i: wq_s.at[pl.ds(pl.multiple_of(i * S, S), S)])
    par_all = Gather(lambda i: par_s.at[i])
    for one in wo_in:
        one.wait()
    dy_in.wait()
    wo_s, dy_s, wu_s = r["wo_s"], r["dy_s"], r["wu_s"]
    wo_top = Gather(lambda i: wo_s.at[i, pl.ds(0, LANES)])
    wo_low = Gather(lambda i: wo_s.at[i, pl.ds(S, S - LANES)])
    dy_all = Gather(lambda i: dy_s.at[i])
    up_sends = [
        wires.send(
            r["wup"].at[:, pl.ds(pl.multiple_of(flip(w, k) * FS, FS), FS)],
            wu_s.at[w],
            wdev(flip(w, k)),
        )
        for k in (2, 3, 1)
    ]
    inner_side = jnp.where(hg < 2, 1, 0)
    tokens[0].arrived(1, inner_side)
    tokens[0].arrived(1, 1 - inner_side)
    par_all.relay()
    ws_all.relay()
    tokens[1].arrived(1, inner_side)
    tokens[1].arrived(1, 1 - inner_side)
    par_all.finish()

    pars = jnp.concatenate([par_s[i][:, :S] for i in range(GROUPS)], axis=1)
    gain_one, bias_one, out_b, gain_two, bias_two, down_b = [
        pars[i : i + 1] for i in (0, 1, 4, 5, 6, 7)
    ]
    up_b = r["bup"][...].astype(F32)[None, :]
    own_par = par_s[hg]
    v_tile, v_last = own_par[3:4, :LANES], own_par[3:4, LANES:]
    qkv_b = jnp.concatenate(
        [own_par[2:3, :], jnp.zeros((1, LANES), F32), pltpu.roll(v_last, LANES // 2, 1), v_tile],
        axis=1,
    )
    ws_all.finish()
    tok_in.wait()

    kv_first = wires.take(2 * GROUPS)

    def kv_copy(block, j):
        rows = pl.ds(pl.multiple_of(block * R + j * rows_two, rows_two), rows_two)
        return wires.copy(
            kv_first + 2 * block + j, kv_s.at[0, rows], kv_s.at[1, rows], xdev
        )

    def project(block, j):
        rows = pl.ds(pl.multiple_of(j * rows_two, rows_two), rows_two)
        unit, unused = unit_rows(x_s[block, rows, :].astype(F32))
        normed = (unit * gain_one + bias_one).astype(BF)
        h1_s[block, rows, :] = normed
        qkv = dot_nn(normed, wq_s[...]) + qkv_b
        queries = qkv[:, : 2 * LANES].astype(BF).astype(F32) * 0.125
        q_s[0, block, rows, :] = jnp.where(low_half, queries[:, :LANES], 0.0).astype(BF)
        q_s[1, block, rows, :] = jnp.where(low_half, 0.0, queries[:, :LANES]).astype(BF)
        q_s[2, block, rows, :] = queries[:, LANES:].astype(BF)
        kv_rows = pl.ds(pl.multiple_of(block * R + j * rows_two, rows_two), rows_two)
        kv_s[0, kv_rows, :] = qkv[:, 2 * LANES :].astype(BF)
        kv_copy(block, j).start()

    def near_project(i, carry):
        away = jnp.where(i < 2, 0, jnp.where(i < 4, 1, 3)) * (1 - 2 * (1 - inner_side))
        block = (hg + 2 * GROUPS + jnp.where(i < 4, away, (1 - 2 * inner_side))) % GROUPS

        @pl.when((i < 4) | ((hg > 0) & (hg < last)))
        def _():
            project(block, i % 2)

        return carry

    lax.fori_loop(0, 6, near_project, 0)

    def far_project(i, carry):
        d = i + 2
        block = (hg + GROUPS - d * (1 - 2 * inner_side)) % GROUPS
        for j, one in enumerate(tokens):
            one.arrived(d, inner_side)

            @pl.when(jnp.where(hg < 2, hg + d <= last, hg >= d))
            def _():
                project(block, j)

        return carry

    lax.fori_loop(0, 2, far_project, 0)
    wo_top.relay()
    wo_low.relay()
    doc_ends = []
    for i in range(n_doc):
        doc_ends.append(r["doc"][0, i] + (doc_ends[-1] if i else 0))

    def doc_ids(positions):
        return sum([(positions >= end).astype(jnp.int32) for end in doc_ends])

    key_at = lax.broadcasted_iota(jnp.int32, (1, half), 1)
    key_block = sum([(key_at >= i * R).astype(jnp.int32) for i in range(1, GROUPS)])
    key_base = key_at + key_block * (R * (G - 1))
    key_ids = [doc_ids(key_base + px * R), doc_ids(key_base + (1 - px) * R)]
    KT, VT, KO = (0, 0, LANES), (2 * LANES, 2 * LANES, LANES), (0, 0, LANES)
    e_s, li_s, oa_s, os_s, or_s = r["e_s"], r["li_s"], r["oa_s"], r["os_s"], r["or_s"]
    of_s = r["of_s"]

    def pack(target, first, final):
        target[0:R, :] = first.astype(BF)
        turned = pltpu.roll(final[rows_two:, :], LANES // 2, 1)
        target[R : R + rows_two, :] = jnp.where(low_half, turned, final[:rows_two, :]).astype(BF)

    def unpack(source, target):
        target[:, :LANES] = source[0:R, :]
        both = source[R : R + rows_two, :].astype(F32)
        target[0:rows_two, LANES:] = jnp.where(low_half, 0.0, both).astype(BF)
        turned = pltpu.roll(both, LANES // 2, 1)
        target[rows_two:, LANES:] = jnp.where(low_half, 0.0, turned).astype(BF)

    class Turn:
        def __init__(self, source, target):
            self.source, self.target = source, target
            self.first_at = wires.take(GROUPS)
            for i in (1, 2, 3):
                wires.later(self.message((hg + i) % GROUPS))

        def message(self, block):
            index = self.first_at + (block - hg + GROUPS) % GROUPS
            return wires.copy(index, self.source.at[block], self.target.at[hg], zdev(block))

        def arrived(self, block):
            index = self.first_at + (hg - block + GROUPS) % GROUPS
            wires.copy(index, self.target.at[block], self.target.at[block], left).wait_recv()

    on_s = r["on_s"]
    o_turn = Turn(os_s, on_s)

    def row_ids_of(block):
        row_at = (block * G + px) * R + lax.broadcasted_iota(jnp.int32, (R, 1), 0)
        return doc_ids(row_at)

    def attend_side(block, side):
        row_ids = row_ids_of(block)
        same = row_ids == key_ids[side]
        scores = [
            jnp.where(
                same, dot_nt(q_s[h, block], kv_s[side, :, KT[h] : KT[h] + LANES]), NEG_START
            )
            for h in range(3)
        ]
        tops = [jnp.max(one, axis=-1, keepdims=True) for one in scores]
        weights = [jnp.exp(one - top) for one, top in zip(scores, tops, strict=True)]
        mixed = []
        for h in range(3):
            rounded = weights[h].astype(BF)
            e_s[h, block, side] = rounded
            mixed.append(dot_nn(rounded, kv_s[side, :, VT[h] : VT[h] + LANES]))
        totals = [jnp.sum(one, axis=-1, keepdims=True) for one in weights]
        return tops, totals, mixed

    def attend_own(block, carry):
        tops, totals, mixed = attend_side(block, 0)
        for h in range(3):
            li_s[0, h, block] = jnp.broadcast_to(tops[h], (R, LANES))
            li_s[1, h, block] = jnp.broadcast_to(totals[h], (R, LANES))
            of_s[h, block] = mixed[h]
        return carry

    lax.fori_loop(0, GROUPS, attend_own, 0)
    dy_all.relay()
    for b in range(GROUPS):
        for j in (0, 1):
            kv_copy(b, j).wait_recv()
            wires.later(kv_copy(b, j))

    def attend(step, carry):
        block = by_distance(step)
        tops, totals, mixed = attend_side(block, 1)
        outs = []
        for h in range(3):
            top, total = tops[h], totals[h]
            own_top = li_s[0, h, block]
            both_top = jnp.maximum(own_top, top)
            own_part, part = jnp.exp(own_top - both_top), jnp.exp(top - both_top)
            inverse = 1.0 / (li_s[1, h, block] * own_part + total * part)
            own_part, part = own_part * inverse, part * inverse
            li_s[0, h, block] = own_part
            li_s[1, h, block] = part
            outs.append(of_s[h, block] * own_part + mixed[h] * part)
        first = jnp.where(low_half, outs[0], outs[1])
        final = jnp.where(low_half, 0.0, outs[2])
        oa_s[block, :, :LANES] = first
        oa_s[block, :, LANES:] = final
        pack(os_s.at[block], first, final)

        @pl.when(step < last)
        def _():
            o_turn.message(block).start()

        return carry

    lax.fori_loop(0, GROUPS, attend, 0)
    unpack(os_s.at[hg], or_s.at[hg])
    dy_all.finish()
    wd_in.wait()
    wd_s, dkv_s = r["wd_s"], r["dkv_s"]

    def top_rows(slot):
        return slot // 2, pl.ds(pl.multiple_of((slot % 2) * R, R), R)

    def top_part(slot, carry):
        dkv_s[top_rows(slot)] = dot_nt(dy_s[slot], wd_s[...])
        return carry

    lax.fori_loop(0, GROUPS, top_part, 0)
    wo_top.finish()
    wo_low.finish()
    for i in (1, 2, 3):
        there = (hg + i) % GROUPS
        o_turn.arrived(there)
        unpack(on_s.at[there], or_s.at[there])

    middle = x_s[hg].astype(F32) + out_b
    for i in range(GROUPS):
        middle += dot_nn(or_s[i], wo_s[i])
    x1_s, h2_s, g_s, da_s = r["x1_s"], r["h2_s"], r["g_s"], r["da_s"]
    x1_s[...] = middle
    unit_two, scale_two = unit_rows(middle)
    h2_s[w] = (unit_two * gain_two + bias_two).astype(BF)
    halves = [pl.ds(0, rows_two), pl.ds(rows_two, rows_two)]
    h2_all = [Gather(lambda i, part=part: h2_s.at[i, part]) for part in halves]
    wu_in.wait()
    for one in up_sends:
        one.wait_recv()
    ph_s, hr_s = r["ph_s"], r["hr_s"]
    ph = [
        Reduce(lambda i, part=part: ph_s.at[i, part], hr_s.at[k]) for k, part in enumerate(halves)
    ]

    def up_and_back(slot, start, count):
        rows = pl.ds(start, count)
        hidden = dot_nn(h2_s[slot, rows, :], wu_s[...].reshape(D, FS)) + up_b
        square = hidden * hidden
        inner = math.sqrt(2.0 / math.pi) * (hidden + 0.044715 * (square * hidden))
        bent = jnp.tanh(inner)
        g_s[slot, rows, :] = (0.5 * hidden * (1.0 + bent)).astype(BF)
        slope = 0.5 * (1.0 + bent) + 0.5 * hidden * (1.0 - bent * bent) * (
            math.sqrt(2.0 / math.pi) * (1.0 + 3.0 * 0.044715 * square)
        )
        top_at = pl.ds(pl.multiple_of((slot % 2) * R + start, rows_two), count)
        grad_hidden = (dkv_s[slot // 2, top_at, :] * slope).astype(BF)
        da_s[slot, rows, :] = grad_hidden
        ph_s[slot, rows, :] = dot_nt(grad_hidden, wu_s[...].reshape(D, FS)).astype(BF)

    def mlp_near(j, carry):
        @pl.when(j == 1)
        def _():
            for one in h2_all:
                one.to_sib.wait_recv()

        up_and_back(flip(w, j), 0, R)
        return carry

    lax.fori_loop(0, 2, mlp_near, 0)
    for one in ph:
        one.b.start()
    on_copies = [
        wires.plan(h2_s.at[w2, part], h2_s.at[w2, part], sib) for part in halves
    ]
    for k in (0, 1):
        h2_all[k].to_across.wait_recv()
        on_copies[k].start()
        up_and_back(w2, k * rows_two, rows_two)
        if k == 1:
            ph[0].combine()
        on_copies[k].wait_recv()
        up_and_back(w3, k * rows_two, rows_two)
        ph[k].a.start()

    gus_s, gas_s, gds_s, py_s = r["gus_s"], r["gas_s"], r["gds_s"], r["py_s"]
    cols = gas_s.shape[1]

    def up_grad(i, carry):
        at = pl.ds(pl.multiple_of(i * 2 * S, 2 * S), 2 * S)
        gus_s[pl.ds(2 * i, 2)] = (
            dot_tn(h2_s[:, :, at].reshape(half, 2 * S), da_s[...].reshape(half, FS))
            .astype(BF)
            .reshape(2, 2, S // 2, FS)
        )
        return carry

    def down_grad(i, carry):
        at = pl.ds(pl.multiple_of(i * 256, 256), 256)
        both = dot_tn(g_s[:, :, at].reshape(half, 256), dy_s[...].reshape(half, D)).astype(BF)
        gas_s[at, :] = both[:, :cols]
        gds_s[at, :] = both[:, cols:]
        return carry

    def y_part(j, carry):
        py_s[j] = dot_nn(g_s[j], wd_s[...]).astype(BF)
        return carry

    class Spread:
        def __init__(self, part, recv, slot, to_x):
            self.sum = LineSum(part, recv)
            self.gather = LineGather(slot, to_x)

        def turn(self):
            def put(total):
                self.gather.slot(hg)[...] = total.astype(BF)

            self.sum.final(put)
            self.gather.start()

    class Share:
        def __init__(self, rows):
            self.rows = rows
            self.at = wires.take(n_ctx)
            for i in range(1, n_ctx):
                wires.later(self.message(i))

        def message(self, i):
            return wires.copy(self.at + i, self.rows.at[c], self.rows.at[c], ctx_peers[i - 1])

        def start(self):
            for i in range(1, n_ctx):
                self.message(i).start()

        def total(self):
            for i in range(1, n_ctx):
                wires.copy(self.at + i, self.rows.at[c], self.rows.at[c], left).wait_recv()
            return sum([self.rows[i] for i in range(n_ctx)])

    n = S // 2
    n_down = FS // 8
    quarter = n // GROUPS
    ga_f, gd_f, gu_s, up_f = r["gda"], r["gdb"], r["gu_s"], r["gup"]
    mine = pl.ds(pl.multiple_of(px * n, 8), n)
    theirs = pl.ds(pl.multiple_of((1 - px) * n, 8), n)

    def down_rows(b):
        return pl.ds(pl.multiple_of(px * (4 * n_down) + b * n_down, 8), n_down)

    down_here = pl.ds(pl.multiple_of(px * (4 * n_down), 8), 4 * n_down)
    down_there = pl.ds(pl.multiple_of((1 - px) * (4 * n_down), 8), 4 * n_down)
    py = Reduce(lambda i: py_s.at[i], r["yr_s"])
    up_x = wires.plan(gus_s.at[:, 1 - px], r["gux_s"], xdev)
    up_y_first = wires.take(GROUPS)

    def up_y(k, out):
        to = flip(w, k)
        return wires.copy(
            up_y_first + k, gus_s.at[to, px], gu_s.at[w if out else to], wdev(to)
        )

    for k in (1, 2, 3):
        wires.later(up_y(k, True))
    up = Spread(lambda b: gu_s.at[b], r["gul_s"], lambda b: up_f.at[b, px], True)
    down_x = wires.plan(gds_s.at[down_there], r["gdx_s"], xdev)
    down = Spread(
        lambda b: gds_s.at[down_rows(b)], r["gdl_s"], lambda b: gd_f.at[down_rows(b)], True
    )
    gat_s, gax_s = r["gat_s"], r["gax_s"]

    def across_rows(b):
        return pl.ds(pl.multiple_of(b * 2 * n_down + px * n_down, 8), n_down)

    most = Spread(
        lambda b: gas_s.at[pl.ds(pl.multiple_of(b * 2 * n_down, 8), 2 * n_down)],
        r["gal_s"],
        lambda b: ga_f.at[across_rows(b)],
        True,
    )
    most_x = wires.plan(gat_s.at[1 - px], gax_s, xdev)
    dz_s, dos_s, dor_s = r["dz_s"], r["dos_s"], r["dor_s"]
    don_s = r["don_s"]
    do_turn = Turn(dos_s, don_s)
    early, early_x_s, early_z_s = r["early_s"], r["early_x_s"], r["early_z_s"]
    late = r["late_s"]
    early_x = wires.plan(early, early_x_s, xdev)
    early_first = wires.take(GROUPS)

    def early_z(i):
        return wires.copy(
            early_first + i, early_z_s.at[hg], early_z_s.at[hg], zdev((hg + i) % GROUPS)
        )

    for i in (1, 2, 3):
        wires.later(early_z(i))
    late_all = Share(late)
    gos_s, gor_s = r["gos_s"], r["gor_s"]
    go_s, gox_s, gop_s, gon_s, go_f = r["go_s"], r["gox_s"], r["gop_s"], r["gon_s"], r["gout"]
    go = Reduce(lambda i: gos_s.at[i], gor_s)
    go_x = wires.plan(go_s.at[theirs], gox_s, xdev)
    go_turn = Turn(gop_s, gon_s)
    go_first = wires.take(GROUPS)

    def go_back(i):
        piece = go_f.at[px, hg]
        return wires.copy(go_first + i, piece, piece, zdev((hg + i) % GROUPS))

    for i in (1, 2, 3):
        wires.later(go_back(i))
    go_x2 = wires.plan(go_f.at[px], go_f.at[px], xdev)
    kvt_s, kvr_s, ph1_s, gqs_s = r["kvt_s"], r["kvr_s"], r["ph1_s"], r["gqs_s"]
    kv_back = wires.plan(kvt_s, kvr_s, xdev)
    h1_sum = LineSum(lambda b: ph1_s.at[b], r["h1r_s"])
    gq = Reduce(lambda i: gqs_s.at[pl.ds(pl.multiple_of(i * S, S), S)], r["gqr_s"])
    gqc_s, gqx_s, gqkv = r["gqc_s"], r["gqx_s"], r["gqkv"]
    qx = wires.plan(gqc_s.at[theirs], gqx_s, xdev)
    q_line = LineGather(lambda b: gqkv.at[b, mine], True)
    vecs, vecr = r["vecs_s"], r["vecr_s"]
    vec_first = wires.take(GROUPS)

    def vec_send(k):
        return wires.copy(
            vec_first + k, vecs.at[flip(w, k)], vecr.at[k - 1], wdev(flip(w, k))
        )

    for k in (1, 2, 3):
        wires.later(vec_send(k))
    dq_s, dqkv_s, df_s = r["dq_s"], r["dqkv_s"], r["df_s"]

    steps = {}

    def step_of(name):
        def keep(body):
            steps[name] = body
            return body

        return keep

    @step_of("up_xin")
    def _():
        up_x.wait_recv()
        here = gus_s.at[:, px]
        here[...] = sum_bf(here[...], r["gux_s"][...])
        gu_s[w] = gus_s[w, px]
        for k in (2, 3, 1):
            up_y(k, True).start()

    @step_of("up_in")
    def _():
        for k in (1, 2, 3):
            up_y(k, False).wait_recv()
        up.sum.ends()

    @step_of("D_in")
    def _():
        down_x.wait_recv()
        gds_s[down_here, :] = sum_bf(gds_s[down_here, :], r["gdx_s"][...])
        down.sum.ends()

    steps["D_xout"] = down_x.start
    for i in range(3):
        steps["A_e%d" % i] = partial(most.sum.ends, (i,))
    steps["A2a"] = partial(most.sum.second, (0,))
    steps["A2b"] = partial(most.sum.second, (1,))
    steps["A3"] = most.sum.third

    @step_of("A_out")
    def _():
        def put(total):
            gat_s[...] = total.astype(BF).reshape(2, n_down, cols)

        most.sum.final(put)
        most_x.start()

    @step_of("A_turn")
    def _():
        most_x.wait_recv()
        ga_f[across_rows(hg), :] = sum_bf(gat_s[px], gax_s[...])
        most.gather.start()

    for name, chain in (("U", up), ("D", down)):
        steps[name + "2a"] = partial(chain.sum.second, (0,))
        steps[name + "2b"] = partial(chain.sum.second, (1,))
        steps[name + "3"] = chain.sum.third
        steps[name + "_turn"] = chain.turn
    for name, line in (("U", up.gather), ("D", down.gather), ("A", most.gather), ("q", q_line)):
        steps[name + "_i1"] = partial(line.inner, 1)
        steps[name + "_o1"] = partial(line.outer, 1)
        steps[name + "_i2"] = partial(line.inner, 2)
        steps[name + "_i3"] = partial(line.inner, 3)
    steps["H2a"] = partial(h1_sum.second, (0,))
    steps["H2b"] = partial(h1_sum.second, (1,))
    steps["H3"] = h1_sum.third
    steps["h1_e2"] = partial(h1_sum.ends, (2,))
    steps["go_combine"] = go.combine
    steps["py_combine"] = py.combine
    steps["gq_comb"] = gq.combine

    @step_of("go_out")
    def _():
        go_s[...] = go.finish().astype(BF)
        go_x.start()

    @step_of("go_in")
    def _():
        go_x.wait_recv()
        go_half = go_s[mine, :].astype(F32) + gox_s[...].astype(F32)
        for b in range(GROUPS):
            gop_s[b] = go_half[b * quarter : (b + 1) * quarter].astype(BF)
        for i in (2, 1, 3):
            go_turn.message((hg + i) % GROUPS).start()

    @step_of("go_turn")
    def _():
        for i in (1, 2, 3):
            go_turn.arrived((hg + i) % GROUPS)
        go_total = gop_s[hg].astype(F32)
        for i in (1, 2, 3):
            go_total = go_total + gon_s[(hg + i) % GROUPS].astype(F32)
        go_f[px, hg] = go_total.astype(BF)
        for i in (2, 1, 3):
            go_back(i).start()

    @step_of("go_done")
    def _():
        for i in (1, 2, 3):
            go_back(i).wait_recv()
        go_x2.start()

    @step_of("go_fin")
    def _():
        go_x2.wait_recv()

    steps["early"] = early_x.start

    @step_of("early2")
    def _():
        early_x.wait_recv()
        early_z_s[hg] = early[...] + early_x_s[...]
        for i in (1, 2, 3):
            early_z(i).start()

    @step_of("kv_in")
    def _():
        kv_back.wait_recv()
        dqkv_s[:, 2 * LANES :] = jnp.transpose(sum_bf(dkv_s[0], kvr_s[...]))

    @step_of("h1_part")
    def _():
        def h1_part(step, carry):
            block = by_distance(step)
            rows = pl.ds(pl.multiple_of(block * R, R), R)
            ph1_s[block] = dot_nt(dqkv_s[rows, :], wq_s[...]).astype(BF)
            h1_sum.ends_block(block)
            return carry

        lax.fori_loop(0, GROUPS, h1_part, 0)

    @step_of("qkv_grad")
    def _():
        def qkv_grad(i, carry):
            at = pl.ds(pl.multiple_of(i * 256, 256), 256)
            gqs_s[at, :] = dot_tn(h1_s[:, :, at].reshape(half, 256), dqkv_s[...]).astype(BF)
            return carry

        lax.fori_loop(0, D // 256, qkv_grad, 0)
        gq.start()
        late[c, :, 2 * D : 2 * D + 2 * LANES] = rows_sum(dqkv_s[:, : 2 * LANES].astype(F32))
        late[c, :, 2 * D + 2 * LANES :] = rows_sum(dqkv_s[:, 3 * LANES :].astype(F32))

    @step_of("gq_fin")
    def _():
        gqc_s[...] = gq.finish().astype(BF)
        qx.start()

    @step_of("q_start")
    def _():
        qx.wait_recv()
        gqkv[hg, mine, :] = sum_bf(gqc_s[mine, :], gqx_s[...])
        q_line.start()

    @step_of("h1_fin")
    def _():
        def keep_h1(total):
            df_s[...] = total

        h1_sum.final(keep_h1)
        grad_one = df_s[...]
        unit_one, scale_one = unit_rows(x_s[hg].astype(F32))
        grad_in = dz_s[...] + unit_rows_back(grad_one, unit_one, scale_one, gain_one)
        r["dx"][...] = grad_in.astype(BF)
        late[c, :, 0:D] = rows_sum(grad_one * unit_one)
        late[c, :, D : 2 * D] = rows_sum(grad_one)
        late_all.start()

    @step_of("layer_out")
    def _():
        r["y"][...] = (x1_s[...] + py.finish() + down_b).astype(BF)

    @step_of("small")
    def _():
        for i in (1, 2, 3):
            there = (hg + i) % GROUPS
            wires.copy(early_first + GROUPS - i, early_z_s.at[there], early_z_s.at[there], left).wait_recv()
        ones = sum([early_z_s[i] for i in range(GROUPS)])
        twos = late_all.total()
        bq_all, bv_all = [], []
        for g in range(GROUPS):
            group_sum = sum([late[g * G + i][:, 2 * D :] for i in range(G)])
            bq_all.append(group_sum[:, :S])
            v_end = pltpu.roll(group_sum[:, 2 * LANES : 3 * LANES], LANES // 2, 1)[:, : S - LANES]
            bv_all.append(jnp.concatenate([group_sum[:, 3 * LANES :], v_end], axis=1))
        vectors = [twos[:, 0:D], twos[:, D : 2 * D]] + [
            ones[:, i * D : (i + 1) * D] for i in range(4)
        ]
        for i in range(GROUPS):
            for j, one in enumerate(vectors):
                vecs[i, :, j * 256 : j * 256 + S] = one[:, i * S : (i + 1) * S]
            vecs[i, :, 6 * 256 : 6 * 256 + S] = bq_all[i]
            vecs[i, :, 7 * 256 : 7 * 256 + S] = bv_all[i]
        r["vec"][:, 8 * 256 :] = ones[:, 4 * D :]
        for k in (1, 2, 3):
            vec_send(k).start()

    carried = {}

    @step_of("up_grad")
    def _():
        lax.fori_loop(0, 2, up_grad, 0)
        up_x.start()

    steps["ph_combine"] = ph[1].combine

    @step_of("down_grad")
    def _():
        lax.fori_loop(0, FS // 256, down_grad, 0)

    @step_of("y_part")
    def _():
        lax.fori_loop(0, GROUPS, y_part, 0)
        py.start()

    @step_of("wait_ph")
    def _():
        carried["two"] = jnp.concatenate([one.finish() for one in ph], axis=0)

    @step_of("ln2")
    def _():
        grad_two = carried["two"]
        unit_two, scale_two = unit_rows(x1_s[...])
        top = r["dy_s"][w].astype(F32)
        grad_middle = top + unit_rows_back(grad_two, unit_two, scale_two, gain_two)
        dz = grad_middle.astype(BF)
        dz_s[...] = grad_middle
        carried["dz"], carried["unit"], carried["top"] = dz, unit_two, top

        def out_back(step, carry):
            block = by_distance(step)
            grad_o = dot_nt(dz, wo_s[block])
            pack(dos_s.at[block], grad_o[:, :LANES], grad_o[:, LANES:])

            @pl.when(step < last)
            def _():
                do_turn.message(block).start()

            return carry

        lax.fori_loop(0, GROUPS, out_back, 0)

    @step_of("sums")
    def _():
        unpack(dos_s.at[hg], dor_s.at[hg])
        early[:, 0:D] = rows_sum(carried["dz"].astype(F32))
        early[:, D : 2 * D] = rows_sum(carried["two"] * carried["unit"])
        early[:, 2 * D : 3 * D] = rows_sum(carried["two"])
        early[:, 3 * D : 4 * D] = rows_sum(carried["top"])
        early[:, 4 * D :] = rows_sum(da_s[...].reshape(half, FS).astype(F32))

    @step_of("out_grad")
    def _():
        for i in range(GROUPS):
            piece = dot_tn(or_s[i], carried["dz"])
            gos_s[i, 0:LANES, :] = piece[0:LANES, :].astype(BF)
            gos_s[i, LANES:S, :] = piece[S:, :].astype(BF)
        go.start()
        dkv_s[...] = jnp.zeros(dkv_s.shape, F32)

    def back_block(block, side):
        outs = dor_s[block].astype(F32)
        kept = oa_s[block]
        scaled = []
        for h in range(3):
            tile = 0 if h < 2 else LANES
            keep = low_half if h == 0 else jnp.logical_not(low_half)
            scaled.append(
                jnp.where(keep, outs[:, tile : tile + LANES], 0.0) * li_s[side, h, block]
            )
        deltas = [
            jnp.sum(
                scaled[h] * kept[:, KO[h] : KO[h] + LANES], axis=-1, keepdims=True
            )
            for h in range(3)
        ]
        rounded = [one.astype(BF) for one in scaled]
        grad_probs = [
            dot_nt(rounded[h], kv_s[side, :, VT[h] : VT[h] + LANES]) for h in range(3)
        ]
        grad_scores = [
            (e_s[h, block, side].astype(F32) * (grad_probs[h] - deltas[h])).astype(BF)
            for h in range(3)
        ]
        grads_q = [
            dot_nn(grad_scores[h], kv_s[side, :, KT[h] : KT[h] + LANES]) for h in range(3)
        ]
        for h in range(3):
            dkv_s[side, KT[h] : KT[h] + LANES, :] += dot_tn(q_s[h, block], grad_scores[h])
            dkv_s[side, VT[h] : VT[h] + LANES, :] += dot_tn(rounded[h], e_s[h, block, side])
        first = jnp.where(low_half, grads_q[0], grads_q[1]) * 0.125
        final = jnp.where(low_half, grads_q[2], 0.0) * 0.125
        if side == 1:
            dq_s[block, :, :LANES] = first
            dq_s[block, :, LANES:] = final
        else:
            rows = pl.ds(pl.multiple_of(block * R, R), R)
            dqkv_s[rows, :LANES] = (dq_s[block, :, :LANES] + first).astype(BF)
            dqkv_s[rows, LANES : 2 * LANES] = (dq_s[block, :, LANES:] + final).astype(BF)

    def nearest(step):
        return by_distance(last - step)

    @step_of("kv_out")
    def _():
        kvt_s[...] = dkv_s[1].astype(BF)
        kv_back.start()

    @step_of("fin")
    def _():
        for k in (1, 2, 3):
            vec_send(k).wait_recv()
        r["vec"][:, 0 : 8 * 256] = vecs[w] + vecr[0] + vecr[1] + vecr[2]
        down.gather.done()
        most.gather.done()
        up.gather.done()
        q_line.done()

    def attention_back(side, plans):
        def body(step, carry):
            block = nearest(step)
            if side == 1:

                @pl.when(step > 0)
                def _():
                    do_turn.arrived(block)
                    unpack(don_s.at[block], dor_s.at[block])

            back_block(block, side)
            for k, names in enumerate(plans):
                if names:

                    @pl.when(step == k)
                    def _():
                        for name in names:
                            steps[name]()

            return carry

        lax.fori_loop(0, GROUPS, body, 0)

    at = 0
    order = ORDER
    while at < len(order):
        name = order[at]
        at += 1
        if name in ("bo0", "bw0"):
            plans, kind = [[]], name[:2]
            while at < len(order) and (order[at][:2] == kind or len(plans) < GROUPS):
                if order[at][:2] == kind:
                    plans.append([])
                else:
                    plans[-1].append(order[at])
                at += 1
            attention_back(1 if kind == "bo" else 0, plans)
        else:
            steps[name]()
    assert wires.used == SEMS
    wires.drain()


def widen_kernel(S, names, *refs):
    r = dict(zip(names, refs, strict=True))
    n = S // 2
    started = []

    def send(source, target):
        one = pltpu.make_async_copy(source, target, r["sems"].at[len(started)])
        one.start()
        started.append(one)

    def put(name, at, value):
        r[name + "_b"][at] = value
        send(r[name + "_b"].at[at], r[name + "_o"].at[at])

    send(r["y"], r["y_o"])
    send(r["dx"], r["dx_o"])
    put("out", (slice(None),), r["out"][...].astype(F32))

    def heads(pieces):
        return jnp.concatenate(
            [r["qkv"][i, :, a:b].astype(F32) for i in range(GROUPS) for a, b in pieces], axis=1
        )

    put("q", (slice(None),), heads([(0, S)]))
    put("k", (slice(None),), heads([(2 * LANES, 2 * LANES + S)]))
    put("v", (slice(None),), heads([(4 * LANES, 5 * LANES), (2 * LANES + S, 4 * LANES)]))
    FS = r["up"].shape[3]
    for i in range(GROUPS):
        rows = slice(i * S, (i + 1) * S)
        both = [r[name][rows, :].astype(F32) for name in ("da", "db")]
        put("down", (rows, slice(None)), jnp.concatenate(both, axis=1))
        for j in (0, 1):
            at = (slice(j * n, (j + 1) * n), slice(i * FS, (i + 1) * FS))
            put("up", at, r["up"][i, j].astype(F32))
    at = 0
    for i in range(9):
        one = r["vec%d" % i]
        one[...] = r["vec"][0, at : at + one.shape[0]]
        at += max(one.shape[0], 256)
    for one in started:
        one.wait()


SEMS = 167
SEND_SEMS = 4


def fast_device(mesh_sizes, *arrays):
    (tokens, doc_lengths, out_grad, norm1_gain, norm1_bias, w_query, b_query, w_key, w_value,
     b_value, w_out, b_out, norm2_gain, norm2_bias, w_up, b_up, w_down, b_down) = arrays
    n_ctx, n_wsh = mesh_sizes
    R, D = tokens.shape[1], tokens.shape[2]
    S, FS, n_doc = D // GROUPS, w_down.shape[0], doc_lengths.shape[1]
    half, QW = GROUPS * R, 5 * LANES

    smem = pl.BlockSpec(memory_space=pltpu.SMEM)
    vmem = pl.BlockSpec(memory_space=pltpu.VMEM)
    anywhere = pl.BlockSpec(memory_space=pl.ANY)
    inputs = [
        ("doc", doc_lengths, smem),
        ("tok", tokens[0], anywhere),
        ("dy", out_grad[0], anywhere),
        ("wq", w_query, anywhere),
        ("wk", w_key, anywhere),
        ("wv", w_value, anywhere),
        ("wout", w_out, anywhere),
        ("wup", w_up, anywhere),
        ("wdown", w_down, anywhere),
        ("n1g", norm1_gain, vmem),
        ("n1b", norm1_bias, vmem),
        ("bq", b_query, vmem),
        ("bv", b_value, vmem),
        ("bo", b_out, vmem),
        ("n2g", norm2_gain, vmem),
        ("n2b", norm2_bias, vmem),
        ("bd", b_down, vmem),
        ("bup", b_up, vmem),
    ]
    n_up = S // 2
    outputs = [
        ("y", (R, D), BF),
        ("dx", (R, D), BF),
        ("gda", (FS, 2 * D // 3), BF),
        ("gdb", (FS, D // 3), BF),
        ("gup", (GROUPS, 2, n_up, FS), BF),
        ("gout", (2, GROUPS, S // 8, D), BF),
        ("gqkv", (GROUPS, S, QW), BF),
        ("vec", (1, 8 * 256 + FS), F32),
    ]
    scratch = [
        ("x_s", (GROUPS, R, D), BF),
        ("h1_s", (GROUPS, R, D), BF),
        ("win_s", (3, S, D), BF),
        ("wq_s", (D, QW), BF),
        ("par_s", (GROUPS, 8, 2 * LANES), F32),
        ("q_s", (3, GROUPS, R, LANES), BF),
        ("kv_s", (2, half, 3 * LANES), BF),
        ("e_s", (3, GROUPS, 2, R, half), BF),
        ("li_s", (2, 3, GROUPS, R, LANES), F32),
        ("of_s", (3, GROUPS, R, LANES), F32),
        ("oa_s", (GROUPS, R, 2 * LANES), F32),
        ("os_s", (GROUPS, R + R // 2, LANES), BF),
        ("on_s", (GROUPS, R + R // 2, LANES), BF),
        ("or_s", (GROUPS, R, 2 * LANES), BF),
        ("wo_s", (GROUPS, 2 * LANES, D), BF),
        ("wu_s", (GROUPS, S, FS), BF),
        ("wd_s", (FS, D), BF),
        ("dy_s", (GROUPS, R, D), BF),
        ("x1_s", (R, D), F32),
        ("h2_s", (GROUPS, R, D), BF),
        ("g_s", (GROUPS, R, FS), BF),
        ("da_s", (GROUPS, R, FS), BF),
        ("ph_s", (GROUPS, R, D), BF),
        ("hr_s", (2, 4, R // 2, D), BF),
        ("py_s", (GROUPS, R, D), BF),
        ("yr_s", (4, R, D), BF),
        ("dz_s", (R, D), F32),
        ("dos_s", (GROUPS, R + R // 2, LANES), BF),
        ("don_s", (GROUPS, R + R // 2, LANES), BF),
        ("dor_s", (GROUPS, R, 2 * LANES), BF),
        ("dkv_s", (2, 3 * LANES, half), F32),
        ("kvt_s", (3 * LANES, half), BF),
        ("kvr_s", (3 * LANES, half), BF),
        ("dq_s", (GROUPS, R, 2 * LANES), F32),
        ("dqkv_s", (half, QW), BF),
        ("ph1_s", (GROUPS, R, D), BF),
        ("h1r_s", (6, R, D), BF),
        ("df_s", (R, D), F32),
        ("gas_s", (FS, 2 * D // 3), BF),
        ("gal_s", (6, FS // 4, 2 * D // 3), BF),
        ("gat_s", (2, FS // 8, 2 * D // 3), BF),
        ("gax_s", (FS // 8, 2 * D // 3), BF),
        ("gds_s", (FS, D // 3), BF),
        ("gdx_s", (FS // 2, D // 3), BF),
        ("gdl_s", (6, FS // 8, D // 3), BF),
        ("gus_s", (GROUPS, 2, S // 2, FS), BF),
        ("gu_s", (GROUPS, n_up, FS), BF),
        ("gux_s", (GROUPS, S // 2, FS), BF),
        ("gul_s", (6, n_up, FS), BF),
        ("go_s", (S, D), BF),
        ("gox_s", (S // 2, D), BF),
        ("gop_s", (GROUPS, S // 8, D), BF),
        ("gon_s", (GROUPS, S // 8, D), BF),
        ("gos_s", (GROUPS, S, D), BF),
        ("gor_s", (4, S, D), BF),
        ("gqs_s", (D, QW), BF),
        ("gqr_s", (4, S, QW), BF),
        ("gqc_s", (S, QW), BF),
        ("gqx_s", (S // 2, QW), BF),
        ("early_s", (1, 4 * D + FS), F32),
        ("early_x_s", (1, 4 * D + FS), F32),
        ("early_z_s", (GROUPS, 1, 4 * D + FS), F32),
        ("late_s", (n_ctx, 1, 2 * D + 4 * LANES), F32),
        ("vecs_s", (GROUPS, 1, 8 * 256), F32),
        ("vecr_s", (3, 1, 8 * 256), F32),
    ]
    sems = [("send_sems", SEND_SEMS), ("recv_sems", SEMS), ("local_sems", 9)]
    names = [one[0] for one in inputs + outputs + scratch + sems]
    y, dx, g_da, g_db, g_up, g_out, g_qkv, vec = pl.pallas_call(
        partial(layer_kernel, (n_ctx, n_doc, R, D, S, FS), names),
        out_shape=[pltpu.VMEM(shape, dtype) for name, shape, dtype in outputs],
        in_specs=[spec for name, value, spec in inputs],
        out_specs=[vmem] * len(outputs),
        scratch_shapes=[pltpu.VMEM(shape, dtype) for name, shape, dtype in scratch]
        + [pltpu.SemaphoreType.DMA((count,)) for name, count in sems],
        compiler_params=pltpu.CompilerParams(
            collective_id=0, has_side_effects=True, vmem_limit_bytes=62000000
        ),
        name="layer",
    )(*[value for name, value, spec in inputs])

    big = [
        ("y", (R, D), BF),
        ("dx", (R, D), BF),
        ("down", (FS, D), F32),
        ("up", (S, GROUPS * FS), F32),
        ("out", (2, GROUPS, S // 8, D), F32),
        ("q", (S, D), F32),
        ("k", (S, D), F32),
        ("v", (S, D), F32),
    ]
    vectors = [("vec%d" % i, size) for i, size in enumerate([S] * 8 + [FS])]
    names = ["y", "dx", "da", "db", "up", "out", "qkv", "vec"]
    names += [name + "_o" for name, shape, dtype in big] + [name for name, size in vectors]
    names += [name + "_b" for name, shape, dtype in big[2:]] + ["sems"]
    wide = pl.pallas_call(
        partial(widen_kernel, S, names),
        in_specs=[vmem] * 8,
        out_specs=[anywhere] * len(big) + [vmem] * len(vectors),
        out_shape=[jax.ShapeDtypeStruct(shape, dtype) for name, shape, dtype in big]
        + [jax.ShapeDtypeStruct((size,), F32) for name, size in vectors],
        scratch_shapes=[pltpu.VMEM(shape, dtype) for name, shape, dtype in big[2:]]
        + [pltpu.SemaphoreType.DMA((18,))],
        compiler_params=pltpu.CompilerParams(vmem_limit_bytes=24000000),
        name="widen",
    )(y, dx, g_da, g_db, g_up, g_out, g_qkv, vec)
    y, dx, down, up, out, q, k, v, n1g, n1b, bo, n2g, n2b, bd, bq, bv, bup = wide
    return (
        y[None], dx[None], n1g, n1b, q, bq, k, v, bv, out.reshape(S, D), bo, n2g, n2b, up, bup, down, bd,
    )


def solution(mesh):
    in_specs = (
        P("wsh", "ctx", None),
        P("wsh", None),
        P("wsh", "ctx", None),
        P("wsh"),
        P("wsh"),
        P("wsh", None),
        P("wsh"),
        P("wsh", None),
        P("wsh", None),
        P("wsh"),
        P("wsh", None),
        P("wsh"),
        P("wsh"),
        P("wsh"),
        P("wsh", None),
        P("wsh"),
        P("wsh", None),
        P("wsh"),
    )
    out_specs = (
        P("wsh", "ctx", None),
        P("wsh", "ctx", None),
        P("wsh"),
        P("wsh"),
        P("wsh", None),
        P("wsh"),
        P("wsh", None),
        P("wsh", None),
        P("wsh"),
        P("wsh", None),
        P("wsh"),
        P("wsh"),
        P("wsh"),
        P("wsh", None),
        P("wsh"),
        P("wsh", None),
        P("wsh"),
    )
    sizes = (mesh.shape["ctx"], mesh.shape["wsh"])
    body = partial(fast_device, sizes) if sizes == (2 * GROUPS, GROUPS) else per_device
    return jax.shard_map(
        body, mesh=mesh, in_specs=in_specs, out_specs=out_specs, check_vma=False
    )
```

```python
from functools import partial
import math

import jax
import jax.numpy as jnp
from jax import lax
from jax.experimental import pallas as pl
from jax.experimental.pallas import tpu as pltpu
from jax.sharding import PartitionSpec as P

HEADS = 12


EPS = 1e-06
NEG_START = -1e30


def norm_rows(inputs, norm_gain, norm_bias):
    row_mean = jnp.mean(inputs, axis=-1, keepdims=True)
    centred = inputs - row_mean
    variance = jnp.mean(centred * centred, axis=-1, keepdims=True)
    return centred * lax.rsqrt(variance + EPS) * norm_gain + norm_bias


def doc_of(positions, doc_ends):
    return jnp.sum((positions[:, None] >= doc_ends[None, :]).astype(jnp.int32), axis=1)


def dot_plain(left, right):
    return jnp.dot(left, right, preferred_element_type=jnp.float32)


def dot_left(left, right):
    return lax.dot_general(
        left, right, (((0,), (0,)), ((), ())), preferred_element_type=jnp.float32
    )


def dot_right(left, right):
    return lax.dot_general(
        left, right, (((1,), (1,)), ((), ())), preferred_element_type=jnp.float32
    )


def masked_scores(query_heads, key_heads, query_ids, key_ids, score_scale):
    raw_scores = (
        jnp.einsum("qhd,khd->hqk", query_heads, key_heads, preferred_element_type=jnp.float32)
        * score_scale
    )
    same_doc = (query_ids[:, None] == key_ids[None, :])[None]
    return jnp.where(same_doc, raw_scores, -jnp.inf)


def per_device(
    tokens,
    doc_lengths,
    out_grad,
    norm1_gain,
    norm1_bias,
    w_query,
    b_query,
    w_key,
    w_value,
    b_value,
    w_out,
    b_out,
    norm2_gain,
    norm2_bias,
    w_up,
    b_up,
    w_down,
    b_down,
):
    (
        gain_one,
        bias_one,
        query_w,
        query_b,
        key_w,
        value_w,
        value_b,
        out_w,
        out_b,
        gain_two,
        bias_two,
        up_w,
        up_b,
        down_w,
        down_b,
    ) = (
        lax.all_gather(norm1_gain, "wsh", axis=0, tiled=True),
        lax.all_gather(norm1_bias, "wsh", axis=0, tiled=True),
        lax.all_gather(w_query, "wsh", axis=0, tiled=True),
        lax.all_gather(b_query, "wsh", axis=0, tiled=True),
        lax.all_gather(w_key, "wsh", axis=0, tiled=True),
        lax.all_gather(w_value, "wsh", axis=0, tiled=True),
        lax.all_gather(b_value, "wsh", axis=0, tiled=True),
        lax.all_gather(w_out, "wsh", axis=0, tiled=True),
        lax.all_gather(b_out, "wsh", axis=0, tiled=True),
        lax.all_gather(norm2_gain, "wsh", axis=0, tiled=True),
        lax.all_gather(norm2_bias, "wsh", axis=0, tiled=True),
        lax.all_gather(w_up, "wsh", axis=0, tiled=True),
        lax.all_gather(b_up, "wsh", axis=0, tiled=True),
        lax.all_gather(w_down, "wsh", axis=0, tiled=True),
        lax.all_gather(b_down, "wsh", axis=0, tiled=True),
    )
    row_count = tokens.shape[1]
    model_width = tokens.shape[2]
    head_dim = model_width // HEADS
    score_scale = head_dim ** (-0.5)
    first_gain = gain_one.astype(jnp.float32)
    first_bias = bias_one.astype(jnp.float32)
    second_gain = gain_two.astype(jnp.float32)
    second_bias = bias_two.astype(jnp.float32)
    inputs = tokens[0].astype(jnp.float32)
    doc_ends = jnp.cumsum(doc_lengths[0])
    own_ids = doc_of(
        lax.axis_index("ctx") * row_count + jnp.arange(row_count, dtype=jnp.int32), doc_ends
    )
    normed_one = norm_rows(inputs, first_gain, first_bias).astype(jnp.bfloat16)
    queries = (dot_plain(normed_one, query_w) + query_b.astype(jnp.float32)).astype(jnp.bfloat16)
    key_rows = dot_plain(normed_one, key_w).astype(jnp.bfloat16)
    values = (dot_plain(normed_one, value_w) + value_b.astype(jnp.float32)).astype(jnp.bfloat16)
    key_all, value_all = (
        lax.all_gather(key_rows, "ctx", axis=0, tiled=True),
        lax.all_gather(values, "ctx", axis=0, tiled=True),
    )
    total_rows = key_all.shape[0]
    key_block = math.gcd(total_rows, 2048)
    block_count = total_rows // key_block
    key_stack = key_all.reshape(block_count, key_block, HEADS, head_dim)
    value_stack = value_all.reshape(block_count, key_block, HEADS, head_dim)
    id_stack = doc_of(jnp.arange(total_rows, dtype=jnp.int32), doc_ends).reshape(
        block_count, key_block
    )
    query_heads = queries.reshape(row_count, HEADS, head_dim)

    def lse_step(running, block_in):
        run_max, run_sum = running
        key_heads, key_ids = block_in
        scores = masked_scores(query_heads, key_heads, own_ids, key_ids, score_scale)
        new_max = jnp.maximum(run_max, jnp.max(scores, axis=-1))
        new_sum = run_sum * jnp.exp(run_max - new_max) + jnp.sum(
            jnp.exp(scores - new_max[:, :, None]), axis=-1
        )
        return ((new_max, new_sum), None)

    start_max = jnp.full((HEADS, row_count), NEG_START, jnp.float32)
    (final_max, final_sum), unused = lax.scan(
        lse_step, (start_max, jnp.zeros_like(start_max)), (key_stack, id_stack)
    )
    log_total = final_max + jnp.log(final_sum)

    def out_step(running, block_in):
        key_heads, value_heads, key_ids = block_in
        scores = masked_scores(query_heads, key_heads, own_ids, key_ids, score_scale)
        attn_prob = jnp.exp(scores - log_total[:, :, None]).astype(jnp.bfloat16)
        return (
            running
            + jnp.einsum(
                "hqk,khd->qhd", attn_prob, value_heads, preferred_element_type=jnp.float32
            ),
            None,
        )

    attn_sum, unused = lax.scan(
        out_step,
        jnp.zeros((row_count, HEADS, head_dim), jnp.float32),
        (key_stack, value_stack, id_stack),
    )
    attended = attn_sum.reshape(row_count, model_width).astype(jnp.bfloat16)
    middle = inputs + dot_plain(attended, out_w) + out_b.astype(jnp.float32)
    normed_two = norm_rows(middle, second_gain, second_bias).astype(jnp.bfloat16)
    hidden = dot_plain(normed_two, up_w) + up_b.astype(jnp.float32)
    active = jax.nn.gelu(hidden, approximate=True).astype(jnp.bfloat16)
    output = middle + dot_plain(active, down_w) + down_b.astype(jnp.float32)
    top_grad = out_grad[0]
    top_float = top_grad.astype(jnp.float32)
    grad_down_w = dot_left(active, top_grad)
    grad_down_b = jnp.sum(top_float, axis=0)
    grad_active = dot_right(top_grad, down_w)
    unused, gelu_pull = jax.vjp(partial(jax.nn.gelu, approximate=True), hidden)
    grad_hidden = gelu_pull(grad_active)[0].astype(jnp.bfloat16)
    grad_up_w = dot_left(normed_two, grad_hidden)
    grad_up_b = jnp.sum(grad_hidden.astype(jnp.float32), axis=0)
    grad_normed_two = dot_right(grad_hidden, up_w)
    unused, second_pull = jax.vjp(norm_rows, middle, second_gain, second_bias)
    grad_middle, grad_gain_two, grad_bias_two = second_pull(grad_normed_two)
    grad_middle = grad_middle + top_float
    grad_branch = grad_middle.astype(jnp.bfloat16)
    grad_out_w = dot_left(attended, grad_branch)
    grad_out_b = jnp.sum(grad_branch.astype(jnp.float32), axis=0)
    grad_attended = dot_right(grad_branch, out_w).astype(jnp.bfloat16)
    grad_heads = grad_attended.reshape(row_count, HEADS, head_dim)
    row_delta = jnp.sum(grad_heads.astype(jnp.float32) * attn_sum, axis=-1)
    head_delta = row_delta.T
    query_start = jnp.zeros((row_count, HEADS, head_dim), jnp.float32)

    def full_step(grad_query, block_in):
        key_heads, value_heads, key_ids = block_in
        scores = masked_scores(query_heads, key_heads, own_ids, key_ids, score_scale)
        attn_prob = jnp.exp(scores - log_total[:, :, None])
        grad_prob = jnp.einsum(
            "qhd,khd->hqk", grad_heads, value_heads, preferred_element_type=jnp.float32
        )
        grad_score = (attn_prob * (grad_prob - head_delta[:, :, None])).astype(jnp.bfloat16)
        grad_query = grad_query + jnp.einsum(
            "hqk,khd->qhd", grad_score, key_heads, preferred_element_type=jnp.float32
        )
        grad_key = (
            jnp.einsum("hqk,qhd->khd", grad_score, query_heads, preferred_element_type=jnp.float32)
            * score_scale
        )
        grad_value = jnp.einsum(
            "hqk,qhd->khd",
            attn_prob.astype(jnp.bfloat16),
            grad_heads,
            preferred_element_type=jnp.float32,
        )
        return (
            grad_query,
            (grad_key.reshape(key_block, model_width), grad_value.reshape(key_block, model_width)),
        )

    grad_query, key_terms = lax.scan(full_step, query_start, (key_stack, value_stack, id_stack))
    key_grad, value_grad = (
        lax.psum_scatter(
            key_terms[0].reshape(total_rows, model_width), "ctx", scatter_dimension=0, tiled=True
        ),
        lax.psum_scatter(
            key_terms[1].reshape(total_rows, model_width), "ctx", scatter_dimension=0, tiled=True
        ),
    )
    grad_query_rows = (
        (grad_query * score_scale).reshape(row_count, model_width).astype(jnp.bfloat16)
    )
    grad_key_rows = key_grad.astype(jnp.bfloat16)
    grad_value_rows = value_grad.astype(jnp.bfloat16)
    grad_query_w = dot_left(normed_one, grad_query_rows)
    grad_query_b = jnp.sum(grad_query_rows.astype(jnp.float32), axis=0)
    grad_key_w = dot_left(normed_one, grad_key_rows)
    grad_value_w = dot_left(normed_one, grad_value_rows)
    grad_value_b = jnp.sum(grad_value_rows.astype(jnp.float32), axis=0)
    grad_normed_one = (
        dot_right(grad_query_rows, query_w)
        + dot_right(grad_key_rows, key_w)
        + dot_right(grad_value_rows, value_w)
    )
    unused, first_pull = jax.vjp(norm_rows, inputs, first_gain, first_bias)
    grad_inputs, grad_gain_one, grad_bias_one = first_pull(grad_normed_one)
    grad_inputs = grad_inputs + grad_middle
    (
        share_gain_one,
        share_bias_one,
        share_query_w,
        share_query_b,
        share_key_w,
        share_value_w,
        share_value_b,
        share_out_w,
        share_out_b,
        share_gain_two,
        share_bias_two,
        share_up_w,
        share_up_b,
        share_down_w,
        share_down_b,
    ) = (
        lax.psum_scatter(
            grad_gain_one.astype(jnp.bfloat16), "wsh", scatter_dimension=0, tiled=True
        ).astype(jnp.float32),
        lax.psum_scatter(
            grad_bias_one.astype(jnp.bfloat16), "wsh", scatter_dimension=0, tiled=True
        ).astype(jnp.float32),
        lax.psum_scatter(
            grad_query_w.astype(jnp.bfloat16), "wsh", scatter_dimension=0, tiled=True
        ).astype(jnp.float32),
        lax.psum_scatter(
            grad_query_b.astype(jnp.bfloat16), "wsh", scatter_dimension=0, tiled=True
        ).astype(jnp.float32),
        lax.psum_scatter(
            grad_key_w.astype(jnp.bfloat16), "wsh", scatter_dimension=0, tiled=True
        ).astype(jnp.float32),
        lax.psum_scatter(
            grad_value_w.astype(jnp.bfloat16), "wsh", scatter_dimension=0, tiled=True
        ).astype(jnp.float32),
        lax.psum_scatter(
            grad_value_b.astype(jnp.bfloat16), "wsh", scatter_dimension=0, tiled=True
        ).astype(jnp.float32),
        lax.psum_scatter(
            grad_out_w.astype(jnp.bfloat16), "wsh", scatter_dimension=0, tiled=True
        ).astype(jnp.float32),
        lax.psum_scatter(
            grad_out_b.astype(jnp.bfloat16), "wsh", scatter_dimension=0, tiled=True
        ).astype(jnp.float32),
        lax.psum_scatter(
            grad_gain_two.astype(jnp.bfloat16), "wsh", scatter_dimension=0, tiled=True
        ).astype(jnp.float32),
        lax.psum_scatter(
            grad_bias_two.astype(jnp.bfloat16), "wsh", scatter_dimension=0, tiled=True
        ).astype(jnp.float32),
        lax.psum_scatter(
            grad_up_w.astype(jnp.bfloat16), "wsh", scatter_dimension=0, tiled=True
        ).astype(jnp.float32),
        lax.psum_scatter(
            grad_up_b.astype(jnp.bfloat16), "wsh", scatter_dimension=0, tiled=True
        ).astype(jnp.float32),
        lax.psum_scatter(
            grad_down_w.astype(jnp.bfloat16), "wsh", scatter_dimension=0, tiled=True
        ).astype(jnp.float32),
        lax.psum_scatter(
            grad_down_b.astype(jnp.bfloat16), "wsh", scatter_dimension=0, tiled=True
        ).astype(jnp.float32),
    )
    totals = lax.psum(
        (
            share_gain_one,
            share_bias_one,
            share_query_w,
            share_query_b,
            share_key_w,
            share_value_w,
            share_value_b,
            share_out_w,
            share_out_b,
            share_gain_two,
            share_bias_two,
            share_up_w,
            share_up_b,
            share_down_w,
            share_down_b,
        ),
        "ctx",
    )
    return (
        output.astype(jnp.bfloat16)[None],
        grad_inputs.astype(jnp.bfloat16)[None],
        totals[0],
        totals[1],
        totals[2],
        totals[3],
        totals[4],
        totals[5],
        totals[6],
        totals[7],
        totals[8],
        totals[9],
        totals[10],
        totals[11],
        totals[12],
        totals[13],
        totals[14],
    )


MESH = pl.DeviceIdType.MESH
F32 = jnp.float32
BF = jnp.bfloat16
GROUPS = 4
LANES = 128


def flip(value, mask):
    return ((value // 2 + mask // 2) % 2) * 2 + (value + mask) % 2


def dot_nn(left, right):
    return lax.dot_general(left, right, (((1,), (0,)), ((), ())), preferred_element_type=F32)


def dot_nt(left, right):
    return lax.dot_general(left, right, (((1,), (1,)), ((), ())), preferred_element_type=F32)


def dot_tn(left, right):
    return lax.dot_general(left, right, (((0,), (0,)), ((), ())), preferred_element_type=F32)


def unit_rows(inputs):
    row_mean = jnp.mean(inputs, axis=-1, keepdims=True)
    centred = inputs - row_mean
    variance = jnp.mean(centred * centred, axis=-1, keepdims=True)
    scale = lax.rsqrt(variance + EPS)
    return centred * scale, scale


def unit_rows_back(grad_normed, unit, scale, gain):
    grad_unit = grad_normed * gain
    return scale * (
        grad_unit
        - jnp.mean(grad_unit, axis=-1, keepdims=True)
        - unit * jnp.mean(grad_unit * unit, axis=-1, keepdims=True)
    )


def rows_sum(values):
    return jnp.sum(values, axis=0, keepdims=True)


def sum_bf(*values):
    return sum([one.astype(F32) for one in values]).astype(BF)


class Wires:
    def __init__(self, send_sems, recv_sems):
        self.send_sems, self.recv_sems, self.used, self.started = send_sems, recv_sems, 0, []

    def take(self, count=1):
        first = self.used
        self.used += count
        return first

    def copy(self, index, source, target, device):
        return pltpu.make_async_remote_copy(
            src_ref=source,
            dst_ref=target,
            send_sem=self.send_sems.at[index % SEND_SEMS],
            recv_sem=self.recv_sems.at[index],
            device_id=device,
            device_id_type=MESH,
        )

    def send(self, source, target, device):
        one = self.copy(self.take(), source, target, device)
        one.start()
        self.started.append((one, None))
        return one

    def later(self, one, when=None):
        self.started.append((one, when))
        return one

    def plan(self, source, target, device):
        return self.later(self.copy(self.take(), source, target, device))

    def drain(self):
        for one, when in self.started:
            if when is None:
                one.wait_send()
            else:
                pl.when(when)(one.wait_send)


ORDER = (
    "up_grad", "ph_combine", "down_grad", "A_e0", "A_e1", "D_xout", "y_part", "wait_ph", "ln2",
    "sums", "early", "A2a", "out_grad", "bo0", "bo1", "bo2", "A2b", "up_xin", "A_e2", "D_in", "bo3",
    "kv_out", "bw0", "A3", "D2a", "D2b", "early2", "bw1", "go_combine", "up_in", "A_out", "D3",
    "py_combine", "U2a", "bw2", "bw3", "U2b", "D_turn", "U3", "go_out", "kv_in", "qkv_grad", "D_o1",
    "A_turn", "gq_comb", "D_i1", "U_turn", "h1_part", "D_i2", "G2a", "A_o1", "gq_fin", "A_i1",
    "G2b", "U_i1", "A_i2", "U_o1", "H2a", "q_start", "h1_e2", "A_i3", "G3", "U_i2", "go_in", "H3",
    "q_o1", "q_i1", "H2b", "G_turn", "U_i3", "q_i2", "layer_out", "G_o1", "h1_fin", "D_i3", "G_i1",
    "q_i3", "small", "G_i2", "G_i3", "fin",
)


def layer_kernel(sizes, names, *refs):
    n_ctx, n_doc, R, D, S, FS = sizes
    r = dict(zip(names, refs, strict=True))
    G = n_ctx // GROUPS
    last = GROUPS - 1
    half = GROUPS * R
    c = lax.axis_index("ctx")
    w = lax.axis_index("wsh")
    hg, px = c // G, c % G

    def zdev(group):
        return {"ctx": group * G + px, "wsh": w}

    def wdev(index):
        return {"ctx": c, "wsh": index}

    xdev = {"ctx": hg * G + 1 - px, "wsh": w}
    left, right = zdev((hg + last) % GROUPS), zdev((hg + 1) % GROUPS)
    w1, w2, w3 = flip(w, 1), flip(w, 2), flip(w, 3)
    sib, across, diag = wdev(w1), wdev(w2), wdev(w3)
    wires = Wires(r["send_sems"], r["recv_sems"])
    lane = lax.broadcasted_iota(jnp.int32, (1, LANES), 1)
    low_half = lane < LANES // 2

    def pick(table):
        return sum([jnp.where(hg == i, one, 0) for i, one in enumerate(table)])

    def by_distance(step):
        return (
            jnp.where(step == 0, pick((3, 3, 0, 0)), 0)
            + jnp.where(step == 1, pick((2, 0, 3, 1)), 0)
            + jnp.where(step == 2, pick((1, 2, 1, 2)), 0)
            + jnp.where(step == 3, hg, 0)
        )

    local = r["local_sems"]

    def fetch(index, source, target):
        one = pltpu.make_async_copy(source, target, local.at[index])
        one.start()
        return one

    tok_in = fetch(0, r["tok"], r["x_s"].at[hg])
    qkv_in = [fetch(1 + i, r[name], r["win_s"].at[i]) for i, name in enumerate(("wq", "wk", "wv"))]
    dy_in = fetch(4, r["dy"], r["dy_s"].at[w])
    wo_in = [
        fetch(5, r["wout"].at[pl.ds(0, LANES)], r["wo_s"].at[w, pl.ds(0, LANES)]),
        fetch(6, r["wout"].at[pl.ds(LANES, S - LANES)], r["wo_s"].at[w, pl.ds(S, S - LANES)]),
    ]
    wu_in = fetch(7, r["wup"].at[:, pl.ds(pl.multiple_of(w * FS, FS), FS)], r["wu_s"].at[w])
    wd_in = fetch(8, r["wdown"], r["wd_s"])

    barrier = pltpu.get_barrier_semaphore()
    ctx_peers = [{"ctx": (c + i) % n_ctx, "wsh": w} for i in range(1, n_ctx)]
    partners = ctx_peers + [sib, across, diag]
    for partner in partners:
        pl.semaphore_signal(barrier, inc=1, device_id=partner, device_id_type=MESH)

    pl.semaphore_wait(barrier, len(partners))

    class Gather:
        def __init__(self, slot):
            self.slot = slot
            self.to_across = wires.send(slot(w), slot(w), across)
            self.to_sib = wires.send(slot(w), slot(w), sib)

        def relay(self):
            self.to_across.wait_recv()
            self.on = wires.send(self.slot(w2), self.slot(w2), sib)

        def finish(self):
            self.to_sib.wait_recv()
            self.on.wait_recv()

    class Reduce:
        def __init__(self, part, recv):
            self.part, self.recv = part, recv
            self.a = wires.plan(part(w3), recv.at[0], sib)
            self.b = wires.plan(part(w1), recv.at[1], sib)
            self.c = wires.plan(recv.at[3], recv.at[2], across)

        def start(self):
            self.a.start()
            self.b.start()

        def combine(self):
            self.a.wait_recv()
            self.recv[3] = sum_bf(self.part(w2)[...], self.recv[0])
            self.c.start()

        def finish(self):
            self.b.wait_recv()
            self.c.wait_recv()
            return (
                self.part(w)[...].astype(F32)
                + self.recv[1].astype(F32)
                + self.recv[2].astype(F32)
            )

    class LineSum:
        def __init__(self, part, recv):
            self.part, self.recv = part, recv
            self.first_at = wires.take(5)
            for i in range(3):
                wires.later(self.message(i, True), hg > i)
                wires.later(self.message(i, False), hg < last - i)

        def message(self, i, leftward):
            block, slot = (i, i) if leftward else (last - i, 3 + i)
            return wires.copy(
                self.first_at + (i if leftward else 4 - i), self.part(block), self.recv.at[slot], left if leftward else right
            )

        def ends_block(self, block):
            for i in range(2):

                @pl.when((hg == last) & (block == i))
                def _():
                    self.message(i, True).start()

                @pl.when((hg == 0) & (block == last - i))
                def _():
                    self.message(i, False).start()

        def ends(self, which=(0, 1, 2)):
            for i in which:

                @pl.when(hg == last)
                def _():
                    self.message(i, True).start()

                @pl.when(hg == 0)
                def _():
                    self.message(i, False).start()

        def pass_on(self, position, i, leftward):
            @pl.when(hg == position)
            def _():
                one = self.message(i, leftward)
                one.wait_recv()
                block, slot = (i, i) if leftward else (last - i, 3 + i)
                self.part(block)[...] = sum_bf(self.part(block)[...], self.recv[slot])
                one.start()

        def second(self, which=(0, 1)):
            for i in which:
                self.pass_on(2, i, True)
                self.pass_on(1, i, False)

        def third(self):
            self.pass_on(1, 0, True)
            self.pass_on(2, 0, False)

        def final(self, put):
            for position in range(GROUPS):

                @pl.when(hg == position)
                def _():
                    total = self.part(position)[...].astype(F32)
                    if position < last:
                        self.message(position, True).wait_recv()
                        total = total + self.recv[position].astype(F32)
                    if position > 0:
                        self.message(last - position, False).wait_recv()
                        total = total + self.recv[3 + last - position].astype(F32)
                    put(total)

    class LineGather:
        def __init__(self, slot, to_x, own=None):
            self.slot, self.to_x, self.own = slot, to_x, own
            self.first_at = wires.take(3)
            self.x_at = wires.take(GROUPS) if to_x else None
            for d in (1, 2, 3):
                wires.later(self.message(d, 0), (hg >= d - 1) & (hg < last))
                wires.later(self.message(d, 1), (hg + d - 1 <= last) & (hg > 0))
            if to_x:
                for b in range(GROUPS):
                    wires.later(self.x_message(b))

        def message(self, d, side):
            block = (hg + GROUPS + (1 - d) * (1 - 2 * side)) % GROUPS
            device = zdev((hg + GROUPS + 1 - 2 * side) % GROUPS)
            first = self.own is not None and isinstance(d, int) and d == 1
            source = self.own if first else self.slot(block)
            return wires.copy(self.first_at + (3 - d) * (1 - side) + (d - 1) * side, source, self.slot(block), device)

        def x_message(self, block):
            return wires.copy(self.x_at + block, self.slot(block), self.slot(block), xdev)

        def start(self):
            pl.when(hg < last)(self.message(1, 0).start)
            pl.when(hg > 0)(self.message(1, 1).start)
            if self.to_x:
                self.x_message(hg).start()

        def arrived(self, d, side, then=None):
            block = (hg + GROUPS - d * (1 - 2 * side)) % GROUPS
            here = jnp.where(side == 0, (hg >= d).astype(jnp.int32), (hg + d <= last).astype(jnp.int32))
            onward = here * jnp.where(side == 0, (hg < last).astype(jnp.int32), (hg > 0).astype(jnp.int32))

            @pl.when(here == 1)
            def _():
                wires.copy(
                    self.first_at + (3 - d) * (1 - side) + (d - 1) * side, self.slot(block), self.slot(block), left
                ).wait_recv()

            @pl.when(onward == 1)
            def _():
                self.message(d + 1, side).start()

            @pl.when(here == 1)
            def _():
                if self.to_x:
                    self.x_message(block).start()
                if then is not None:
                    then(block)

        def inner(self, d):
            self.arrived(d, jnp.where(hg < 2, 1, 0))

        def outer(self, d):
            self.arrived(d, jnp.where(hg < 2, 0, 1))

        def done(self):
            for b in range(GROUPS):
                self.x_message(b).wait_recv()

    x_s, h1_s, q_s, kv_s = r["x_s"], r["h1_s"], r["q_s"], r["kv_s"]
    rows_two = R // 2
    tokens = [
        LineGather(
            lambda b, j=j: x_s.at[b, pl.ds(j * rows_two, rows_two)],
            False,
            r["tok"].at[pl.ds(j * rows_two, rows_two)],
        )
        for j in (0, 1)
    ]
    for one in tokens:
        one.start()
    for one in qkv_in:
        one.wait()
    own_w = pl.ds(pl.multiple_of(w * S, S), S)
    win, wq_s = r["win_s"], r["wq_s"]
    for g in range(GROUPS):

        @pl.when(hg == g)
        def _():
            a = g * S
            wq_s[own_w, 0:S] = win[0, :, a : a + S]
            wq_s[own_w, S : 2 * LANES] = jnp.zeros((S, 2 * LANES - S), BF)
            wq_s[own_w, 2 * LANES : 2 * LANES + S] = win[1, :, a : a + S]
            wq_s[own_w, 2 * LANES + S : 4 * LANES] = win[2, :, a + LANES : a + S]
            wq_s[own_w, 4 * LANES : 5 * LANES] = win[2, :, a : a + LANES]

    par_s = r["par_s"]
    par_s[w] = jnp.zeros((8, 2 * LANES), F32)
    for i, name in enumerate(("n1g", "n1b", "bq", "bv", "bo", "n2g", "n2b", "bd")):
        par_s[w, i : i + 1, 0:S] = r[name][...].astype(F32)[None, :]
    r["wo_s"][:, LANES:S, :] = jnp.zeros((GROUPS, S - LANES, D), BF)
    ws_all = Gather(lambda i: wq_s.at[pl.ds(pl.multiple_of(i * S, S), S)])
    par_all = Gather(lambda i: par_s.at[i])
    for one in wo_in:
        one.wait()
    dy_in.wait()
    wo_s, dy_s, wu_s = r["wo_s"], r["dy_s"], r["wu_s"]
    wo_top = Gather(lambda i: wo_s.at[i, pl.ds(0, LANES)])
    wo_low = Gather(lambda i: wo_s.at[i, pl.ds(S, S - LANES)])
    dy_all = Gather(lambda i: dy_s.at[i])
    up_sends = [
        wires.send(
            r["wup"].at[:, pl.ds(pl.multiple_of(flip(w, k) * FS, FS), FS)],
            wu_s.at[w],
            wdev(flip(w, k)),
        )
        for k in (2, 3, 1)
    ]
    inner_side = jnp.where(hg < 2, 1, 0)
    tokens[0].arrived(1, inner_side)
    tokens[0].arrived(1, 1 - inner_side)
    par_all.relay()
    ws_all.relay()
    tokens[1].arrived(1, inner_side)
    tokens[1].arrived(1, 1 - inner_side)
    par_all.finish()

    pars = jnp.concatenate([par_s[i][:, :S] for i in range(GROUPS)], axis=1)
    gain_one, bias_one, out_b, gain_two, bias_two, down_b = [
        pars[i : i + 1] for i in (0, 1, 4, 5, 6, 7)
    ]
    up_b = r["bup"][...].astype(F32)[None, :]
    own_par = par_s[hg]
    v_tile, v_last = own_par[3:4, :LANES], own_par[3:4, LANES:]
    qkv_b = jnp.concatenate(
        [own_par[2:3, :], jnp.zeros((1, LANES), F32), pltpu.roll(v_last, LANES // 2, 1), v_tile],
        axis=1,
    )
    ws_all.finish()
    tok_in.wait()

    kv_first = wires.take(2 * GROUPS)

    def kv_copy(block, j):
        rows = pl.ds(pl.multiple_of(block * R + j * rows_two, rows_two), rows_two)
        return wires.copy(
            kv_first + 2 * block + j, kv_s.at[0, rows], kv_s.at[1, rows], xdev
        )

    def project(block, j):
        rows = pl.ds(pl.multiple_of(j * rows_two, rows_two), rows_two)
        unit, unused = unit_rows(x_s[block, rows, :].astype(F32))
        normed = (unit * gain_one + bias_one).astype(BF)
        h1_s[block, rows, :] = normed
        qkv = dot_nn(normed, wq_s[...]) + qkv_b
        queries = qkv[:, : 2 * LANES].astype(BF).astype(F32) * 0.125
        q_s[0, block, rows, :] = jnp.where(low_half, queries[:, :LANES], 0.0).astype(BF)
        q_s[1, block, rows, :] = jnp.where(low_half, 0.0, queries[:, :LANES]).astype(BF)
        q_s[2, block, rows, :] = queries[:, LANES:].astype(BF)
        kv_rows = pl.ds(pl.multiple_of(block * R + j * rows_two, rows_two), rows_two)
        kv_s[0, kv_rows, :] = qkv[:, 2 * LANES :].astype(BF)
        kv_copy(block, j).start()

    def near_project(i, carry):
        away = jnp.where(i < 2, 0, jnp.where(i < 4, 1, 3)) * (1 - 2 * (1 - inner_side))
        block = (hg + 2 * GROUPS + jnp.where(i < 4, away, (1 - 2 * inner_side))) % GROUPS

        @pl.when((i < 4) | ((hg > 0) & (hg < last)))
        def _():
            project(block, i % 2)

        return carry

    tokens[0].arrived(2, inner_side)
    lax.fori_loop(0, 3, near_project, 0)
    tokens[1].arrived(2, inner_side)
    lax.fori_loop(3, 6, near_project, 0)

    def far_project(i, carry):
        d = i + 2
        block = (hg + GROUPS - d * (1 - 2 * inner_side)) % GROUPS
        for j, one in enumerate(tokens):

            @pl.when(d > 2)
            def _():
                one.arrived(d, inner_side)

            @pl.when(jnp.where(hg < 2, hg + d <= last, hg >= d))
            def _():
                project(block, j)

        return carry

    lax.fori_loop(0, 2, far_project, 0)
    wo_top.relay()
    wo_low.relay()
    doc_ends = []
    for i in range(n_doc):
        doc_ends.append(r["doc"][0, i] + (doc_ends[-1] if i else 0))

    def doc_ids(positions):
        return sum([(positions >= end).astype(jnp.int32) for end in doc_ends])

    key_at = lax.broadcasted_iota(jnp.int32, (1, half), 1)
    key_block = sum([(key_at >= i * R).astype(jnp.int32) for i in range(1, GROUPS)])
    key_base = key_at + key_block * (R * (G - 1))
    key_ids = [doc_ids(key_base + px * R), doc_ids(key_base + (1 - px) * R)]
    KT, VT, KO = (0, 0, LANES), (2 * LANES, 2 * LANES, LANES), (0, 0, LANES)
    e_s, li_s, oa_s, os_s, or_s = r["e_s"], r["li_s"], r["oa_s"], r["os_s"], r["or_s"]
    of_s = r["of_s"]

    def pack(target, first, final):
        target[0:R, :] = first.astype(BF)
        turned = pltpu.roll(final[rows_two:, :], LANES // 2, 1)
        target[R : R + rows_two, :] = jnp.where(low_half, turned, final[:rows_two, :]).astype(BF)

    def unpack(source, target):
        target[:, :LANES] = source[0:R, :]
        both = source[R : R + rows_two, :].astype(F32)
        target[0:rows_two, LANES:] = jnp.where(low_half, 0.0, both).astype(BF)
        turned = pltpu.roll(both, LANES // 2, 1)
        target[rows_two:, LANES:] = jnp.where(low_half, 0.0, turned).astype(BF)

    class Turn:
        def __init__(self, source, target):
            self.source, self.target = source, target
            self.first_at = wires.take(GROUPS - 1)
            for i in (1, 2, 3):
                wires.later(self.message((hg + i) % GROUPS))

        def message(self, block):
            index = self.first_at + (block - hg + GROUPS) % GROUPS - 1
            return wires.copy(index, self.source.at[block], self.target.at[hg], zdev(block))

        def arrived(self, block):
            index = self.first_at + (hg - block + GROUPS) % GROUPS - 1
            wires.copy(index, self.target.at[block], self.target.at[block], left).wait_recv()

    on_s = r["on_s"]
    o_turn = Turn(os_s, on_s)

    def row_ids_of(block):
        row_at = (block * G + px) * R + lax.broadcasted_iota(jnp.int32, (R, 1), 0)
        return doc_ids(row_at)

    def attend_side(block, side):
        row_ids = row_ids_of(block)
        same = row_ids == key_ids[side]
        scores = [
            jnp.where(
                same, dot_nt(q_s[h, block], kv_s[side, :, KT[h] : KT[h] + LANES]), NEG_START
            )
            for h in range(3)
        ]
        tops = [jnp.max(one, axis=-1, keepdims=True) for one in scores]
        weights = [jnp.exp(one - top) for one, top in zip(scores, tops, strict=True)]
        mixed = []
        for h in range(3):
            rounded = weights[h].astype(BF)
            e_s[h, block, side] = rounded
            mixed.append(dot_nn(rounded, kv_s[side, :, VT[h] : VT[h] + LANES]))
        totals = [jnp.sum(one, axis=-1, keepdims=True) for one in weights]
        return tops, totals, mixed

    def attend_own(block, carry):
        tops, totals, mixed = attend_side(block, 0)
        for h in range(3):
            li_s[0, h, block] = jnp.broadcast_to(tops[h], (R, LANES))
            li_s[1, h, block] = jnp.broadcast_to(totals[h], (R, LANES))
            of_s[h, block] = mixed[h]
        return carry

    lax.fori_loop(0, GROUPS, attend_own, 0)
    for b in range(GROUPS):
        for j in (0, 1):
            kv_copy(b, j).wait_recv()
            wires.later(kv_copy(b, j))

    def attend(step, carry):
        block = by_distance(step)
        tops, totals, mixed = attend_side(block, 1)
        outs = []
        for h in range(3):
            top, total = tops[h], totals[h]
            own_top = li_s[0, h, block]
            both_top = jnp.maximum(own_top, top)
            own_part, part = jnp.exp(own_top - both_top), jnp.exp(top - both_top)
            inverse = 1.0 / (li_s[1, h, block] * own_part + total * part)
            own_part, part = own_part * inverse, part * inverse
            li_s[0, h, block] = own_part
            li_s[1, h, block] = part
            outs.append(of_s[h, block] * own_part + mixed[h] * part)
        first = jnp.where(low_half, outs[0], outs[1])
        final = jnp.where(low_half, 0.0, outs[2])
        oa_s[block, :, :LANES] = first
        oa_s[block, :, LANES:] = final
        pack(os_s.at[block], first, final)

        @pl.when(step < last)
        def _():
            o_turn.message(block).start()

        return carry

    lax.fori_loop(0, GROUPS, attend, 0)
    dy_all.relay()
    unpack(os_s.at[hg], or_s.at[hg])
    dy_all.finish()
    wd_in.wait()
    wd_s, dkv_s = r["wd_s"], r["dkv_s"]

    def top_rows(slot):
        return slot // 2, pl.ds(pl.multiple_of((slot % 2) * R, R), R)

    def top_part(slot, carry):
        dkv_s[top_rows(slot)] = dot_nt(dy_s[slot], wd_s[...])
        return carry

    lax.fori_loop(0, GROUPS, top_part, 0)
    wo_top.finish()
    wo_low.finish()
    for i in (1, 2, 3):
        there = (hg + i) % GROUPS
        o_turn.arrived(there)
        unpack(on_s.at[there], or_s.at[there])

    middle = x_s[hg].astype(F32) + out_b
    for i in range(GROUPS):
        middle += dot_nn(or_s[i], wo_s[i])
    x1_s, h2_s, g_s, da_s = r["x1_s"], r["h2_s"], r["g_s"], r["da_s"]
    x1_s[...] = middle
    unit_two, scale_two = unit_rows(middle)
    h2_s[w] = (unit_two * gain_two + bias_two).astype(BF)
    halves = [pl.ds(0, rows_two), pl.ds(rows_two, rows_two)]
    h2_all = [Gather(lambda i, part=part: h2_s.at[i, part]) for part in halves]
    wu_in.wait()
    for one in up_sends:
        one.wait_recv()
    ph_s, hr_s = r["ph_s"], r["hr_s"]
    ph = [
        Reduce(lambda i, part=part: ph_s.at[i, part], hr_s.at[k]) for k, part in enumerate(halves)
    ]

    def up_and_back(slot, start, count):
        rows = pl.ds(start, count)
        hidden = dot_nn(h2_s[slot, rows, :], wu_s[...].reshape(D, FS)) + up_b
        square = hidden * hidden
        inner = math.sqrt(2.0 / math.pi) * (hidden + 0.044715 * (square * hidden))
        bent = jnp.tanh(inner)
        g_s[slot, rows, :] = (0.5 * hidden * (1.0 + bent)).astype(BF)
        slope = 0.5 * (1.0 + bent) + 0.5 * hidden * (1.0 - bent * bent) * (
            math.sqrt(2.0 / math.pi) * (1.0 + 3.0 * 0.044715 * square)
        )
        top_at = pl.ds(pl.multiple_of((slot % 2) * R + start, rows_two), count)
        grad_hidden = (dkv_s[slot // 2, top_at, :] * slope).astype(BF)
        da_s[slot, rows, :] = grad_hidden
        ph_s[slot, rows, :] = dot_nt(grad_hidden, wu_s[...].reshape(D, FS)).astype(BF)

    def mlp_near(j, carry):
        @pl.when(j == 1)
        def _():
            for one in h2_all:
                one.to_sib.wait_recv()

        up_and_back(flip(w, j), 0, R)
        return carry

    lax.fori_loop(0, 2, mlp_near, 0)
    for one in ph:
        one.b.start()
    on_copies = [
        wires.plan(h2_s.at[w2, part], h2_s.at[w2, part], sib) for part in halves
    ]
    for k in (0, 1):
        h2_all[k].to_across.wait_recv()
        on_copies[k].start()
        up_and_back(w2, k * rows_two, rows_two)
        if k == 1:
            ph[0].combine()
        on_copies[k].wait_recv()
        up_and_back(w3, k * rows_two, rows_two)
        ph[k].a.start()

    gus_s, gas_s, gds_s, py_s = r["gus_s"], r["gas_s"], r["gds_s"], r["py_s"]
    cols = gas_s.shape[1]

    up_x_first = wires.take(2)

    def up_x(i):
        part = pl.ds(2 * i, 2)
        return wires.copy(up_x_first + i, gus_s.at[part, 1 - px], r["gux_s"].at[part], xdev)

    for i in (0, 1):
        wires.later(up_x(i))

    def up_grad(i, carry):
        at = pl.ds(pl.multiple_of(i * 2 * S, 2 * S), 2 * S)
        gus_s[pl.ds(2 * i, 2)] = (
            dot_tn(h2_s[:, :, at].reshape(half, 2 * S), da_s[...].reshape(half, FS))
            .astype(BF)
            .reshape(2, 2, S // 2, FS)
        )
        up_x(i).start()
        return carry

    def down_grad(i, carry):
        at = pl.ds(pl.multiple_of(i * 256, 256), 256)
        both = dot_tn(g_s[:, :, at].reshape(half, 256), dy_s[...].reshape(half, D)).astype(BF)
        gas_s[at, :] = both[:, :cols]
        gds_s[at, :] = both[:, cols:]
        return carry

    def y_part(j, carry):
        py_s[j] = dot_nn(g_s[j], wd_s[...]).astype(BF)
        return carry

    class Spread:
        def __init__(self, part, recv, slot, to_x):
            self.sum = LineSum(part, recv)
            self.gather = LineGather(slot, to_x)

        def turn(self):
            def put(total):
                self.gather.slot(hg)[...] = total.astype(BF)

            self.sum.final(put)
            self.gather.start()

    class Share:
        def __init__(self, rows):
            self.rows = rows
            self.at = wires.take(n_ctx - 1) - 1
            for i in range(1, n_ctx):
                wires.later(self.message(i))

        def message(self, i):
            return wires.copy(self.at + i, self.rows.at[c], self.rows.at[c], ctx_peers[i - 1])

        def start(self):
            for i in range(1, n_ctx):
                self.message(i).start()

        def total(self):
            for i in range(1, n_ctx):
                wires.copy(self.at + i, self.rows.at[c], self.rows.at[c], left).wait_recv()
            return sum([self.rows[i] for i in range(n_ctx)])

    n = S // 2
    n_down = FS // 8
    ga_f, gd_f, gu_s, up_f = r["gda"], r["gdb"], r["gu_s"], r["gup"]
    mine = pl.ds(pl.multiple_of(px * n, 8), n)
    theirs = pl.ds(pl.multiple_of((1 - px) * n, 8), n)

    def down_rows(b):
        return pl.ds(pl.multiple_of(px * (4 * n_down) + b * n_down, 8), n_down)

    down_here = pl.ds(pl.multiple_of(px * (4 * n_down), 8), 4 * n_down)
    down_there = pl.ds(pl.multiple_of((1 - px) * (4 * n_down), 8), 4 * n_down)
    py = Reduce(lambda i: py_s.at[i], r["yr_s"])
    up_y_first = wires.take(3) - 1

    def up_y(k, out):
        to = flip(w, k)
        return wires.copy(
            up_y_first + k, gus_s.at[to, px], gu_s.at[w if out else to], wdev(to)
        )

    for k in (1, 2, 3):
        wires.later(up_y(k, True))
    up = Spread(lambda b: gu_s.at[b], r["gul_s"], lambda b: up_f.at[b, px], True)
    down_x = wires.plan(gds_s.at[down_there], r["gdx_s"], xdev)
    down = Spread(
        lambda b: gds_s.at[down_rows(b)], r["gdl_s"], lambda b: gd_f.at[down_rows(b)], True
    )
    gat_s, gax_s = r["gat_s"], r["gax_s"]

    def across_rows(b):
        return pl.ds(pl.multiple_of(b * 2 * n_down + px * n_down, 8), n_down)

    most = Spread(
        lambda b: gas_s.at[pl.ds(pl.multiple_of(b * 2 * n_down, 8), 2 * n_down)],
        r["gal_s"],
        lambda b: ga_f.at[across_rows(b)],
        True,
    )
    most_x = wires.plan(gat_s.at[1 - px], gax_s, xdev)
    dz_s, dos_s, dor_s = r["dz_s"], r["dos_s"], r["dor_s"]
    don_s = r["don_s"]
    do_turn = Turn(dos_s, don_s)
    early, early_x_s, early_z_s = r["early_s"], r["early_x_s"], r["early_z_s"]
    late = r["late_s"]
    early_x = wires.plan(early, early_x_s, xdev)
    early_first = wires.take(3) - 1

    def early_z(i):
        return wires.copy(
            early_first + i, early_z_s.at[hg], early_z_s.at[hg], zdev((hg + i) % GROUPS)
        )

    for i in (1, 2, 3):
        wires.later(early_z(i))
    late_all = Share(late)
    gos_s, gor_s = r["gos_s"], r["gor_s"]
    go_s, gox_s, god_s, go_f = r["go_s"], r["gox_s"], r["god_s"], r["gout"]
    go = Reduce(lambda i: gos_s.at[i], gor_s)
    quarter = S // GROUPS

    def quarter_rows(b):
        return pl.ds(pl.multiple_of(b * quarter, 8), quarter)

    go_all = Spread(
        lambda b: go_s.at[quarter_rows(b)],
        r["gol_s"],
        lambda b: go_f.at[quarter_rows(b)],
        False,
    )
    go_x = wires.plan(god_s, gox_s, xdev)
    kvt_s, kvr_s, ph1_s, gqs_s = r["kvt_s"], r["kvr_s"], r["ph1_s"], r["gqs_s"]
    kv_back = wires.plan(kvt_s, kvr_s, xdev)
    h1_sum = LineSum(lambda b: ph1_s.at[b], r["h1r_s"])
    gq = Reduce(lambda i: gqs_s.at[pl.ds(pl.multiple_of(i * S, S), S)], r["gqr_s"])
    gqc_s, gqx_s, gqkv = r["gqc_s"], r["gqx_s"], r["gqkv"]
    qx = wires.plan(gqc_s.at[theirs], gqx_s, xdev)
    q_line = LineGather(lambda b: gqkv.at[b, mine], True)
    vecs, vecr = r["vecs_s"], r["vecr_s"]
    vec_first = wires.take(3) - 1

    def vec_send(k):
        return wires.copy(
            vec_first + k, vecs.at[flip(w, k)], vecr.at[k - 1], wdev(flip(w, k))
        )

    for k in (1, 2, 3):
        wires.later(vec_send(k))
    dq_s, dqkv_s, df_s = r["dq_s"], r["dqkv_s"], r["df_s"]

    steps = {}

    def step_of(name):
        def keep(body):
            steps[name] = body
            return body

        return keep

    @step_of("up_xin")
    def _():
        for i in (0, 1):
            up_x(i).wait_recv()
        here = gus_s.at[:, px]
        here[...] = sum_bf(here[...], r["gux_s"][...])
        gu_s[w] = gus_s[w, px]
        for k in (2, 3, 1):
            up_y(k, True).start()

    @step_of("up_in")
    def _():
        for k in (1, 2, 3):
            up_y(k, False).wait_recv()
        up.sum.ends()

    @step_of("D_in")
    def _():
        down_x.wait_recv()
        gds_s[down_here, :] = sum_bf(gds_s[down_here, :], r["gdx_s"][...])
        down.sum.ends()

    steps["D_xout"] = down_x.start
    for i in range(3):
        steps["A_e%d" % i] = partial(most.sum.ends, (i,))
    steps["A2a"] = partial(most.sum.second, (0,))
    steps["A2b"] = partial(most.sum.second, (1,))
    steps["A3"] = most.sum.third

    @step_of("A_out")
    def _():
        def put(total):
            gat_s[...] = total.astype(BF).reshape(2, n_down, cols)

        most.sum.final(put)
        most_x.start()

    @step_of("A_turn")
    def _():
        most_x.wait_recv()
        ga_f[across_rows(hg), :] = sum_bf(gat_s[px], gax_s[...])
        most.gather.start()

    for name, chain in (("U", up), ("D", down)):
        steps[name + "2a"] = partial(chain.sum.second, (0,))
        steps[name + "2b"] = partial(chain.sum.second, (1,))
        steps[name + "3"] = chain.sum.third
        steps[name + "_turn"] = chain.turn
    for name, line in (("U", up.gather), ("D", down.gather), ("A", most.gather), ("G", go_all.gather), ("q", q_line)):
        steps[name + "_i1"] = partial(line.inner, 1)
        steps[name + "_o1"] = partial(line.outer, 1)
        steps[name + "_i2"] = partial(line.inner, 2)
        steps[name + "_i3"] = partial(line.inner, 3)
    steps["H2a"] = partial(h1_sum.second, (0,))
    steps["H2b"] = partial(h1_sum.second, (1,))
    steps["H3"] = h1_sum.third
    steps["h1_e2"] = partial(h1_sum.ends, (2,))
    steps["go_combine"] = go.combine
    steps["py_combine"] = py.combine
    steps["gq_comb"] = gq.combine

    steps["G2a"] = partial(go_all.sum.second, (0,))
    steps["G2b"] = partial(go_all.sum.second, (1,))
    steps["G3"] = go_all.sum.third

    @step_of("go_out")
    def _():
        go_s[...] = go.finish().astype(BF)
        go_all.sum.ends()

    @step_of("go_in")
    def _():
        def put(total):
            god_s[...] = total.astype(BF)

        go_all.sum.final(put)
        go_x.start()

    @step_of("G_turn")
    def _():
        go_x.wait_recv()
        go_f[quarter_rows(hg), :] = sum_bf(god_s[...], gox_s[...])
        go_all.gather.start()

    steps["early"] = early_x.start

    @step_of("early2")
    def _():
        early_x.wait_recv()
        early_z_s[hg] = early[...] + early_x_s[...]
        for i in (1, 2, 3):
            early_z(i).start()

    @step_of("kv_in")
    def _():
        kv_back.wait_recv()
        dqkv_s[:, 2 * LANES :] = jnp.transpose(sum_bf(dkv_s[0], kvr_s[...]))

    @step_of("h1_part")
    def _():
        def h1_part(step, carry):
            block = by_distance(step)
            rows = pl.ds(pl.multiple_of(block * R, R), R)
            ph1_s[block] = dot_nt(dqkv_s[rows, :], wq_s[...]).astype(BF)
            h1_sum.ends_block(block)
            return carry

        lax.fori_loop(0, GROUPS, h1_part, 0)

    @step_of("qkv_grad")
    def _():
        def qkv_grad(i, carry):
            at = pl.ds(pl.multiple_of(i * 256, 256), 256)
            gqs_s[at, :] = dot_tn(h1_s[:, :, at].reshape(half, 256), dqkv_s[...]).astype(BF)
            return carry

        lax.fori_loop(0, D // 256, qkv_grad, 0)
        gq.start()
        late[c, :, 2 * D : 2 * D + 2 * LANES] = rows_sum(dqkv_s[:, : 2 * LANES].astype(F32))
        late[c, :, 2 * D + 2 * LANES :] = rows_sum(dqkv_s[:, 3 * LANES :].astype(F32))

    @step_of("gq_fin")
    def _():
        gqc_s[...] = gq.finish().astype(BF)
        qx.start()

    @step_of("q_start")
    def _():
        qx.wait_recv()
        gqkv[hg, mine, :] = sum_bf(gqc_s[mine, :], gqx_s[...])
        q_line.start()

    @step_of("h1_fin")
    def _():
        def keep_h1(total):
            df_s[...] = total

        h1_sum.final(keep_h1)
        grad_one = df_s[...]
        unit_one, scale_one = unit_rows(x_s[hg].astype(F32))
        grad_in = dz_s[...] + unit_rows_back(grad_one, unit_one, scale_one, gain_one)
        r["dx"][...] = grad_in.astype(BF)
        late[c, :, 0:D] = rows_sum(grad_one * unit_one)
        late[c, :, D : 2 * D] = rows_sum(grad_one)
        late_all.start()

    @step_of("layer_out")
    def _():
        r["y"][...] = (x1_s[...] + py.finish() + down_b).astype(BF)

    @step_of("small")
    def _():
        for i in (1, 2, 3):
            there = (hg + i) % GROUPS
            wires.copy(early_first + GROUPS - i, early_z_s.at[there], early_z_s.at[there], left).wait_recv()
        ones = sum([early_z_s[i] for i in range(GROUPS)])
        twos = late_all.total()
        bq_all, bv_all = [], []
        for g in range(GROUPS):
            group_sum = sum([late[g * G + i][:, 2 * D :] for i in range(G)])
            bq_all.append(group_sum[:, :S])
            v_end = pltpu.roll(group_sum[:, 2 * LANES : 3 * LANES], LANES // 2, 1)[:, : S - LANES]
            bv_all.append(jnp.concatenate([group_sum[:, 3 * LANES :], v_end], axis=1))
        vectors = [twos[:, 0:D], twos[:, D : 2 * D]] + [
            ones[:, i * D : (i + 1) * D] for i in range(4)
        ]
        for i in range(GROUPS):
            for j, one in enumerate(vectors):
                vecs[i, :, j * 256 : j * 256 + S] = one[:, i * S : (i + 1) * S]
            vecs[i, :, 6 * 256 : 6 * 256 + S] = bq_all[i]
            vecs[i, :, 7 * 256 : 7 * 256 + S] = bv_all[i]
        r["vec"][:, 8 * 256 :] = ones[:, 4 * D :]
        for k in (1, 2, 3):
            vec_send(k).start()

    carried = {}

    @step_of("up_grad")
    def _():
        lax.fori_loop(0, 2, up_grad, 0)

    steps["ph_combine"] = ph[1].combine

    @step_of("down_grad")
    def _():
        lax.fori_loop(0, FS // 256, down_grad, 0)

    @step_of("y_part")
    def _():
        lax.fori_loop(0, GROUPS, y_part, 0)
        py.start()

    @step_of("wait_ph")
    def _():
        carried["two"] = jnp.concatenate([one.finish() for one in ph], axis=0)

    @step_of("ln2")
    def _():
        grad_two = carried["two"]
        unit_two, scale_two = unit_rows(x1_s[...])
        top = r["dy_s"][w].astype(F32)
        grad_middle = top + unit_rows_back(grad_two, unit_two, scale_two, gain_two)
        dz = grad_middle.astype(BF)
        dz_s[...] = grad_middle
        carried["dz"], carried["unit"], carried["top"] = dz, unit_two, top

        def out_back(step, carry):
            block = by_distance(step)
            grad_o = dot_nt(dz, wo_s[block])
            pack(dos_s.at[block], grad_o[:, :LANES], grad_o[:, LANES:])

            @pl.when(step < last)
            def _():
                do_turn.message(block).start()

            return carry

        lax.fori_loop(0, GROUPS, out_back, 0)

    @step_of("sums")
    def _():
        unpack(dos_s.at[hg], dor_s.at[hg])
        early[:, 0:D] = rows_sum(carried["dz"].astype(F32))
        early[:, D : 2 * D] = rows_sum(carried["two"] * carried["unit"])
        early[:, 2 * D : 3 * D] = rows_sum(carried["two"])
        early[:, 3 * D : 4 * D] = rows_sum(carried["top"])
        early[:, 4 * D :] = rows_sum(da_s[...].reshape(half, FS).astype(F32))

    @step_of("out_grad")
    def _():
        for i in range(GROUPS):
            piece = dot_tn(or_s[i], carried["dz"])
            gos_s[i, 0:LANES, :] = piece[0:LANES, :].astype(BF)
            gos_s[i, LANES:S, :] = piece[S:, :].astype(BF)
        go.start()
        dkv_s[...] = jnp.zeros(dkv_s.shape, F32)

    def back_block(block, side):
        outs = dor_s[block].astype(F32)
        kept = oa_s[block]
        scaled = []
        for h in range(3):
            tile = 0 if h < 2 else LANES
            keep = low_half if h == 0 else jnp.logical_not(low_half)
            scaled.append(
                jnp.where(keep, outs[:, tile : tile + LANES], 0.0) * li_s[side, h, block]
            )
        deltas = [
            jnp.sum(
                scaled[h] * kept[:, KO[h] : KO[h] + LANES], axis=-1, keepdims=True
            )
            for h in range(3)
        ]
        rounded = [one.astype(BF) for one in scaled]
        grad_probs = [
            dot_nt(rounded[h], kv_s[side, :, VT[h] : VT[h] + LANES]) for h in range(3)
        ]
        grad_scores = [
            (e_s[h, block, side].astype(F32) * (grad_probs[h] - deltas[h])).astype(BF)
            for h in range(3)
        ]
        grads_q = [
            dot_nn(grad_scores[h], kv_s[side, :, KT[h] : KT[h] + LANES]) for h in range(3)
        ]
        for h in range(3):
            dkv_s[side, KT[h] : KT[h] + LANES, :] += dot_tn(q_s[h, block], grad_scores[h])
            dkv_s[side, VT[h] : VT[h] + LANES, :] += dot_tn(rounded[h], e_s[h, block, side])
        first = jnp.where(low_half, grads_q[0], grads_q[1]) * 0.125
        final = jnp.where(low_half, grads_q[2], 0.0) * 0.125
        if side == 1:
            dq_s[block, :, :LANES] = first
            dq_s[block, :, LANES:] = final
        else:
            rows = pl.ds(pl.multiple_of(block * R, R), R)
            dqkv_s[rows, :LANES] = (dq_s[block, :, :LANES] + first).astype(BF)
            dqkv_s[rows, LANES : 2 * LANES] = (dq_s[block, :, LANES:] + final).astype(BF)

    def nearest(step):
        return by_distance(last - step)

    @step_of("kv_out")
    def _():
        kvt_s[...] = dkv_s[1].astype(BF)
        kv_back.start()

    @step_of("fin")
    def _():
        for k in (1, 2, 3):
            vec_send(k).wait_recv()
        r["vec"][:, 0 : 8 * 256] = vecs[w] + vecr[0] + vecr[1] + vecr[2]
        down.gather.done()
        most.gather.done()
        up.gather.done()
        q_line.done()

    def attention_back(side, plans):
        def body(step, carry):
            block = nearest(step)
            if side == 1:

                @pl.when(step > 0)
                def _():
                    do_turn.arrived(block)
                    unpack(don_s.at[block], dor_s.at[block])

            back_block(block, side)
            for k, names in enumerate(plans):
                if names:

                    @pl.when(step == k)
                    def _():
                        for name in names:
                            steps[name]()

            return carry

        lax.fori_loop(0, GROUPS, body, 0)

    at = 0
    order = ORDER
    while at < len(order):
        name = order[at]
        at += 1
        if name in ("bo0", "bw0"):
            plans, kind = [[]], name[:2]
            while at < len(order) and (order[at][:2] == kind or len(plans) < GROUPS):
                if order[at][:2] == kind:
                    plans.append([])
                else:
                    plans[-1].append(order[at])
                at += 1
            attention_back(1 if kind == "bo" else 0, plans)
        else:
            steps[name]()
    assert wires.used == SEMS
    wires.drain()


def widen_kernel(S, names, *refs):
    r = dict(zip(names, refs, strict=True))
    n = S // 2
    started = []

    def send(source, target):
        one = pltpu.make_async_copy(source, target, r["sems"].at[len(started)])
        one.start()
        started.append(one)

    def put(name, at, value):
        r[name + "_b"][at] = value
        send(r[name + "_b"].at[at], r[name + "_o"].at[at])

    send(r["y"], r["y_o"])
    send(r["dx"], r["dx_o"])
    put("out", (slice(None),), r["out"][...].astype(F32))

    def heads(pieces):
        return jnp.concatenate(
            [r["qkv"][i, :, a:b].astype(F32) for i in range(GROUPS) for a, b in pieces], axis=1
        )

    put("q", (slice(None),), heads([(0, S)]))
    put("k", (slice(None),), heads([(2 * LANES, 2 * LANES + S)]))
    put("v", (slice(None),), heads([(4 * LANES, 5 * LANES), (2 * LANES + S, 4 * LANES)]))
    FS = r["up"].shape[3]
    for i in range(GROUPS):
        rows = slice(i * S, (i + 1) * S)
        both = [r[name][rows, :].astype(F32) for name in ("da", "db")]
        put("down", (rows, slice(None)), jnp.concatenate(both, axis=1))
        for j in (0, 1):
            at = (slice(j * n, (j + 1) * n), slice(i * FS, (i + 1) * FS))
            put("up", at, r["up"][i, j].astype(F32))
    at = 0
    for i in range(9):
        one = r["vec%d" % i]
        one[...] = r["vec"][0, at : at + one.shape[0]]
        at += max(one.shape[0], 256)
    for one in started:
        one.wait()


SEMS = 139
SEND_SEMS = 4


def fast_device(mesh_sizes, *arrays):
    (tokens, doc_lengths, out_grad, norm1_gain, norm1_bias, w_query, b_query, w_key, w_value,
     b_value, w_out, b_out, norm2_gain, norm2_bias, w_up, b_up, w_down, b_down) = arrays
    n_ctx, n_wsh = mesh_sizes
    R, D = tokens.shape[1], tokens.shape[2]
    S, FS, n_doc = D // GROUPS, w_down.shape[0], doc_lengths.shape[1]
    half, QW = GROUPS * R, 5 * LANES

    smem = pl.BlockSpec(memory_space=pltpu.SMEM)
    vmem = pl.BlockSpec(memory_space=pltpu.VMEM)
    anywhere = pl.BlockSpec(memory_space=pl.ANY)
    inputs = [
        ("doc", doc_lengths, smem),
        ("tok", tokens[0], anywhere),
        ("dy", out_grad[0], anywhere),
        ("wq", w_query, anywhere),
        ("wk", w_key, anywhere),
        ("wv", w_value, anywhere),
        ("wout", w_out, anywhere),
        ("wup", w_up, anywhere),
        ("wdown", w_down, anywhere),
        ("n1g", norm1_gain, vmem),
        ("n1b", norm1_bias, vmem),
        ("bq", b_query, vmem),
        ("bv", b_value, vmem),
        ("bo", b_out, vmem),
        ("n2g", norm2_gain, vmem),
        ("n2b", norm2_bias, vmem),
        ("bd", b_down, vmem),
        ("bup", b_up, vmem),
    ]
    n_up = S // 2
    outputs = [
        ("y", (R, D), BF),
        ("dx", (R, D), BF),
        ("gda", (FS, 2 * D // 3), BF),
        ("gdb", (FS, D // 3), BF),
        ("gup", (GROUPS, 2, n_up, FS), BF),
        ("gout", (S, D), BF),
        ("gqkv", (GROUPS, S, QW), BF),
        ("vec", (1, 8 * 256 + FS), F32),
    ]
    scratch = [
        ("x_s", (GROUPS, R, D), BF),
        ("h1_s", (GROUPS, R, D), BF),
        ("win_s", (3, S, D), BF),
        ("wq_s", (D, QW), BF),
        ("par_s", (GROUPS, 8, 2 * LANES), F32),
        ("q_s", (3, GROUPS, R, LANES), BF),
        ("kv_s", (2, half, 3 * LANES), BF),
        ("e_s", (3, GROUPS, 2, R, half), BF),
        ("li_s", (2, 3, GROUPS, R, LANES), F32),
        ("of_s", (3, GROUPS, R, LANES), F32),
        ("oa_s", (GROUPS, R, 2 * LANES), F32),
        ("os_s", (GROUPS, R + R // 2, LANES), BF),
        ("on_s", (GROUPS, R + R // 2, LANES), BF),
        ("or_s", (GROUPS, R, 2 * LANES), BF),
        ("wo_s", (GROUPS, 2 * LANES, D), BF),
        ("wu_s", (GROUPS, S, FS), BF),
        ("wd_s", (FS, D), BF),
        ("dy_s", (GROUPS, R, D), BF),
        ("x1_s", (R, D), F32),
        ("h2_s", (GROUPS, R, D), BF),
        ("g_s", (GROUPS, R, FS), BF),
        ("da_s", (GROUPS, R, FS), BF),
        ("ph_s", (GROUPS, R, D), BF),
        ("hr_s", (2, 4, R // 2, D), BF),
        ("py_s", (GROUPS, R, D), BF),
        ("yr_s", (4, R, D), BF),
        ("dz_s", (R, D), F32),
        ("dos_s", (GROUPS, R + R // 2, LANES), BF),
        ("don_s", (GROUPS, R + R // 2, LANES), BF),
        ("dor_s", (GROUPS, R, 2 * LANES), BF),
        ("dkv_s", (2, 3 * LANES, half), F32),
        ("kvt_s", (3 * LANES, half), BF),
        ("kvr_s", (3 * LANES, half), BF),
        ("dq_s", (GROUPS, R, 2 * LANES), F32),
        ("dqkv_s", (half, QW), BF),
        ("ph1_s", (GROUPS, R, D), BF),
        ("h1r_s", (6, R, D), BF),
        ("df_s", (R, D), F32),
        ("gas_s", (FS, 2 * D // 3), BF),
        ("gal_s", (6, FS // 4, 2 * D // 3), BF),
        ("gat_s", (2, FS // 8, 2 * D // 3), BF),
        ("gax_s", (FS // 8, 2 * D // 3), BF),
        ("gds_s", (FS, D // 3), BF),
        ("gdx_s", (FS // 2, D // 3), BF),
        ("gdl_s", (6, FS // 8, D // 3), BF),
        ("gus_s", (GROUPS, 2, S // 2, FS), BF),
        ("gu_s", (GROUPS, n_up, FS), BF),
        ("gux_s", (GROUPS, S // 2, FS), BF),
        ("gul_s", (6, n_up, FS), BF),
        ("go_s", (S, D), BF),
        ("gox_s", (S // GROUPS, D), BF),
        ("god_s", (S // GROUPS, D), BF),
        ("gol_s", (6, S // GROUPS, D), BF),
        ("gos_s", (GROUPS, S, D), BF),
        ("gor_s", (4, S, D), BF),
        ("gqs_s", (D, QW), BF),
        ("gqr_s", (4, S, QW), BF),
        ("gqc_s", (S, QW), BF),
        ("gqx_s", (S // 2, QW), BF),
        ("early_s", (1, 4 * D + FS), F32),
        ("early_x_s", (1, 4 * D + FS), F32),
        ("early_z_s", (GROUPS, 1, 4 * D + FS), F32),
        ("late_s", (n_ctx, 1, 2 * D + 4 * LANES), F32),
        ("vecs_s", (GROUPS, 1, 8 * 256), F32),
        ("vecr_s", (3, 1, 8 * 256), F32),
    ]
    sems = [("send_sems", SEND_SEMS), ("recv_sems", SEMS), ("local_sems", 9)]
    names = [one[0] for one in inputs + outputs + scratch + sems]
    y, dx, g_da, g_db, g_up, g_out, g_qkv, vec = pl.pallas_call(
        partial(layer_kernel, (n_ctx, n_doc, R, D, S, FS), names),
        out_shape=[pltpu.VMEM(shape, dtype) for name, shape, dtype in outputs],
        in_specs=[spec for name, value, spec in inputs],
        out_specs=[vmem] * len(outputs),
        scratch_shapes=[pltpu.VMEM(shape, dtype) for name, shape, dtype in scratch]
        + [pltpu.SemaphoreType.DMA((count,)) for name, count in sems],
        compiler_params=pltpu.CompilerParams(
            collective_id=0, has_side_effects=True, vmem_limit_bytes=62300000
        ),
        name="layer",
    )(*[value for name, value, spec in inputs])

    big = [
        ("y", (R, D), BF),
        ("dx", (R, D), BF),
        ("down", (FS, D), F32),
        ("up", (S, GROUPS * FS), F32),
        ("out", (S, D), F32),
        ("q", (S, D), F32),
        ("k", (S, D), F32),
        ("v", (S, D), F32),
    ]
    vectors = [("vec%d" % i, size) for i, size in enumerate([S] * 8 + [FS])]
    names = ["y", "dx", "da", "db", "up", "out", "qkv", "vec"]
    names += [name + "_o" for name, shape, dtype in big] + [name for name, size in vectors]
    names += [name + "_b" for name, shape, dtype in big[2:]] + ["sems"]
    wide = pl.pallas_call(
        partial(widen_kernel, S, names),
        in_specs=[vmem] * 8,
        out_specs=[anywhere] * len(big) + [vmem] * len(vectors),
        out_shape=[jax.ShapeDtypeStruct(shape, dtype) for name, shape, dtype in big]
        + [jax.ShapeDtypeStruct((size,), F32) for name, size in vectors],
        scratch_shapes=[pltpu.VMEM(shape, dtype) for name, shape, dtype in big[2:]]
        + [pltpu.SemaphoreType.DMA((18,))],
        compiler_params=pltpu.CompilerParams(vmem_limit_bytes=24000000),
        name="widen",
    )(y, dx, g_da, g_db, g_up, g_out, g_qkv, vec)
    y, dx, down, up, out, q, k, v, n1g, n1b, bo, n2g, n2b, bd, bq, bv, bup = wide
    return (
        y[None], dx[None], n1g, n1b, q, bq, k, v, bv, out, bo, n2g, n2b, up, bup, down, bd,
    )


def solution(mesh):
    in_specs = (
        P("wsh", "ctx", None),
        P("wsh", None),
        P("wsh", "ctx", None),
        P("wsh"),
        P("wsh"),
        P("wsh", None),
        P("wsh"),
        P("wsh", None),
        P("wsh", None),
        P("wsh"),
        P("wsh", None),
        P("wsh"),
        P("wsh"),
        P("wsh"),
        P("wsh", None),
        P("wsh"),
        P("wsh", None),
        P("wsh"),
    )
    out_specs = (
        P("wsh", "ctx", None),
        P("wsh", "ctx", None),
        P("wsh"),
        P("wsh"),
        P("wsh", None),
        P("wsh"),
        P("wsh", None),
        P("wsh", None),
        P("wsh"),
        P("wsh", None),
        P("wsh"),
        P("wsh"),
        P("wsh"),
        P("wsh", None),
        P("wsh"),
        P("wsh", None),
        P("wsh"),
    )
    sizes = (mesh.shape["ctx"], mesh.shape["wsh"])
    body = partial(fast_device, sizes) if sizes == (2 * GROUPS, GROUPS) else per_device
    return jax.shard_map(
        body, mesh=mesh, in_specs=in_specs, out_specs=out_specs, check_vma=False
    )
```

```python
from functools import partial
import math

import jax
import jax.numpy as jnp
from jax import lax
from jax.experimental import pallas as pl
from jax.experimental.pallas import tpu as pltpu
from jax.sharding import PartitionSpec as P

HEADS = 12


EPS = 1e-06
NEG_START = -1e30


def norm_rows(inputs, norm_gain, norm_bias):
    row_mean = jnp.mean(inputs, axis=-1, keepdims=True)
    centred = inputs - row_mean
    variance = jnp.mean(centred * centred, axis=-1, keepdims=True)
    return centred * lax.rsqrt(variance + EPS) * norm_gain + norm_bias


def doc_of(positions, doc_ends):
    return jnp.sum((positions[:, None] >= doc_ends[None, :]).astype(jnp.int32), axis=1)


def dot_plain(left, right):
    return jnp.dot(left, right, preferred_element_type=jnp.float32)


def dot_left(left, right):
    return lax.dot_general(
        left, right, (((0,), (0,)), ((), ())), preferred_element_type=jnp.float32
    )


def dot_right(left, right):
    return lax.dot_general(
        left, right, (((1,), (1,)), ((), ())), preferred_element_type=jnp.float32
    )


def masked_scores(query_heads, key_heads, query_ids, key_ids, score_scale):
    raw_scores = (
        jnp.einsum("qhd,khd->hqk", query_heads, key_heads, preferred_element_type=jnp.float32)
        * score_scale
    )
    same_doc = (query_ids[:, None] == key_ids[None, :])[None]
    return jnp.where(same_doc, raw_scores, -jnp.inf)


def per_device(
    tokens,
    doc_lengths,
    out_grad,
    norm1_gain,
    norm1_bias,
    w_query,
    b_query,
    w_key,
    w_value,
    b_value,
    w_out,
    b_out,
    norm2_gain,
    norm2_bias,
    w_up,
    b_up,
    w_down,
    b_down,
):
    (
        gain_one,
        bias_one,
        query_w,
        query_b,
        key_w,
        value_w,
        value_b,
        out_w,
        out_b,
        gain_two,
        bias_two,
        up_w,
        up_b,
        down_w,
        down_b,
    ) = (
        lax.all_gather(norm1_gain, "wsh", axis=0, tiled=True),
        lax.all_gather(norm1_bias, "wsh", axis=0, tiled=True),
        lax.all_gather(w_query, "wsh", axis=0, tiled=True),
        lax.all_gather(b_query, "wsh", axis=0, tiled=True),
        lax.all_gather(w_key, "wsh", axis=0, tiled=True),
        lax.all_gather(w_value, "wsh", axis=0, tiled=True),
        lax.all_gather(b_value, "wsh", axis=0, tiled=True),
        lax.all_gather(w_out, "wsh", axis=0, tiled=True),
        lax.all_gather(b_out, "wsh", axis=0, tiled=True),
        lax.all_gather(norm2_gain, "wsh", axis=0, tiled=True),
        lax.all_gather(norm2_bias, "wsh", axis=0, tiled=True),
        lax.all_gather(w_up, "wsh", axis=0, tiled=True),
        lax.all_gather(b_up, "wsh", axis=0, tiled=True),
        lax.all_gather(w_down, "wsh", axis=0, tiled=True),
        lax.all_gather(b_down, "wsh", axis=0, tiled=True),
    )
    row_count = tokens.shape[1]
    model_width = tokens.shape[2]
    head_dim = model_width // HEADS
    score_scale = head_dim ** (-0.5)
    first_gain = gain_one.astype(jnp.float32)
    first_bias = bias_one.astype(jnp.float32)
    second_gain = gain_two.astype(jnp.float32)
    second_bias = bias_two.astype(jnp.float32)
    inputs = tokens[0].astype(jnp.float32)
    doc_ends = jnp.cumsum(doc_lengths[0])
    own_ids = doc_of(
        lax.axis_index("ctx") * row_count + jnp.arange(row_count, dtype=jnp.int32), doc_ends
    )
    normed_one = norm_rows(inputs, first_gain, first_bias).astype(jnp.bfloat16)
    queries = (dot_plain(normed_one, query_w) + query_b.astype(jnp.float32)).astype(jnp.bfloat16)
    key_rows = dot_plain(normed_one, key_w).astype(jnp.bfloat16)
    values = (dot_plain(normed_one, value_w) + value_b.astype(jnp.float32)).astype(jnp.bfloat16)
    key_all, value_all = (
        lax.all_gather(key_rows, "ctx", axis=0, tiled=True),
        lax.all_gather(values, "ctx", axis=0, tiled=True),
    )
    total_rows = key_all.shape[0]
    key_block = math.gcd(total_rows, 2048)
    block_count = total_rows // key_block
    key_stack = key_all.reshape(block_count, key_block, HEADS, head_dim)
    value_stack = value_all.reshape(block_count, key_block, HEADS, head_dim)
    id_stack = doc_of(jnp.arange(total_rows, dtype=jnp.int32), doc_ends).reshape(
        block_count, key_block
    )
    query_heads = queries.reshape(row_count, HEADS, head_dim)

    def lse_step(running, block_in):
        run_max, run_sum = running
        key_heads, key_ids = block_in
        scores = masked_scores(query_heads, key_heads, own_ids, key_ids, score_scale)
        new_max = jnp.maximum(run_max, jnp.max(scores, axis=-1))
        new_sum = run_sum * jnp.exp(run_max - new_max) + jnp.sum(
            jnp.exp(scores - new_max[:, :, None]), axis=-1
        )
        return ((new_max, new_sum), None)

    start_max = jnp.full((HEADS, row_count), NEG_START, jnp.float32)
    (final_max, final_sum), unused = lax.scan(
        lse_step, (start_max, jnp.zeros_like(start_max)), (key_stack, id_stack)
    )
    log_total = final_max + jnp.log(final_sum)

    def out_step(running, block_in):
        key_heads, value_heads, key_ids = block_in
        scores = masked_scores(query_heads, key_heads, own_ids, key_ids, score_scale)
        attn_prob = jnp.exp(scores - log_total[:, :, None]).astype(jnp.bfloat16)
        return (
            running
            + jnp.einsum(
                "hqk,khd->qhd", attn_prob, value_heads, preferred_element_type=jnp.float32
            ),
            None,
        )

    attn_sum, unused = lax.scan(
        out_step,
        jnp.zeros((row_count, HEADS, head_dim), jnp.float32),
        (key_stack, value_stack, id_stack),
    )
    attended = attn_sum.reshape(row_count, model_width).astype(jnp.bfloat16)
    middle = inputs + dot_plain(attended, out_w) + out_b.astype(jnp.float32)
    normed_two = norm_rows(middle, second_gain, second_bias).astype(jnp.bfloat16)
    hidden = dot_plain(normed_two, up_w) + up_b.astype(jnp.float32)
    active = jax.nn.gelu(hidden, approximate=True).astype(jnp.bfloat16)
    output = middle + dot_plain(active, down_w) + down_b.astype(jnp.float32)
    top_grad = out_grad[0]
    top_float = top_grad.astype(jnp.float32)
    grad_down_w = dot_left(active, top_grad)
    grad_down_b = jnp.sum(top_float, axis=0)
    grad_active = dot_right(top_grad, down_w)
    unused, gelu_pull = jax.vjp(partial(jax.nn.gelu, approximate=True), hidden)
    grad_hidden = gelu_pull(grad_active)[0].astype(jnp.bfloat16)
    grad_up_w = dot_left(normed_two, grad_hidden)
    grad_up_b = jnp.sum(grad_hidden.astype(jnp.float32), axis=0)
    grad_normed_two = dot_right(grad_hidden, up_w)
    unused, second_pull = jax.vjp(norm_rows, middle, second_gain, second_bias)
    grad_middle, grad_gain_two, grad_bias_two = second_pull(grad_normed_two)
    grad_middle = grad_middle + top_float
    grad_branch = grad_middle.astype(jnp.bfloat16)
    grad_out_w = dot_left(attended, grad_branch)
    grad_out_b = jnp.sum(grad_branch.astype(jnp.float32), axis=0)
    grad_attended = dot_right(grad_branch, out_w).astype(jnp.bfloat16)
    grad_heads = grad_attended.reshape(row_count, HEADS, head_dim)
    row_delta = jnp.sum(grad_heads.astype(jnp.float32) * attn_sum, axis=-1)
    head_delta = row_delta.T
    query_start = jnp.zeros((row_count, HEADS, head_dim), jnp.float32)

    def full_step(grad_query, block_in):
        key_heads, value_heads, key_ids = block_in
        scores = masked_scores(query_heads, key_heads, own_ids, key_ids, score_scale)
        attn_prob = jnp.exp(scores - log_total[:, :, None])
        grad_prob = jnp.einsum(
            "qhd,khd->hqk", grad_heads, value_heads, preferred_element_type=jnp.float32
        )
        grad_score = (attn_prob * (grad_prob - head_delta[:, :, None])).astype(jnp.bfloat16)
        grad_query = grad_query + jnp.einsum(
            "hqk,khd->qhd", grad_score, key_heads, preferred_element_type=jnp.float32
        )
        grad_key = (
            jnp.einsum("hqk,qhd->khd", grad_score, query_heads, preferred_element_type=jnp.float32)
            * score_scale
        )
        grad_value = jnp.einsum(
            "hqk,qhd->khd",
            attn_prob.astype(jnp.bfloat16),
            grad_heads,
            preferred_element_type=jnp.float32,
        )
        return (
            grad_query,
            (grad_key.reshape(key_block, model_width), grad_value.reshape(key_block, model_width)),
        )

    grad_query, key_terms = lax.scan(full_step, query_start, (key_stack, value_stack, id_stack))
    key_grad, value_grad = (
        lax.psum_scatter(
            key_terms[0].reshape(total_rows, model_width), "ctx", scatter_dimension=0, tiled=True
        ),
        lax.psum_scatter(
            key_terms[1].reshape(total_rows, model_width), "ctx", scatter_dimension=0, tiled=True
        ),
    )
    grad_query_rows = (
        (grad_query * score_scale).reshape(row_count, model_width).astype(jnp.bfloat16)
    )
    grad_key_rows = key_grad.astype(jnp.bfloat16)
    grad_value_rows = value_grad.astype(jnp.bfloat16)
    grad_query_w = dot_left(normed_one, grad_query_rows)
    grad_query_b = jnp.sum(grad_query_rows.astype(jnp.float32), axis=0)
    grad_key_w = dot_left(normed_one, grad_key_rows)
    grad_value_w = dot_left(normed_one, grad_value_rows)
    grad_value_b = jnp.sum(grad_value_rows.astype(jnp.float32), axis=0)
    grad_normed_one = (
        dot_right(grad_query_rows, query_w)
        + dot_right(grad_key_rows, key_w)
        + dot_right(grad_value_rows, value_w)
    )
    unused, first_pull = jax.vjp(norm_rows, inputs, first_gain, first_bias)
    grad_inputs, grad_gain_one, grad_bias_one = first_pull(grad_normed_one)
    grad_inputs = grad_inputs + grad_middle
    (
        share_gain_one,
        share_bias_one,
        share_query_w,
        share_query_b,
        share_key_w,
        share_value_w,
        share_value_b,
        share_out_w,
        share_out_b,
        share_gain_two,
        share_bias_two,
        share_up_w,
        share_up_b,
        share_down_w,
        share_down_b,
    ) = (
        lax.psum_scatter(
            grad_gain_one.astype(jnp.bfloat16), "wsh", scatter_dimension=0, tiled=True
        ).astype(jnp.float32),
        lax.psum_scatter(
            grad_bias_one.astype(jnp.bfloat16), "wsh", scatter_dimension=0, tiled=True
        ).astype(jnp.float32),
        lax.psum_scatter(
            grad_query_w.astype(jnp.bfloat16), "wsh", scatter_dimension=0, tiled=True
        ).astype(jnp.float32),
        lax.psum_scatter(
            grad_query_b.astype(jnp.bfloat16), "wsh", scatter_dimension=0, tiled=True
        ).astype(jnp.float32),
        lax.psum_scatter(
            grad_key_w.astype(jnp.bfloat16), "wsh", scatter_dimension=0, tiled=True
        ).astype(jnp.float32),
        lax.psum_scatter(
            grad_value_w.astype(jnp.bfloat16), "wsh", scatter_dimension=0, tiled=True
        ).astype(jnp.float32),
        lax.psum_scatter(
            grad_value_b.astype(jnp.bfloat16), "wsh", scatter_dimension=0, tiled=True
        ).astype(jnp.float32),
        lax.psum_scatter(
            grad_out_w.astype(jnp.bfloat16), "wsh", scatter_dimension=0, tiled=True
        ).astype(jnp.float32),
        lax.psum_scatter(
            grad_out_b.astype(jnp.bfloat16), "wsh", scatter_dimension=0, tiled=True
        ).astype(jnp.float32),
        lax.psum_scatter(
            grad_gain_two.astype(jnp.bfloat16), "wsh", scatter_dimension=0, tiled=True
        ).astype(jnp.float32),
        lax.psum_scatter(
            grad_bias_two.astype(jnp.bfloat16), "wsh", scatter_dimension=0, tiled=True
        ).astype(jnp.float32),
        lax.psum_scatter(
            grad_up_w.astype(jnp.bfloat16), "wsh", scatter_dimension=0, tiled=True
        ).astype(jnp.float32),
        lax.psum_scatter(
            grad_up_b.astype(jnp.bfloat16), "wsh", scatter_dimension=0, tiled=True
        ).astype(jnp.float32),
        lax.psum_scatter(
            grad_down_w.astype(jnp.bfloat16), "wsh", scatter_dimension=0, tiled=True
        ).astype(jnp.float32),
        lax.psum_scatter(
            grad_down_b.astype(jnp.bfloat16), "wsh", scatter_dimension=0, tiled=True
        ).astype(jnp.float32),
    )
    totals = lax.psum(
        (
            share_gain_one,
            share_bias_one,
            share_query_w,
            share_query_b,
            share_key_w,
            share_value_w,
            share_value_b,
            share_out_w,
            share_out_b,
            share_gain_two,
            share_bias_two,
            share_up_w,
            share_up_b,
            share_down_w,
            share_down_b,
        ),
        "ctx",
    )
    return (
        output.astype(jnp.bfloat16)[None],
        grad_inputs.astype(jnp.bfloat16)[None],
        totals[0],
        totals[1],
        totals[2],
        totals[3],
        totals[4],
        totals[5],
        totals[6],
        totals[7],
        totals[8],
        totals[9],
        totals[10],
        totals[11],
        totals[12],
        totals[13],
        totals[14],
    )


MESH = pl.DeviceIdType.MESH
F32 = jnp.float32
BF = jnp.bfloat16
GROUPS = 4
LANES = 128


def flip(value, mask):
    return ((value // 2 + mask // 2) % 2) * 2 + (value + mask) % 2


def dot_nn(left, right):
    return lax.dot_general(left, right, (((1,), (0,)), ((), ())), preferred_element_type=F32)


def dot_nt(left, right):
    return lax.dot_general(left, right, (((1,), (1,)), ((), ())), preferred_element_type=F32)


def dot_tn(left, right):
    return lax.dot_general(left, right, (((0,), (0,)), ((), ())), preferred_element_type=F32)


def unit_rows(inputs):
    row_mean = jnp.mean(inputs, axis=-1, keepdims=True)
    centred = inputs - row_mean
    variance = jnp.mean(centred * centred, axis=-1, keepdims=True)
    scale = lax.rsqrt(variance + EPS)
    return centred * scale, scale


def unit_rows_back(grad_normed, unit, scale, gain):
    grad_unit = grad_normed * gain
    return scale * (
        grad_unit
        - jnp.mean(grad_unit, axis=-1, keepdims=True)
        - unit * jnp.mean(grad_unit * unit, axis=-1, keepdims=True)
    )


def rows_sum(values):
    return jnp.sum(values, axis=0, keepdims=True)


def sum_bf(*values):
    return sum([one.astype(F32) for one in values]).astype(BF)


class Wires:
    def __init__(self, send_sems, recv_sems):
        self.send_sems, self.recv_sems, self.used, self.started = send_sems, recv_sems, 0, []

    def take(self, count=1):
        first = self.used
        self.used += count
        return first

    def copy(self, index, source, target, device):
        return pltpu.make_async_remote_copy(
            src_ref=source,
            dst_ref=target,
            send_sem=self.send_sems.at[index % SEND_SEMS],
            recv_sem=self.recv_sems.at[index],
            device_id=device,
            device_id_type=MESH,
        )

    def send(self, source, target, device):
        one = self.copy(self.take(), source, target, device)
        one.start()
        self.started.append((one, None))
        return one

    def later(self, one, when=None):
        self.started.append((one, when))
        return one

    def plan(self, source, target, device):
        return self.later(self.copy(self.take(), source, target, device))

    def drain(self):
        for one, when in self.started:
            if when is None:
                one.wait_send()
            else:
                pl.when(when)(one.wait_send)


ORDER = (
    "up_grad", "ph_combine", "down_grad", "A_e0", "A_e1", "D_xout", "y_part", "wait_ph", "ln2",
    "sums", "early", "A2a", "out_grad", "bo0", "bo1", "bo2", "A2b", "up_xin", "A_e2", "D_in", "bo3",
    "kv_out", "bw0", "A3", "D2a", "D2b", "early2", "bw1", "go_combine", "up_in", "A_out", "D3",
    "py_combine", "U2a", "bw2", "bw3", "U2b", "D_turn", "U3", "go_out", "kv_in", "qkv_grad", "D_o1",
    "A_turn", "gq_comb", "D_i1", "U_turn", "h1_part", "D_i2", "G2a", "A_o1", "gq_fin", "A_i1",
    "G2b", "U_i1", "A_i2", "U_o1", "H2a", "q_start", "h1_e2", "A_i3", "G3", "U_i2", "go_in", "H3",
    "q_o1", "q_i1", "H2b", "G_turn", "U_i3", "q_i2", "layer_out", "G_o1", "h1_fin", "D_i3", "G_i1",
    "q_i3", "small", "G_i2", "G_i3", "fin",
)


def layer_kernel(sizes, names, *refs):
    n_ctx, n_doc, R, D, S, FS = sizes
    r = dict(zip(names, refs, strict=True))
    G = n_ctx // GROUPS
    last = GROUPS - 1
    half = GROUPS * R
    c = lax.axis_index("ctx")
    w = lax.axis_index("wsh")
    hg, px = c // G, c % G

    def zdev(group):
        return {"ctx": group * G + px, "wsh": w}

    def wdev(index):
        return {"ctx": c, "wsh": index}

    xdev = {"ctx": hg * G + 1 - px, "wsh": w}
    left, right = zdev((hg + last) % GROUPS), zdev((hg + 1) % GROUPS)
    w1, w2, w3 = flip(w, 1), flip(w, 2), flip(w, 3)
    sib, across, diag = wdev(w1), wdev(w2), wdev(w3)
    wires = Wires(r["send_sems"], r["recv_sems"])
    lane = lax.broadcasted_iota(jnp.int32, (1, LANES), 1)
    low_half = lane < LANES // 2

    def pick(table):
        return sum([jnp.where(hg == i, one, 0) for i, one in enumerate(table)])

    def by_distance(step):
        return (
            jnp.where(step == 0, pick((3, 3, 0, 0)), 0)
            + jnp.where(step == 1, pick((2, 0, 3, 1)), 0)
            + jnp.where(step == 2, pick((1, 2, 1, 2)), 0)
            + jnp.where(step == 3, hg, 0)
        )

    local = r["local_sems"]

    def fetch(index, source, target):
        one = pltpu.make_async_copy(source, target, local.at[index])
        one.start()
        return one

    tok_in = fetch(0, r["tok"], r["x_s"].at[hg])
    qkv_in = [fetch(1 + i, r[name], r["win_s"].at[i]) for i, name in enumerate(("wq", "wk", "wv"))]
    dy_in = fetch(4, r["dy"], r["dy_s"].at[w])
    wo_in = [
        fetch(5, r["wout"].at[pl.ds(0, LANES)], r["wo_s"].at[w, pl.ds(0, LANES)]),
        fetch(6, r["wout"].at[pl.ds(LANES, S - LANES)], r["wo_s"].at[w, pl.ds(S, S - LANES)]),
    ]
    wu_in = fetch(7, r["wup"].at[:, pl.ds(pl.multiple_of(w * FS, FS), FS)], r["wu_s"].at[w])
    wd_in = fetch(8, r["wdown"], r["wd_s"])

    barrier = pltpu.get_barrier_semaphore()
    ctx_peers = [{"ctx": (c + i) % n_ctx, "wsh": w} for i in range(1, n_ctx)]
    partners = ctx_peers + [sib, across, diag]
    for partner in partners:
        pl.semaphore_signal(barrier, inc=1, device_id=partner, device_id_type=MESH)

    pl.semaphore_wait(barrier, len(partners))

    class Gather:
        def __init__(self, slot):
            self.slot = slot
            self.to_across = wires.send(slot(w), slot(w), across)
            self.to_sib = wires.send(slot(w), slot(w), sib)

        def relay(self):
            self.to_across.wait_recv()
            self.on = wires.send(self.slot(w2), self.slot(w2), sib)

        def finish(self):
            self.to_sib.wait_recv()
            self.on.wait_recv()

    class Reduce:
        def __init__(self, part, recv):
            self.part, self.recv = part, recv
            self.a = wires.plan(part(w3), recv.at[0], sib)
            self.b = wires.plan(part(w1), recv.at[1], sib)
            self.c = wires.plan(recv.at[3], recv.at[2], across)

        def start(self):
            self.a.start()
            self.b.start()

        def combine(self):
            self.a.wait_recv()
            self.recv[3] = sum_bf(self.part(w2)[...], self.recv[0])
            self.c.start()

        def finish(self):
            self.b.wait_recv()
            self.c.wait_recv()
            return (
                self.part(w)[...].astype(F32)
                + self.recv[1].astype(F32)
                + self.recv[2].astype(F32)
            )

    class LineSum:
        def __init__(self, part, recv):
            self.part, self.recv = part, recv
            self.first_at = wires.take(5)
            for i in range(3):
                wires.later(self.message(i, True), hg > i)
                wires.later(self.message(i, False), hg < last - i)

        def message(self, i, leftward):
            block, slot = (i, i) if leftward else (last - i, 3 + i)
            return wires.copy(
                self.first_at + (i if leftward else 4 - i), self.part(block), self.recv.at[slot], left if leftward else right
            )

        def ends_block(self, block):
            for i in range(2):

                @pl.when((hg == last) & (block == i))
                def _():
                    self.message(i, True).start()

                @pl.when((hg == 0) & (block == last - i))
                def _():
                    self.message(i, False).start()

        def ends(self, which=(0, 1, 2)):
            for i in which:

                @pl.when(hg == last)
                def _():
                    self.message(i, True).start()

                @pl.when(hg == 0)
                def _():
                    self.message(i, False).start()

        def pass_on(self, position, i, leftward):
            @pl.when(hg == position)
            def _():
                one = self.message(i, leftward)
                one.wait_recv()
                block, slot = (i, i) if leftward else (last - i, 3 + i)
                self.part(block)[...] = sum_bf(self.part(block)[...], self.recv[slot])
                one.start()

        def second(self, which=(0, 1)):
            for i in which:
                self.pass_on(2, i, True)
                self.pass_on(1, i, False)

        def third(self):
            self.pass_on(1, 0, True)
            self.pass_on(2, 0, False)

        def final(self, put):
            for position in range(GROUPS):

                @pl.when(hg == position)
                def _():
                    total = self.part(position)[...].astype(F32)
                    if position < last:
                        self.message(position, True).wait_recv()
                        total = total + self.recv[position].astype(F32)
                    if position > 0:
                        self.message(last - position, False).wait_recv()
                        total = total + self.recv[3 + last - position].astype(F32)
                    put(total)

    class LineGather:
        def __init__(self, slot, to_x, own=None):
            self.slot, self.to_x, self.own = slot, to_x, own
            self.first_at = wires.take(3)
            self.x_at = wires.take(GROUPS) if to_x else None
            for d in (1, 2, 3):
                wires.later(self.message(d, 0), (hg >= d - 1) & (hg < last))
                wires.later(self.message(d, 1), (hg + d - 1 <= last) & (hg > 0))
            if to_x:
                for b in range(GROUPS):
                    wires.later(self.x_message(b))

        def message(self, d, side):
            block = (hg + GROUPS + (1 - d) * (1 - 2 * side)) % GROUPS
            device = zdev((hg + GROUPS + 1 - 2 * side) % GROUPS)
            first = self.own is not None and isinstance(d, int) and d == 1
            source = self.own if first else self.slot(block)
            return wires.copy(self.first_at + (3 - d) * (1 - side) + (d - 1) * side, source, self.slot(block), device)

        def x_message(self, block):
            return wires.copy(self.x_at + block, self.slot(block), self.slot(block), xdev)

        def start(self):
            pl.when(hg < last)(self.message(1, 0).start)
            pl.when(hg > 0)(self.message(1, 1).start)
            if self.to_x:
                self.x_message(hg).start()

        def arrived(self, d, side, then=None):
            block = (hg + GROUPS - d * (1 - 2 * side)) % GROUPS
            here = jnp.where(side == 0, (hg >= d).astype(jnp.int32), (hg + d <= last).astype(jnp.int32))
            onward = here * jnp.where(side == 0, (hg < last).astype(jnp.int32), (hg > 0).astype(jnp.int32))

            @pl.when(here == 1)
            def _():
                wires.copy(
                    self.first_at + (3 - d) * (1 - side) + (d - 1) * side, self.slot(block), self.slot(block), left
                ).wait_recv()

            @pl.when(onward == 1)
            def _():
                self.message(d + 1, side).start()

            @pl.when(here == 1)
            def _():
                if self.to_x:
                    self.x_message(block).start()
                if then is not None:
                    then(block)

        def inner(self, d):
            self.arrived(d, jnp.where(hg < 2, 1, 0))

        def outer(self, d):
            self.arrived(d, jnp.where(hg < 2, 0, 1))

        def done(self):
            for b in range(GROUPS):
                self.x_message(b).wait_recv()

    x_s, h1_s, q_s, kv_s = r["x_s"], r["h1_s"], r["q_s"], r["kv_s"]
    rows_two = R // 2
    tokens = [
        LineGather(
            lambda b, j=j: x_s.at[b, pl.ds(j * rows_two, rows_two)],
            False,
            r["tok"].at[pl.ds(j * rows_two, rows_two)],
        )
        for j in (0, 1)
    ]
    for one in tokens:
        one.start()
    for one in qkv_in:
        one.wait()
    own_w = pl.ds(pl.multiple_of(w * S, S), S)
    win, wq_s = r["win_s"], r["wq_s"]
    for g in range(GROUPS):

        @pl.when(hg == g)
        def _():
            a = g * S
            wq_s[own_w, 0:S] = win[0, :, a : a + S]
            wq_s[own_w, S : 2 * LANES] = jnp.zeros((S, 2 * LANES - S), BF)
            wq_s[own_w, 2 * LANES : 2 * LANES + S] = win[1, :, a : a + S]
            wq_s[own_w, 2 * LANES + S : 4 * LANES] = win[2, :, a + LANES : a + S]
            wq_s[own_w, 4 * LANES : 5 * LANES] = win[2, :, a : a + LANES]

    par_s = r["par_s"]
    par_s[w] = jnp.zeros((8, 2 * LANES), F32)
    for i, name in enumerate(("n1g", "n1b", "bq", "bv", "bo", "n2g", "n2b", "bd")):
        par_s[w, i : i + 1, 0:S] = r[name][...].astype(F32)[None, :]
    r["wo_s"][:, LANES:S, :] = jnp.zeros((GROUPS, S - LANES, D), BF)
    ws_all = Gather(lambda i: wq_s.at[pl.ds(pl.multiple_of(i * S, S), S)])
    par_all = Gather(lambda i: par_s.at[i])
    for one in wo_in:
        one.wait()
    dy_in.wait()
    wo_s, dy_s, wu_s = r["wo_s"], r["dy_s"], r["wu_s"]
    wo_top = Gather(lambda i: wo_s.at[i, pl.ds(0, LANES)])
    wo_low = Gather(lambda i: wo_s.at[i, pl.ds(S, S - LANES)])
    dy_all = Gather(lambda i: dy_s.at[i])
    up_sends = [
        wires.send(
            r["wup"].at[:, pl.ds(pl.multiple_of(flip(w, k) * FS, FS), FS)],
            wu_s.at[w],
            wdev(flip(w, k)),
        )
        for k in (2, 3, 1)
    ]
    inner_side = jnp.where(hg < 2, 1, 0)
    tokens[0].arrived(1, inner_side)
    tokens[0].arrived(1, 1 - inner_side)
    par_all.relay()
    ws_all.relay()
    tokens[1].arrived(1, inner_side)
    tokens[1].arrived(1, 1 - inner_side)
    par_all.finish()

    pars = jnp.concatenate([par_s[i][:, :S] for i in range(GROUPS)], axis=1)
    gain_one, bias_one, out_b, gain_two, bias_two, down_b = [
        pars[i : i + 1] for i in (0, 1, 4, 5, 6, 7)
    ]
    up_b = r["bup"][...].astype(F32)[None, :]
    own_par = par_s[hg]
    v_tile, v_last = own_par[3:4, :LANES], own_par[3:4, LANES:]
    qkv_b = jnp.concatenate(
        [own_par[2:3, :], jnp.zeros((1, LANES), F32), pltpu.roll(v_last, LANES // 2, 1), v_tile],
        axis=1,
    )
    ws_all.finish()
    tok_in.wait()

    kv_first = wires.take(2 * GROUPS)

    def kv_copy(block, j):
        rows = pl.ds(pl.multiple_of(block * R + j * rows_two, rows_two), rows_two)
        return wires.copy(
            kv_first + 2 * block + j, kv_s.at[0, rows], kv_s.at[1, rows], xdev
        )

    def project(block, j):
        rows = pl.ds(pl.multiple_of(j * rows_two, rows_two), rows_two)
        unit, unused = unit_rows(x_s[block, rows, :].astype(F32))
        normed = (unit * gain_one + bias_one).astype(BF)
        h1_s[block, rows, :] = normed
        qkv = dot_nn(normed, wq_s[...]) + qkv_b
        queries = qkv[:, : 2 * LANES].astype(BF).astype(F32) * 0.125
        q_s[0, block, rows, :] = jnp.where(low_half, queries[:, :LANES], 0.0).astype(BF)
        q_s[1, block, rows, :] = jnp.where(low_half, 0.0, queries[:, :LANES]).astype(BF)
        q_s[2, block, rows, :] = queries[:, LANES:].astype(BF)
        kv_rows = pl.ds(pl.multiple_of(block * R + j * rows_two, rows_two), rows_two)
        kv_s[0, kv_rows, :] = qkv[:, 2 * LANES :].astype(BF)
        kv_copy(block, j).start()

    def near_project(i, carry):
        away = jnp.where(i < 2, 0, jnp.where(i < 4, 1, 3)) * (1 - 2 * (1 - inner_side))
        block = (hg + 2 * GROUPS + jnp.where(i < 4, away, (1 - 2 * inner_side))) % GROUPS

        @pl.when((i < 4) | ((hg > 0) & (hg < last)))
        def _():
            project(block, i % 2)

        return carry

    tokens[0].arrived(2, inner_side)
    lax.fori_loop(0, 3, near_project, 0)
    tokens[1].arrived(2, inner_side)
    lax.fori_loop(3, 6, near_project, 0)

    def far_project(i, carry):
        d = i + 2
        block = (hg + GROUPS - d * (1 - 2 * inner_side)) % GROUPS
        for j, one in enumerate(tokens):

            @pl.when(d > 2)
            def _():
                one.arrived(d, inner_side)

            @pl.when(jnp.where(hg < 2, hg + d <= last, hg >= d))
            def _():
                project(block, j)

        return carry

    lax.fori_loop(0, 2, far_project, 0)
    wo_top.relay()
    wo_low.relay()
    doc_ends = []
    for i in range(n_doc):
        doc_ends.append(r["doc"][0, i] + (doc_ends[-1] if i else 0))

    def doc_ids(positions):
        return sum([(positions >= end).astype(jnp.int32) for end in doc_ends])

    key_at = lax.broadcasted_iota(jnp.int32, (1, half), 1)
    key_block = sum([(key_at >= i * R).astype(jnp.int32) for i in range(1, GROUPS)])
    key_base = key_at + key_block * (R * (G - 1))
    key_ids = [doc_ids(key_base + px * R), doc_ids(key_base + (1 - px) * R)]
    KT, VT, KO = (0, 0, LANES), (2 * LANES, 2 * LANES, LANES), (0, 0, LANES)
    e_s, li_s, oa_s, os_s, or_s = r["e_s"], r["li_s"], r["oa_s"], r["os_s"], r["or_s"]
    of_s = r["of_s"]

    def pack(target, first, final):
        target[0:R, :] = first.astype(BF)
        turned = pltpu.roll(final[rows_two:, :], LANES // 2, 1)
        target[R : R + rows_two, :] = jnp.where(low_half, turned, final[:rows_two, :]).astype(BF)

    def unpack(source, target):
        target[:, :LANES] = source[0:R, :]
        both = source[R : R + rows_two, :].astype(F32)
        target[0:rows_two, LANES:] = jnp.where(low_half, 0.0, both).astype(BF)
        turned = pltpu.roll(both, LANES // 2, 1)
        target[rows_two:, LANES:] = jnp.where(low_half, 0.0, turned).astype(BF)

    class Turn:
        def __init__(self, source, target):
            self.source, self.target = source, target
            self.first_at = wires.take(GROUPS - 1)
            for i in (1, 2, 3):
                wires.later(self.message((hg + i) % GROUPS))

        def message(self, block):
            index = self.first_at + (block - hg + GROUPS) % GROUPS - 1
            return wires.copy(index, self.source.at[block], self.target.at[hg], zdev(block))

        def arrived(self, block):
            index = self.first_at + (hg - block + GROUPS) % GROUPS - 1
            wires.copy(index, self.target.at[block], self.target.at[block], left).wait_recv()

    on_s = r["on_s"]
    o_turn = Turn(os_s, on_s)

    def row_ids_of(block):
        row_at = (block * G + px) * R + lax.broadcasted_iota(jnp.int32, (R, 1), 0)
        return doc_ids(row_at)

    def attend_side(block, side):
        row_ids = row_ids_of(block)
        same = row_ids == key_ids[side]
        scores = [
            jnp.where(
                same, dot_nt(q_s[h, block], kv_s[side, :, KT[h] : KT[h] + LANES]), NEG_START
            )
            for h in range(3)
        ]
        tops = [jnp.max(one, axis=-1, keepdims=True) for one in scores]
        weights = [jnp.exp(one - top) for one, top in zip(scores, tops, strict=True)]
        mixed = []
        for h in range(3):
            rounded = weights[h].astype(BF)
            e_s[h, block, side] = rounded
            mixed.append(dot_nn(rounded, kv_s[side, :, VT[h] : VT[h] + LANES]))
        totals = [jnp.sum(one, axis=-1, keepdims=True) for one in weights]
        return tops, totals, mixed

    def attend_own(block, carry):
        tops, totals, mixed = attend_side(block, 0)
        for h in range(3):
            li_s[0, h, block] = jnp.broadcast_to(tops[h], (R, LANES))
            li_s[1, h, block] = jnp.broadcast_to(totals[h], (R, LANES))
            of_s[h, block] = mixed[h]
        return carry

    lax.fori_loop(0, GROUPS, attend_own, 0)
    for b in range(GROUPS):
        for j in (0, 1):
            kv_copy(b, j).wait_recv()
            wires.later(kv_copy(b, j))

    def attend(step, carry):
        block = by_distance(step)
        tops, totals, mixed = attend_side(block, 1)
        outs = []
        for h in range(3):
            top, total = tops[h], totals[h]
            own_top = li_s[0, h, block]
            both_top = jnp.maximum(own_top, top)
            own_part, part = jnp.exp(own_top - both_top), jnp.exp(top - both_top)
            inverse = 1.0 / (li_s[1, h, block] * own_part + total * part)
            own_part, part = own_part * inverse, part * inverse
            li_s[0, h, block] = own_part
            li_s[1, h, block] = part
            outs.append(of_s[h, block] * own_part + mixed[h] * part)
        first = jnp.where(low_half, outs[0], outs[1])
        final = jnp.where(low_half, 0.0, outs[2])
        oa_s[block, :, :LANES] = first
        oa_s[block, :, LANES:] = final
        pack(os_s.at[block], first, final)

        @pl.when(step < last)
        def _():
            o_turn.message(block).start()

        return carry

    lax.fori_loop(0, GROUPS, attend, 0)
    dy_all.relay()
    unpack(os_s.at[hg], or_s.at[hg])
    dy_all.finish()
    wd_in.wait()
    wd_s, dkv_s = r["wd_s"], r["dkv_s"]

    def top_rows(slot):
        return slot // 2, pl.ds(pl.multiple_of((slot % 2) * R, R), R)

    def top_part(slot, carry):
        dkv_s[top_rows(slot)] = dot_nt(dy_s[slot], wd_s[...])
        return carry

    lax.fori_loop(0, GROUPS, top_part, 0)
    wo_top.finish()
    wo_low.finish()
    for i in (1, 2, 3):
        there = (hg + i) % GROUPS
        o_turn.arrived(there)
        unpack(on_s.at[there], or_s.at[there])

    middle = x_s[hg].astype(F32) + out_b
    for i in range(GROUPS):
        middle += dot_nn(or_s[i], wo_s[i])
    x1_s, h2_s, g_s, da_s = r["x1_s"], r["h2_s"], r["g_s"], r["da_s"]
    x1_s[...] = middle
    unit_two, scale_two = unit_rows(middle)
    h2_s[w] = (unit_two * gain_two + bias_two).astype(BF)
    halves = [pl.ds(0, rows_two), pl.ds(rows_two, rows_two)]
    h2_all = [Gather(lambda i, part=part: h2_s.at[i, part]) for part in halves]
    wu_in.wait()
    for one in up_sends:
        one.wait_recv()
    ph_s, hr_s = r["ph_s"], r["hr_s"]
    ph = [
        Reduce(lambda i, part=part: ph_s.at[i, part], hr_s.at[k]) for k, part in enumerate(halves)
    ]

    def up_and_back(slot, start, count):
        rows = pl.ds(start, count)
        hidden = dot_nn(h2_s[slot, rows, :], wu_s[...].reshape(D, FS)) + up_b
        square = hidden * hidden
        inner = math.sqrt(2.0 / math.pi) * (hidden + 0.044715 * (square * hidden))
        bent = jnp.tanh(inner)
        g_s[slot, rows, :] = (0.5 * hidden * (1.0 + bent)).astype(BF)
        slope = 0.5 * (1.0 + bent) + 0.5 * hidden * (1.0 - bent * bent) * (
            math.sqrt(2.0 / math.pi) * (1.0 + 3.0 * 0.044715 * square)
        )
        top_at = pl.ds(pl.multiple_of((slot % 2) * R + start, rows_two), count)
        grad_hidden = (dkv_s[slot // 2, top_at, :] * slope).astype(BF)
        da_s[slot, rows, :] = grad_hidden
        ph_s[slot, rows, :] = dot_nt(grad_hidden, wu_s[...].reshape(D, FS)).astype(BF)

    def mlp_near(j, carry):
        @pl.when(j == 1)
        def _():
            for one in h2_all:
                one.to_sib.wait_recv()

        up_and_back(flip(w, j), 0, R)
        return carry

    lax.fori_loop(0, 2, mlp_near, 0)
    for one in ph:
        one.b.start()
    on_copies = [
        wires.plan(h2_s.at[w2, part], h2_s.at[w2, part], sib) for part in halves
    ]
    for k in (0, 1):
        h2_all[k].to_across.wait_recv()
        on_copies[k].start()
        up_and_back(w2, k * rows_two, rows_two)
        if k == 1:
            ph[0].combine()
        on_copies[k].wait_recv()
        up_and_back(w3, k * rows_two, rows_two)
        ph[k].a.start()

    gus_s, gas_s, gds_s, py_s = r["gus_s"], r["gas_s"], r["gds_s"], r["py_s"]
    cols = gas_s.shape[1]

    up_x_first = wires.take(2)

    def up_x(i):
        part = pl.ds(2 * i, 2)
        return wires.copy(up_x_first + i, gus_s.at[part, 1 - px], r["gux_s"].at[part], xdev)

    for i in (0, 1):
        wires.later(up_x(i))

    def up_grad(i, carry):
        at = pl.ds(pl.multiple_of(i * 2 * S, 2 * S), 2 * S)
        gus_s[pl.ds(2 * i, 2)] = (
            dot_tn(h2_s[:, :, at].reshape(half, 2 * S), da_s[...].reshape(half, FS))
            .astype(BF)
            .reshape(2, 2, S // 2, FS)
        )
        up_x(i).start()
        return carry

    def down_grad(i, carry):
        at = pl.ds(pl.multiple_of(i * 256, 256), 256)
        both = dot_tn(g_s[:, :, at].reshape(half, 256), dy_s[...].reshape(half, D)).astype(BF)
        gas_s[at, :] = both[:, :cols]
        gds_s[at, :] = both[:, cols:]
        return carry

    def y_part(j, carry):
        py_s[j] = dot_nn(g_s[j], wd_s[...]).astype(BF)
        return carry

    class Spread:
        def __init__(self, part, recv, slot, to_x):
            self.sum = LineSum(part, recv)
            self.gather = LineGather(slot, to_x)

        def turn(self):
            def put(total):
                self.gather.slot(hg)[...] = total.astype(BF)

            self.sum.final(put)
            self.gather.start()

    class Share:
        def __init__(self, rows):
            self.rows = rows
            self.at = wires.take(n_ctx - 1) - 1
            for i in range(1, n_ctx):
                wires.later(self.message(i))

        def message(self, i):
            return wires.copy(self.at + i, self.rows.at[c], self.rows.at[c], ctx_peers[i - 1])

        def start(self):
            for i in range(1, n_ctx):
                self.message(i).start()

        def total(self):
            for i in range(1, n_ctx):
                wires.copy(self.at + i, self.rows.at[c], self.rows.at[c], left).wait_recv()
            return sum([self.rows[i] for i in range(n_ctx)])

    n = S // 2
    n_down = FS // 8
    ga_f, gd_f, gu_s, up_f = r["gda"], r["gdb"], r["gu_s"], r["gup"]
    mine = pl.ds(pl.multiple_of(px * n, 8), n)
    theirs = pl.ds(pl.multiple_of((1 - px) * n, 8), n)

    def down_rows(b):
        return pl.ds(pl.multiple_of(px * (4 * n_down) + b * n_down, 8), n_down)

    down_here = pl.ds(pl.multiple_of(px * (4 * n_down), 8), 4 * n_down)
    down_there = pl.ds(pl.multiple_of((1 - px) * (4 * n_down), 8), 4 * n_down)
    py = Reduce(lambda i: py_s.at[i], r["yr_s"])
    up_y_first = wires.take(3) - 1

    def up_y(k, out):
        to = flip(w, k)
        return wires.copy(
            up_y_first + k, gus_s.at[to, px], gu_s.at[w if out else to], wdev(to)
        )

    for k in (1, 2, 3):
        wires.later(up_y(k, True))
    up = Spread(lambda b: gu_s.at[b], r["gul_s"], lambda b: up_f.at[b, px], True)
    down_x = wires.plan(gds_s.at[down_there], r["gdx_s"], xdev)
    down = Spread(
        lambda b: gds_s.at[down_rows(b)], r["gdl_s"], lambda b: gd_f.at[down_rows(b)], True
    )
    gat_s, gax_s = r["gat_s"], r["gax_s"]

    def across_rows(b):
        return pl.ds(pl.multiple_of(b * 2 * n_down + px * n_down, 8), n_down)

    most = Spread(
        lambda b: gas_s.at[pl.ds(pl.multiple_of(b * 2 * n_down, 8), 2 * n_down)],
        r["gal_s"],
        lambda b: ga_f.at[across_rows(b)],
        True,
    )
    most_x = wires.plan(gat_s.at[1 - px], gax_s, xdev)
    dz_s, dos_s, dor_s = r["dz_s"], r["dos_s"], r["dor_s"]
    don_s = r["don_s"]
    do_turn = Turn(dos_s, don_s)
    early, early_x_s, early_z_s = r["early_s"], r["early_x_s"], r["early_z_s"]
    late = r["late_s"]
    early_x = wires.plan(early, early_x_s, xdev)
    early_first = wires.take(3) - 1

    def early_z(i):
        return wires.copy(
            early_first + i, early_z_s.at[hg], early_z_s.at[hg], zdev((hg + i) % GROUPS)
        )

    for i in (1, 2, 3):
        wires.later(early_z(i))
    late_all = Share(late)
    gos_s, gor_s = r["gos_s"], r["gor_s"]
    go_s, gox_s, god_s, go_f = r["go_s"], r["gox_s"], r["god_s"], r["gout"]
    go = Reduce(lambda i: gos_s.at[i], gor_s)
    quarter = S // GROUPS

    def quarter_rows(b):
        return pl.ds(pl.multiple_of(b * quarter, 8), quarter)

    go_all = Spread(
        lambda b: go_s.at[quarter_rows(b)],
        r["gol_s"],
        lambda b: go_f.at[quarter_rows(b)],
        False,
    )
    go_x = wires.plan(god_s, gox_s, xdev)
    kvt_s, kvr_s, ph1_s, gqs_s = r["kvt_s"], r["kvr_s"], r["ph1_s"], r["gqs_s"]
    kv_back = wires.plan(kvt_s, kvr_s, xdev)
    h1_sum = LineSum(lambda b: ph1_s.at[b], r["h1r_s"])
    gq = Reduce(lambda i: gqs_s.at[pl.ds(pl.multiple_of(i * S, S), S)], r["gqr_s"])
    gqc_s, gqx_s, gqkv = r["gqc_s"], r["gqx_s"], r["gqkv"]
    qx = wires.plan(gqc_s.at[theirs], gqx_s, xdev)
    q_line = LineGather(lambda b: gqkv.at[b, mine], True)
    vecs, vecr = r["vecs_s"], r["vecr_s"]
    vec_first = wires.take(3) - 1

    def vec_send(k):
        return wires.copy(
            vec_first + k, vecs.at[flip(w, k)], vecr.at[k - 1], wdev(flip(w, k))
        )

    for k in (1, 2, 3):
        wires.later(vec_send(k))
    dq_s, dqkv_s, df_s = r["dq_s"], r["dqkv_s"], r["df_s"]

    steps = {}

    def step_of(name):
        def keep(body):
            steps[name] = body
            return body

        return keep

    @step_of("up_xin")
    def _():
        for i in (0, 1):
            up_x(i).wait_recv()
        here = gus_s.at[:, px]
        here[...] = sum_bf(here[...], r["gux_s"][...])
        gu_s[w] = gus_s[w, px]
        for k in (2, 3, 1):
            up_y(k, True).start()

    @step_of("up_in")
    def _():
        for k in (1, 2, 3):
            up_y(k, False).wait_recv()
        up.sum.ends()

    @step_of("D_in")
    def _():
        down_x.wait_recv()
        gds_s[down_here, :] = sum_bf(gds_s[down_here, :], r["gdx_s"][...])
        down.sum.ends()

    steps["D_xout"] = down_x.start
    for i in range(3):
        steps["A_e%d" % i] = partial(most.sum.ends, (i,))
    steps["A2a"] = partial(most.sum.second, (0,))
    steps["A2b"] = partial(most.sum.second, (1,))
    steps["A3"] = most.sum.third

    @step_of("A_out")
    def _():
        def put(total):
            gat_s[...] = total.astype(BF).reshape(2, n_down, cols)

        most.sum.final(put)
        most_x.start()

    @step_of("A_turn")
    def _():
        most_x.wait_recv()
        ga_f[across_rows(hg), :] = sum_bf(gat_s[px], gax_s[...])
        most.gather.start()

    for name, chain in (("U", up), ("D", down)):
        steps[name + "2a"] = partial(chain.sum.second, (0,))
        steps[name + "2b"] = partial(chain.sum.second, (1,))
        steps[name + "3"] = chain.sum.third
        steps[name + "_turn"] = chain.turn
    for name, line in (("U", up.gather), ("D", down.gather), ("A", most.gather), ("G", go_all.gather), ("q", q_line)):
        steps[name + "_i1"] = partial(line.inner, 1)
        steps[name + "_o1"] = partial(line.outer, 1)
        steps[name + "_i2"] = partial(line.inner, 2)
        steps[name + "_i3"] = partial(line.inner, 3)
    steps["H2a"] = partial(h1_sum.second, (0,))
    steps["H2b"] = partial(h1_sum.second, (1,))
    steps["H3"] = h1_sum.third
    steps["h1_e2"] = partial(h1_sum.ends, (2,))
    steps["go_combine"] = go.combine
    steps["py_combine"] = py.combine
    steps["gq_comb"] = gq.combine

    steps["G2a"] = partial(go_all.sum.second, (0,))
    steps["G2b"] = partial(go_all.sum.second, (1,))
    steps["G3"] = go_all.sum.third

    @step_of("go_out")
    def _():
        go_s[...] = go.finish().astype(BF)
        go_all.sum.ends()

    @step_of("go_in")
    def _():
        def put(total):
            god_s[...] = total.astype(BF)

        go_all.sum.final(put)
        go_x.start()

    @step_of("G_turn")
    def _():
        go_x.wait_recv()
        go_f[quarter_rows(hg), :] = sum_bf(god_s[...], gox_s[...])
        go_all.gather.start()

    steps["early"] = early_x.start

    @step_of("early2")
    def _():
        early_x.wait_recv()
        early_z_s[hg] = early[...] + early_x_s[...]
        for i in (1, 2, 3):
            early_z(i).start()

    @step_of("kv_in")
    def _():
        kv_back.wait_recv()
        dqkv_s[:, 2 * LANES :] = jnp.transpose(sum_bf(dkv_s[0], kvr_s[...]))

    @step_of("h1_part")
    def _():
        def h1_part(step, carry):
            block = by_distance(step)
            rows = pl.ds(pl.multiple_of(block * R, R), R)
            ph1_s[block] = dot_nt(dqkv_s[rows, :], wq_s[...]).astype(BF)
            h1_sum.ends_block(block)
            return carry

        lax.fori_loop(0, GROUPS, h1_part, 0)

    @step_of("qkv_grad")
    def _():
        def qkv_grad(i, carry):
            at = pl.ds(pl.multiple_of(i * 256, 256), 256)
            gqs_s[at, :] = dot_tn(h1_s[:, :, at].reshape(half, 256), dqkv_s[...]).astype(BF)
            return carry

        lax.fori_loop(0, D // 256, qkv_grad, 0)
        gq.start()
        late[c, :, 2 * D : 2 * D + 2 * LANES] = rows_sum(dqkv_s[:, : 2 * LANES].astype(F32))
        late[c, :, 2 * D + 2 * LANES :] = rows_sum(dqkv_s[:, 3 * LANES :].astype(F32))

    @step_of("gq_fin")
    def _():
        gqc_s[...] = gq.finish().astype(BF)
        qx.start()

    @step_of("q_start")
    def _():
        qx.wait_recv()
        gqkv[hg, mine, :] = sum_bf(gqc_s[mine, :], gqx_s[...])
        q_line.start()

    @step_of("h1_fin")
    def _():
        def keep_h1(total):
            df_s[...] = total

        h1_sum.final(keep_h1)
        grad_one = df_s[...]
        unit_one, scale_one = unit_rows(x_s[hg].astype(F32))
        grad_in = dz_s[...] + unit_rows_back(grad_one, unit_one, scale_one, gain_one)
        r["dx"][...] = grad_in.astype(BF)
        late[c, :, 0:D] = rows_sum(grad_one * unit_one)
        late[c, :, D : 2 * D] = rows_sum(grad_one)
        late_all.start()

    @step_of("layer_out")
    def _():
        r["y"][...] = (x1_s[...] + py.finish() + down_b).astype(BF)

    @step_of("small")
    def _():
        for i in (1, 2, 3):
            there = (hg + i) % GROUPS
            wires.copy(early_first + GROUPS - i, early_z_s.at[there], early_z_s.at[there], left).wait_recv()
        ones = sum([early_z_s[i] for i in range(GROUPS)])
        twos = late_all.total()
        bq_all, bv_all = [], []
        for g in range(GROUPS):
            group_sum = sum([late[g * G + i][:, 2 * D :] for i in range(G)])
            bq_all.append(group_sum[:, :S])
            v_end = pltpu.roll(group_sum[:, 2 * LANES : 3 * LANES], LANES // 2, 1)[:, : S - LANES]
            bv_all.append(jnp.concatenate([group_sum[:, 3 * LANES :], v_end], axis=1))
        vectors = [twos[:, 0:D], twos[:, D : 2 * D]] + [
            ones[:, i * D : (i + 1) * D] for i in range(4)
        ]
        for i in range(GROUPS):
            for j, one in enumerate(vectors):
                vecs[i, :, j * 256 : j * 256 + S] = one[:, i * S : (i + 1) * S]
            vecs[i, :, 6 * 256 : 6 * 256 + S] = bq_all[i]
            vecs[i, :, 7 * 256 : 7 * 256 + S] = bv_all[i]
        r["vec"][:, 8 * 256 :] = ones[:, 4 * D :]
        for k in (1, 2, 3):
            vec_send(k).start()

    carried = {}

    @step_of("up_grad")
    def _():
        lax.fori_loop(0, 2, up_grad, 0)

    steps["ph_combine"] = ph[1].combine

    @step_of("down_grad")
    def _():
        lax.fori_loop(0, FS // 256, down_grad, 0)

    @step_of("y_part")
    def _():
        lax.fori_loop(0, GROUPS, y_part, 0)
        py.start()
        dkv_s[...] = jnp.zeros(dkv_s.shape, F32)

    @step_of("wait_ph")
    def _():
        carried["two"] = jnp.concatenate([one.finish() for one in ph], axis=0)

    @step_of("ln2")
    def _():
        grad_two = carried["two"]
        unit_two, scale_two = unit_rows(x1_s[...])
        top = r["dy_s"][w].astype(F32)
        grad_middle = top + unit_rows_back(grad_two, unit_two, scale_two, gain_two)
        dz = grad_middle.astype(BF)
        dz_s[...] = grad_middle
        carried["dz"], carried["unit"], carried["top"] = dz, unit_two, top

        def out_back(step, carry):
            block = by_distance(step)
            grad_o = dot_nt(dz, wo_s[block])
            pack(dos_s.at[block], grad_o[:, :LANES], grad_o[:, LANES:])

            @pl.when(step < last)
            def _():
                do_turn.message(block).start()

            return carry

        lax.fori_loop(0, GROUPS, out_back, 0)

    @step_of("sums")
    def _():
        unpack(dos_s.at[hg], dor_s.at[hg])
        early[:, 0:D] = rows_sum(carried["dz"].astype(F32))
        early[:, D : 2 * D] = rows_sum(carried["two"] * carried["unit"])
        early[:, 2 * D : 3 * D] = rows_sum(carried["two"])
        early[:, 3 * D : 4 * D] = rows_sum(carried["top"])
        early[:, 4 * D :] = rows_sum(da_s[...].reshape(half, FS).astype(F32))

    @step_of("out_grad")
    def _():
        for i in range(GROUPS):
            piece = dot_tn(or_s[i], carried["dz"])
            gos_s[i, 0:LANES, :] = piece[0:LANES, :].astype(BF)
            gos_s[i, LANES:S, :] = piece[S:, :].astype(BF)
        go.start()

    def back_block(block, side):
        outs = dor_s[block].astype(F32)
        kept = oa_s[block]
        scaled = []
        for h in range(3):
            tile = 0 if h < 2 else LANES
            keep = low_half if h == 0 else jnp.logical_not(low_half)
            scaled.append(
                jnp.where(keep, outs[:, tile : tile + LANES], 0.0) * li_s[side, h, block]
            )
        deltas = [
            jnp.sum(
                scaled[h] * kept[:, KO[h] : KO[h] + LANES], axis=-1, keepdims=True
            )
            for h in range(3)
        ]
        rounded = [one.astype(BF) for one in scaled]
        grad_probs = [
            dot_nt(rounded[h], kv_s[side, :, VT[h] : VT[h] + LANES]) for h in range(3)
        ]
        grad_scores = [
            (e_s[h, block, side].astype(F32) * (grad_probs[h] - deltas[h])).astype(BF)
            for h in range(3)
        ]
        grads_q = [
            dot_nn(grad_scores[h], kv_s[side, :, KT[h] : KT[h] + LANES]) for h in range(3)
        ]
        for h in range(3):
            dkv_s[side, KT[h] : KT[h] + LANES, :] += dot_tn(q_s[h, block], grad_scores[h])
            dkv_s[side, VT[h] : VT[h] + LANES, :] += dot_tn(rounded[h], e_s[h, block, side])
        first = jnp.where(low_half, grads_q[0], grads_q[1]) * 0.125
        final = jnp.where(low_half, grads_q[2], 0.0) * 0.125
        if side == 1:
            dq_s[block, :, :LANES] = first
            dq_s[block, :, LANES:] = final
        else:
            rows = pl.ds(pl.multiple_of(block * R, R), R)
            dqkv_s[rows, :LANES] = (dq_s[block, :, :LANES] + first).astype(BF)
            dqkv_s[rows, LANES : 2 * LANES] = (dq_s[block, :, LANES:] + final).astype(BF)

    def nearest(step):
        return by_distance(last - step)

    @step_of("kv_out")
    def _():
        kvt_s[...] = dkv_s[1].astype(BF)
        kv_back.start()

    @step_of("fin")
    def _():
        for k in (1, 2, 3):
            vec_send(k).wait_recv()
        r["vec"][:, 0 : 8 * 256] = vecs[w] + vecr[0] + vecr[1] + vecr[2]
        down.gather.done()
        most.gather.done()
        up.gather.done()
        q_line.done()

    def attention_back(side, plans):
        def body(step, carry):
            block = nearest(step)
            if side == 1:

                @pl.when(step > 0)
                def _():
                    do_turn.arrived(block)
                    unpack(don_s.at[block], dor_s.at[block])

            back_block(block, side)
            for k, names in enumerate(plans):
                if names:

                    @pl.when(step == k)
                    def _():
                        for name in names:
                            steps[name]()

            return carry

        lax.fori_loop(0, GROUPS, body, 0)

    at = 0
    order = ORDER
    while at < len(order):
        name = order[at]
        at += 1
        if name in ("bo0", "bw0"):
            plans, kind = [[]], name[:2]
            while at < len(order) and (order[at][:2] == kind or len(plans) < GROUPS):
                if order[at][:2] == kind:
                    plans.append([])
                else:
                    plans[-1].append(order[at])
                at += 1
            attention_back(1 if kind == "bo" else 0, plans)
        else:
            steps[name]()
    assert wires.used == SEMS
    wires.drain()


def widen_kernel(S, names, *refs):
    r = dict(zip(names, refs, strict=True))
    n = S // 2
    started = []

    def send(source, target):
        one = pltpu.make_async_copy(source, target, r["sems"].at[len(started)])
        one.start()
        started.append(one)

    def put(name, at, value):
        r[name + "_b"][at] = value
        send(r[name + "_b"].at[at], r[name + "_o"].at[at])

    send(r["y"], r["y_o"])
    send(r["dx"], r["dx_o"])
    put("out", (slice(None),), r["out"][...].astype(F32))

    def heads(pieces):
        return jnp.concatenate(
            [r["qkv"][i, :, a:b].astype(F32) for i in range(GROUPS) for a, b in pieces], axis=1
        )

    put("q", (slice(None),), heads([(0, S)]))
    put("k", (slice(None),), heads([(2 * LANES, 2 * LANES + S)]))
    put("v", (slice(None),), heads([(4 * LANES, 5 * LANES), (2 * LANES + S, 4 * LANES)]))
    FS = r["up"].shape[3]
    for i in range(GROUPS):
        rows = slice(i * S, (i + 1) * S)
        both = [r[name][rows, :].astype(F32) for name in ("da", "db")]
        put("down", (rows, slice(None)), jnp.concatenate(both, axis=1))
        for j in (0, 1):
            at = (slice(j * n, (j + 1) * n), slice(i * FS, (i + 1) * FS))
            put("up", at, r["up"][i, j].astype(F32))
    at = 0
    for i in range(9):
        one = r["vec%d" % i]
        one[...] = r["vec"][0, at : at + one.shape[0]]
        at += max(one.shape[0], 256)
    for one in started:
        one.wait()


SEMS = 139
SEND_SEMS = 4


def fast_device(mesh_sizes, *arrays):
    (tokens, doc_lengths, out_grad, norm1_gain, norm1_bias, w_query, b_query, w_key, w_value,
     b_value, w_out, b_out, norm2_gain, norm2_bias, w_up, b_up, w_down, b_down) = arrays
    n_ctx, n_wsh = mesh_sizes
    R, D = tokens.shape[1], tokens.shape[2]
    S, FS, n_doc = D // GROUPS, w_down.shape[0], doc_lengths.shape[1]
    half, QW = GROUPS * R, 5 * LANES

    smem = pl.BlockSpec(memory_space=pltpu.SMEM)
    vmem = pl.BlockSpec(memory_space=pltpu.VMEM)
    anywhere = pl.BlockSpec(memory_space=pl.ANY)
    inputs = [
        ("doc", doc_lengths, smem),
        ("tok", tokens[0], anywhere),
        ("dy", out_grad[0], anywhere),
        ("wq", w_query, anywhere),
        ("wk", w_key, anywhere),
        ("wv", w_value, anywhere),
        ("wout", w_out, anywhere),
        ("wup", w_up, anywhere),
        ("wdown", w_down, anywhere),
        ("n1g", norm1_gain, vmem),
        ("n1b", norm1_bias, vmem),
        ("bq", b_query, vmem),
        ("bv", b_value, vmem),
        ("bo", b_out, vmem),
        ("n2g", norm2_gain, vmem),
        ("n2b", norm2_bias, vmem),
        ("bd", b_down, vmem),
        ("bup", b_up, vmem),
    ]
    n_up = S // 2
    outputs = [
        ("y", (R, D), BF),
        ("dx", (R, D), BF),
        ("gda", (FS, 2 * D // 3), BF),
        ("gdb", (FS, D // 3), BF),
        ("gup", (GROUPS, 2, n_up, FS), BF),
        ("gout", (S, D), BF),
        ("gqkv", (GROUPS, S, QW), BF),
        ("vec", (1, 8 * 256 + FS), F32),
    ]
    scratch = [
        ("x_s", (GROUPS, R, D), BF),
        ("h1_s", (GROUPS, R, D), BF),
        ("win_s", (3, S, D), BF),
        ("wq_s", (D, QW), BF),
        ("par_s", (GROUPS, 8, 2 * LANES), F32),
        ("q_s", (3, GROUPS, R, LANES), BF),
        ("kv_s", (2, half, 3 * LANES), BF),
        ("e_s", (3, GROUPS, 2, R, half), BF),
        ("li_s", (2, 3, GROUPS, R, LANES), F32),
        ("of_s", (3, GROUPS, R, LANES), F32),
        ("oa_s", (GROUPS, R, 2 * LANES), F32),
        ("os_s", (GROUPS, R + R // 2, LANES), BF),
        ("on_s", (GROUPS, R + R // 2, LANES), BF),
        ("or_s", (GROUPS, R, 2 * LANES), BF),
        ("wo_s", (GROUPS, 2 * LANES, D), BF),
        ("wu_s", (GROUPS, S, FS), BF),
        ("wd_s", (FS, D), BF),
        ("dy_s", (GROUPS, R, D), BF),
        ("x1_s", (R, D), F32),
        ("h2_s", (GROUPS, R, D), BF),
        ("g_s", (GROUPS, R, FS), BF),
        ("da_s", (GROUPS, R, FS), BF),
        ("ph_s", (GROUPS, R, D), BF),
        ("hr_s", (2, 4, R // 2, D), BF),
        ("py_s", (GROUPS, R, D), BF),
        ("yr_s", (4, R, D), BF),
        ("dz_s", (R, D), F32),
        ("dos_s", (GROUPS, R + R // 2, LANES), BF),
        ("don_s", (GROUPS, R + R // 2, LANES), BF),
        ("dor_s", (GROUPS, R, 2 * LANES), BF),
        ("dkv_s", (2, 3 * LANES, half), F32),
        ("kvt_s", (3 * LANES, half), BF),
        ("kvr_s", (3 * LANES, half), BF),
        ("dq_s", (GROUPS, R, 2 * LANES), F32),
        ("dqkv_s", (half, QW), BF),
        ("ph1_s", (GROUPS, R, D), BF),
        ("h1r_s", (6, R, D), BF),
        ("df_s", (R, D), F32),
        ("gas_s", (FS, 2 * D // 3), BF),
        ("gal_s", (6, FS // 4, 2 * D // 3), BF),
        ("gat_s", (2, FS // 8, 2 * D // 3), BF),
        ("gax_s", (FS // 8, 2 * D // 3), BF),
        ("gds_s", (FS, D // 3), BF),
        ("gdx_s", (FS // 2, D // 3), BF),
        ("gdl_s", (6, FS // 8, D // 3), BF),
        ("gus_s", (GROUPS, 2, S // 2, FS), BF),
        ("gu_s", (GROUPS, n_up, FS), BF),
        ("gux_s", (GROUPS, S // 2, FS), BF),
        ("gul_s", (6, n_up, FS), BF),
        ("go_s", (S, D), BF),
        ("gox_s", (S // GROUPS, D), BF),
        ("god_s", (S // GROUPS, D), BF),
        ("gol_s", (6, S // GROUPS, D), BF),
        ("gos_s", (GROUPS, S, D), BF),
        ("gor_s", (4, S, D), BF),
        ("gqs_s", (D, QW), BF),
        ("gqr_s", (4, S, QW), BF),
        ("gqc_s", (S, QW), BF),
        ("gqx_s", (S // 2, QW), BF),
        ("early_s", (1, 4 * D + FS), F32),
        ("early_x_s", (1, 4 * D + FS), F32),
        ("early_z_s", (GROUPS, 1, 4 * D + FS), F32),
        ("late_s", (n_ctx, 1, 2 * D + 4 * LANES), F32),
        ("vecs_s", (GROUPS, 1, 8 * 256), F32),
        ("vecr_s", (3, 1, 8 * 256), F32),
    ]
    sems = [("send_sems", SEND_SEMS), ("recv_sems", SEMS), ("local_sems", 9)]
    names = [one[0] for one in inputs + outputs + scratch + sems]
    y, dx, g_da, g_db, g_up, g_out, g_qkv, vec = pl.pallas_call(
        partial(layer_kernel, (n_ctx, n_doc, R, D, S, FS), names),
        out_shape=[pltpu.VMEM(shape, dtype) for name, shape, dtype in outputs],
        in_specs=[spec for name, value, spec in inputs],
        out_specs=[vmem] * len(outputs),
        scratch_shapes=[pltpu.VMEM(shape, dtype) for name, shape, dtype in scratch]
        + [pltpu.SemaphoreType.DMA((count,)) for name, count in sems],
        compiler_params=pltpu.CompilerParams(
            collective_id=0, has_side_effects=True, vmem_limit_bytes=62300000
        ),
        name="layer",
    )(*[value for name, value, spec in inputs])

    big = [
        ("y", (R, D), BF),
        ("dx", (R, D), BF),
        ("down", (FS, D), F32),
        ("up", (S, GROUPS * FS), F32),
        ("out", (S, D), F32),
        ("q", (S, D), F32),
        ("k", (S, D), F32),
        ("v", (S, D), F32),
    ]
    vectors = [("vec%d" % i, size) for i, size in enumerate([S] * 8 + [FS])]
    names = ["y", "dx", "da", "db", "up", "out", "qkv", "vec"]
    names += [name + "_o" for name, shape, dtype in big] + [name for name, size in vectors]
    names += [name + "_b" for name, shape, dtype in big[2:]] + ["sems"]
    wide = pl.pallas_call(
        partial(widen_kernel, S, names),
        in_specs=[vmem] * 8,
        out_specs=[anywhere] * len(big) + [vmem] * len(vectors),
        out_shape=[jax.ShapeDtypeStruct(shape, dtype) for name, shape, dtype in big]
        + [jax.ShapeDtypeStruct((size,), F32) for name, size in vectors],
        scratch_shapes=[pltpu.VMEM(shape, dtype) for name, shape, dtype in big[2:]]
        + [pltpu.SemaphoreType.DMA((18,))],
        compiler_params=pltpu.CompilerParams(vmem_limit_bytes=24000000),
        name="widen",
    )(y, dx, g_da, g_db, g_up, g_out, g_qkv, vec)
    y, dx, down, up, out, q, k, v, n1g, n1b, bo, n2g, n2b, bd, bq, bv, bup = wide
    return (
        y[None], dx[None], n1g, n1b, q, bq, k, v, bv, out, bo, n2g, n2b, up, bup, down, bd,
    )


def solution(mesh):
    in_specs = (
        P("wsh", "ctx", None),
        P("wsh", None),
        P("wsh", "ctx", None),
        P("wsh"),
        P("wsh"),
        P("wsh", None),
        P("wsh"),
        P("wsh", None),
        P("wsh", None),
        P("wsh"),
        P("wsh", None),
        P("wsh"),
        P("wsh"),
        P("wsh"),
        P("wsh", None),
        P("wsh"),
        P("wsh", None),
        P("wsh"),
    )
    out_specs = (
        P("wsh", "ctx", None),
        P("wsh", "ctx", None),
        P("wsh"),
        P("wsh"),
        P("wsh", None),
        P("wsh"),
        P("wsh", None),
        P("wsh", None),
        P("wsh"),
        P("wsh", None),
        P("wsh"),
        P("wsh"),
        P("wsh"),
        P("wsh", None),
        P("wsh"),
        P("wsh", None),
        P("wsh"),
    )
    sizes = (mesh.shape["ctx"], mesh.shape["wsh"])
    body = partial(fast_device, sizes) if sizes == (2 * GROUPS, GROUPS) else per_device
    return jax.shard_map(
        body, mesh=mesh, in_specs=in_specs, out_specs=out_specs, check_vma=False
    )
```
